32 devices in a mesh: dp: 8 (over z, y), tensor: 4 (over x, core).
Axes of the slice: x: 2, y: 2, z: 4, core: 2. Of those that a mesh axis runs over, the one named last changes fastest.
Arguments:
- tokens: bfloat16 [16384, 1024], P(('dp', 'tensor')), may hold values from -6 to 6
- output_cotangent: bfloat16 [16384, 1024], P(('dp', 'tensor')), may hold values from -6 to 6
- lengths: int32 [8], P('dp'), may hold values from 1024 to 2048, as said below
- block_place: int32 [8, 32], P('dp'), may hold values from 0 to 31, each once within a row
- random_blocks: int32 [8, 16, 32, 3], P('dp', 'tensor'), may hold values from 0 to 31
- qkv_weight: bfloat16 [1024, 3, 1024], P('dp', None, 'tensor'), may hold values from -0.1875 to 0.1875
- out_weight: bfloat16 [1024, 1024], P('dp', 'tensor'), may hold values from -0.75 to 0.75
- up_weight: bfloat16 [1024, 4096], P('dp', 'tensor'), may hold values from -0.1875 to 0.1875
- down_weight: bfloat16 [1024, 4096], P('dp', 'tensor'), may hold values from -0.09375 to 0.09375
- vectors: float32 [8, 1024], P(None, ('dp', 'tensor')), may hold values from -2 to 2
- hidden_bias: float32 [1, 4096], P(None, ('dp', 'tensor')), may hold values from -3 to 3
Outputs:
- output: bfloat16 [16384, 1024], P(('dp', 'tensor'))
- input_grad: bfloat16 [16384, 1024], P(('dp', 'tensor'))
- qkv_weight_grad: float32 [1024, 3, 1024], P('dp', None, 'tensor')
- out_weight_grad: float32 [1024, 1024], P('dp', 'tensor')
- up_weight_grad: float32 [1024, 4096], P('dp', 'tensor')
- down_weight_grad: float32 [1024, 4096], P('dp', 'tensor')
- vectors_grad: float32 [8, 1024], P(None, ('dp', 'tensor'))
- hidden_bias_grad: float32 [1, 4096], P(None, ('dp', 'tensor'))
The draws below stay inside these ranges and needn't reach their ends.
Inputs may be any that keep to these rules, and one draw needn't show every extreme that they name: `lengths`: one sequence has exactly 2048 tokens. `block_place`: each row is a permutation.
All inputs are finite; a program needn't handle non-finite values.
Results may differ from the reference program's by a relative error of at most 0.015.
Values may be sent and summed in bfloat16 or wider, within the bound.
No kernel may reach another device: no remote copies, remote signals or barrier semaphores. Data moves between devices by JAX's collectives and lax.ppermute only.
A program may use at most 192 MiB of HBM per device.

```python
import jax
import jax.numpy as jnp
from jax import lax

D = 1024
HEADS = 16
HEAD_DIM = 64
FF = 4096
BLOCK = 64
RAND = 3
SLOT = 2048
NBLK = 32
SEQS = 8
TOKENS = 16384
LEAST = 1024


def draw_lengths(key, part):
    key_values, key_place = jax.random.split(key)
    drawn_lengths = jax.random.randint(key_values, (SEQS,), LEAST, SLOT + 1)
    full_index = jax.random.randint(key_place, (), 0, SEQS)
    return jnp.where(jnp.arange(SEQS) == full_index, SLOT, drawn_lengths).astype(jnp.int32)


def draw_vectors(key, part):
    base_draw = jnp.clip(jax.random.normal(key, (8, D), jnp.float32), -4.0, 4.0)
    row_number = jnp.arange(8)[:, None]
    gain_rows = (row_number == 0) | (row_number == 2)
    return jnp.where(gain_rows, 1.0 + 0.2 * base_draw, 0.5 * base_draw).astype(jnp.float32)


def with_ends(values, stream_key, low, largest):
    longest = values.shape.index(max(values.shape))
    spots = []
    for shift in (0, 1):
        where = [jax.random.randint(jax.random.fold_in(stream_key, axis), (), 0, length) for axis, length in enumerate(values.shape)]
        where[longest] = (where[longest] + shift) % values.shape[longest]
        spots.append(tuple(where))
    return values.at[spots[0]].set(low).at[spots[1]].set(largest)


def block_scale(rng, dims, cuts, low, high):
    loudness = 1.0
    for position, parts in cuts:
        heights = jax.random.uniform(jax.random.fold_in(jax.random.fold_in(rng, 6), position), (parts,), jnp.float32, low / len(cuts), high / len(cuts))
        loudness = loudness * jnp.repeat(jnp.exp(heights), dims[position] // parts).reshape((-1,) + (1,) * (len(dims) - 1 - position))
    return loudness


def scatter_about(rng, dims, deviation, most, shards=(), kind=jnp.bfloat16):
    gain = block_scale(rng, dims, shards, -0.22, 0.18) if shards else 1.0
    array = jax.random.normal(rng, dims, jnp.float32) * deviation * gain
    return jnp.minimum(jnp.maximum(array, -most), most).astype(kind)


def setup_inputs(seed: int = 0) -> dict:
    keys = jax.random.split(jax.random.key(seed), 12)
    tokens = scatter_about(keys[0], (TOKENS, D), 1.0, 6.0, ((0, 32),))
    output_cotangent = scatter_about(keys[1], (TOKENS, D), 1.0, 6.0, ((0, 32),))
    lengths = draw_lengths(jax.random.fold_in(keys[11], 71), 0)
    block_place = jax.vmap(lambda own: jax.random.permutation(own, NBLK))(jax.random.split(keys[3], SEQS)).reshape((SEQS, NBLK)).astype(jnp.int32)
    random_blocks = with_ends(jax.random.randint(keys[4], (SEQS, HEADS, NBLK, RAND), 0, NBLK), jax.random.fold_in(keys[4], 1), 0, NBLK - 1).astype(jnp.int32)
    qkv_weight = scatter_about(keys[5], (D, 3, D), D ** -0.5, 0.1875, ((0, 8), (2, 4)))
    out_weight = scatter_about(keys[6], (D, D), (D // 16) ** -0.5, 0.75, ((0, 8), (1, 4)))
    up_weight = scatter_about(keys[7], (D, FF), D ** -0.5, 0.1875, ((0, 8), (1, 4)))
    down_weight = scatter_about(keys[8], (D, FF), FF ** -0.5, 0.09375, ((0, 8), (1, 4)))
    vectors = draw_vectors(jax.random.fold_in(keys[11], 71), 0)
    hidden_bias = scatter_about(keys[10], (1, FF), 0.5, 3.0, ((1, 32),), jnp.float32)
    return {"tokens": tokens, "output_cotangent": output_cotangent, "lengths": lengths, "block_place": block_place, "random_blocks": random_blocks, "qkv_weight": qkv_weight, "out_weight": out_weight, "up_weight": up_weight, "down_weight": down_weight, "vectors": vectors, "hidden_bias": hidden_bias}


EPS = 1e-05
NEGATIVE = -1e+30
HIGHEST = lax.Precision.HIGHEST

@jax.custom_vjp
def low(v):
    return lax.optimization_barrier(v.astype(jnp.bfloat16)).astype(jnp.float32)

@jax.custom_vjp
def low_back(v):
    return v

def low_keep(v):
    return (low(v), None)

def low_pass(kept, grad):
    return (grad,)

def back_keep(v):
    return (v, None)

def back_low(kept, grad):
    return (low(grad),)
low.defvjp(low_keep, low_pass)
low_back.defvjp(back_keep, back_low)

def layer_norm(input_rows, gain_row, shift_row):
    centred = input_rows - lax.optimization_barrier(jnp.mean(input_rows, axis=-1, keepdims=True))
    variance = lax.optimization_barrier(jnp.mean(centred * centred, axis=-1, keepdims=True))
    return centred * lax.rsqrt(variance + EPS) * gain_row + shift_row

def block_masks(length, placing, chosen):
    nblocks = (length + BLOCK - 1) // BLOCK
    query_seq = placing[:, None]
    key_seq = placing[None, :]
    common = (query_seq == 0) | (query_seq == nblocks - 1) | (key_seq == 0) | (key_seq == nblocks - 1) | (jnp.abs(query_seq - key_seq) <= 1)
    by_query = jnp.take(chosen, placing, axis=1)
    random_hit = jnp.any(by_query[:, :, None, :] == key_seq[None, :, :, None], axis=-1)
    allowed = common[None] | random_hit
    positions = placing[:, None] * BLOCK + jnp.arange(BLOCK, dtype=jnp.int32)[None, :]
    return (allowed, positions < length)

def attend_slot(queries, key_rows, value_rows, allowed, key_valid):
    tile_rows = min(512, SLOT)
    per_tile = tile_rows // BLOCK
    score_scale = HEAD_DIM ** (-0.5)

    def one_tile(number):
        query_tile = lax.dynamic_slice_in_dim(queries, number * tile_rows, tile_rows, 0)
        allowed_tile = lax.dynamic_slice_in_dim(allowed, number * per_tile, per_tile, 1)
        scores = low_back(jnp.einsum('qhd,khd->hqk', query_tile, key_rows, precision=HIGHEST) * score_scale)
        scores = scores.reshape(HEADS, per_tile, BLOCK, NBLK, BLOCK)
        keep_mask = allowed_tile[:, :, None, :, None] & key_valid[None, None, None, :, :]
        scores = jnp.where(keep_mask, scores, NEGATIVE).reshape(HEADS, tile_rows, SLOT)
        row_top = lax.optimization_barrier(jnp.max(scores, axis=-1, keepdims=True))
        weights = jnp.exp(scores - row_top)
        probabilities = low(weights / lax.optimization_barrier(jnp.sum(weights, axis=-1, keepdims=True)))
        return jnp.einsum('hqk,khd->qhd', probabilities, value_rows, precision=HIGHEST)
    context_tiles = lax.map(jax.checkpoint(one_tile), jnp.arange(SLOT // tile_rows, dtype=jnp.int32))
    return context_tiles.reshape(SLOT, HEADS * HEAD_DIM)

def slot_forward(residual_in, length, placing, chosen, qkv_weight, out_weight, up_weight, down_weight, vectors, hidden_bias):
    allowed, key_valid = block_masks(length, placing, chosen)
    normed_one = low(layer_norm(residual_in, vectors[0], vectors[1]))
    projected = jnp.einsum('td,dcf->ctf', normed_one, qkv_weight, precision=HIGHEST)
    head_shape = (SLOT, HEADS, HEAD_DIM)
    queries = low(low_back(projected[0] + vectors[6])).reshape(head_shape)
    key_rows = low(low_back(projected[1])).reshape(head_shape)
    value_rows = low(low_back(projected[2] + vectors[7])).reshape(head_shape)
    context = low(low_back(attend_slot(queries, key_rows, value_rows, allowed, key_valid)))
    attended = low_back(jnp.einsum('tf,df->td', context, out_weight, precision=HIGHEST))
    middle = residual_in + attended + vectors[4]
    normed_two = low(layer_norm(middle, vectors[2], vectors[3]))
    hidden = low_back(jnp.dot(normed_two, up_weight, precision=HIGHEST) + hidden_bias[0])
    active = low(jax.nn.gelu(hidden, approximate=True))
    return middle + jnp.einsum('tf,df->td', active, down_weight, precision=HIGHEST) + vectors[5]

def reference(tokens, output_cotangent, lengths, block_place, random_blocks, qkv_weight, out_weight, up_weight, down_weight, vectors, hidden_bias):
    weight_set = (qkv_weight.astype(jnp.float32), out_weight.astype(jnp.float32), up_weight.astype(jnp.float32), down_weight.astype(jnp.float32), vectors.astype(jnp.float32), hidden_bias.astype(jnp.float32))
    input_rows = tokens.astype(jnp.float32).reshape(SEQS, SLOT, D)

    def whole(rows_all, weights_all):

        def one_slot(packed):
            residual_in, length, placing, chosen = packed
            return slot_forward(residual_in, length, placing, chosen, *weights_all)
        return lax.map(jax.checkpoint(one_slot), (rows_all, lengths, block_place, random_blocks))
    outputs, pullback = jax.vjp(whole, input_rows, weight_set)
    grad_inputs, grad_weights = pullback(output_cotangent.astype(jnp.float32).reshape(SEQS, SLOT, D))
    return (outputs.reshape(TOKENS, D).astype(jnp.bfloat16), grad_inputs.reshape(TOKENS, D).astype(jnp.bfloat16), grad_weights[0], grad_weights[1], grad_weights[2], grad_weights[3], grad_weights[4], grad_weights[5])
```

```python
import functools

import jax
import jax.numpy as jnp
from jax import lax
from jax.experimental import pallas as pl
from jax.experimental.pallas import tpu as pltpu
from jax.sharding import PartitionSpec as P

HEAD_DIM = 64
BLOCK = 64
PAIR = 2 * HEAD_DIM
SLOTS = 8
CHUNK = 512
EPS = 1e-05
NEGATIVE = -1e30
F32 = jnp.float32
BF16 = jnp.bfloat16
NT = (((1,), (1,)), ((), ()))
NN = (((1,), (0,)), ((), ()))
TN = (((0,), (0,)), ((), ()))


def matmul(left, right, dims):
    return lax.dot_general(left, right, dims, preferred_element_type=F32)


def swapped(value, axis, bit):
    count = lax.axis_size(axis)
    return lax.ppermute(value, axis, [(i, i ^ bit) for i in range(count)])


def bits_of(axis):
    count = lax.axis_size(axis)
    return [1 << b for b in range(count.bit_length() - 1)]


def gathered_parts(value, axis):
    parts = {0: value}
    for bit in reversed(bits_of(axis)):
        parts.update({k | bit: swapped(p, axis, bit) for k, p in list(parts.items())})
    return [parts[k] for k in range(len(parts))]


def summed_part(parts, axis):
    left = dict(enumerate(parts))
    for bit in bits_of(axis):
        kept = {}
        for k in sorted(left, reverse=True):
            if k & bit == 0:
                arrived = swapped(left[k | bit].astype(BF16), axis, bit)
                kept[k] = left[k].astype(F32) + arrived.astype(F32)
        left = kept
    return left[0]


def exchanged_parts(parts, axis):
    return [p if k == 0 else swapped(p, axis, k) for k, p in enumerate(parts)]


def summed_everywhere(value, axes):
    size = value.shape[0]
    value = jnp.pad(value, (0, -size % 1024)).reshape(-1, 128)
    for axis in axes:
        for bit in bits_of(axis):
            value = value + swapped(value, axis, bit)
    return value.reshape(-1)[:size]


def sent_and_summed(value, axis):
    count = lax.axis_size(axis)
    blocks = value.reshape(count, value.shape[0] // count, *value.shape[1:])
    arrived = lax.all_to_all(blocks, axis, 0, 0, tiled=True)
    return jnp.sum(arrived.astype(F32), axis=0)


def attention_tables(length, place, chosen):
    count = place.shape[0]
    heads = chosen.shape[0]
    nblocks = (length + BLOCK - 1) // BLOCK
    last = nblocks - 1
    number = jnp.arange(count, dtype=jnp.int32)
    same = jnp.zeros_like(number)
    common = jnp.stack([same, same + last, number - 1, number, number + 1], axis=1)
    middle = (number > 0) & (number < last)
    good = jnp.stack(
        [
            middle | (number > last),
            middle | (number > last),
            (number - 1 > 0) & (number - 1 < last) & (number != last),
            middle,
            (number + 1 < last) & (number > 0),
        ],
        axis=1,
    )
    drawn = jnp.transpose(chosen, (1, 2, 0))
    away = number[:, None, None]
    fresh = (
        (drawn > 0)
        & (drawn < last)
        & (jnp.abs(drawn - away) > 1)
        & (away > 0)
        & (away != last)
    )
    first, second, third = drawn[:, 0], drawn[:, 1], drawn[:, 2]
    fresh = jnp.stack(
        [
            fresh[:, 0],
            fresh[:, 1] & (second != first),
            fresh[:, 2] & (third != first) & (third != second),
        ],
        axis=1,
    )
    flags = jnp.concatenate(
        [jnp.broadcast_to(good[:, :, None], (count, 5, heads)), fresh], axis=1
    )
    bias = jnp.where(flags, 0.0, NEGATIVE).astype(F32)
    bias = jnp.broadcast_to(bias[..., None], (*bias.shape, HEAD_DIM))
    bias = bias.reshape(count, SLOTS, heads * HEAD_DIM)
    wanted = jnp.concatenate([common, drawn.reshape(count, -1)], axis=1)
    hit = wanted[:, :, None] == place[None, None, :]
    stored = jnp.sum(jnp.where(hit, number[None, None, :], 0), axis=-1).astype(jnp.int32)
    limits = jnp.clip(length - BLOCK * place, 0, BLOCK).astype(jnp.int32)
    ends = jnp.stack([last, length - BLOCK * last]).astype(jnp.int32)
    return stored, limits, ends, bias


def block_rows(index):
    return pl.ds(pl.multiple_of(index * BLOCK, BLOCK), BLOCK)


def spread(rows, heads):
    lane = lax.broadcasted_iota(jnp.int32, (1, heads * HEAD_DIM), 1)
    zero = jnp.zeros_like(rows)
    return jnp.concatenate(
        [jnp.where(lane // HEAD_DIM == h, rows, zero) for h in range(heads)], axis=0
    )


def collapse(full, heads):
    lane = lax.broadcasted_iota(jnp.int32, (1, PAIR), 1)
    pieces = []
    for pair in range(heads // 2):
        cols = slice(PAIR * pair, PAIR * (pair + 1))
        even = full[2 * pair * HEAD_DIM : (2 * pair + 1) * HEAD_DIM, cols]
        odd = full[(2 * pair + 1) * HEAD_DIM : (2 * pair + 2) * HEAD_DIM, cols]
        pieces.append(jnp.where(lane < HEAD_DIM, even, odd))
    return jnp.concatenate(pieces, axis=1)


def gathered_keys(ref, start, stored, number, heads):
    width = heads * HEAD_DIM
    lane = lax.broadcasted_iota(jnp.int32, (1, PAIR), 1)
    parts = [ref[block_rows(stored[number, s]), start : start + width] for s in range(5)]
    for s in range(3):
        pieces = []
        for pair in range(heads // 2):
            cols = slice(start + PAIR * pair, start + PAIR * (pair + 1))
            at = 5 + heads * s + 2 * pair
            even = ref[block_rows(stored[number, at]), cols]
            odd = ref[block_rows(stored[number, at + 1]), cols]
            pieces.append(jnp.where(lane < HEAD_DIM, even, odd))
        parts.append(jnp.concatenate(pieces, axis=1))
    return jnp.concatenate(parts, axis=0)


def slot(value, index):
    return value[BLOCK * index : BLOCK * (index + 1)]


def biased(scores, bias, last_rows):
    row = lax.broadcasted_iota(jnp.int32, (BLOCK, 1), 0)
    parts = [slot(scores, s) + bias[s : s + 1] for s in range(SLOTS)]
    parts[1] = jnp.where(row < last_rows, parts[1], NEGATIVE)
    return parts


def total(parts):
    return functools.reduce(jnp.add, parts)


def attend_kernel(heads, stored, limits, ends, qkv_ref, bias_ref, out_ref, log_ref, keep_ref):
    count = bias_ref.shape[0]
    width = heads * HEAD_DIM
    scale = jnp.asarray(HEAD_DIM**-0.5, BF16)

    def item(number):
        here = block_rows(stored[number, 3])
        queries = spread(qkv_ref[here, :width] * scale, heads)
        keys = gathered_keys(qkv_ref, width, stored, number, heads)
        parts = biased(matmul(keys, queries, NT), bias_ref[number], ends[1])
        top = jnp.max(functools.reduce(jnp.maximum, parts), axis=0, keepdims=True)
        weights = [jnp.exp(p - top) for p in parts]
        row_total = jnp.sum(total(weights), axis=0, keepdims=True)
        inverse = 1.0 / row_total
        probs = jnp.concatenate([(p * inverse).astype(BF16) for p in weights], axis=0)
        values = gathered_keys(qkv_ref, 2 * width, stored, number, heads)
        out_ref[here, :] = collapse(matmul(probs, values, TN), heads).astype(BF16)
        log_ref[pl.ds(number, 1), :] = top + jnp.log(row_total)

    def step(number, carry):
        item(number)
        return carry

    lax.fori_loop(1, count, step, 0)

    row = lax.broadcasted_iota(jnp.int32, (BLOCK, 1), 0)
    per = CHUNK // BLOCK
    chunks = count // per

    def chunk_rows(chunk):
        return pl.ds(pl.multiple_of(chunk * CHUNK, CHUNK), CHUNK)

    for end in range(2):
        number = 0 if end == 0 else ends[0]
        here = block_rows(stored[number, 3])
        queries = spread(qkv_ref[here, :width] * scale, heads)

        def scores(chunk, top):
            at = chunk_rows(chunk)
            found = matmul(qkv_ref[at, width : 2 * width], queries, NT)
            parts = [
                jnp.where(row < limits[chunk * per + s], slot(found, s), NEGATIVE)
                for s in range(per)
            ]
            keep_ref[at, :] = jnp.concatenate(parts, axis=0)
            return jnp.maximum(top, functools.reduce(jnp.maximum, parts))

        top = lax.fori_loop(0, chunks, scores, jnp.full((BLOCK, width), NEGATIVE, F32))
        top = jnp.max(top, axis=0, keepdims=True)

        def exponents(chunk, row_total):
            at = chunk_rows(chunk)
            weights = jnp.exp(keep_ref[at, :] - top)
            keep_ref[at, :] = weights
            return row_total + total([slot(weights, s) for s in range(per)])

        row_total = lax.fori_loop(0, chunks, exponents, jnp.zeros((BLOCK, width), F32))
        row_total = jnp.sum(row_total, axis=0, keepdims=True)
        inverse = 1.0 / row_total

        def contexts(chunk, found):
            at = chunk_rows(chunk)
            probs = (keep_ref[at, :] * inverse).astype(BF16)
            return found + matmul(probs, qkv_ref[at, 2 * width :], TN)

        found = lax.fori_loop(0, chunks, contexts, jnp.zeros((width, width), F32))
        out_ref[here, :] = collapse(found, heads).astype(BF16)
        log_ref[pl.ds(number, 1), :] = top + jnp.log(row_total)


def attend_back_kernel(
    heads,
    stored,
    limits,
    ends,
    qkv_ref,
    grad_ref,
    bias_ref,
    log_ref,
    out_ref,
    keys_acc,
    values_acc,
    probs_ref,
    inner_ref,
):
    count = bias_ref.shape[0]
    width = heads * HEAD_DIM
    scale = jnp.asarray(HEAD_DIM**-0.5, BF16)
    lane = lax.broadcasted_iota(jnp.int32, (1, PAIR), 1)
    keys_acc[...] = jnp.zeros_like(keys_acc)
    values_acc[...] = jnp.zeros_like(values_acc)

    def accumulate(acc, value, number):
        for s in range(5):
            acc[block_rows(stored[number, s]), :] += slot(value, s)
        for s in range(3):
            for h in range(heads):
                cols = slice(PAIR * (h // 2), PAIR * (h // 2 + 1))
                mine = (lane < HEAD_DIM) == (h % 2 == 0)
                term = jnp.where(mine, slot(value, 5 + s)[:, cols], 0.0)
                acc[block_rows(stored[number, 5 + heads * s + h]), cols] += term

    def item(number):
        here = block_rows(stored[number, 3])
        queries = spread(qkv_ref[here, :width] * scale, heads)
        grads = spread(grad_ref[here, :], heads)
        keys = gathered_keys(qkv_ref, width, stored, number, heads)
        values = gathered_keys(qkv_ref, 2 * width, stored, number, heads)
        log_total = log_ref[pl.ds(number, 1), :]
        parts = biased(matmul(keys, queries, NT), bias_ref[number], ends[1])
        probs = [jnp.exp(p - log_total) for p in parts]
        found = matmul(values, grads, NT)
        found = [slot(found, s) for s in range(SLOTS)]
        inner = total([p * d for p, d in zip(probs, found)])
        inner = jnp.sum(inner, axis=0, keepdims=True)
        grad_scores = jnp.concatenate(
            [(p * (d - inner)).astype(BF16) for p, d in zip(probs, found)], axis=0
        )
        probs_low = jnp.concatenate([p.astype(BF16) for p in probs], axis=0)
        accumulate(values_acc, matmul(probs_low, grads, NN), number)
        accumulate(keys_acc, matmul(grad_scores, queries, NN), number)
        grad_queries = collapse(matmul(grad_scores, keys, TN), heads) * HEAD_DIM**-0.5
        out_ref[here, :width] = grad_queries.astype(BF16)

    def step(number, carry):
        item(number)
        return carry

    lax.fori_loop(1, count, step, 0)

    row = lax.broadcasted_iota(jnp.int32, (BLOCK, 1), 0)
    per = CHUNK // BLOCK
    chunks = count // per

    def chunk_rows(chunk):
        return pl.ds(pl.multiple_of(chunk * CHUNK, CHUNK), CHUNK)

    for end in range(2):
        number = 0 if end == 0 else ends[0]
        here = block_rows(stored[number, 3])
        queries = spread(qkv_ref[here, :width] * scale, heads)
        grads = spread(grad_ref[here, :], heads)
        log_total = log_ref[pl.ds(number, 1), :]

        def first(chunk, inner):
            at = chunk_rows(chunk)
            scores = matmul(qkv_ref[at, width : 2 * width], queries, NT)
            parts = [
                jnp.where(row < limits[chunk * per + s], slot(scores, s), NEGATIVE)
                for s in range(per)
            ]
            probs = jnp.exp(jnp.concatenate(parts, axis=0) - log_total)
            found = matmul(qkv_ref[at, 2 * width :], grads, NT)
            probs_ref[at, :] = probs
            inner_ref[at, :] = found
            both = probs * found
            return inner + total([slot(both, s) for s in range(per)])

        inner = lax.fori_loop(0, chunks, first, jnp.zeros((BLOCK, width), F32))
        inner = jnp.sum(inner, axis=0, keepdims=True)

        def second(chunk, grad_queries):
            at = chunk_rows(chunk)
            probs = probs_ref[at, :]
            grad_scores = (probs * (inner_ref[at, :] - inner)).astype(BF16)
            values_acc[at, :] += matmul(probs.astype(BF16), grads, NN)
            keys_acc[at, :] += matmul(grad_scores, queries, NN)
            return grad_queries + matmul(grad_scores, qkv_ref[at, width : 2 * width], TN)

        found = lax.fori_loop(0, chunks, second, jnp.zeros((width, width), F32))
        out_ref[here, :width] = (collapse(found, heads) * HEAD_DIM**-0.5).astype(BF16)

    out_ref[:, width : 2 * width] = keys_acc[...].astype(BF16)
    out_ref[:, 2 * width :] = values_acc[...].astype(BF16)


def in_smem():
    return pl.BlockSpec(memory_space=pltpu.SMEM)


def in_vmem():
    return pl.BlockSpec(memory_space=pltpu.VMEM)


def attention_cost(qkv, matmuls):
    rows, width = qkv.shape
    width //= 3
    return pl.CostEstimate(
        flops=2 * matmuls * rows * CHUNK * width,
        bytes_accessed=12 * rows * width,
        transcendentals=rows * CHUNK * width // HEAD_DIM,
    )


def attend(qkv, tables, heads):
    stored, limits, ends, bias = tables
    rows, width = qkv.shape[0], heads * HEAD_DIM
    return pl.pallas_call(
        functools.partial(attend_kernel, heads),
        out_shape=(
            jax.ShapeDtypeStruct((rows, width), BF16),
            jax.ShapeDtypeStruct((rows // BLOCK, width), F32),
        ),
        in_specs=[in_smem()] * 3 + [in_vmem()] * 2,
        out_specs=(in_vmem(), in_vmem()),
        scratch_shapes=[pltpu.VMEM((rows, width), F32)],
        compiler_params=pltpu.CompilerParams(vmem_limit_bytes=32 << 20),
        cost_estimate=attention_cost(qkv, 8),
        name="attend",
    )(stored, limits, ends, qkv, bias)


def attend_back(qkv, grad_context, log_totals, tables, heads):
    stored, limits, ends, bias = tables
    rows, width = qkv.shape[0], heads * HEAD_DIM
    return pl.pallas_call(
        functools.partial(attend_back_kernel, heads),
        out_shape=jax.ShapeDtypeStruct(qkv.shape, BF16),
        in_specs=[in_smem()] * 3 + [in_vmem()] * 4,
        out_specs=in_vmem(),
        scratch_shapes=[pltpu.VMEM((rows, width), F32)] * 4,
        compiler_params=pltpu.CompilerParams(vmem_limit_bytes=32 << 20),
        cost_estimate=attention_cost(qkv, 16),
        name="attend_back",
    )(stored, limits, ends, qkv, grad_context, bias, log_totals)


def unit_rows(rows):
    centred = rows - jnp.mean(rows, axis=-1, keepdims=True)
    inverse = lax.rsqrt(jnp.mean(centred * centred, axis=-1, keepdims=True) + EPS)
    return centred * inverse, inverse


def norm_back(grad_normed, unit, inverse, gain):
    grad_unit = grad_normed * gain
    return inverse * (
        grad_unit
        - jnp.mean(grad_unit, axis=-1, keepdims=True)
        - unit * jnp.mean(grad_unit * unit, axis=-1, keepdims=True)
    )


def gelu_tanh(pre_active):
    return jax.nn.gelu(pre_active, approximate=True)


def per_device(
    tokens,
    output_cotangent,
    lengths,
    block_place,
    random_blocks,
    qkv_weight,
    out_weight,
    up_weight,
    down_weight,
    vectors,
    hidden_bias,
):
    ways = lax.axis_size("tensor")
    spread_ways = lax.axis_size("dp")
    position = lax.axis_index("tensor")
    index = lax.axis_index("dp") * ways + position
    near = tokens.shape[0]
    rows = near * ways
    features = tokens.shape[1]
    width = qkv_weight.shape[2]
    heads = width // HEAD_DIM
    units = up_weight.shape[1]
    own = features // spread_ways
    piece = vectors.shape[1]
    unit_piece = hidden_bias.shape[1]

    def quarters(value):
        return [value[k * near : (k + 1) * near] for k in range(ways)]

    residual = tokens.astype(F32)
    unit_one, inverse_one = unit_rows(residual)
    unit_all = jnp.concatenate(gathered_parts(unit_one.astype(BF16), "tensor"), axis=0)

    qkv_flat = qkv_weight.reshape(own, 3 * width)
    qkv_full = lax.all_gather(qkv_flat, "dp", axis=0, tiled=True)
    out_group = lax.all_gather(out_weight, "dp", axis=0, tiled=True)
    up_full = lax.all_gather(up_weight, "dp", axis=0, tiled=True)
    down_full = lax.all_gather(down_weight, "dp", axis=0, tiled=True)

    small = jnp.zeros((8, features), F32)
    small = lax.dynamic_update_slice(small, vectors, (0, index * piece))
    small_hidden = jnp.zeros((1, units * ways), F32)
    small_hidden = lax.dynamic_update_slice(small_hidden, hidden_bias, (0, index * unit_piece))
    packed = jnp.concatenate([small.reshape(-1), small_hidden.reshape(-1)])
    packed = summed_everywhere(packed, ("tensor", "dp"))
    vectors_full = packed[: 8 * features].reshape(8, features)
    hidden_full = packed[8 * features :]
    bias_query = lax.dynamic_slice_in_dim(vectors_full[6], position * width, width)
    bias_value = lax.dynamic_slice_in_dim(vectors_full[7], position * width, width)
    bias_qkv = jnp.concatenate([bias_query, jnp.zeros_like(bias_query), bias_value])
    bias_hidden = lax.dynamic_slice_in_dim(hidden_full, position * units, units)

    placed = block_place[0].reshape(ways, -1)
    order = position ^ jnp.arange(ways, dtype=jnp.int32)
    chosen_rows = order[:, None, None] == jnp.arange(ways, dtype=jnp.int32)[None, :, None]
    place = jnp.sum(jnp.where(chosen_rows, placed[None], 0), axis=1).reshape(-1)
    tables = attention_tables(lengths[0], place, random_blocks[0])

    normed_one_all = (unit_all.astype(F32) * vectors_full[0] + vectors_full[1]).astype(BF16)
    qkv = (matmul(normed_one_all, qkv_full, NN) + bias_qkv).astype(BF16)
    context, log_totals = attend(qkv, tables, heads)

    out_all = jnp.concatenate(gathered_parts(out_group, "tensor"), axis=1)
    context_near = jnp.concatenate(exchanged_parts(quarters(context), "tensor"), axis=1)
    middle = residual + matmul(context_near, out_all, NT) + vectors_full[4]
    unit_two, inverse_two = unit_rows(middle)
    normed_two = (unit_two * vectors_full[2] + vectors_full[3]).astype(BF16)
    normed_two_all = jnp.concatenate(gathered_parts(normed_two, "tensor"), axis=0)
    grad_all = jnp.concatenate(gathered_parts(output_cotangent, "tensor"), axis=0)

    hidden = matmul(normed_two_all, up_full, NN) + bias_hidden
    active, gelu_pullback = jax.vjp(gelu_tanh, hidden)
    active = active.astype(BF16)
    grad_hidden = gelu_pullback(matmul(grad_all, down_full, NN))[0].astype(BF16)
    grad_normed_two = summed_part(quarters(matmul(grad_hidden, up_full, NT)), "tensor")
    feed_out = summed_part(quarters(matmul(active, down_full, NT)), "tensor")
    output = (middle + feed_out + vectors_full[5]).astype(BF16)
    up_weight_grad = sent_and_summed(matmul(normed_two_all, grad_hidden, TN).astype(BF16), "dp")
    down_weight_grad = sent_and_summed(matmul(grad_all, active, TN).astype(BF16), "dp")
    sum_hidden = jnp.sum(grad_hidden, axis=0, dtype=F32)

    cotangent = output_cotangent.astype(F32)
    grad_middle = cotangent + norm_back(grad_normed_two, unit_two, inverse_two, vectors_full[2])
    grad_attended = grad_middle.astype(BF16)
    grad_heads = matmul(grad_attended, out_all, NN).astype(BF16)
    grad_heads = [grad_heads[:, k * width : (k + 1) * width] for k in range(ways)]
    grad_context = jnp.concatenate(exchanged_parts(grad_heads, "tensor"), axis=0)
    grad_qkv = attend_back(qkv, grad_context, log_totals, tables, heads)

    raw_qkv = matmul(unit_all, grad_qkv, TN)
    sum_qkv = jnp.sum(grad_qkv, axis=0, dtype=F32)
    qkv_wide = qkv_full.astype(F32)
    gain_one = jnp.sum(raw_qkv * qkv_wide, axis=1)
    shift_one = jnp.sum(sum_qkv * qkv_wide, axis=1)
    grad_normed_one = summed_part(quarters(matmul(grad_qkv, qkv_full, NT)), "tensor")
    out_grad = matmul(grad_attended, context_near, TN)
    out_grad = [out_grad[:, k * width : (k + 1) * width] for k in range(ways)]
    out_grad = summed_part(out_grad, "tensor").astype(BF16)
    sent = jnp.concatenate([raw_qkv.astype(BF16), out_grad], axis=1)
    arrived = sent_and_summed(sent, "dp")

    input_grad = (
        grad_middle + norm_back(grad_normed_one, unit_one, inverse_one, vectors_full[0])
    ).astype(BF16)

    by_feature = jnp.stack(
        [
            gain_one,
            shift_one,
            jnp.sum(grad_normed_two * unit_two, axis=0),
            jnp.sum(grad_normed_two, axis=0),
            jnp.sum(grad_middle, axis=0),
            jnp.sum(cotangent, axis=0),
        ]
    )
    by_feature = jnp.transpose(by_feature.reshape(6, spread_ways, own), (1, 0, 2))
    by_head = jnp.concatenate([sum_qkv, sum_hidden])
    by_head = jnp.broadcast_to(by_head[None], (spread_ways, by_head.shape[0]))
    extras = jnp.concatenate([by_feature.reshape(spread_ways, -1), by_head], axis=1)
    extras = jnp.sum(lax.all_to_all(extras, "dp", 0, 0, tiled=True), axis=0)
    sum_qkv = extras[6 * own : 6 * own + 3 * width]
    sum_hidden = extras[6 * own + 3 * width :]
    head_sums = jnp.zeros((2, features), F32)
    head_sums = lax.dynamic_update_slice(
        head_sums,
        jnp.stack([sum_qkv[:width], sum_qkv[2 * width :]]),
        (0, position * width),
    )
    hidden_sums = lax.dynamic_update_slice(
        jnp.zeros((units * ways,), F32), sum_hidden, (position * units,)
    )
    packed = jnp.concatenate([extras[: 6 * own], head_sums.reshape(-1), hidden_sums])
    packed = summed_everywhere(packed, ("tensor",))
    by_feature = packed[: 6 * own].reshape(6, own)
    head_sums = packed[6 * own : 6 * own + 2 * features].reshape(2, features)
    hidden_sums = packed[6 * own + 2 * features :]
    vectors_grad = jnp.concatenate(
        [
            lax.dynamic_slice_in_dim(by_feature, position * piece, piece, axis=1),
            lax.dynamic_slice_in_dim(head_sums, index * piece, piece, axis=1),
        ],
        axis=0,
    )
    hidden_bias_grad = lax.dynamic_slice_in_dim(hidden_sums, index * unit_piece, unit_piece)

    mine = lax.dynamic_slice_in_dim(
        vectors_full[:2], lax.axis_index("dp") * own, own, axis=1
    )
    qkv_weight_grad = mine[0][:, None] * arrived[:, : 3 * width] + mine[1][:, None] * sum_qkv
    return (
        output,
        input_grad,
        qkv_weight_grad.reshape(own, 3, width),
        arrived[:, 3 * width :],
        up_weight_grad,
        down_weight_grad,
        vectors_grad,
        hidden_bias_grad[None, :],
    )


def solution(mesh):
    placed = (
        P(("dp", "tensor"), None),
        P(("dp", "tensor"), None),
        P("dp"),
        P("dp", None),
        P("dp", "tensor", None, None),
        P("dp", None, "tensor"),
        P("dp", "tensor"),
        P("dp", "tensor"),
        P("dp", "tensor"),
        P(None, ("dp", "tensor")),
        P(None, ("dp", "tensor")),
    )
    return jax.shard_map(
        per_device,
        mesh=mesh,
        in_specs=placed,
        out_specs=(
            P(("dp", "tensor"), None),
            P(("dp", "tensor"), None),
            P("dp", None, "tensor"),
            P("dp", "tensor"),
            P("dp", "tensor"),
            P("dp", "tensor"),
            P(None, ("dp", "tensor")),
            P(None, ("dp", "tensor")),
        ),
        check_vma=False,
    )
```

```python
import functools

import jax
import jax.numpy as jnp
from jax import lax
from jax.experimental import pallas as pl
from jax.experimental.pallas import tpu as pltpu
from jax.sharding import PartitionSpec as P

HEAD_DIM = 64
BLOCK = 64
PAIR = 2 * HEAD_DIM
SLOTS = 8
CHUNK = 512
EPS = 1e-05
NEGATIVE = -1e30
F32 = jnp.float32
BF16 = jnp.bfloat16
NT = (((1,), (1,)), ((), ()))
NN = (((1,), (0,)), ((), ()))
TN = (((0,), (0,)), ((), ()))


def matmul(left, right, dims):
    return lax.dot_general(left, right, dims, preferred_element_type=F32)


def swapped(value, axis, bit):
    count = lax.axis_size(axis)
    return lax.ppermute(value, axis, [(i, i ^ bit) for i in range(count)])


def bits_of(axis):
    count = lax.axis_size(axis)
    return [1 << b for b in range(count.bit_length() - 1)]


def gathered_parts(value, axis):
    parts = {0: value}
    for bit in reversed(bits_of(axis)):
        parts.update({k | bit: swapped(p, axis, bit) for k, p in list(parts.items())})
    return [parts[k] for k in range(len(parts))]


def summed_part(parts, axis, after=None):
    left = dict(enumerate(parts))
    bits = bits_of(axis)
    for bit in bits:
        kept = {}
        for k in sorted(left, reverse=True):
            if k & bit == 0:
                going = left[k | bit].astype(BF16)
                if after is not None and bit == bits[-1]:
                    going, _ = lax.optimization_barrier((going, after))
                kept[k] = left[k].astype(F32) + swapped(going, axis, bit).astype(F32)
        left = kept
    return left[0]


def exchanged_parts(parts, axis):
    return [p if k == 0 else swapped(p, axis, k) for k, p in enumerate(parts)]


def summed_everywhere(value, axes):
    size = value.shape[0]
    value = jnp.pad(value, (0, -size % 1024)).reshape(-1, 128)
    for axis in axes:
        for bit in bits_of(axis):
            value = value + swapped(value, axis, bit)
    return value.reshape(-1)[:size]


def sent_and_summed(value, axis):
    count = lax.axis_size(axis)
    blocks = value.reshape(count, value.shape[0] // count, *value.shape[1:])
    arrived = lax.all_to_all(blocks, axis, 0, 0, tiled=True)
    return jnp.sum(arrived.astype(F32), axis=0)


def attention_tables(length, place, chosen):
    count = place.shape[0]
    heads = chosen.shape[0]
    nblocks = (length + BLOCK - 1) // BLOCK
    last = nblocks - 1
    number = jnp.arange(count, dtype=jnp.int32)
    same = jnp.zeros_like(number)
    common = jnp.stack([same, same + last, number - 1, number, number + 1], axis=1)
    middle = (number > 0) & (number < last)
    good = jnp.stack(
        [
            middle | (number > last),
            middle | (number > last),
            (number - 1 > 0) & (number - 1 < last) & (number != last),
            middle,
            (number + 1 < last) & (number > 0),
        ],
        axis=1,
    )
    drawn = jnp.transpose(chosen, (1, 2, 0))
    away = number[:, None, None]
    fresh = (
        (drawn > 0)
        & (drawn < last)
        & (jnp.abs(drawn - away) > 1)
        & (away > 0)
        & (away != last)
    )
    first, second, third = drawn[:, 0], drawn[:, 1], drawn[:, 2]
    fresh = jnp.stack(
        [
            fresh[:, 0],
            fresh[:, 1] & (second != first),
            fresh[:, 2] & (third != first) & (third != second),
        ],
        axis=1,
    )
    flags = jnp.concatenate(
        [jnp.broadcast_to(good[:, :, None], (count, 5, heads)), fresh], axis=1
    )
    bias = jnp.where(flags, 0.0, NEGATIVE).astype(F32)
    bias = jnp.broadcast_to(bias[..., None], (*bias.shape, HEAD_DIM))
    bias = bias.reshape(count, SLOTS, heads * HEAD_DIM)
    wanted = jnp.concatenate([common, drawn.reshape(count, -1)], axis=1)
    hit = wanted[:, :, None] == place[None, None, :]
    stored = jnp.sum(jnp.where(hit, number[None, None, :], 0), axis=-1).astype(jnp.int32)
    limits = jnp.clip(length - BLOCK * place, 0, BLOCK).astype(jnp.int32)
    ends = jnp.stack([last, length - BLOCK * last]).astype(jnp.int32)
    return stored, limits, ends, bias


def block_rows(index):
    return pl.ds(pl.multiple_of(index * BLOCK, BLOCK), BLOCK)


def spread(rows, heads):
    lane = lax.broadcasted_iota(jnp.int32, (1, heads * HEAD_DIM), 1)
    zero = jnp.zeros_like(rows)
    return jnp.concatenate(
        [jnp.where(lane // HEAD_DIM == h, rows, zero) for h in range(heads)], axis=0
    )


def collapse(full, heads):
    lane = lax.broadcasted_iota(jnp.int32, (1, PAIR), 1)
    pieces = []
    for pair in range(heads // 2):
        cols = slice(PAIR * pair, PAIR * (pair + 1))
        even = full[2 * pair * HEAD_DIM : (2 * pair + 1) * HEAD_DIM, cols]
        odd = full[(2 * pair + 1) * HEAD_DIM : (2 * pair + 2) * HEAD_DIM, cols]
        pieces.append(jnp.where(lane < HEAD_DIM, even, odd))
    return jnp.concatenate(pieces, axis=1)


def gathered_keys(ref, start, stored, number, heads):
    width = heads * HEAD_DIM
    lane = lax.broadcasted_iota(jnp.int32, (1, PAIR), 1)
    parts = [ref[block_rows(stored[number, s]), start : start + width] for s in range(5)]
    for s in range(3):
        pieces = []
        for pair in range(heads // 2):
            cols = slice(start + PAIR * pair, start + PAIR * (pair + 1))
            at = 5 + heads * s + 2 * pair
            even = ref[block_rows(stored[number, at]), cols]
            odd = ref[block_rows(stored[number, at + 1]), cols]
            pieces.append(jnp.where(lane < HEAD_DIM, even, odd))
        parts.append(jnp.concatenate(pieces, axis=1))
    return jnp.concatenate(parts, axis=0)


def slot(value, index):
    return value[BLOCK * index : BLOCK * (index + 1)]


def biased(scores, bias, last_rows):
    row = lax.broadcasted_iota(jnp.int32, (BLOCK, 1), 0)
    parts = [slot(scores, s) + bias[s : s + 1] for s in range(SLOTS)]
    parts[1] = jnp.where(row < last_rows, parts[1], NEGATIVE)
    return parts


def total(parts):
    return functools.reduce(jnp.add, parts)


def attend_kernel(heads, stored, limits, ends, qkv_ref, bias_ref, out_ref, log_ref, keep_ref):
    count = bias_ref.shape[0]
    width = heads * HEAD_DIM
    scale = jnp.asarray(HEAD_DIM**-0.5, BF16)

    def item(number):
        here = block_rows(stored[number, 3])
        queries = spread(qkv_ref[here, :width] * scale, heads)
        keys = gathered_keys(qkv_ref, width, stored, number, heads)
        parts = biased(matmul(keys, queries, NT), bias_ref[number], ends[1])
        top = jnp.max(functools.reduce(jnp.maximum, parts), axis=0, keepdims=True)
        weights = [jnp.exp(p - top) for p in parts]
        row_total = jnp.sum(total(weights), axis=0, keepdims=True)
        inverse = 1.0 / row_total
        probs = jnp.concatenate([(p * inverse).astype(BF16) for p in weights], axis=0)
        values = gathered_keys(qkv_ref, 2 * width, stored, number, heads)
        out_ref[here, :] = collapse(matmul(probs, values, TN), heads).astype(BF16)
        log_ref[pl.ds(number, 1), :] = top + jnp.log(row_total)

    def step(group, carry):
        for part in range(4):
            item(1 + group * 4 + part)
        return carry

    lax.fori_loop(0, (count - 1) // 4, step, 0)
    for number in range(1 + (count - 1) // 4 * 4, count):
        item(number)

    row = lax.broadcasted_iota(jnp.int32, (BLOCK, 1), 0)
    per = CHUNK // BLOCK
    chunks = count // per

    def chunk_rows(chunk):
        return pl.ds(pl.multiple_of(chunk * CHUNK, CHUNK), CHUNK)

    numbers = [0, ends[0]]
    rows_of = [block_rows(stored[number, 3]) for number in numbers]
    queries = [spread(qkv_ref[at, :width] * scale, heads) for at in rows_of]

    def scores(chunk, tops):
        at = chunk_rows(chunk)
        keys = qkv_ref[at, width : 2 * width]
        found = []
        for end in range(2):
            raw = matmul(keys, queries[end], NT)
            parts = [
                jnp.where(row < limits[chunk * per + s], slot(raw, s), NEGATIVE)
                for s in range(per)
            ]
            keep_ref[end, at, :] = jnp.concatenate(parts, axis=0)
            found.append(jnp.maximum(tops[end], functools.reduce(jnp.maximum, parts)))
        return tuple(found)

    tops = lax.fori_loop(0, chunks, scores, (jnp.full((BLOCK, width), NEGATIVE, F32),) * 2)
    tops = [jnp.max(top, axis=0, keepdims=True) for top in tops]

    def exponents(chunk, totals):
        at = chunk_rows(chunk)
        found = []
        for end in range(2):
            weights = jnp.exp(keep_ref[end, at, :] - tops[end])
            keep_ref[end, at, :] = weights
            found.append(totals[end] + total([slot(weights, s) for s in range(per)]))
        return tuple(found)

    totals = lax.fori_loop(0, chunks, exponents, (jnp.zeros((BLOCK, width), F32),) * 2)
    totals = [jnp.sum(found, axis=0, keepdims=True) for found in totals]
    inverses = [1.0 / found for found in totals]

    def contexts(chunk, sums):
        at = chunk_rows(chunk)
        values = qkv_ref[at, 2 * width :]
        return tuple(
            sums[end] + matmul((keep_ref[end, at, :] * inverses[end]).astype(BF16), values, TN)
            for end in range(2)
        )

    sums = lax.fori_loop(0, chunks, contexts, (jnp.zeros((width, width), F32),) * 2)
    for end in range(2):
        out_ref[rows_of[end], :] = collapse(sums[end], heads).astype(BF16)
        log_ref[pl.ds(numbers[end], 1), :] = tops[end] + jnp.log(totals[end])


def attend_back_kernel(
    heads,
    stored,
    limits,
    ends,
    qkv_ref,
    grad_ref,
    bias_ref,
    log_ref,
    out_ref,
    keys_acc,
    values_acc,
    probs_ref,
    inner_ref,
):
    count = bias_ref.shape[0]
    width = heads * HEAD_DIM
    scale = jnp.asarray(HEAD_DIM**-0.5, BF16)
    lane = lax.broadcasted_iota(jnp.int32, (1, PAIR), 1)
    keys_acc[...] = jnp.zeros_like(keys_acc)
    values_acc[...] = jnp.zeros_like(values_acc)

    def accumulate(acc, value, number):
        for s in range(5):
            acc[block_rows(stored[number, s]), :] += slot(value, s)
        for s in range(3):
            for h in range(heads):
                cols = slice(PAIR * (h // 2), PAIR * (h // 2 + 1))
                mine = (lane < HEAD_DIM) == (h % 2 == 0)
                term = jnp.where(mine, slot(value, 5 + s)[:, cols], 0.0)
                acc[block_rows(stored[number, 5 + heads * s + h]), cols] += term

    def item(number):
        here = block_rows(stored[number, 3])
        queries = spread(qkv_ref[here, :width] * scale, heads)
        grads = spread(grad_ref[here, :], heads)
        keys = gathered_keys(qkv_ref, width, stored, number, heads)
        values = gathered_keys(qkv_ref, 2 * width, stored, number, heads)
        log_total = log_ref[pl.ds(number, 1), :]
        parts = biased(matmul(keys, queries, NT), bias_ref[number], ends[1])
        probs = [jnp.exp(p - log_total) for p in parts]
        found = matmul(values, grads, NT)
        found = [slot(found, s) for s in range(SLOTS)]
        inner = total([p * d for p, d in zip(probs, found)])
        inner = jnp.sum(inner, axis=0, keepdims=True)
        grad_scores = jnp.concatenate(
            [(p * (d - inner)).astype(BF16) for p, d in zip(probs, found)], axis=0
        )
        probs_low = jnp.concatenate([p.astype(BF16) for p in probs], axis=0)
        accumulate(values_acc, matmul(probs_low, grads, NN), number)
        accumulate(keys_acc, matmul(grad_scores, queries, NN), number)
        grad_queries = collapse(matmul(grad_scores, keys, TN), heads) * HEAD_DIM**-0.5
        out_ref[here, :width] = grad_queries.astype(BF16)

    def step(group, carry):
        for part in range(4):
            item(1 + group * 4 + part)
        return carry

    lax.fori_loop(0, (count - 1) // 4, step, 0)
    for number in range(1 + (count - 1) // 4 * 4, count):
        item(number)

    row = lax.broadcasted_iota(jnp.int32, (BLOCK, 1), 0)
    per = CHUNK // BLOCK
    chunks = count // per

    def chunk_rows(chunk):
        return pl.ds(pl.multiple_of(chunk * CHUNK, CHUNK), CHUNK)

    numbers = [0, ends[0]]
    rows_of = [block_rows(stored[number, 3]) for number in numbers]
    queries = [spread(qkv_ref[at, :width] * scale, heads) for at in rows_of]
    grads = [spread(grad_ref[at, :], heads) for at in rows_of]
    log_rows = [log_ref[pl.ds(number, 1), :] for number in numbers]

    def first(chunk, inners):
        at = chunk_rows(chunk)
        keys = qkv_ref[at, width : 2 * width]
        values = qkv_ref[at, 2 * width :]
        sums = []
        for end in range(2):
            scores = matmul(keys, queries[end], NT)
            parts = [
                jnp.where(row < limits[chunk * per + s], slot(scores, s), NEGATIVE)
                for s in range(per)
            ]
            probs = jnp.exp(jnp.concatenate(parts, axis=0) - log_rows[end])
            found = matmul(values, grads[end], NT)
            probs_ref[end, at, :] = probs
            inner_ref[end, at, :] = found
            both = probs * found
            sums.append(inners[end] + total([slot(both, s) for s in range(per)]))
        return tuple(sums)

    inners = lax.fori_loop(0, chunks, first, (jnp.zeros((BLOCK, width), F32),) * 2)
    inners = [jnp.sum(inner, axis=0, keepdims=True) for inner in inners]

    def second(chunk, sums):
        at = chunk_rows(chunk)
        keys = qkv_ref[at, width : 2 * width]
        found, to_values, to_keys = [], values_acc[at, :], keys_acc[at, :]
        for end in range(2):
            probs = probs_ref[end, at, :]
            grad_scores = (probs * (inner_ref[end, at, :] - inners[end])).astype(BF16)
            to_values = to_values + matmul(probs.astype(BF16), grads[end], NN)
            to_keys = to_keys + matmul(grad_scores, queries[end], NN)
            found.append(sums[end] + matmul(grad_scores, keys, TN))
        out_ref[at, width : 2 * width] = to_keys.astype(BF16)
        out_ref[at, 2 * width :] = to_values.astype(BF16)
        return tuple(found)

    sums = lax.fori_loop(0, chunks, second, (jnp.zeros((width, width), F32),) * 2)
    for end in range(2):
        grad_queries = collapse(sums[end], heads) * HEAD_DIM**-0.5
        out_ref[rows_of[end], :width] = grad_queries.astype(BF16)


def in_smem():
    return pl.BlockSpec(memory_space=pltpu.SMEM)


def in_vmem():
    return pl.BlockSpec(memory_space=pltpu.VMEM)


def attention_cost(qkv, matmuls):
    rows, width = qkv.shape
    width //= 3
    return pl.CostEstimate(
        flops=2 * matmuls * rows * CHUNK * width,
        bytes_accessed=12 * rows * width,
        transcendentals=rows * CHUNK * width // HEAD_DIM,
    )


def attend(qkv, tables, heads):
    stored, limits, ends, bias = tables
    rows, width = qkv.shape[0], heads * HEAD_DIM
    return pl.pallas_call(
        functools.partial(attend_kernel, heads),
        out_shape=(
            jax.ShapeDtypeStruct((rows, width), BF16),
            jax.ShapeDtypeStruct((rows // BLOCK, width), F32),
        ),
        in_specs=[in_smem()] * 3 + [in_vmem()] * 2,
        out_specs=(in_vmem(), in_vmem()),
        scratch_shapes=[pltpu.VMEM((2, rows, width), F32)],
        compiler_params=pltpu.CompilerParams(vmem_limit_bytes=32 << 20),
        cost_estimate=attention_cost(qkv, 8),
        name="attend",
    )(stored, limits, ends, qkv, bias)


def attend_back(qkv, grad_context, log_totals, tables, heads):
    stored, limits, ends, bias = tables
    rows, width = qkv.shape[0], heads * HEAD_DIM
    return pl.pallas_call(
        functools.partial(attend_back_kernel, heads),
        out_shape=jax.ShapeDtypeStruct(qkv.shape, BF16),
        in_specs=[in_smem()] * 3 + [in_vmem()] * 4,
        out_specs=in_vmem(),
        scratch_shapes=[pltpu.VMEM((rows, width), F32)] * 2
        + [pltpu.VMEM((2, rows, width), F32)] * 2,
        compiler_params=pltpu.CompilerParams(vmem_limit_bytes=32 << 20),
        cost_estimate=attention_cost(qkv, 16),
        name="attend_back",
    )(stored, limits, ends, qkv, grad_context, bias, log_totals)


TILE = 256


def pick(refs):
    per = pl.num_programs(0) // len(refs)
    value = refs[0][...]
    for k, ref in enumerate(refs[1:], 1):
        value = jnp.where(pl.program_id(0) >= k * per, ref[...], value)
    return value


def tile_specs(arrays):
    def spec(k, value):
        tiles = value.shape[0] // TILE
        return pl.BlockSpec(
            (TILE, value.shape[1]), lambda i: (jnp.clip(i - k * tiles, 0, tiles - 1), 0)
        )

    return [spec(k, value) for k, value in enumerate(arrays)]


def gelu_and_slope(pre):
    scale = (2.0 / 3.141592653589793) ** 0.5
    square = pre * pre
    bent = jnp.tanh(scale * pre * (1.0 + 0.044715 * square))
    half = 0.5 + 0.5 * bent
    slope = half + (0.5 * scale) * pre * (1.0 - bent * bent) * (1.0 + 0.134145 * square)
    return pre * half, slope


def feed_kernel(parts, *refs):
    normed = pick(refs[:parts])
    grads = pick(refs[parts : 2 * parts])
    weight_ref, bias_ref, active_ref, grad_ref, back_ref, out_ref = refs[2 * parts :]
    units = bias_ref.shape[1]
    up = weight_ref[:, :units]
    down = weight_ref[:, units:]
    active, slope = gelu_and_slope(matmul(normed, up, NN) + bias_ref[...])
    active = active.astype(BF16)
    grad_hidden = (matmul(grads, down, NN) * slope).astype(BF16)
    back_ref[...] = matmul(grad_hidden, up, NT).astype(BF16)
    out_ref[...] = matmul(active, down, NT).astype(BF16)
    active_ref[...] = active
    grad_ref[...] = grad_hidden


def feed(normed, grads, weights, bias):
    rows = sum(value.shape[0] for value in normed)
    features, units = weights.shape[0], bias.shape[1]
    shapes = [(rows, units), (rows, units), (rows, features), (rows, features)]
    once = pl.BlockSpec(weights.shape, lambda i: (0, 0), pipeline_mode=pl.Buffered(1))
    return pl.pallas_call(
        functools.partial(feed_kernel, len(normed)),
        grid=(rows // TILE,),
        out_shape=[jax.ShapeDtypeStruct(shape, BF16) for shape in shapes],
        in_specs=tile_specs(normed)
        + tile_specs(grads)
        + [once, pl.BlockSpec(bias.shape, lambda i: (0, 0))],
        out_specs=[pl.BlockSpec((TILE, shape[1]), lambda i: (i, 0)) for shape in shapes],
        compiler_params=pltpu.CompilerParams(vmem_limit_bytes=40 << 20),
        cost_estimate=pl.CostEstimate(
            flops=8 * rows * features * units,
            bytes_accessed=12 * rows * features + 4 * features * units,
            transcendentals=rows * units,
        ),
        name="feed",
    )(*normed, *grads, weights, bias)


def feed_grads_kernel(counts, *refs):
    groups, start = [], 0
    for count in counts:
        groups.append(pick(refs[start : start + count]))
        start += count
    normed, grads, active, grad_hidden = groups
    out_ref, sum_ref, acc_ref = refs[start:]
    units = sum_ref.shape[1]

    @pl.when(pl.program_id(0) == 0)
    def _():
        acc_ref[...] = jnp.zeros_like(acc_ref)
        sum_ref[...] = jnp.zeros_like(sum_ref)

    acc_ref[:, :units] += matmul(normed, grad_hidden, TN)
    acc_ref[:, units:] += matmul(grads, active, TN)
    sum_ref[...] += jnp.sum(grad_hidden.astype(F32), axis=0, keepdims=True)

    @pl.when(pl.program_id(0) == pl.num_programs(0) - 1)
    def _():
        out_ref[...] = acc_ref[...].astype(BF16)


def feed_grads(normed, grads, active, grad_hidden):
    rows = sum(value.shape[0] for value in normed)
    features, units = normed[0].shape[1], active[0].shape[1]
    groups = [normed, grads, active, grad_hidden]
    return pl.pallas_call(
        functools.partial(feed_grads_kernel, [len(group) for group in groups]),
        grid=(rows // TILE,),
        out_shape=[
            jax.ShapeDtypeStruct((features, 2 * units), BF16),
            jax.ShapeDtypeStruct((1, units), F32),
        ],
        in_specs=[spec for group in groups for spec in tile_specs(group)],
        out_specs=[
            pl.BlockSpec((features, 2 * units), lambda i: (0, 0)),
            pl.BlockSpec((1, units), lambda i: (0, 0)),
        ],
        scratch_shapes=[pltpu.VMEM((features, 2 * units), F32)],
        compiler_params=pltpu.CompilerParams(vmem_limit_bytes=48 << 20),
        cost_estimate=pl.CostEstimate(
            flops=4 * rows * features * units,
            bytes_accessed=8 * rows * features + 4 * features * units,
            transcendentals=0,
        ),
        name="feed_grads",
    )(*normed, *grads, *active, *grad_hidden)


def unit_rows(rows):
    centred = rows - jnp.mean(rows, axis=-1, keepdims=True)
    inverse = lax.rsqrt(jnp.mean(centred * centred, axis=-1, keepdims=True) + EPS)
    return centred * inverse, inverse


def norm_back(grad_normed, unit, inverse, gain):
    grad_unit = grad_normed * gain
    return inverse * (
        grad_unit
        - jnp.mean(grad_unit, axis=-1, keepdims=True)
        - unit * jnp.mean(grad_unit * unit, axis=-1, keepdims=True)
    )


def per_device(
    tokens,
    output_cotangent,
    lengths,
    block_place,
    random_blocks,
    qkv_weight,
    out_weight,
    up_weight,
    down_weight,
    vectors,
    hidden_bias,
):
    ways = lax.axis_size("tensor")
    spread_ways = lax.axis_size("dp")
    position = lax.axis_index("tensor")
    index = lax.axis_index("dp") * ways + position
    near = tokens.shape[0]
    rows = near * ways
    features = tokens.shape[1]
    width = qkv_weight.shape[2]
    heads = width // HEAD_DIM
    units = up_weight.shape[1]
    own = features // spread_ways
    piece = vectors.shape[1]
    unit_piece = hidden_bias.shape[1]

    def quarters(value):
        return [value[k * near : (k + 1) * near] for k in range(ways)]

    residual = tokens.astype(F32)
    unit_one, inverse_one = unit_rows(residual)
    unit_all = jnp.concatenate(gathered_parts(unit_one.astype(BF16), "tensor"), axis=0)

    attention_flat = jnp.concatenate([qkv_weight.reshape(own, 3 * width), out_weight], axis=1)
    attention_full = lax.all_gather(attention_flat, "dp", axis=0, tiled=True)
    qkv_full = attention_full[:, : 3 * width]
    out_group = attention_full[:, 3 * width :]
    feed_flat = jnp.concatenate([up_weight, down_weight], axis=1)
    feed_full = lax.all_gather(feed_flat, "dp", axis=0, tiled=True)

    small = jnp.zeros((8, features), F32)
    small = lax.dynamic_update_slice(small, vectors, (0, index * piece))
    small_hidden = jnp.zeros((1, units * ways), F32)
    small_hidden = lax.dynamic_update_slice(small_hidden, hidden_bias, (0, index * unit_piece))
    packed = jnp.concatenate([small.reshape(-1), small_hidden.reshape(-1)])
    packed = summed_everywhere(packed, ("tensor", "dp"))
    vectors_full = packed[: 8 * features].reshape(8, features)
    hidden_full = packed[8 * features :]
    bias_query = lax.dynamic_slice_in_dim(vectors_full[6], position * width, width)
    bias_value = lax.dynamic_slice_in_dim(vectors_full[7], position * width, width)
    bias_qkv = jnp.concatenate([bias_query, jnp.zeros_like(bias_query), bias_value])
    bias_hidden = lax.dynamic_slice_in_dim(hidden_full, position * units, units)[None]

    placed = block_place[0].reshape(ways, -1)
    order = position ^ jnp.arange(ways, dtype=jnp.int32)
    chosen_rows = order[:, None, None] == jnp.arange(ways, dtype=jnp.int32)[None, :, None]
    place = jnp.sum(jnp.where(chosen_rows, placed[None], 0), axis=1).reshape(-1)
    tables = attention_tables(lengths[0], place, random_blocks[0])

    normed_one_all = (unit_all.astype(F32) * vectors_full[0] + vectors_full[1]).astype(BF16)
    qkv = (matmul(normed_one_all, qkv_full, NN) + bias_qkv).astype(BF16)
    context, log_totals = attend(qkv, tables, heads)

    out_all = jnp.concatenate(gathered_parts(out_group, "tensor"), axis=1)
    context_near = jnp.concatenate(exchanged_parts(quarters(context), "tensor"), axis=1)
    middle = residual + matmul(context_near, out_all, NT) + vectors_full[4]
    unit_two, inverse_two = unit_rows(middle)
    normed_two = (unit_two * vectors_full[2] + vectors_full[3]).astype(BF16)
    normed_parts = gathered_parts(normed_two, "tensor")
    grad_parts = gathered_parts(output_cotangent, "tensor")

    half = ways // 2
    active, grad_hidden, back_parts, out_parts = [], [], [], []
    for k in range(0, ways, half):
        found = feed(normed_parts[k : k + half], grad_parts[k : k + half], feed_full, bias_hidden)
        active.append(found[0])
        grad_hidden.append(found[1])
        back_parts += [found[2][n * near : (n + 1) * near] for n in range(half)]
        out_parts += [found[3][n * near : (n + 1) * near] for n in range(half)]
    grad_normed_two = summed_part(back_parts, "tensor")
    feed_sums, sum_hidden = feed_grads(normed_parts, grad_parts, active, grad_hidden)
    grad_normed_two, feed_sums = lax.optimization_barrier((grad_normed_two, feed_sums))
    feed_weight_grads = lax.psum_scatter(feed_sums, "dp", scatter_dimension=0, tiled=True)
    feed_weight_grads = feed_weight_grads.astype(F32)
    sum_hidden = sum_hidden[0]

    cotangent = output_cotangent.astype(F32)
    grad_middle = cotangent + norm_back(grad_normed_two, unit_two, inverse_two, vectors_full[2])
    grad_attended = grad_middle.astype(BF16)
    grad_heads = matmul(grad_attended, out_all, NN).astype(BF16)
    grad_heads = [grad_heads[:, k * width : (k + 1) * width] for k in range(ways)]
    grad_context = jnp.concatenate(exchanged_parts(grad_heads, "tensor"), axis=0)
    feed_out = summed_part(out_parts, "tensor", after=grad_context)
    output = (middle + feed_out + vectors_full[5]).astype(BF16)
    grad_qkv = attend_back(qkv, grad_context, log_totals, tables, heads)

    raw_qkv = matmul(unit_all, grad_qkv, TN)
    sum_qkv = jnp.sum(grad_qkv, axis=0, dtype=F32)
    qkv_wide = qkv_full.astype(F32)
    gain_one = jnp.sum(raw_qkv * qkv_wide, axis=1)
    shift_one = jnp.sum(sum_qkv * qkv_wide, axis=1)
    grad_normed_one = summed_part(quarters(matmul(grad_qkv, qkv_full, NT)), "tensor")
    out_grad = matmul(grad_attended, context_near, TN)
    out_grad = [out_grad[:, k * width : (k + 1) * width] for k in range(ways)]
    out_grad = summed_part(out_grad, "tensor").astype(BF16)
    sent = jnp.concatenate([raw_qkv.astype(BF16), out_grad], axis=1)
    arrived = sent_and_summed(sent, "dp")

    input_grad = (
        grad_middle + norm_back(grad_normed_one, unit_one, inverse_one, vectors_full[0])
    ).astype(BF16)

    by_feature = jnp.stack(
        [
            gain_one,
            shift_one,
            jnp.sum(grad_normed_two * unit_two, axis=0),
            jnp.sum(grad_normed_two, axis=0),
            jnp.sum(grad_middle, axis=0),
            jnp.sum(cotangent, axis=0),
        ]
    )
    by_feature = jnp.transpose(by_feature.reshape(6, spread_ways, own), (1, 0, 2))
    by_head = jnp.concatenate([sum_qkv, sum_hidden])
    by_head = jnp.broadcast_to(by_head[None], (spread_ways, by_head.shape[0]))
    extras = jnp.concatenate([by_feature.reshape(spread_ways, -1), by_head], axis=1)
    extras = jnp.sum(lax.all_to_all(extras, "dp", 0, 0, tiled=True), axis=0)
    sum_qkv = extras[6 * own : 6 * own + 3 * width]
    sum_hidden = extras[6 * own + 3 * width :]
    head_sums = jnp.zeros((2, features), F32)
    head_sums = lax.dynamic_update_slice(
        head_sums,
        jnp.stack([sum_qkv[:width], sum_qkv[2 * width :]]),
        (0, position * width),
    )
    hidden_sums = lax.dynamic_update_slice(
        jnp.zeros((units * ways,), F32), sum_hidden, (position * units,)
    )
    packed = jnp.concatenate([extras[: 6 * own], head_sums.reshape(-1), hidden_sums])
    packed = summed_everywhere(packed, ("tensor",))
    by_feature = packed[: 6 * own].reshape(6, own)
    head_sums = packed[6 * own : 6 * own + 2 * features].reshape(2, features)
    hidden_sums = packed[6 * own + 2 * features :]
    vectors_grad = jnp.concatenate(
        [
            lax.dynamic_slice_in_dim(by_feature, position * piece, piece, axis=1),
            lax.dynamic_slice_in_dim(head_sums, index * piece, piece, axis=1),
        ],
        axis=0,
    )
    hidden_bias_grad = lax.dynamic_slice_in_dim(hidden_sums, index * unit_piece, unit_piece)

    mine = lax.dynamic_slice_in_dim(
        vectors_full[:2], lax.axis_index("dp") * own, own, axis=1
    )
    qkv_weight_grad = mine[0][:, None] * arrived[:, : 3 * width] + mine[1][:, None] * sum_qkv
    return (
        output,
        input_grad,
        qkv_weight_grad.reshape(own, 3, width),
        arrived[:, 3 * width :],
        feed_weight_grads[:, :units],
        feed_weight_grads[:, units:],
        vectors_grad,
        hidden_bias_grad[None, :],
    )


def solution(mesh):
    placed = (
        P(("dp", "tensor"), None),
        P(("dp", "tensor"), None),
        P("dp"),
        P("dp", None),
        P("dp", "tensor", None, None),
        P("dp", None, "tensor"),
        P("dp", "tensor"),
        P("dp", "tensor"),
        P("dp", "tensor"),
        P(None, ("dp", "tensor")),
        P(None, ("dp", "tensor")),
    )
    return jax.shard_map(
        per_device,
        mesh=mesh,
        in_specs=placed,
        out_specs=(
            P(("dp", "tensor"), None),
            P(("dp", "tensor"), None),
            P("dp", None, "tensor"),
            P("dp", "tensor"),
            P("dp", "tensor"),
            P("dp", "tensor"),
            P(None, ("dp", "tensor")),
            P(None, ("dp", "tensor")),
        ),
        check_vma=False,
    )
```

```python
import functools

import jax
import jax.numpy as jnp
from jax import lax
from jax.experimental import pallas as pl
from jax.experimental.pallas import tpu as pltpu
from jax.sharding import PartitionSpec as P

HEAD_DIM = 64
BLOCK = 64
PAIR = 2 * HEAD_DIM
SLOTS = 8
CHUNK = 512
EPS = 1e-05
NEGATIVE = -1e30
F32 = jnp.float32
BF16 = jnp.bfloat16
NT = (((1,), (1,)), ((), ()))
NN = (((1,), (0,)), ((), ()))
TN = (((0,), (0,)), ((), ()))


def matmul(left, right, dims):
    return lax.dot_general(left, right, dims, preferred_element_type=F32)


def swapped(value, axis, bit):
    count = lax.axis_size(axis)
    return lax.ppermute(value, axis, [(i, i ^ bit) for i in range(count)])


def bits_of(axis):
    count = lax.axis_size(axis)
    return [1 << b for b in range(count.bit_length() - 1)]


def far(value, axis):
    return swapped(value, axis, bits_of(axis)[-1])


def gathered_parts(value, far_value, axis):
    bits = bits_of(axis)
    parts = {0: value, bits[-1]: far_value}
    for bit in reversed(bits[:-1]):
        parts.update({k | bit: swapped(p, axis, bit) for k, p in list(parts.items())})
    return [parts[k] for k in range(len(parts))]


def summed_part(parts, axis, after=None):
    left = dict(enumerate(parts))
    bits = bits_of(axis)
    for bit in bits:
        kept = {}
        for k in sorted(left, reverse=True):
            if k & bit == 0:
                going = left[k | bit].astype(BF16)
                if after is not None and bit == bits[-1]:
                    going, _ = lax.optimization_barrier((going, after))
                kept[k] = left[k].astype(F32) + swapped(going, axis, bit).astype(F32)
        left = kept
    return left[0]


def exchanged_parts(parts, axis):
    return [p if k == 0 else swapped(p, axis, k) for k, p in enumerate(parts)]


def summed_everywhere(value, axes):
    size = value.shape[0]
    value = jnp.pad(value, (0, -size % 1024)).reshape(-1, 128)
    for axis in axes:
        for bit in bits_of(axis):
            value = value + swapped(value, axis, bit)
    return value.reshape(-1)[:size]


def sent_and_summed(value, axis):
    count = lax.axis_size(axis)
    blocks = value.reshape(count, value.shape[0] // count, *value.shape[1:])
    arrived = lax.all_to_all(blocks, axis, 0, 0, tiled=True)
    return jnp.sum(arrived.astype(F32), axis=0)


def attention_tables(length, place, chosen):
    count = place.shape[0]
    heads = chosen.shape[0]
    nblocks = (length + BLOCK - 1) // BLOCK
    last = nblocks - 1
    number = jnp.arange(count, dtype=jnp.int32)
    same = jnp.zeros_like(number)
    common = jnp.stack([same, same + last, number - 1, number, number + 1], axis=1)
    middle = (number > 0) & (number < last)
    good = jnp.stack(
        [
            middle | (number > last),
            middle | (number > last),
            (number - 1 > 0) & (number - 1 < last) & (number != last),
            middle,
            (number + 1 < last) & (number > 0),
        ],
        axis=1,
    )
    drawn = jnp.transpose(chosen, (1, 2, 0))
    away = number[:, None, None]
    fresh = (
        (drawn > 0)
        & (drawn < last)
        & (jnp.abs(drawn - away) > 1)
        & (away > 0)
        & (away != last)
    )
    first, second, third = drawn[:, 0], drawn[:, 1], drawn[:, 2]
    fresh = jnp.stack(
        [
            fresh[:, 0],
            fresh[:, 1] & (second != first),
            fresh[:, 2] & (third != first) & (third != second),
        ],
        axis=1,
    )
    flags = jnp.concatenate(
        [jnp.broadcast_to(good[:, :, None], (count, 5, heads)), fresh], axis=1
    )
    bias = jnp.where(flags, 0.0, NEGATIVE).astype(F32)
    bias = jnp.broadcast_to(bias[..., None], (*bias.shape, HEAD_DIM))
    bias = bias.reshape(count, SLOTS, heads * HEAD_DIM)
    wanted = jnp.concatenate([common, drawn.reshape(count, -1)], axis=1)
    hit = wanted[:, :, None] == place[None, None, :]
    stored = jnp.sum(jnp.where(hit, number[None, None, :], 0), axis=-1).astype(jnp.int32)
    limits = jnp.clip(length - BLOCK * place, 0, BLOCK).astype(jnp.int32)
    ends = jnp.stack([last, length - BLOCK * last]).astype(jnp.int32)
    return stored, limits, ends, bias


def block_rows(index):
    return pl.ds(pl.multiple_of(index * BLOCK, BLOCK), BLOCK)


def spread(rows, heads):
    lane = lax.broadcasted_iota(jnp.int32, (1, heads * HEAD_DIM), 1)
    zero = jnp.zeros_like(rows)
    return jnp.concatenate(
        [jnp.where(lane // HEAD_DIM == h, rows, zero) for h in range(heads)], axis=0
    )


def collapse(full, heads):
    lane = lax.broadcasted_iota(jnp.int32, (1, PAIR), 1)
    pieces = []
    for pair in range(heads // 2):
        cols = slice(PAIR * pair, PAIR * (pair + 1))
        even = full[2 * pair * HEAD_DIM : (2 * pair + 1) * HEAD_DIM, cols]
        odd = full[(2 * pair + 1) * HEAD_DIM : (2 * pair + 2) * HEAD_DIM, cols]
        pieces.append(jnp.where(lane < HEAD_DIM, even, odd))
    return jnp.concatenate(pieces, axis=1)


def gathered_keys(ref, start, stored, number, heads):
    width = heads * HEAD_DIM
    lane = lax.broadcasted_iota(jnp.int32, (1, PAIR), 1)
    parts = [ref[block_rows(stored[number, s]), start : start + width] for s in range(5)]
    for s in range(3):
        pieces = []
        for pair in range(heads // 2):
            cols = slice(start + PAIR * pair, start + PAIR * (pair + 1))
            at = 5 + heads * s + 2 * pair
            even = ref[block_rows(stored[number, at]), cols]
            odd = ref[block_rows(stored[number, at + 1]), cols]
            pieces.append(jnp.where(lane < HEAD_DIM, even, odd))
        parts.append(jnp.concatenate(pieces, axis=1))
    return jnp.concatenate(parts, axis=0)


def slot(value, index):
    return value[BLOCK * index : BLOCK * (index + 1)]


def biased(scores, bias, last_rows):
    row = lax.broadcasted_iota(jnp.int32, (BLOCK, 1), 0)
    parts = [slot(scores, s) + bias[s : s + 1] for s in range(SLOTS)]
    parts[1] = jnp.where(row < last_rows, parts[1], NEGATIVE)
    return parts


def total(parts):
    return functools.reduce(jnp.add, parts)


def attend_kernel(heads, stored, limits, ends, qkv_ref, bias_ref, out_ref, log_ref, keep_ref):
    count = bias_ref.shape[0]
    width = heads * HEAD_DIM
    scale = jnp.asarray(HEAD_DIM**-0.5, BF16)

    def item(number):
        here = block_rows(stored[number, 3])
        queries = spread(qkv_ref[here, :width] * scale, heads)
        keys = gathered_keys(qkv_ref, width, stored, number, heads)
        parts = biased(matmul(keys, queries, NT), bias_ref[number], ends[1])
        top = jnp.max(functools.reduce(jnp.maximum, parts), axis=0, keepdims=True)
        weights = [jnp.exp(p - top) for p in parts]
        row_total = jnp.sum(total(weights), axis=0, keepdims=True)
        inverse = 1.0 / row_total
        probs = jnp.concatenate([(p * inverse).astype(BF16) for p in weights], axis=0)
        values = gathered_keys(qkv_ref, 2 * width, stored, number, heads)
        out_ref[here, :] = collapse(matmul(probs, values, TN), heads).astype(BF16)
        log_ref[pl.ds(number, 1), :] = top + jnp.log(row_total)

    def step(group, carry):
        for part in range(4):
            item(1 + group * 4 + part)
        return carry

    lax.fori_loop(0, (count - 1) // 4, step, 0)
    for number in range(1 + (count - 1) // 4 * 4, count):
        item(number)

    row = lax.broadcasted_iota(jnp.int32, (BLOCK, 1), 0)
    per = CHUNK // BLOCK
    chunks = count // per

    def chunk_rows(chunk):
        return pl.ds(pl.multiple_of(chunk * CHUNK, CHUNK), CHUNK)

    numbers = [0, ends[0]]
    rows_of = [block_rows(stored[number, 3]) for number in numbers]
    queries = [spread(qkv_ref[at, :width] * scale, heads) for at in rows_of]

    def scores(chunk, tops):
        at = chunk_rows(chunk)
        keys = qkv_ref[at, width : 2 * width]
        found = []
        for end in range(2):
            raw = matmul(keys, queries[end], NT)
            parts = [
                jnp.where(row < limits[chunk * per + s], slot(raw, s), NEGATIVE)
                for s in range(per)
            ]
            keep_ref[end, at, :] = jnp.concatenate(parts, axis=0)
            found.append(jnp.maximum(tops[end], functools.reduce(jnp.maximum, parts)))
        return tuple(found)

    tops = lax.fori_loop(0, chunks, scores, (jnp.full((BLOCK, width), NEGATIVE, F32),) * 2)
    tops = [jnp.max(top, axis=0, keepdims=True) for top in tops]

    def exponents(chunk, totals):
        at = chunk_rows(chunk)
        found = []
        for end in range(2):
            weights = jnp.exp(keep_ref[end, at, :] - tops[end])
            keep_ref[end, at, :] = weights
            found.append(totals[end] + total([slot(weights, s) for s in range(per)]))
        return tuple(found)

    totals = lax.fori_loop(0, chunks, exponents, (jnp.zeros((BLOCK, width), F32),) * 2)
    totals = [jnp.sum(found, axis=0, keepdims=True) for found in totals]
    inverses = [1.0 / found for found in totals]

    def contexts(chunk, sums):
        at = chunk_rows(chunk)
        values = qkv_ref[at, 2 * width :]
        return tuple(
            sums[end] + matmul((keep_ref[end, at, :] * inverses[end]).astype(BF16), values, TN)
            for end in range(2)
        )

    sums = lax.fori_loop(0, chunks, contexts, (jnp.zeros((width, width), F32),) * 2)
    for end in range(2):
        out_ref[rows_of[end], :] = collapse(sums[end], heads).astype(BF16)
        log_ref[pl.ds(numbers[end], 1), :] = tops[end] + jnp.log(totals[end])


def attend_back_kernel(
    heads,
    stored,
    limits,
    ends,
    qkv_ref,
    grad_ref,
    bias_ref,
    log_ref,
    out_ref,
    keys_acc,
    values_acc,
    probs_ref,
    inner_ref,
):
    count = bias_ref.shape[0]
    width = heads * HEAD_DIM
    scale = jnp.asarray(HEAD_DIM**-0.5, BF16)
    lane = lax.broadcasted_iota(jnp.int32, (1, PAIR), 1)
    keys_acc[...] = jnp.zeros_like(keys_acc)
    values_acc[...] = jnp.zeros_like(values_acc)

    def accumulate(acc, value, number):
        for s in range(5):
            acc[block_rows(stored[number, s]), :] += slot(value, s)
        for s in range(3):
            for h in range(heads):
                cols = slice(PAIR * (h // 2), PAIR * (h // 2 + 1))
                mine = (lane < HEAD_DIM) == (h % 2 == 0)
                term = jnp.where(mine, slot(value, 5 + s)[:, cols], 0.0)
                acc[block_rows(stored[number, 5 + heads * s + h]), cols] += term

    def item(number):
        here = block_rows(stored[number, 3])
        queries = spread(qkv_ref[here, :width] * scale, heads)
        grads = spread(grad_ref[here, :], heads)
        keys = gathered_keys(qkv_ref, width, stored, number, heads)
        values = gathered_keys(qkv_ref, 2 * width, stored, number, heads)
        log_total = log_ref[pl.ds(number, 1), :]
        parts = biased(matmul(keys, queries, NT), bias_ref[number], ends[1])
        probs = [jnp.exp(p - log_total) for p in parts]
        found = matmul(values, grads, NT)
        found = [slot(found, s) for s in range(SLOTS)]
        inner = total([p * d for p, d in zip(probs, found)])
        inner = jnp.sum(inner, axis=0, keepdims=True)
        grad_scores = jnp.concatenate(
            [(p * (d - inner)).astype(BF16) for p, d in zip(probs, found)], axis=0
        )
        probs_low = jnp.concatenate([p.astype(BF16) for p in probs], axis=0)
        accumulate(values_acc, matmul(probs_low, grads, NN), number)
        accumulate(keys_acc, matmul(grad_scores, queries, NN), number)
        grad_queries = collapse(matmul(grad_scores, keys, TN), heads) * HEAD_DIM**-0.5
        out_ref[here, :width] = grad_queries.astype(BF16)

    def step(group, carry):
        for part in range(4):
            item(1 + group * 4 + part)
        return carry

    lax.fori_loop(0, (count - 1) // 4, step, 0)
    for number in range(1 + (count - 1) // 4 * 4, count):
        item(number)

    row = lax.broadcasted_iota(jnp.int32, (BLOCK, 1), 0)
    per = CHUNK // BLOCK
    chunks = count // per

    def chunk_rows(chunk):
        return pl.ds(pl.multiple_of(chunk * CHUNK, CHUNK), CHUNK)

    numbers = [0, ends[0]]
    rows_of = [block_rows(stored[number, 3]) for number in numbers]
    queries = [spread(qkv_ref[at, :width] * scale, heads) for at in rows_of]
    grads = [spread(grad_ref[at, :], heads) for at in rows_of]
    log_rows = [log_ref[pl.ds(number, 1), :] for number in numbers]

    def first(chunk, inners):
        at = chunk_rows(chunk)
        keys = qkv_ref[at, width : 2 * width]
        values = qkv_ref[at, 2 * width :]
        sums = []
        for end in range(2):
            scores = matmul(keys, queries[end], NT)
            parts = [
                jnp.where(row < limits[chunk * per + s], slot(scores, s), NEGATIVE)
                for s in range(per)
            ]
            probs = jnp.exp(jnp.concatenate(parts, axis=0) - log_rows[end])
            found = matmul(values, grads[end], NT)
            probs_ref[end, at, :] = probs
            inner_ref[end, at, :] = found
            both = probs * found
            sums.append(inners[end] + total([slot(both, s) for s in range(per)]))
        return tuple(sums)

    inners = lax.fori_loop(0, chunks, first, (jnp.zeros((BLOCK, width), F32),) * 2)
    inners = [jnp.sum(inner, axis=0, keepdims=True) for inner in inners]

    def second(chunk, sums):
        at = chunk_rows(chunk)
        keys = qkv_ref[at, width : 2 * width]
        found, to_values, to_keys = [], values_acc[at, :], keys_acc[at, :]
        for end in range(2):
            probs = probs_ref[end, at, :]
            grad_scores = (probs * (inner_ref[end, at, :] - inners[end])).astype(BF16)
            to_values = to_values + matmul(probs.astype(BF16), grads[end], NN)
            to_keys = to_keys + matmul(grad_scores, queries[end], NN)
            found.append(sums[end] + matmul(grad_scores, keys, TN))
        out_ref[at, width : 2 * width] = to_keys.astype(BF16)
        out_ref[at, 2 * width :] = to_values.astype(BF16)
        return tuple(found)

    sums = lax.fori_loop(0, chunks, second, (jnp.zeros((width, width), F32),) * 2)
    for end in range(2):
        grad_queries = collapse(sums[end], heads) * HEAD_DIM**-0.5
        out_ref[rows_of[end], :width] = grad_queries.astype(BF16)


def in_smem():
    return pl.BlockSpec(memory_space=pltpu.SMEM)


def in_vmem():
    return pl.BlockSpec(memory_space=pltpu.VMEM)


def attention_cost(qkv, matmuls):
    rows, width = qkv.shape
    width //= 3
    return pl.CostEstimate(
        flops=2 * matmuls * rows * CHUNK * width,
        bytes_accessed=12 * rows * width,
        transcendentals=rows * CHUNK * width // HEAD_DIM,
    )


def attend(qkv, tables, heads):
    stored, limits, ends, bias = tables
    rows, width = qkv.shape[0], heads * HEAD_DIM
    return pl.pallas_call(
        functools.partial(attend_kernel, heads),
        out_shape=(
            jax.ShapeDtypeStruct((rows, width), BF16),
            jax.ShapeDtypeStruct((rows // BLOCK, width), F32),
        ),
        in_specs=[in_smem()] * 3 + [in_vmem()] * 2,
        out_specs=(in_vmem(), in_vmem()),
        scratch_shapes=[pltpu.VMEM((2, rows, width), F32)],
        compiler_params=pltpu.CompilerParams(vmem_limit_bytes=32 << 20),
        cost_estimate=attention_cost(qkv, 8),
        name="attend",
    )(stored, limits, ends, qkv, bias)


def attend_back(qkv, grad_context, log_totals, tables, heads):
    stored, limits, ends, bias = tables
    rows, width = qkv.shape[0], heads * HEAD_DIM
    return pl.pallas_call(
        functools.partial(attend_back_kernel, heads),
        out_shape=jax.ShapeDtypeStruct(qkv.shape, BF16),
        in_specs=[in_smem()] * 3 + [in_vmem()] * 4,
        out_specs=in_vmem(),
        scratch_shapes=[pltpu.VMEM((rows, width), F32)] * 2
        + [pltpu.VMEM((2, rows, width), F32)] * 2,
        compiler_params=pltpu.CompilerParams(vmem_limit_bytes=32 << 20),
        cost_estimate=attention_cost(qkv, 16),
        name="attend_back",
    )(stored, limits, ends, qkv, grad_context, bias, log_totals)


TILE = 256


def pick(refs):
    per = pl.num_programs(0) // len(refs)
    value = refs[0][...]
    for k, ref in enumerate(refs[1:], 1):
        value = jnp.where(pl.program_id(0) >= k * per, ref[...], value)
    return value


def tile_specs(arrays):
    def spec(k, value):
        tiles = value.shape[0] // TILE
        return pl.BlockSpec(
            (TILE, value.shape[1]), lambda i: (jnp.clip(i - k * tiles, 0, tiles - 1), 0)
        )

    return [spec(k, value) for k, value in enumerate(arrays)]


def gelu_and_slope(pre):
    scale = (2.0 / 3.141592653589793) ** 0.5
    square = pre * pre
    bent = jnp.tanh(scale * pre * (1.0 + 0.044715 * square))
    half = 0.5 + 0.5 * bent
    slope = half + (0.5 * scale) * pre * (1.0 - bent * bent) * (1.0 + 0.134145 * square)
    return pre * half, slope


def feed_kernel(parts, *refs):
    normed = pick(refs[:parts])
    grads = pick(refs[parts : 2 * parts])
    weight_ref, bias_ref, active_ref, grad_ref, back_ref, out_ref = refs[2 * parts :]
    units = bias_ref.shape[1]
    up = weight_ref[:, :units]
    down = weight_ref[:, units:]
    active, slope = gelu_and_slope(matmul(normed, up, NN) + bias_ref[...])
    active = active.astype(BF16)
    grad_hidden = (matmul(grads, down, NN) * slope).astype(BF16)
    back_ref[...] = matmul(grad_hidden, up, NT).astype(BF16)
    out_ref[...] = matmul(active, down, NT).astype(BF16)
    active_ref[...] = active
    grad_ref[...] = grad_hidden


def feed(normed, grads, weights, bias):
    rows = sum(value.shape[0] for value in normed)
    features, units = weights.shape[0], bias.shape[1]
    shapes = [(rows, units), (rows, units), (rows, features), (rows, features)]
    once = pl.BlockSpec(weights.shape, lambda i: (0, 0), pipeline_mode=pl.Buffered(1))
    return pl.pallas_call(
        functools.partial(feed_kernel, len(normed)),
        grid=(rows // TILE,),
        out_shape=[jax.ShapeDtypeStruct(shape, BF16) for shape in shapes],
        in_specs=tile_specs(normed)
        + tile_specs(grads)
        + [once, pl.BlockSpec(bias.shape, lambda i: (0, 0))],
        out_specs=[pl.BlockSpec((TILE, shape[1]), lambda i: (i, 0)) for shape in shapes],
        compiler_params=pltpu.CompilerParams(vmem_limit_bytes=62 << 20),
        cost_estimate=pl.CostEstimate(
            flops=8 * rows * features * units,
            bytes_accessed=12 * rows * features + 4 * features * units,
            transcendentals=rows * units,
        ),
        name="feed",
    )(*normed, *grads, weights, bias)


def feed_grads_kernel(counts, *refs):
    groups, start = [], 0
    for count in counts:
        groups.append(pick(refs[start : start + count]))
        start += count
    normed, grads, active, grad_hidden = groups
    out_ref, sum_ref, acc_ref = refs[start:]
    units = sum_ref.shape[1]

    @pl.when(pl.program_id(0) == 0)
    def _():
        acc_ref[...] = jnp.zeros_like(acc_ref)
        sum_ref[...] = jnp.zeros_like(sum_ref)

    acc_ref[:, :units] += matmul(normed, grad_hidden, TN)
    acc_ref[:, units:] += matmul(grads, active, TN)
    sum_ref[...] += jnp.sum(grad_hidden.astype(F32), axis=0, keepdims=True)

    @pl.when(pl.program_id(0) == pl.num_programs(0) - 1)
    def _():
        out_ref[...] = acc_ref[...].astype(BF16)


def feed_grads(normed, grads, active, grad_hidden):
    rows = sum(value.shape[0] for value in normed)
    features, units = normed[0].shape[1], active[0].shape[1]
    groups = [normed, grads, active, grad_hidden]
    return pl.pallas_call(
        functools.partial(feed_grads_kernel, [len(group) for group in groups]),
        grid=(rows // TILE,),
        out_shape=[
            jax.ShapeDtypeStruct((features, 2 * units), BF16),
            jax.ShapeDtypeStruct((1, units), F32),
        ],
        in_specs=[spec for group in groups for spec in tile_specs(group)],
        out_specs=[
            pl.BlockSpec((features, 2 * units), lambda i: (0, 0)),
            pl.BlockSpec((1, units), lambda i: (0, 0)),
        ],
        scratch_shapes=[pltpu.VMEM((features, 2 * units), F32)],
        compiler_params=pltpu.CompilerParams(vmem_limit_bytes=62 << 20),
        cost_estimate=pl.CostEstimate(
            flops=4 * rows * features * units,
            bytes_accessed=8 * rows * features + 4 * features * units,
            transcendentals=0,
        ),
        name="feed_grads",
    )(*normed, *grads, *active, *grad_hidden)


def unit_rows(rows):
    centred = rows - jnp.mean(rows, axis=-1, keepdims=True)
    inverse = lax.rsqrt(jnp.mean(centred * centred, axis=-1, keepdims=True) + EPS)
    return centred * inverse, inverse


def norm_back(grad_normed, unit, inverse, gain):
    grad_unit = grad_normed * gain
    return inverse * (
        grad_unit
        - jnp.mean(grad_unit, axis=-1, keepdims=True)
        - unit * jnp.mean(grad_unit * unit, axis=-1, keepdims=True)
    )


def per_device(
    tokens,
    output_cotangent,
    lengths,
    block_place,
    random_blocks,
    qkv_weight,
    out_weight,
    up_weight,
    down_weight,
    vectors,
    hidden_bias,
):
    ways = lax.axis_size("tensor")
    spread_ways = lax.axis_size("dp")
    position = lax.axis_index("tensor")
    index = lax.axis_index("dp") * ways + position
    near = tokens.shape[0]
    rows = near * ways
    features = tokens.shape[1]
    width = qkv_weight.shape[2]
    heads = width // HEAD_DIM
    units = up_weight.shape[1]
    own = features // spread_ways
    piece = vectors.shape[1]
    unit_piece = hidden_bias.shape[1]

    def quarters(value):
        return [value[k * near : (k + 1) * near] for k in range(ways)]

    residual = tokens.astype(F32)
    unit_one, inverse_one = unit_rows(residual)
    unit_near = unit_one.astype(BF16)
    unit_far = far(unit_near, "tensor")
    unit_all = jnp.concatenate(gathered_parts(unit_near, unit_far, "tensor"), axis=0)
    cotangent_near, _ = lax.optimization_barrier((output_cotangent, unit_far))
    cotangent_far = far(cotangent_near, "tensor")

    attention_flat = jnp.concatenate([qkv_weight.reshape(own, 3 * width), out_weight], axis=1)
    attention_full = lax.all_gather(attention_flat, "dp", axis=0, tiled=True)
    attention_full, cotangent_far = lax.optimization_barrier((attention_full, cotangent_far))
    grad_parts = gathered_parts(output_cotangent, cotangent_far, "tensor")
    qkv_full = attention_full[:, : 3 * width]
    out_group = attention_full[:, 3 * width :]
    feed_flat = jnp.concatenate([up_weight, down_weight], axis=1)
    feed_full = lax.all_gather(feed_flat, "dp", axis=0, tiled=True)

    small = jnp.zeros((8, features), F32)
    small = lax.dynamic_update_slice(small, vectors, (0, index * piece))
    small_hidden = jnp.zeros((1, units * ways), F32)
    small_hidden = lax.dynamic_update_slice(small_hidden, hidden_bias, (0, index * unit_piece))
    packed = jnp.concatenate([small.reshape(-1), small_hidden.reshape(-1)])
    packed = summed_everywhere(packed, ("tensor", "dp"))
    vectors_full = packed[: 8 * features].reshape(8, features)
    hidden_full = packed[8 * features :]
    bias_query = lax.dynamic_slice_in_dim(vectors_full[6], position * width, width)
    bias_value = lax.dynamic_slice_in_dim(vectors_full[7], position * width, width)
    bias_qkv = jnp.concatenate([bias_query, jnp.zeros_like(bias_query), bias_value])
    bias_hidden = lax.dynamic_slice_in_dim(hidden_full, position * units, units)[None]

    placed = block_place[0].reshape(ways, -1)
    order = position ^ jnp.arange(ways, dtype=jnp.int32)
    chosen_rows = order[:, None, None] == jnp.arange(ways, dtype=jnp.int32)[None, :, None]
    place = jnp.sum(jnp.where(chosen_rows, placed[None], 0), axis=1).reshape(-1)
    tables = attention_tables(lengths[0], place, random_blocks[0])

    normed_one_all = (unit_all.astype(F32) * vectors_full[0] + vectors_full[1]).astype(BF16)
    qkv = (matmul(normed_one_all, qkv_full, NN) + bias_qkv).astype(BF16)
    out_far = far(out_group, "tensor")
    context, log_totals = attend(qkv, tables, heads)
    context, out_far = lax.optimization_barrier((context, out_far))

    out_all = jnp.concatenate(gathered_parts(out_group, out_far, "tensor"), axis=1)
    context_near = jnp.concatenate(exchanged_parts(quarters(context), "tensor"), axis=1)
    middle = residual + matmul(context_near, out_all, NT) + vectors_full[4]
    unit_two, inverse_two = unit_rows(middle)
    normed_two = (unit_two * vectors_full[2] + vectors_full[3]).astype(BF16)
    half = ways // 2
    normed_far = far(normed_two, "tensor")
    normed_parts = gathered_parts(normed_two, normed_far, "tensor")
    near_half = feed(normed_parts[:half], grad_parts[:half], feed_full, bias_hidden)
    normed_far, near_half = lax.optimization_barrier((normed_far, near_half))
    normed_parts[half:] = gathered_parts(normed_two, normed_far, "tensor")[half:]
    far_half = feed(normed_parts[half:], grad_parts[half:], feed_full, bias_hidden)
    active, grad_hidden, back_parts, out_parts = [
        [both[0], both[1]] for both in zip(near_half, far_half)
    ]
    back_parts = [part for both in back_parts for part in (both[:near], both[near:])]
    out_parts = [part for both in out_parts for part in (both[:near], both[near:])]
    grad_normed_two = summed_part(back_parts, "tensor")
    feed_sums, sum_hidden = feed_grads(normed_parts, grad_parts, active, grad_hidden)
    grad_normed_two, feed_sums = lax.optimization_barrier((grad_normed_two, feed_sums))
    feed_weight_grads = lax.psum_scatter(feed_sums, "dp", scatter_dimension=0, tiled=True)
    feed_weight_grads = feed_weight_grads.astype(F32)
    sum_hidden = sum_hidden[0]

    cotangent = output_cotangent.astype(F32)
    grad_middle = cotangent + norm_back(grad_normed_two, unit_two, inverse_two, vectors_full[2])
    grad_attended = grad_middle.astype(BF16)
    grad_heads = matmul(grad_attended, out_all, NN).astype(BF16)
    grad_heads = [grad_heads[:, k * width : (k + 1) * width] for k in range(ways)]
    grad_context = jnp.concatenate(exchanged_parts(grad_heads, "tensor"), axis=0)
    feed_out = summed_part(out_parts, "tensor", after=grad_context)
    output = (middle + feed_out + vectors_full[5]).astype(BF16)
    grad_qkv = attend_back(qkv, grad_context, log_totals, tables, heads)
    grad_qkv, output = lax.optimization_barrier((grad_qkv, output))

    raw_qkv = matmul(unit_all, grad_qkv, TN)
    sum_qkv = jnp.sum(grad_qkv, axis=0, dtype=F32)
    qkv_wide = qkv_full.astype(F32)
    gain_one = jnp.sum(raw_qkv * qkv_wide, axis=1)
    shift_one = jnp.sum(sum_qkv * qkv_wide, axis=1)
    out_grad = matmul(grad_attended, context_near, TN)
    out_grad = [out_grad[:, k * width : (k + 1) * width] for k in range(ways)]
    out_grad = summed_part(out_grad, "tensor", after=grad_qkv).astype(BF16)
    grad_normed = matmul(grad_qkv, qkv_full, NT)
    grad_normed, out_grad = lax.optimization_barrier((grad_normed, out_grad))
    grad_normed_one = summed_part(quarters(grad_normed), "tensor")
    raw_qkv = sent_and_summed(raw_qkv.astype(BF16), "dp")
    out_grad, _ = lax.optimization_barrier((out_grad, raw_qkv))
    out_weight_grad = sent_and_summed(out_grad, "dp")

    input_grad = (
        grad_middle + norm_back(grad_normed_one, unit_one, inverse_one, vectors_full[0])
    ).astype(BF16)

    by_feature = jnp.stack(
        [
            gain_one,
            shift_one,
            jnp.sum(grad_normed_two * unit_two, axis=0),
            jnp.sum(grad_normed_two, axis=0),
            jnp.sum(grad_middle, axis=0),
            jnp.sum(cotangent, axis=0),
        ]
    )
    by_feature = jnp.transpose(by_feature.reshape(6, spread_ways, own), (1, 0, 2))
    by_head = jnp.concatenate([sum_qkv, sum_hidden])
    by_head = jnp.broadcast_to(by_head[None], (spread_ways, by_head.shape[0]))
    extras = jnp.concatenate([by_feature.reshape(spread_ways, -1), by_head], axis=1)
    extras = jnp.sum(lax.all_to_all(extras, "dp", 0, 0, tiled=True), axis=0)
    sum_qkv = extras[6 * own : 6 * own + 3 * width]
    sum_hidden = extras[6 * own + 3 * width :]
    head_sums = jnp.zeros((2, features), F32)
    head_sums = lax.dynamic_update_slice(
        head_sums,
        jnp.stack([sum_qkv[:width], sum_qkv[2 * width :]]),
        (0, position * width),
    )
    hidden_sums = lax.dynamic_update_slice(
        jnp.zeros((units * ways,), F32), sum_hidden, (position * units,)
    )
    packed = jnp.concatenate([extras[: 6 * own], head_sums.reshape(-1), hidden_sums])
    packed = summed_everywhere(packed, ("tensor",))
    by_feature = packed[: 6 * own].reshape(6, own)
    head_sums = packed[6 * own : 6 * own + 2 * features].reshape(2, features)
    hidden_sums = packed[6 * own + 2 * features :]
    vectors_grad = jnp.concatenate(
        [
            lax.dynamic_slice_in_dim(by_feature, position * piece, piece, axis=1),
            lax.dynamic_slice_in_dim(head_sums, index * piece, piece, axis=1),
        ],
        axis=0,
    )
    hidden_bias_grad = lax.dynamic_slice_in_dim(hidden_sums, index * unit_piece, unit_piece)

    mine = lax.dynamic_slice_in_dim(
        vectors_full[:2], lax.axis_index("dp") * own, own, axis=1
    )
    qkv_weight_grad = mine[0][:, None] * raw_qkv + mine[1][:, None] * sum_qkv
    return (
        output,
        input_grad,
        qkv_weight_grad.reshape(own, 3, width),
        out_weight_grad,
        feed_weight_grads[:, :units],
        feed_weight_grads[:, units:],
        vectors_grad,
        hidden_bias_grad[None, :],
    )


def solution(mesh):
    placed = (
        P(("dp", "tensor"), None),
        P(("dp", "tensor"), None),
        P("dp"),
        P("dp", None),
        P("dp", "tensor", None, None),
        P("dp", None, "tensor"),
        P("dp", "tensor"),
        P("dp", "tensor"),
        P("dp", "tensor"),
        P(None, ("dp", "tensor")),
        P(None, ("dp", "tensor")),
    )
    return jax.shard_map(
        per_device,
        mesh=mesh,
        in_specs=placed,
        out_specs=(
            P(("dp", "tensor"), None),
            P(("dp", "tensor"), None),
            P("dp", None, "tensor"),
            P("dp", "tensor"),
            P("dp", "tensor"),
            P("dp", "tensor"),
            P(None, ("dp", "tensor")),
            P(None, ("dp", "tensor")),
        ),
        check_vma=False,
    )
```

```python
import functools

import jax
import jax.numpy as jnp
from jax import lax
from jax.experimental import pallas as pl
from jax.experimental.pallas import tpu as pltpu
from jax.sharding import PartitionSpec as P

HEAD_DIM = 64
BLOCK = 64
PAIR = 2 * HEAD_DIM
SLOTS = 8
CHUNK = 512
EPS = 1e-05
NEGATIVE = -1e30
F32 = jnp.float32
BF16 = jnp.bfloat16
NT = (((1,), (1,)), ((), ()))
NN = (((1,), (0,)), ((), ()))
TN = (((0,), (0,)), ((), ()))


def matmul(left, right, dims):
    return lax.dot_general(left, right, dims, preferred_element_type=F32)


def swapped(value, axis, bit):
    count = lax.axis_size(axis)
    return lax.ppermute(value, axis, [(i, i ^ bit) for i in range(count)])


def bits_of(axis):
    count = lax.axis_size(axis)
    return [1 << b for b in range(count.bit_length() - 1)]


def far(value, axis):
    return swapped(value, axis, bits_of(axis)[-1])


def gathered_parts(value, far_value, axis):
    bits = bits_of(axis)
    parts = {0: value, bits[-1]: far_value}
    for bit in reversed(bits[:-1]):
        parts.update({k | bit: swapped(p, axis, bit) for k, p in list(parts.items())})
    return [parts[k] for k in range(len(parts))]


def summed_terms(parts, axis, after=None):
    left = dict(enumerate(parts))
    bits = bits_of(axis)
    terms = [parts[0]]
    for bit in bits:
        kept = {}
        for k in sorted(left, reverse=True):
            if k & bit == 0:
                going = left[k | bit]
                if after is not None and bit == bits[-1]:
                    going, _ = lax.optimization_barrier((going, after))
                arrived = swapped(going, axis, bit)
                if k == 0:
                    terms.append(arrived)
                    kept[k] = None
                else:
                    kept[k] = (left[k].astype(F32) + arrived.astype(F32)).astype(BF16)
        left = kept
    return terms


def doubled(value, axis, order):
    blocks = value[None]
    for bit in order:
        blocks = jnp.concatenate([blocks, swapped(blocks, axis, bit)], axis=0)
    return blocks


def halved(blocks, axis, order):
    for bit in reversed(order):
        half = blocks.shape[0] // 2
        arrived = swapped(blocks[half:], axis, bit)
        blocks = (blocks[:half].astype(F32) + arrived.astype(F32)).astype(BF16)
    return blocks[0].astype(F32)


def block_order(axis, order):
    count = lax.axis_size(axis)
    device = [sum(bit for b, bit in enumerate(order) if p >> b & 1) for p in range(count)]
    inverse = [device.index(k) for k in range(count)]
    position = lax.axis_index(axis)
    owner = position ^ jnp.asarray(device, jnp.int32)
    near = position ^ jnp.arange(count, dtype=jnp.int32)
    hit = near[:, None] == jnp.arange(count, dtype=jnp.int32)[None, :]
    place = jnp.sum(jnp.where(hit, jnp.asarray(inverse, jnp.int32)[None, :], 0), axis=1)
    return owner, place.astype(jnp.int32)


def exchanged_parts(parts, axis):
    return [p if k == 0 else swapped(p, axis, k) for k, p in enumerate(parts)]


def summed_everywhere(value, axes):
    size = value.shape[0]
    value = jnp.pad(value, (0, -size % 1024)).reshape(-1, 128)
    for axis in axes:
        for bit in bits_of(axis):
            value = value + swapped(value, axis, bit)
    return value.reshape(-1)[:size]


def sent_and_summed(value, axis):
    count = lax.axis_size(axis)
    blocks = value.reshape(count, value.shape[0] // count, *value.shape[1:])
    arrived = lax.all_to_all(blocks, axis, 0, 0, tiled=True)
    return jnp.sum(arrived.astype(F32), axis=0)


def attention_tables(length, place, chosen):
    count = place.shape[0]
    heads = chosen.shape[0]
    nblocks = (length + BLOCK - 1) // BLOCK
    last = nblocks - 1
    number = jnp.arange(count, dtype=jnp.int32)
    same = jnp.zeros_like(number)
    common = jnp.stack([same, same + last, number - 1, number, number + 1], axis=1)
    middle = (number > 0) & (number < last)
    good = jnp.stack(
        [
            middle | (number > last),
            middle | (number > last),
            (number - 1 > 0) & (number - 1 < last) & (number != last),
            middle,
            (number + 1 < last) & (number > 0),
        ],
        axis=1,
    )
    drawn = jnp.transpose(chosen, (1, 2, 0))
    away = number[:, None, None]
    fresh = (
        (drawn > 0)
        & (drawn < last)
        & (jnp.abs(drawn - away) > 1)
        & (away > 0)
        & (away != last)
    )
    first, second, third = drawn[:, 0], drawn[:, 1], drawn[:, 2]
    fresh = jnp.stack(
        [
            fresh[:, 0],
            fresh[:, 1] & (second != first),
            fresh[:, 2] & (third != first) & (third != second),
        ],
        axis=1,
    )
    flags = jnp.concatenate(
        [jnp.broadcast_to(good[:, :, None], (count, 5, heads)), fresh], axis=1
    )
    bias = jnp.where(flags, 0.0, NEGATIVE).astype(F32)
    bias = jnp.broadcast_to(bias[..., None], (*bias.shape, HEAD_DIM))
    bias = bias.reshape(count, SLOTS, heads * HEAD_DIM)
    wanted = jnp.concatenate([common, drawn.reshape(count, -1)], axis=1)
    hit = wanted[:, :, None] == place[None, None, :]
    stored = jnp.sum(jnp.where(hit, number[None, None, :], 0), axis=-1).astype(jnp.int32)
    limits = jnp.clip(length - BLOCK * place, 0, BLOCK).astype(jnp.int32)
    ends = jnp.stack([last, length - BLOCK * last]).astype(jnp.int32)
    return stored, limits, ends, bias


def block_rows(index):
    return pl.ds(pl.multiple_of(index * BLOCK, BLOCK), BLOCK)


def spread(rows, heads):
    lane = lax.broadcasted_iota(jnp.int32, (1, heads * HEAD_DIM), 1)
    zero = jnp.zeros_like(rows)
    return jnp.concatenate(
        [jnp.where(lane // HEAD_DIM == h, rows, zero) for h in range(heads)], axis=0
    )


def collapse(full, heads):
    lane = lax.broadcasted_iota(jnp.int32, (1, PAIR), 1)
    pieces = []
    for pair in range(heads // 2):
        cols = slice(PAIR * pair, PAIR * (pair + 1))
        even = full[2 * pair * HEAD_DIM : (2 * pair + 1) * HEAD_DIM, cols]
        odd = full[(2 * pair + 1) * HEAD_DIM : (2 * pair + 2) * HEAD_DIM, cols]
        pieces.append(jnp.where(lane < HEAD_DIM, even, odd))
    return jnp.concatenate(pieces, axis=1)


def gathered_keys(ref, start, stored, number, heads):
    width = heads * HEAD_DIM
    lane = lax.broadcasted_iota(jnp.int32, (1, PAIR), 1)
    parts = [ref[block_rows(stored[number, s]), start : start + width] for s in range(5)]
    for s in range(3):
        pieces = []
        for pair in range(heads // 2):
            cols = slice(start + PAIR * pair, start + PAIR * (pair + 1))
            at = 5 + heads * s + 2 * pair
            even = ref[block_rows(stored[number, at]), cols]
            odd = ref[block_rows(stored[number, at + 1]), cols]
            pieces.append(jnp.where(lane < HEAD_DIM, even, odd))
        parts.append(jnp.concatenate(pieces, axis=1))
    return jnp.concatenate(parts, axis=0)


def slot(value, index):
    return value[BLOCK * index : BLOCK * (index + 1)]


def biased(scores, bias, last_rows):
    row = lax.broadcasted_iota(jnp.int32, (BLOCK, 1), 0)
    parts = [slot(scores, s) + bias[s : s + 1] for s in range(SLOTS)]
    parts[1] = jnp.where(row < last_rows, parts[1], NEGATIVE)
    return parts


def total(parts):
    return functools.reduce(jnp.add, parts)


def attend_kernel(heads, stored, limits, ends, qkv_ref, bias_ref, out_ref, log_ref, keep_ref):
    count = bias_ref.shape[0]
    width = heads * HEAD_DIM
    scale = jnp.asarray(HEAD_DIM**-0.5, BF16)

    def item(number):
        here = block_rows(stored[number, 3])
        queries = spread(qkv_ref[here, :width] * scale, heads)
        keys = gathered_keys(qkv_ref, width, stored, number, heads)
        parts = biased(matmul(keys, queries, NT), bias_ref[number], ends[1])
        top = jnp.max(functools.reduce(jnp.maximum, parts), axis=0, keepdims=True)
        weights = [jnp.exp(p - top) for p in parts]
        row_total = jnp.sum(total(weights), axis=0, keepdims=True)
        inverse = 1.0 / row_total
        probs = jnp.concatenate([(p * inverse).astype(BF16) for p in weights], axis=0)
        values = gathered_keys(qkv_ref, 2 * width, stored, number, heads)
        out_ref[here, :] = collapse(matmul(probs, values, TN), heads).astype(BF16)
        log_ref[pl.ds(number, 1), :] = top + jnp.log(row_total)

    def step(group, carry):
        for part in range(4):
            item(1 + group * 4 + part)
        return carry

    lax.fori_loop(0, (count - 1) // 4, step, 0)
    for number in range(1 + (count - 1) // 4 * 4, count):
        item(number)

    row = lax.broadcasted_iota(jnp.int32, (BLOCK, 1), 0)
    per = CHUNK // BLOCK
    chunks = count // per

    def chunk_rows(chunk):
        return pl.ds(pl.multiple_of(chunk * CHUNK, CHUNK), CHUNK)

    numbers = [0, ends[0]]
    rows_of = [block_rows(stored[number, 3]) for number in numbers]
    queries = [spread(qkv_ref[at, :width] * scale, heads) for at in rows_of]

    def scores(chunk, tops):
        at = chunk_rows(chunk)
        keys = qkv_ref[at, width : 2 * width]
        found = []
        for end in range(2):
            raw = matmul(keys, queries[end], NT)
            parts = [
                jnp.where(row < limits[chunk * per + s], slot(raw, s), NEGATIVE)
                for s in range(per)
            ]
            keep_ref[end, at, :] = jnp.concatenate(parts, axis=0)
            found.append(jnp.maximum(tops[end], functools.reduce(jnp.maximum, parts)))
        return tuple(found)

    tops = lax.fori_loop(0, chunks, scores, (jnp.full((BLOCK, width), NEGATIVE, F32),) * 2)
    tops = [jnp.max(top, axis=0, keepdims=True) for top in tops]

    def exponents(chunk, totals):
        at = chunk_rows(chunk)
        found = []
        for end in range(2):
            weights = jnp.exp(keep_ref[end, at, :] - tops[end])
            keep_ref[end, at, :] = weights
            found.append(totals[end] + total([slot(weights, s) for s in range(per)]))
        return tuple(found)

    totals = lax.fori_loop(0, chunks, exponents, (jnp.zeros((BLOCK, width), F32),) * 2)
    totals = [jnp.sum(found, axis=0, keepdims=True) for found in totals]
    inverses = [1.0 / found for found in totals]

    def contexts(chunk, sums):
        at = chunk_rows(chunk)
        values = qkv_ref[at, 2 * width :]
        return tuple(
            sums[end] + matmul((keep_ref[end, at, :] * inverses[end]).astype(BF16), values, TN)
            for end in range(2)
        )

    sums = lax.fori_loop(0, chunks, contexts, (jnp.zeros((width, width), F32),) * 2)
    for end in range(2):
        out_ref[rows_of[end], :] = collapse(sums[end], heads).astype(BF16)
        log_ref[pl.ds(numbers[end], 1), :] = tops[end] + jnp.log(totals[end])


def attend_back_kernel(
    heads,
    stored,
    limits,
    ends,
    qkv_ref,
    grad_ref,
    bias_ref,
    log_ref,
    out_ref,
    keys_acc,
    values_acc,
    probs_ref,
    inner_ref,
):
    count = bias_ref.shape[0]
    width = heads * HEAD_DIM
    scale = jnp.asarray(HEAD_DIM**-0.5, BF16)
    lane = lax.broadcasted_iota(jnp.int32, (1, PAIR), 1)
    keys_acc[...] = jnp.zeros_like(keys_acc)
    values_acc[...] = jnp.zeros_like(values_acc)

    def accumulate(acc, value, number):
        for s in range(5):
            acc[block_rows(stored[number, s]), :] += slot(value, s)
        for s in range(3):
            for h in range(heads):
                cols = slice(PAIR * (h // 2), PAIR * (h // 2 + 1))
                mine = (lane < HEAD_DIM) == (h % 2 == 0)
                term = jnp.where(mine, slot(value, 5 + s)[:, cols], 0.0)
                acc[block_rows(stored[number, 5 + heads * s + h]), cols] += term

    def item(number):
        here = block_rows(stored[number, 3])
        queries = spread(qkv_ref[here, :width] * scale, heads)
        grads = spread(grad_ref[here, :], heads)
        keys = gathered_keys(qkv_ref, width, stored, number, heads)
        values = gathered_keys(qkv_ref, 2 * width, stored, number, heads)
        log_total = log_ref[pl.ds(number, 1), :]
        parts = biased(matmul(keys, queries, NT), bias_ref[number], ends[1])
        probs = [jnp.exp(p - log_total) for p in parts]
        found = matmul(values, grads, NT)
        found = [slot(found, s) for s in range(SLOTS)]
        inner = total([p * d for p, d in zip(probs, found)])
        inner = jnp.sum(inner, axis=0, keepdims=True)
        grad_scores = jnp.concatenate(
            [(p * (d - inner)).astype(BF16) for p, d in zip(probs, found)], axis=0
        )
        probs_low = jnp.concatenate([p.astype(BF16) for p in probs], axis=0)
        accumulate(values_acc, matmul(probs_low, grads, NN), number)
        accumulate(keys_acc, matmul(grad_scores, queries, NN), number)
        grad_queries = collapse(matmul(grad_scores, keys, TN), heads) * HEAD_DIM**-0.5
        out_ref[here, :width] = grad_queries.astype(BF16)

    def step(group, carry):
        for part in range(4):
            item(1 + group * 4 + part)
        return carry

    lax.fori_loop(0, (count - 1) // 4, step, 0)
    for number in range(1 + (count - 1) // 4 * 4, count):
        item(number)

    row = lax.broadcasted_iota(jnp.int32, (BLOCK, 1), 0)
    per = CHUNK // BLOCK
    chunks = count // per

    def chunk_rows(chunk):
        return pl.ds(pl.multiple_of(chunk * CHUNK, CHUNK), CHUNK)

    numbers = [0, ends[0]]
    rows_of = [block_rows(stored[number, 3]) for number in numbers]
    queries = [spread(qkv_ref[at, :width] * scale, heads) for at in rows_of]
    grads = [spread(grad_ref[at, :], heads) for at in rows_of]
    log_rows = [log_ref[pl.ds(number, 1), :] for number in numbers]

    def first(chunk, inners):
        at = chunk_rows(chunk)
        keys = qkv_ref[at, width : 2 * width]
        values = qkv_ref[at, 2 * width :]
        sums = []
        for end in range(2):
            scores = matmul(keys, queries[end], NT)
            parts = [
                jnp.where(row < limits[chunk * per + s], slot(scores, s), NEGATIVE)
                for s in range(per)
            ]
            probs = jnp.exp(jnp.concatenate(parts, axis=0) - log_rows[end])
            found = matmul(values, grads[end], NT)
            probs_ref[end, at, :] = probs
            inner_ref[end, at, :] = found
            both = probs * found
            sums.append(inners[end] + total([slot(both, s) for s in range(per)]))
        return tuple(sums)

    inners = lax.fori_loop(0, chunks, first, (jnp.zeros((BLOCK, width), F32),) * 2)
    inners = [jnp.sum(inner, axis=0, keepdims=True) for inner in inners]

    def second(chunk, sums):
        at = chunk_rows(chunk)
        keys = qkv_ref[at, width : 2 * width]
        found, to_values, to_keys = [], values_acc[at, :], keys_acc[at, :]
        for end in range(2):
            probs = probs_ref[end, at, :]
            grad_scores = (probs * (inner_ref[end, at, :] - inners[end])).astype(BF16)
            to_values = to_values + matmul(probs.astype(BF16), grads[end], NN)
            to_keys = to_keys + matmul(grad_scores, queries[end], NN)
            found.append(sums[end] + matmul(grad_scores, keys, TN))
        out_ref[at, width : 2 * width] = to_keys.astype(BF16)
        out_ref[at, 2 * width :] = to_values.astype(BF16)
        return tuple(found)

    sums = lax.fori_loop(0, chunks, second, (jnp.zeros((width, width), F32),) * 2)
    for end in range(2):
        grad_queries = collapse(sums[end], heads) * HEAD_DIM**-0.5
        out_ref[rows_of[end], :width] = grad_queries.astype(BF16)


def in_smem():
    return pl.BlockSpec(memory_space=pltpu.SMEM)


def in_vmem():
    return pl.BlockSpec(memory_space=pltpu.VMEM)


def attention_cost(qkv, matmuls):
    rows, width = qkv.shape
    width //= 3
    return pl.CostEstimate(
        flops=2 * matmuls * rows * CHUNK * width,
        bytes_accessed=12 * rows * width,
        transcendentals=rows * CHUNK * width // HEAD_DIM,
    )


def attend(qkv, tables, heads):
    stored, limits, ends, bias = tables
    rows, width = qkv.shape[0], heads * HEAD_DIM
    return pl.pallas_call(
        functools.partial(attend_kernel, heads),
        out_shape=(
            jax.ShapeDtypeStruct((rows, width), BF16),
            jax.ShapeDtypeStruct((rows // BLOCK, width), F32),
        ),
        in_specs=[in_smem()] * 3 + [in_vmem()] * 2,
        out_specs=(in_vmem(), in_vmem()),
        scratch_shapes=[pltpu.VMEM((2, rows, width), F32)],
        compiler_params=pltpu.CompilerParams(vmem_limit_bytes=32 << 20),
        cost_estimate=attention_cost(qkv, 8),
        name="attend",
    )(stored, limits, ends, qkv, bias)


def attend_back(qkv, grad_context, log_totals, tables, heads):
    stored, limits, ends, bias = tables
    rows, width = qkv.shape[0], heads * HEAD_DIM
    return pl.pallas_call(
        functools.partial(attend_back_kernel, heads),
        out_shape=jax.ShapeDtypeStruct(qkv.shape, BF16),
        in_specs=[in_smem()] * 3 + [in_vmem()] * 4,
        out_specs=in_vmem(),
        scratch_shapes=[pltpu.VMEM((rows, width), F32)] * 2
        + [pltpu.VMEM((2, rows, width), F32)] * 2,
        compiler_params=pltpu.CompilerParams(vmem_limit_bytes=32 << 20),
        cost_estimate=attention_cost(qkv, 16),
        name="attend_back",
    )(stored, limits, ends, qkv, grad_context, bias, log_totals)


TILE = 256


def pick(refs):
    per = pl.num_programs(0) // len(refs)
    value = refs[0][...]
    for k, ref in enumerate(refs[1:], 1):
        value = jnp.where(pl.program_id(0) >= k * per, ref[...], value)
    return value


def tile_specs(arrays):
    def spec(k, value):
        tiles = value.shape[0] // TILE
        return pl.BlockSpec(
            (TILE, value.shape[1]), lambda i: (jnp.clip(i - k * tiles, 0, tiles - 1), 0)
        )

    return [spec(k, value) for k, value in enumerate(arrays)]


def gelu_and_slope(pre):
    scale = (2.0 / 3.141592653589793) ** 0.5
    square = pre * pre
    bent = jnp.tanh(scale * pre * (1.0 + 0.044715 * square))
    half = 0.5 + 0.5 * bent
    slope = half + (0.5 * scale) * pre * (1.0 - bent * bent) * (1.0 + 0.134145 * square)
    return pre * half, slope


def put(refs, value):
    per = pl.num_programs(0) // len(refs)
    for k, ref in enumerate(refs):

        @pl.when(pl.program_id(0) // per == k)
        def _(ref=ref):
            ref[...] = value


def feed_kernel(parts, *refs):
    normed = pick(refs[:parts])
    grads = pick(refs[parts : 2 * parts])
    weight_ref, bias_ref, active_ref, grad_ref, *quarter_refs = refs[2 * parts :]
    units = bias_ref.shape[1]
    up = weight_ref[:, :units]
    down = weight_ref[:, units:]
    active, slope = gelu_and_slope(matmul(normed, up, NN) + bias_ref[...])
    active = active.astype(BF16)
    grad_hidden = (matmul(grads, down, NN) * slope).astype(BF16)
    put(quarter_refs[:parts], matmul(grad_hidden, up, NT).astype(BF16))
    put(quarter_refs[parts:], matmul(active, down, NT).astype(BF16))
    active_ref[...] = active
    grad_ref[...] = grad_hidden


def feed(normed, grads, weights, bias):
    rows = sum(value.shape[0] for value in normed)
    features, units = weights.shape[0], bias.shape[1]
    whole = pl.BlockSpec((TILE, units), lambda i: (i, 0))
    once = pl.BlockSpec(weights.shape, lambda i: (0, 0), pipeline_mode=pl.Buffered(1))
    return pl.pallas_call(
        functools.partial(feed_kernel, len(normed)),
        grid=(rows // TILE,),
        out_shape=[jax.ShapeDtypeStruct((rows, units), BF16)] * 2
        + [jax.ShapeDtypeStruct(value.shape, BF16) for value in normed] * 2,
        in_specs=tile_specs(normed)
        + tile_specs(grads)
        + [once, pl.BlockSpec(bias.shape, lambda i: (0, 0))],
        out_specs=[whole, whole] + tile_specs(normed) * 2,
        compiler_params=pltpu.CompilerParams(vmem_limit_bytes=62 << 20),
        cost_estimate=pl.CostEstimate(
            flops=8 * rows * features * units,
            bytes_accessed=12 * rows * features + 4 * features * units,
            transcendentals=rows * units,
        ),
        name="feed",
    )(*normed, *grads, weights, bias)


def feed_grads_kernel(counts, *refs):
    groups, start = [], 0
    for count in counts:
        groups.append(pick(refs[start : start + count]))
        start += count
    normed, grads, active, grad_hidden = groups
    out_ref, sum_ref, acc_ref = refs[start:]
    units = sum_ref.shape[1]

    @pl.when(pl.program_id(0) == 0)
    def _():
        acc_ref[...] = jnp.zeros_like(acc_ref)
        sum_ref[...] = jnp.zeros_like(sum_ref)

    acc_ref[:, :units] += matmul(normed, grad_hidden, TN)
    acc_ref[:, units:] += matmul(grads, active, TN)
    sum_ref[...] += jnp.sum(grad_hidden.astype(F32), axis=0, keepdims=True)

    @pl.when(pl.program_id(0) == pl.num_programs(0) - 1)
    def _():
        out_ref[...] = acc_ref[...].astype(BF16)


def feed_grads(normed, grads, active, grad_hidden):
    rows = sum(value.shape[0] for value in normed)
    features, units = normed[0].shape[1], active[0].shape[1]
    groups = [normed, grads, active, grad_hidden]
    return pl.pallas_call(
        functools.partial(feed_grads_kernel, [len(group) for group in groups]),
        grid=(rows // TILE,),
        out_shape=[
            jax.ShapeDtypeStruct((features, 2 * units), BF16),
            jax.ShapeDtypeStruct((1, units), F32),
        ],
        in_specs=[spec for group in groups for spec in tile_specs(group)],
        out_specs=[
            pl.BlockSpec((features, 2 * units), lambda i: (0, 0)),
            pl.BlockSpec((1, units), lambda i: (0, 0)),
        ],
        scratch_shapes=[pltpu.VMEM((features, 2 * units), F32)],
        compiler_params=pltpu.CompilerParams(vmem_limit_bytes=62 << 20),
        cost_estimate=pl.CostEstimate(
            flops=4 * rows * features * units,
            bytes_accessed=8 * rows * features + 4 * features * units,
            transcendentals=0,
        ),
        name="feed_grads",
    )(*normed, *grads, *active, *grad_hidden)


def norm_parts(rows):
    centred = rows - jnp.mean(rows, axis=-1, keepdims=True)
    inverse = lax.rsqrt(jnp.mean(centred * centred, axis=-1, keepdims=True) + EPS)
    return centred * inverse, inverse


def norm_back(grad_normed, unit, inverse, gain):
    grad_unit = grad_normed * gain
    return inverse * (
        grad_unit
        - jnp.mean(grad_unit, axis=-1, keepdims=True)
        - unit * jnp.mean(grad_unit * unit, axis=-1, keepdims=True)
    )


def whole_spec(value):
    return pl.BlockSpec(value.shape, lambda i: (0,) * value.ndim)


def tiled_spec(value, tile=TILE):
    return pl.BlockSpec((tile, value.shape[1]), lambda i: (i, 0))


def like(value, dtype=None):
    return jax.ShapeDtypeStruct(value.shape, dtype or value.dtype)


def limit(mebibytes):
    return pltpu.CompilerParams(vmem_limit_bytes=mebibytes << 20)


def cost(flops, moved):
    return pl.CostEstimate(flops=flops, bytes_accessed=moved, transcendentals=0)


def unit_kernel(rows_ref, unit_ref):
    unit_ref[...] = norm_parts(rows_ref[...].astype(F32))[0].astype(BF16)


def unit_rows(rows):
    return pl.pallas_call(
        unit_kernel,
        grid=(rows.shape[0] // TILE,),
        out_shape=like(rows),
        in_specs=[tiled_spec(rows)],
        out_specs=tiled_spec(rows),
        cost_estimate=cost(8 * rows.size, 4 * rows.size),
        name="unit",
    )(rows)


def project_kernel(parts, owner_a, owner_b, *refs):
    unit = pick(refs[:parts])
    first_ref, last_ref, norm_ref, bias_ref, qkv_ref, weight_ref = refs[parts:]
    count, own, split = first_ref.shape

    @pl.when(pl.program_id(0) == 0)
    def _():
        for p in range(count):
            at = pl.ds(pl.multiple_of(owner_a[p] * own, own), own)
            weight_ref[at, :split] = first_ref[p]
            at = pl.ds(pl.multiple_of(owner_b[p] * own, own), own)
            weight_ref[at, split:] = last_ref[p]

    normed = (unit.astype(F32) * norm_ref[0:1, :] + norm_ref[1:2, :]).astype(BF16)
    qkv_ref[...] = (matmul(normed, weight_ref[...], NN) + bias_ref[...]).astype(BF16)


def project(unit, first, last, owner_a, owner_b, norm, bias):
    rows = sum(value.shape[0] for value in unit)
    features, width = unit[0].shape[1], bias.shape[1]
    qkv = jax.ShapeDtypeStruct((rows, width), BF16)
    weight = jax.ShapeDtypeStruct((features, width), BF16)
    return pl.pallas_call(
        functools.partial(project_kernel, len(unit)),
        grid=(rows // TILE,),
        out_shape=[qkv, weight],
        in_specs=[in_smem()] * 2
        + tile_specs(unit)
        + [whole_spec(value) for value in (first, last, norm, bias)],
        out_specs=[tiled_spec(qkv), whole_spec(weight)],
        compiler_params=limit(40),
        cost_estimate=cost(2 * rows * features * width, 2 * rows * (features + width)),
        name="project",
    )(owner_a, owner_b, *unit, first, last, norm, bias)


def middle_kernel(parts, *refs):
    context_refs, out_refs = refs[:parts], refs[parts : 2 * parts]
    rows_ref, vector_ref, middle_ref, normed_ref = refs[2 * parts :]
    middle = rows_ref[...].astype(F32) + vector_ref[0:1, :]
    for context_ref, out_ref in zip(context_refs, out_refs):
        middle += matmul(context_ref[...], out_ref[...], NT)
    middle_ref[...] = middle
    unit = norm_parts(middle)[0]
    normed_ref[...] = (unit * vector_ref[1:2, :] + vector_ref[2:3, :]).astype(BF16)


def middle_rows(context, out_parts, rows, vectors):
    return pl.pallas_call(
        functools.partial(middle_kernel, len(context)),
        grid=(rows.shape[0] // TILE,),
        out_shape=[like(rows, F32), like(rows)],
        in_specs=[tiled_spec(value) for value in context]
        + [whole_spec(value) for value in out_parts]
        + [tiled_spec(rows), whole_spec(vectors)],
        out_specs=[tiled_spec(rows), tiled_spec(rows)],
        compiler_params=limit(40),
        cost_estimate=cost(2 * rows.size * rows.shape[1], 12 * rows.size),
        name="middle",
    )(*context, *out_parts, rows, vectors)


def middle_back_kernel(terms, parts, *refs):
    term_refs, out_refs = refs[:terms], refs[terms : terms + parts]
    middle_ref, cotangent_ref, vector_ref, grad_ref, low_ref, sum_ref = refs[
        terms + parts : terms + parts + 6
    ]
    head_refs = refs[terms + parts + 6 :]
    grad_normed = total([ref[...].astype(F32) for ref in term_refs])
    unit, inverse = norm_parts(middle_ref[...])
    cotangent = cotangent_ref[...].astype(F32)
    grad = cotangent + norm_back(grad_normed, unit, inverse, vector_ref[1:2, :])
    grad_ref[...] = grad
    low = grad.astype(BF16)
    low_ref[...] = low
    for head_ref, out_ref in zip(head_refs, out_refs):
        head_ref[...] = matmul(low, out_ref[...], NN).astype(BF16)
    sums = [
        jnp.sum(value, axis=0, keepdims=True)
        for value in (grad_normed * unit, grad_normed, grad, cotangent)
    ]
    sums = jnp.concatenate(sums, axis=0)

    @pl.when(pl.program_id(0) == 0)
    def _():
        sum_ref[...] = sums

    @pl.when(pl.program_id(0) > 0)
    def _():
        sum_ref[...] += sums


def middle_back(terms, out_parts, middle, cotangent, vectors):
    rows, features = middle.shape
    sums = jax.ShapeDtypeStruct((4, features), F32)
    head = jax.ShapeDtypeStruct((rows, out_parts[0].shape[1]), BF16)
    return pl.pallas_call(
        functools.partial(middle_back_kernel, len(terms), len(out_parts)),
        grid=(rows // TILE,),
        out_shape=[like(middle), like(middle, BF16), sums] + [head] * len(out_parts),
        in_specs=[tiled_spec(value) for value in terms]
        + [whole_spec(value) for value in out_parts]
        + [tiled_spec(middle), tiled_spec(cotangent), whole_spec(vectors)],
        out_specs=[tiled_spec(middle), tiled_spec(middle), whole_spec(sums)]
        + [tiled_spec(head)] * len(out_parts),
        compiler_params=limit(40),
        cost_estimate=cost(2 * middle.size * features, 20 * middle.size),
        name="middle_back",
    )(*terms, *out_parts, middle, cotangent, vectors)


def qkv_grads_kernel(parts, place_a, place_b, *refs):
    unit_refs = refs[:parts]
    grad_ref, weight_ref, first_ref, last_ref, late_ref, sum_ref = refs[parts:]
    own, split = first_ref.shape[1:]
    near = unit_refs[0].shape[0]

    @pl.when(pl.program_id(0) == 0)
    def _():
        sum_ref[...] = jnp.sum(grad_ref[...].astype(F32), axis=0, keepdims=True)

    raw = total(
        [
            matmul(ref[...], grad_ref[near * k : near * (k + 1), :], TN)
            for k, ref in enumerate(unit_refs)
        ]
    )
    weight = weight_ref[...].astype(F32)
    step = raw.shape[0]
    for b in range(step // own):
        block = pl.program_id(0) * (step // own) + b
        rows = raw[own * b : own * (b + 1)].astype(BF16)
        first_ref[place_a[block]] = rows[:, :split]
        last_ref[place_b[block]] = rows[:, split:]
    for row, value in enumerate((raw * weight, weight * sum_ref[...])):
        lanes = total([value[:, 128 * c : 128 * (c + 1)] for c in range(value.shape[1] // 128)])
        for b in range(step // 128):
            turned = lanes[128 * b : 128 * (b + 1)].T
            found = jnp.sum(turned, axis=0, keepdims=True)
            late_ref[row : row + 1, 128 * b : 128 * (b + 1)] = found


def qkv_grads(unit, grad_qkv, weight, place_a, place_b, split, count):
    features, width = weight.shape
    own = features // count
    step = 256
    first = jax.ShapeDtypeStruct((count, own, split), BF16)
    last = jax.ShapeDtypeStruct((count, own, width - split), BF16)
    late = jax.ShapeDtypeStruct((2, features), F32)
    sums = jax.ShapeDtypeStruct((1, width), F32)
    return pl.pallas_call(
        functools.partial(qkv_grads_kernel, len(unit)),
        grid=(features // step,),
        out_shape=[first, last, late, sums],
        in_specs=[in_smem()] * 2
        + [pl.BlockSpec((value.shape[0], step), lambda i: (0, i)) for value in unit]
        + [whole_spec(grad_qkv), tiled_spec(weight, step)],
        out_specs=[
            whole_spec(first),
            whole_spec(last),
            pl.BlockSpec((2, step), lambda i: (0, i)),
            whole_spec(sums),
        ],
        compiler_params=limit(40),
        cost_estimate=cost(2 * grad_qkv.size * features, 2 * grad_qkv.size + 8 * weight.size),
        name="qkv_grads",
    )(place_a, place_b, *unit, grad_qkv, weight)


def back_rows_kernel(grad_ref, weight_ref, *quarter_refs):
    put(quarter_refs, matmul(grad_ref[...], weight_ref[...], NT).astype(BF16))


def back_rows(grad_qkv, weight, start, quarters, near):
    width = grad_qkv.shape[1]
    features = weight.shape[0]
    tiles = near // TILE
    quarter = jax.ShapeDtypeStruct((near, features), BF16)
    return pl.pallas_call(
        back_rows_kernel,
        grid=(quarters * tiles,),
        out_shape=[quarter] * quarters,
        in_specs=[
            pl.BlockSpec((TILE, width), lambda i: (i + start * tiles, 0)),
            whole_spec(weight),
        ],
        out_specs=tile_specs([quarter] * quarters),
        compiler_params=limit(40),
        cost_estimate=cost(2 * quarters * near * width * features, 4 * quarters * quarter.size),
        name="back_rows",
    )(grad_qkv, weight)


def input_back_kernel(terms, *refs):
    term_refs = refs[:terms]
    rows_ref, middle_ref, vector_ref, out_ref = refs[terms:]
    grad_normed = total([ref[...].astype(F32) for ref in term_refs])
    unit, inverse = norm_parts(rows_ref[...].astype(F32))
    grad = norm_back(grad_normed, unit, inverse, vector_ref[0:1, :])
    out_ref[...] = (middle_ref[...] + grad).astype(BF16)


def input_back(terms, rows, grad_middle, vectors):
    return pl.pallas_call(
        functools.partial(input_back_kernel, len(terms)),
        grid=(rows.shape[0] // TILE,),
        out_shape=like(rows),
        in_specs=[tiled_spec(value) for value in (*terms, rows, grad_middle)]
        + [whole_spec(vectors)],
        out_specs=tiled_spec(rows),
        compiler_params=limit(40),
        cost_estimate=cost(20 * rows.size, 14 * rows.size),
        name="input_back",
    )(*terms, rows, grad_middle, vectors)


def per_device(
    tokens,
    output_cotangent,
    lengths,
    block_place,
    random_blocks,
    qkv_weight,
    out_weight,
    up_weight,
    down_weight,
    vectors,
    hidden_bias,
):
    ways = lax.axis_size("tensor")
    spread_ways = lax.axis_size("dp")
    position = lax.axis_index("tensor")
    index = lax.axis_index("dp") * ways + position
    near = tokens.shape[0]
    rows = near * ways
    features = tokens.shape[1]
    width = qkv_weight.shape[2]
    heads = width // HEAD_DIM
    units = up_weight.shape[1]
    own = features // spread_ways
    piece = vectors.shape[1]
    unit_piece = hidden_bias.shape[1]

    def quarters(value):
        return [value[k * near : (k + 1) * near] for k in range(ways)]

    small = jnp.zeros((8, features), F32)
    small = lax.dynamic_update_slice(small, vectors, (0, index * piece))
    small_hidden = jnp.zeros((1, units * ways), F32)
    small_hidden = lax.dynamic_update_slice(small_hidden, hidden_bias, (0, index * unit_piece))
    packed = jnp.concatenate([small.reshape(-1), small_hidden.reshape(-1)])
    packed = summed_everywhere(packed, ("tensor",))

    unit_near = unit_rows(tokens)
    going, packed = lax.optimization_barrier((unit_near, packed))
    unit_far = far(going, "tensor")
    unit_parts = gathered_parts(unit_near, unit_far, "tensor")
    cotangent_near, _ = lax.optimization_barrier((output_cotangent, unit_far))
    cotangent_far = far(cotangent_near, "tensor")

    bits = bits_of("dp")
    order_a = bits[::-1]
    order_b = bits[:1] + bits[:0:-1]
    owner_a, place_a = block_order("dp", order_a)
    owner_b, place_b = block_order("dp", order_b)
    split = 2 * width
    qkv_flat = qkv_weight.reshape(own, 3 * width)
    first_blocks = doubled(qkv_flat[:, :split], "dp", order_a)
    last_blocks = doubled(qkv_flat[:, split:], "dp", order_b)
    out_own, _ = lax.optimization_barrier((out_weight, last_blocks))
    out_blocks = doubled(out_own, "dp", order_a)
    feed_flat = jnp.concatenate([up_weight, down_weight], axis=1)
    feed_full = lax.all_gather(feed_flat, "dp", axis=0, tiled=True)

    packed = summed_everywhere(packed, ("dp",))
    vectors_full = packed[: 8 * features].reshape(8, features)
    hidden_full = packed[8 * features :]
    bias_query = lax.dynamic_slice_in_dim(vectors_full[6], position * width, width)
    bias_value = lax.dynamic_slice_in_dim(vectors_full[7], position * width, width)
    bias_qkv = jnp.concatenate([bias_query, jnp.zeros_like(bias_query), bias_value])[None]
    bias_hidden = lax.dynamic_slice_in_dim(hidden_full, position * units, units)[None]
    norm_one = vectors_full[:2]
    norm_two = jnp.stack([vectors_full[4], vectors_full[2], vectors_full[3]])

    placed = block_place[0].reshape(ways, -1)
    order = position ^ jnp.arange(ways, dtype=jnp.int32)
    chosen_rows = order[:, None, None] == jnp.arange(ways, dtype=jnp.int32)[None, :, None]
    place = jnp.sum(jnp.where(chosen_rows, placed[None], 0), axis=1).reshape(-1)
    tables = attention_tables(lengths[0], place, random_blocks[0])

    qkv, qkv_full = project(
        unit_parts, first_blocks, last_blocks, owner_a, owner_b, norm_one, bias_qkv
    )
    context, log_totals = attend(qkv, tables, heads)
    placed_blocks = owner_a[:, None] == jnp.arange(spread_ways, dtype=jnp.int32)[None, :]
    out_group = jnp.einsum(
        "pi,prf->irf",
        placed_blocks.astype(BF16),
        out_blocks,
        preferred_element_type=BF16,
    ).reshape(features, width)
    out_going, _ = lax.optimization_barrier((out_group, cotangent_far))
    out_far = far(out_going, "tensor")
    context, out_far, cotangent_far = lax.optimization_barrier(
        (context, out_far, cotangent_far)
    )
    grad_parts = gathered_parts(output_cotangent, cotangent_far, "tensor")

    out_parts = gathered_parts(out_group, out_far, "tensor")
    context_near = exchanged_parts(quarters(context), "tensor")
    middle, normed_two = middle_rows(context_near, out_parts, tokens, norm_two)

    half = ways // 2
    normed_far = far(normed_two, "tensor")
    normed_parts = gathered_parts(normed_two, normed_far, "tensor")
    near_half = feed(normed_parts[:half], grad_parts[:half], feed_full, bias_hidden)
    normed_far, near_half = lax.optimization_barrier((normed_far, near_half))
    normed_parts[half:] = gathered_parts(normed_two, normed_far, "tensor")[half:]
    far_half = feed(normed_parts[half:], grad_parts[half:], feed_full, bias_hidden)
    active, grad_hidden = [near_half[0], far_half[0]], [near_half[1], far_half[1]]
    back_parts = near_half[2 : 2 + half] + far_half[2 : 2 + half]
    feed_parts = near_half[2 + half :] + far_half[2 + half :]
    back_terms = summed_terms(back_parts, "tensor")
    feed_sums, sum_hidden = feed_grads(normed_parts, grad_parts, active, grad_hidden)
    back_terms, feed_sums = lax.optimization_barrier((back_terms, feed_sums))
    feed_weight_grads = lax.psum_scatter(feed_sums, "dp", scatter_dimension=0, tiled=True)
    feed_weight_grads = feed_weight_grads.astype(F32)

    grad_middle, grad_attended, sums_two, *grad_heads = middle_back(
        back_terms, out_parts, middle, output_cotangent, norm_two
    )
    grad_context = jnp.concatenate(exchanged_parts(grad_heads, "tensor"), axis=0)
    feed_terms = summed_terms(feed_parts, "tensor", after=grad_context)
    out_grad = [matmul(grad_attended, part, TN).astype(BF16) for part in context_near]
    grad_qkv = attend_back(qkv, grad_context, log_totals, tables, heads)
    grad_qkv, feed_terms = lax.optimization_barrier((grad_qkv, feed_terms))
    output = (total([term.astype(F32) for term in feed_terms]) + middle + vectors_full[5]).astype(
        BF16
    )

    first_raw, last_raw, late, sum_qkv = qkv_grads(
        unit_parts, grad_qkv, qkv_full, place_a, place_b, split, spread_ways
    )
    far_rows = back_rows(grad_qkv, qkv_full, half, half, near)
    near_rows = back_rows(grad_qkv, qkv_full, 0, half, near)
    normed_one_terms = summed_terms(list(near_rows) + list(far_rows), "tensor")
    first_raw = halved(first_raw, "dp", order_a)
    last_raw = halved(last_raw, "dp", order_b)
    out_terms = summed_terms(out_grad, "tensor", after=grad_qkv)
    out_grad = total([term.astype(F32) for term in out_terms]).astype(BF16)
    out_weight_grad = sent_and_summed(out_grad, "dp")
    input_grad = input_back(normed_one_terms, tokens, grad_middle, norm_one)

    head_sums = lax.dynamic_update_slice(
        jnp.zeros((3, features), F32), sum_qkv.reshape(3, width), (0, position * width)
    )
    hidden_sums = lax.dynamic_update_slice(
        jnp.zeros((1, units * ways), F32), sum_hidden, (0, position * units)
    )
    packed = jnp.concatenate(
        [late.reshape(-1), sums_two.reshape(-1), head_sums.reshape(-1), hidden_sums.reshape(-1)]
    )
    packed = summed_everywhere(packed, ("tensor", "dp"))
    by_feature = packed[: 9 * features].reshape(9, features)
    hidden_sums = packed[9 * features :]
    vectors_grad = lax.dynamic_slice_in_dim(by_feature, index * piece, piece, axis=1)
    vectors_grad = jnp.concatenate([vectors_grad[:7], vectors_grad[8:]], axis=0)
    hidden_bias_grad = lax.dynamic_slice_in_dim(hidden_sums, index * unit_piece, unit_piece)

    sum_qkv = lax.dynamic_slice_in_dim(by_feature[6:], position * width, width, axis=1)
    mine = lax.dynamic_slice_in_dim(norm_one, lax.axis_index("dp") * own, own, axis=1)
    raw = jnp.concatenate([first_raw, last_raw], axis=1).reshape(own, 3, width)
    qkv_weight_grad = mine[0][:, None, None] * raw + mine[1][:, None, None] * sum_qkv
    return (
        output,
        input_grad,
        qkv_weight_grad,
        out_weight_grad,
        feed_weight_grads[:, :units],
        feed_weight_grads[:, units:],
        vectors_grad,
        hidden_bias_grad[None, :],
    )


def solution(mesh):
    placed = (
        P(("dp", "tensor"), None),
        P(("dp", "tensor"), None),
        P("dp"),
        P("dp", None),
        P("dp", "tensor", None, None),
        P("dp", None, "tensor"),
        P("dp", "tensor"),
        P("dp", "tensor"),
        P("dp", "tensor"),
        P(None, ("dp", "tensor")),
        P(None, ("dp", "tensor")),
    )
    return jax.shard_map(
        per_device,
        mesh=mesh,
        in_specs=placed,
        out_specs=(
            P(("dp", "tensor"), None),
            P(("dp", "tensor"), None),
            P("dp", None, "tensor"),
            P("dp", "tensor"),
            P("dp", "tensor"),
            P("dp", "tensor"),
            P(None, ("dp", "tensor")),
            P(None, ("dp", "tensor")),
        ),
        check_vma=False,
    )
```

```python
import functools

import jax
import jax.numpy as jnp
from jax import lax
from jax.experimental import pallas as pl
from jax.experimental.pallas import tpu as pltpu
from jax.sharding import PartitionSpec as P

HEAD_DIM = 64
BLOCK = 64
PAIR = 2 * HEAD_DIM
SLOTS = 8
CHUNK = 512
EPS = 1e-05
NEGATIVE = -1e30
F32 = jnp.float32
BF16 = jnp.bfloat16
NT = (((1,), (1,)), ((), ()))
NN = (((1,), (0,)), ((), ()))
TN = (((0,), (0,)), ((), ()))


def matmul(left, right, dims):
    return lax.dot_general(left, right, dims, preferred_element_type=F32)


def swapped(value, axis, bit):
    count = lax.axis_size(axis)
    return lax.ppermute(value, axis, [(i, i ^ bit) for i in range(count)])


def bits_of(axis):
    count = lax.axis_size(axis)
    return [1 << b for b in range(count.bit_length() - 1)]


def together(*values):
    return lax.optimization_barrier(values)


def far(value, axis):
    return swapped(value, axis, bits_of(axis)[-1])


def gathered_parts(value, far_value, axis):
    bits = bits_of(axis)
    parts = {0: value, bits[-1]: far_value}
    for bit in reversed(bits[:-1]):
        parts.update({k | bit: swapped(p, axis, bit) for k, p in list(parts.items())})
    return [parts[k] for k in range(len(parts))]


def summed_halves(parts, axis):
    left = dict(enumerate(parts))
    terms = [parts[0]]
    for bit in bits_of(axis)[: len(parts).bit_length() - 2]:
        kept = {}
        for k in sorted(left, reverse=True):
            if k & bit == 0:
                arrived = swapped(left[k | bit], axis, bit)
                if k == 0:
                    terms.append(arrived)
                    kept[k] = None
                else:
                    kept[k] = added(left[k], arrived)
        left = kept
    return terms, left[len(parts) // 2]


def added(left, right):
    return (left.astype(F32) + right.astype(F32)).astype(BF16)


def doubled(value, axis, order):
    blocks = value[None]
    for bit in order:
        blocks = jnp.concatenate([blocks, swapped(blocks, axis, bit)], axis=0)
    return blocks


def halved(keep, send, axis, order):
    half = send.shape[0]
    arrived = swapped(send, axis, order[half.bit_length() - 1])
    rest = half // 2
    return added(keep[: half - rest], arrived[: half - rest]), added(
        keep[half - rest :], arrived[half - rest :]
    )


def block_owners(axis, order):
    count = lax.axis_size(axis)
    device = [sum(bit for b, bit in enumerate(order) if p >> b & 1) for p in range(count)]
    return lax.axis_index(axis) ^ jnp.asarray(device, jnp.int32)


def exchanged_parts(parts, axis):
    return [p if k == 0 else swapped(p, axis, k) for k, p in enumerate(parts)]


def summed_everywhere(value, axes):
    size = value.shape[0]
    value = jnp.pad(value, (0, -size % 1024)).reshape(-1, 128)
    for axis in axes:
        for bit in bits_of(axis):
            value = value + swapped(value, axis, bit)
    return value.reshape(-1)[:size]


def sent_and_summed(value, axis):
    count = lax.axis_size(axis)
    blocks = value.reshape(count, value.shape[0] // count, *value.shape[1:])
    arrived = lax.all_to_all(blocks, axis, 0, 0, tiled=True)
    return jnp.sum(arrived.astype(F32), axis=0)


def attention_tables(length, place, chosen):
    count = place.shape[0]
    heads = chosen.shape[0]
    nblocks = (length + BLOCK - 1) // BLOCK
    last = nblocks - 1
    number = jnp.arange(count, dtype=jnp.int32)
    same = jnp.zeros_like(number)
    common = jnp.stack([same, same + last, number - 1, number, number + 1], axis=1)
    middle = (number > 0) & (number < last)
    good = jnp.stack(
        [
            middle | (number > last),
            middle | (number > last),
            (number - 1 > 0) & (number - 1 < last) & (number != last),
            middle,
            (number + 1 < last) & (number > 0),
        ],
        axis=1,
    )
    drawn = jnp.transpose(chosen, (1, 2, 0))
    away = number[:, None, None]
    fresh = (
        (drawn > 0)
        & (drawn < last)
        & (jnp.abs(drawn - away) > 1)
        & (away > 0)
        & (away != last)
    )
    first, second, third = drawn[:, 0], drawn[:, 1], drawn[:, 2]
    fresh = jnp.stack(
        [
            fresh[:, 0],
            fresh[:, 1] & (second != first),
            fresh[:, 2] & (third != first) & (third != second),
        ],
        axis=1,
    )
    flags = jnp.concatenate(
        [jnp.broadcast_to(good[:, :, None], (count, 5, heads)), fresh], axis=1
    )
    bias = jnp.where(flags, 0.0, NEGATIVE).astype(F32)
    bias = jnp.broadcast_to(bias[..., None], (*bias.shape, HEAD_DIM))
    bias = bias.reshape(count, SLOTS, heads * HEAD_DIM)
    wanted = jnp.concatenate([common, drawn.reshape(count, -1)], axis=1)
    hit = wanted[:, :, None] == place[None, None, :]
    stored = jnp.sum(jnp.where(hit, number[None, None, :], 0), axis=-1).astype(jnp.int32)
    limits = jnp.clip(length - BLOCK * place, 0, BLOCK).astype(jnp.int32)
    ends = jnp.stack([last, length - BLOCK * last]).astype(jnp.int32)
    return stored, limits, ends, bias


def block_rows(index):
    return pl.ds(pl.multiple_of(index * BLOCK, BLOCK), BLOCK)


def spread(rows, heads):
    lane = lax.broadcasted_iota(jnp.int32, (1, heads * HEAD_DIM), 1)
    zero = jnp.zeros_like(rows)
    return jnp.concatenate(
        [jnp.where(lane // HEAD_DIM == h, rows, zero) for h in range(heads)], axis=0
    )


def collapse(full, heads):
    lane = lax.broadcasted_iota(jnp.int32, (1, PAIR), 1)
    pieces = []
    for pair in range(heads // 2):
        cols = slice(PAIR * pair, PAIR * (pair + 1))
        even = full[2 * pair * HEAD_DIM : (2 * pair + 1) * HEAD_DIM, cols]
        odd = full[(2 * pair + 1) * HEAD_DIM : (2 * pair + 2) * HEAD_DIM, cols]
        pieces.append(jnp.where(lane < HEAD_DIM, even, odd))
    return jnp.concatenate(pieces, axis=1)


def gathered_keys(ref, start, stored, number, heads):
    width = heads * HEAD_DIM
    lane = lax.broadcasted_iota(jnp.int32, (1, PAIR), 1)
    parts = [ref[block_rows(stored[number, s]), start : start + width] for s in range(5)]
    for s in range(3):
        pieces = []
        for pair in range(heads // 2):
            cols = slice(start + PAIR * pair, start + PAIR * (pair + 1))
            at = 5 + heads * s + 2 * pair
            even = ref[block_rows(stored[number, at]), cols]
            odd = ref[block_rows(stored[number, at + 1]), cols]
            pieces.append(jnp.where(lane < HEAD_DIM, even, odd))
        parts.append(jnp.concatenate(pieces, axis=1))
    return jnp.concatenate(parts, axis=0)


def slot(value, index):
    return value[BLOCK * index : BLOCK * (index + 1)]


def biased(scores, bias, last_rows):
    row = lax.broadcasted_iota(jnp.int32, (BLOCK, 1), 0)
    parts = [slot(scores, s) + bias[s : s + 1] for s in range(SLOTS)]
    parts[1] = jnp.where(row < last_rows, parts[1], NEGATIVE)
    return parts


def total(parts):
    return functools.reduce(jnp.add, parts)


def attend_kernel(heads, stored, limits, ends, qkv_ref, bias_ref, out_ref, log_ref, keep_ref):
    count = bias_ref.shape[0]
    width = heads * HEAD_DIM
    scale = jnp.asarray(HEAD_DIM**-0.5, BF16)

    def item(number):
        here = block_rows(stored[number, 3])
        queries = spread(qkv_ref[here, :width] * scale, heads)
        keys = gathered_keys(qkv_ref, width, stored, number, heads)
        parts = biased(matmul(keys, queries, NT), bias_ref[number], ends[1])
        top = jnp.max(functools.reduce(jnp.maximum, parts), axis=0, keepdims=True)
        weights = [jnp.exp(p - top) for p in parts]
        row_total = jnp.sum(total(weights), axis=0, keepdims=True)
        inverse = 1.0 / row_total
        probs = jnp.concatenate([(p * inverse).astype(BF16) for p in weights], axis=0)
        values = gathered_keys(qkv_ref, 2 * width, stored, number, heads)
        out_ref[here, :] = collapse(matmul(probs, values, TN), heads).astype(BF16)
        log_ref[pl.ds(number, 1), :] = top + jnp.log(row_total)

    def step(group, carry):
        for part in range(4):
            item(1 + group * 4 + part)
        return carry

    lax.fori_loop(0, (count - 1) // 4, step, 0)
    for number in range(1 + (count - 1) // 4 * 4, count):
        item(number)

    row = lax.broadcasted_iota(jnp.int32, (BLOCK, 1), 0)
    per = CHUNK // BLOCK
    chunks = count // per

    def chunk_rows(chunk):
        return pl.ds(pl.multiple_of(chunk * CHUNK, CHUNK), CHUNK)

    numbers = [0, ends[0]]
    rows_of = [block_rows(stored[number, 3]) for number in numbers]
    queries = [spread(qkv_ref[at, :width] * scale, heads) for at in rows_of]

    def scores(chunk, tops):
        at = chunk_rows(chunk)
        keys = qkv_ref[at, width : 2 * width]
        found = []
        for end in range(2):
            raw = matmul(keys, queries[end], NT)
            parts = [
                jnp.where(row < limits[chunk * per + s], slot(raw, s), NEGATIVE)
                for s in range(per)
            ]
            keep_ref[end, at, :] = jnp.concatenate(parts, axis=0)
            found.append(jnp.maximum(tops[end], functools.reduce(jnp.maximum, parts)))
        return tuple(found)

    tops = lax.fori_loop(0, chunks, scores, (jnp.full((BLOCK, width), NEGATIVE, F32),) * 2)
    tops = [jnp.max(top, axis=0, keepdims=True) for top in tops]

    def exponents(chunk, totals):
        at = chunk_rows(chunk)
        found = []
        for end in range(2):
            weights = jnp.exp(keep_ref[end, at, :] - tops[end])
            keep_ref[end, at, :] = weights
            found.append(totals[end] + total([slot(weights, s) for s in range(per)]))
        return tuple(found)

    totals = lax.fori_loop(0, chunks, exponents, (jnp.zeros((BLOCK, width), F32),) * 2)
    totals = [jnp.sum(found, axis=0, keepdims=True) for found in totals]
    inverses = [1.0 / found for found in totals]

    def contexts(chunk, sums):
        at = chunk_rows(chunk)
        values = qkv_ref[at, 2 * width :]
        return tuple(
            sums[end] + matmul((keep_ref[end, at, :] * inverses[end]).astype(BF16), values, TN)
            for end in range(2)
        )

    sums = lax.fori_loop(0, chunks, contexts, (jnp.zeros((width, width), F32),) * 2)
    for end in range(2):
        out_ref[rows_of[end], :] = collapse(sums[end], heads).astype(BF16)
        log_ref[pl.ds(numbers[end], 1), :] = tops[end] + jnp.log(totals[end])


def attend_back_kernel(
    heads,
    stored,
    limits,
    ends,
    qkv_ref,
    grad_ref,
    bias_ref,
    log_ref,
    out_ref,
    keys_acc,
    values_acc,
    probs_ref,
    inner_ref,
):
    count = bias_ref.shape[0]
    width = heads * HEAD_DIM
    scale = jnp.asarray(HEAD_DIM**-0.5, BF16)
    lane = lax.broadcasted_iota(jnp.int32, (1, PAIR), 1)
    keys_acc[...] = jnp.zeros_like(keys_acc)
    values_acc[...] = jnp.zeros_like(values_acc)

    def accumulate(acc, value, number):
        for s in range(5):
            acc[block_rows(stored[number, s]), :] += slot(value, s)
        for s in range(3):
            for h in range(heads):
                cols = slice(PAIR * (h // 2), PAIR * (h // 2 + 1))
                mine = (lane < HEAD_DIM) == (h % 2 == 0)
                term = jnp.where(mine, slot(value, 5 + s)[:, cols], 0.0)
                acc[block_rows(stored[number, 5 + heads * s + h]), cols] += term

    def item(number):
        here = block_rows(stored[number, 3])
        queries = spread(qkv_ref[here, :width] * scale, heads)
        grads = spread(grad_ref[here, :], heads)
        keys = gathered_keys(qkv_ref, width, stored, number, heads)
        values = gathered_keys(qkv_ref, 2 * width, stored, number, heads)
        log_total = log_ref[pl.ds(number, 1), :]
        parts = biased(matmul(keys, queries, NT), bias_ref[number], ends[1])
        probs = [jnp.exp(p - log_total) for p in parts]
        found = matmul(values, grads, NT)
        found = [slot(found, s) for s in range(SLOTS)]
        inner = total([p * d for p, d in zip(probs, found)])
        inner = jnp.sum(inner, axis=0, keepdims=True)
        grad_scores = jnp.concatenate(
            [(p * (d - inner)).astype(BF16) for p, d in zip(probs, found)], axis=0
        )
        probs_low = jnp.concatenate([p.astype(BF16) for p in probs], axis=0)
        accumulate(values_acc, matmul(probs_low, grads, NN), number)
        accumulate(keys_acc, matmul(grad_scores, queries, NN), number)
        grad_queries = collapse(matmul(grad_scores, keys, TN), heads) * HEAD_DIM**-0.5
        out_ref[here, :width] = grad_queries.astype(BF16)

    def step(group, carry):
        for part in range(4):
            item(1 + group * 4 + part)
        return carry

    lax.fori_loop(0, (count - 1) // 4, step, 0)
    for number in range(1 + (count - 1) // 4 * 4, count):
        item(number)

    row = lax.broadcasted_iota(jnp.int32, (BLOCK, 1), 0)
    per = CHUNK // BLOCK
    chunks = count // per

    def chunk_rows(chunk):
        return pl.ds(pl.multiple_of(chunk * CHUNK, CHUNK), CHUNK)

    numbers = [0, ends[0]]
    rows_of = [block_rows(stored[number, 3]) for number in numbers]
    queries = [spread(qkv_ref[at, :width] * scale, heads) for at in rows_of]
    grads = [spread(grad_ref[at, :], heads) for at in rows_of]
    log_rows = [log_ref[pl.ds(number, 1), :] for number in numbers]

    def first(chunk, inners):
        at = chunk_rows(chunk)
        keys = qkv_ref[at, width : 2 * width]
        values = qkv_ref[at, 2 * width :]
        sums = []
        for end in range(2):
            scores = matmul(keys, queries[end], NT)
            parts = [
                jnp.where(row < limits[chunk * per + s], slot(scores, s), NEGATIVE)
                for s in range(per)
            ]
            probs = jnp.exp(jnp.concatenate(parts, axis=0) - log_rows[end])
            found = matmul(values, grads[end], NT)
            probs_ref[end, at, :] = probs
            inner_ref[end, at, :] = found
            both = probs * found
            sums.append(inners[end] + total([slot(both, s) for s in range(per)]))
        return tuple(sums)

    inners = lax.fori_loop(0, chunks, first, (jnp.zeros((BLOCK, width), F32),) * 2)
    inners = [jnp.sum(inner, axis=0, keepdims=True) for inner in inners]

    def second(chunk, sums):
        at = chunk_rows(chunk)
        keys = qkv_ref[at, width : 2 * width]
        found, to_values, to_keys = [], values_acc[at, :], keys_acc[at, :]
        for end in range(2):
            probs = probs_ref[end, at, :]
            grad_scores = (probs * (inner_ref[end, at, :] - inners[end])).astype(BF16)
            to_values = to_values + matmul(probs.astype(BF16), grads[end], NN)
            to_keys = to_keys + matmul(grad_scores, queries[end], NN)
            found.append(sums[end] + matmul(grad_scores, keys, TN))
        out_ref[at, width : 2 * width] = to_keys.astype(BF16)
        out_ref[at, 2 * width :] = to_values.astype(BF16)
        return tuple(found)

    sums = lax.fori_loop(0, chunks, second, (jnp.zeros((width, width), F32),) * 2)
    for end in range(2):
        grad_queries = collapse(sums[end], heads) * HEAD_DIM**-0.5
        out_ref[rows_of[end], :width] = grad_queries.astype(BF16)


def in_smem():
    return pl.BlockSpec(memory_space=pltpu.SMEM)


def in_vmem():
    return pl.BlockSpec(memory_space=pltpu.VMEM)


def attention_cost(qkv, matmuls):
    rows, width = qkv.shape
    width //= 3
    return pl.CostEstimate(
        flops=2 * matmuls * rows * CHUNK * width,
        bytes_accessed=12 * rows * width,
        transcendentals=rows * CHUNK * width // HEAD_DIM,
    )


def attend(qkv, tables, heads):
    stored, limits, ends, bias = tables
    rows, width = qkv.shape[0], heads * HEAD_DIM
    return pl.pallas_call(
        functools.partial(attend_kernel, heads),
        out_shape=(
            jax.ShapeDtypeStruct((rows, width), BF16),
            jax.ShapeDtypeStruct((rows // BLOCK, width), F32),
        ),
        grid=(1,),
        in_specs=[in_smem()] * 3 + [in_vmem()] * 2,
        out_specs=(
            pl.BlockSpec((rows, width), lambda i: (0, 0)),
            pl.BlockSpec((rows // BLOCK, width), lambda i: (0, 0)),
        ),
        scratch_shapes=[pltpu.VMEM((2, rows, width), F32)],
        compiler_params=pltpu.CompilerParams(vmem_limit_bytes=32 << 20),
        cost_estimate=attention_cost(qkv, 8),
        name="attend",
    )(stored, limits, ends, qkv, bias)


def attend_back(qkv, grad_context, log_totals, tables, heads):
    stored, limits, ends, bias = tables
    rows, width = qkv.shape[0], heads * HEAD_DIM
    return pl.pallas_call(
        functools.partial(attend_back_kernel, heads),
        out_shape=jax.ShapeDtypeStruct(qkv.shape, BF16),
        grid=(1,),
        in_specs=[in_smem()] * 3 + [in_vmem()] * 4,
        out_specs=pl.BlockSpec(qkv.shape, lambda i: (0, 0)),
        scratch_shapes=[pltpu.VMEM((rows, width), F32)] * 2
        + [pltpu.VMEM((2, rows, width), F32)] * 2,
        compiler_params=pltpu.CompilerParams(vmem_limit_bytes=32 << 20),
        cost_estimate=attention_cost(qkv, 16),
        name="attend_back",
    )(stored, limits, ends, qkv, grad_context, bias, log_totals)


TILE = 256


def gelu_and_slope(pre):
    scale = (2.0 / 3.141592653589793) ** 0.5
    square = pre * pre
    bent = jnp.tanh(scale * pre * (1.0 + 0.044715 * square))
    half = 0.5 + 0.5 * bent
    slope = half + (0.5 * scale) * pre * (1.0 - bent * bent) * (1.0 + 0.134145 * square)
    return pre * half, slope


def pick(refs):
    per = pl.num_programs(0) // len(refs)
    value = refs[0][...]
    for k, ref in enumerate(refs[1:], 1):
        value = jnp.where(pl.program_id(0) >= k * per, ref[...], value)
    return value


def put(refs, value):
    per = pl.num_programs(0) // len(refs)
    for k, ref in enumerate(refs):
        ref[...] = jnp.where(pl.program_id(0) // per == k, value, ref[...])


def feed_kernel(quarters, taken, *refs):
    normed = pick(refs[:quarters])
    grads = pick(refs[quarters : 2 * quarters])
    weight_ref, bias_ref = refs[2 * quarters : 2 * quarters + 2]
    results = refs[2 * quarters + 2 + taken :]
    units = bias_ref.shape[1]
    up = weight_ref[:, :units]
    down = weight_ref[:, units:]
    active, slope = gelu_and_slope(matmul(normed, up, NN) + bias_ref[...])
    active = active.astype(BF16)
    grad_hidden = (matmul(grads, down, NN) * slope).astype(BF16)
    put(results[:quarters], matmul(grad_hidden, up, NT).astype(BF16))
    put(results[quarters : 2 * quarters], matmul(active, down, NT).astype(BF16))
    for ref, value in zip(results[2 * quarters :], (normed, grad_hidden, grads, active)):
        ref[...] = value


def tile_specs(arrays):
    def spec(k, value):
        tiles = value.shape[0] // TILE
        return pl.BlockSpec(
            (TILE, value.shape[1]), lambda i: (jnp.clip(i - k * tiles, 0, tiles - 1), 0)
        )

    return [spec(k, value) for k, value in enumerate(arrays)]


def feed(normed, grads, weights, bias, stacks, start, quarters):
    rows, features = normed[0].shape
    units = bias.shape[1]
    here = len(normed)
    tiles = rows // TILE
    stacked = [jax.ShapeDtypeStruct((rows * quarters, n), BF16) for n in (features, units) * 2]
    once = pl.BlockSpec(weights.shape, lambda i: (0, 0), pipeline_mode=pl.Buffered(1))
    found = pl.pallas_call(
        functools.partial(feed_kernel, here, len(stacks)),
        grid=(here * tiles,),
        out_shape=[like(value) for value in normed] * 2 + stacked,
        in_specs=tile_specs(normed)
        + tile_specs(grads)
        + [once, whole_spec(bias)]
        + [pl.BlockSpec(memory_space=pl.ANY)] * len(stacks),
        out_specs=tile_specs(normed) * 2
        + [
            pl.BlockSpec((TILE, value.shape[1]), lambda i: (i + start * tiles, 0))
            for value in stacked
        ],
        input_output_aliases={2 * here + 2 + n: 2 * here + n for n in range(len(stacks))},
        compiler_params=limit(62),
        cost_estimate=pl.CostEstimate(
            flops=8 * here * rows * features * units,
            bytes_accessed=16 * here * rows * features + 4 * features * units,
            transcendentals=here * rows * units,
        ),
        name="feed",
    )(*normed, *grads, weights, bias, *stacks)
    return found[:here], found[here : 2 * here], found[2 * here :]


def feed_grads_kernel(normed_ref, grad_ref, grads_ref, active_ref, out_ref, sum_ref, acc_ref):
    units = sum_ref.shape[1]
    grad_hidden = grad_ref[...]

    @pl.when(pl.program_id(0) == 0)
    def _():
        acc_ref[...] = jnp.zeros_like(acc_ref)
        sum_ref[...] = jnp.zeros_like(sum_ref)

    acc_ref[:, :units] += matmul(normed_ref[...], grad_hidden, TN)
    acc_ref[:, units:] += matmul(grads_ref[...], active_ref[...], TN)
    sum_ref[...] += jnp.sum(grad_hidden.astype(F32), axis=0, keepdims=True)

    @pl.when(pl.program_id(0) == pl.num_programs(0) - 1)
    def _():
        out_ref[...] = acc_ref[...].astype(BF16)


def feed_grads(stacks):
    rows, features = stacks[0].shape
    units = stacks[1].shape[1]
    sums = jax.ShapeDtypeStruct((features, 2 * units), BF16)
    hidden = jax.ShapeDtypeStruct((1, units), F32)
    return pl.pallas_call(
        feed_grads_kernel,
        grid=(rows // (2 * TILE),),
        out_shape=[sums, hidden],
        in_specs=[tiled_spec(value, 2 * TILE) for value in stacks],
        out_specs=[whole_spec(sums), whole_spec(hidden)],
        scratch_shapes=[pltpu.VMEM(sums.shape, F32)],
        compiler_params=limit(62),
        cost_estimate=cost(4 * rows * features * units, 8 * rows * features),
        name="feed_grads",
    )(*stacks)


def norm_parts(rows):
    centred = rows - jnp.mean(rows, axis=-1, keepdims=True)
    inverse = lax.rsqrt(jnp.mean(centred * centred, axis=-1, keepdims=True) + EPS)
    return centred * inverse, inverse


def norm_back(grad_normed, unit, inverse, gain):
    grad_unit = grad_normed * gain
    return inverse * (
        grad_unit
        - jnp.mean(grad_unit, axis=-1, keepdims=True)
        - unit * jnp.mean(grad_unit * unit, axis=-1, keepdims=True)
    )


def whole_spec(value):
    return pl.BlockSpec(value.shape, lambda i: (0,) * value.ndim)


def tiled_spec(value, tile=TILE):
    return pl.BlockSpec((tile, value.shape[1]), lambda i: (i, 0))


def like(value, dtype=None):
    return jax.ShapeDtypeStruct(value.shape, dtype or value.dtype)


def limit(mebibytes):
    return pltpu.CompilerParams(vmem_limit_bytes=mebibytes << 20)


def cost(flops, moved):
    return pl.CostEstimate(flops=flops, bytes_accessed=moved, transcendentals=0)


def unit_kernel(rows_ref, unit_ref):
    unit_ref[...] = norm_parts(rows_ref[...].astype(F32))[0].astype(BF16)


def unit_rows(rows):
    return pl.pallas_call(
        unit_kernel,
        grid=(rows.shape[0] // TILE,),
        out_shape=like(rows),
        in_specs=[tiled_spec(rows)],
        out_specs=tiled_spec(rows),
        compiler_params=limit(62),
        cost_estimate=cost(8 * rows.size, 4 * rows.size),
        name="unit",
    )(rows)


def project_kernel(parts, owner_a, owner_b, *refs):
    unit_refs = refs[:parts]
    first_ref, last_ref, norm_ref, bias_ref, qkv_ref, weight_ref, out_ref = refs[parts:]
    count, own, split = first_ref.shape
    near = unit_refs[0].shape[0]
    rest = weight_ref.shape[1] - split

    @pl.when(pl.program_id(0) == 0)
    def _():
        for p in range(count):
            at = pl.ds(pl.multiple_of(owner_a[p] * own, own), own)
            weight_ref[at, :split] = first_ref[p]
            at = pl.ds(pl.multiple_of(owner_b[p] * own, own), own)
            weight_ref[at, split:] = last_ref[p, :, :rest]
            out_ref[at, :] = last_ref[p, :, rest:]

    for k, ref in enumerate(unit_refs):

        @pl.when(pl.program_id(0) == k)
        def _(ref=ref):
            def tile(i, carry):
                at = pl.ds(pl.multiple_of(i * TILE, TILE), TILE)
                normed = ref[at, :].astype(F32) * norm_ref[0:1, :] + norm_ref[1:2, :]
                found = matmul(normed.astype(BF16), weight_ref[...], NN) + bias_ref[...]
                qkv_ref[at, :] = found.astype(BF16)
                return carry

            lax.fori_loop(0, near // TILE, tile, 0)


def project(unit, first, last, owner_a, owner_b, norm, bias):
    rows = sum(value.shape[0] for value in unit)
    features, width = unit[0].shape[1], bias.shape[1]
    more = first.shape[2] + last.shape[2] - width
    qkv = jax.ShapeDtypeStruct((rows, width), BF16)
    weights = [jax.ShapeDtypeStruct((features, n), BF16) for n in (width, more)]
    return pl.pallas_call(
        functools.partial(project_kernel, len(unit)),
        grid=(len(unit),),
        out_shape=[qkv, *weights],
        in_specs=[in_smem()] * 2 + [in_vmem()] * (len(unit) + 4),
        out_specs=[tiled_spec(qkv, rows // len(unit))] + [whole_spec(value) for value in weights],
        compiler_params=limit(32),
        cost_estimate=cost(2 * rows * features * width, 2 * rows * (features + width)),
        name="project",
    )(owner_a, owner_b, *unit, first, last, norm, bias)


def middle_kernel(parts, *refs):
    context_refs, out_refs = refs[:parts], refs[parts : 2 * parts]
    rows_ref, vector_ref, middle_ref, normed_ref = refs[2 * parts :]
    middle = rows_ref[...].astype(F32) + vector_ref[0:1, :]
    for context_ref, out_ref in zip(context_refs, out_refs):
        middle += matmul(context_ref[...], out_ref[...], NT)
    middle_ref[...] = middle
    unit = norm_parts(middle)[0]
    normed_ref[...] = (unit * vector_ref[1:2, :] + vector_ref[2:3, :]).astype(BF16)


def middle_rows(context, out_parts, rows, vectors):
    return pl.pallas_call(
        functools.partial(middle_kernel, len(context)),
        grid=(rows.shape[0] // TILE,),
        out_shape=[like(rows, F32), like(rows)],
        in_specs=[tiled_spec(value) for value in context]
        + [whole_spec(value) for value in out_parts]
        + [tiled_spec(rows), whole_spec(vectors)],
        out_specs=[tiled_spec(rows), tiled_spec(rows)],
        compiler_params=limit(62),
        cost_estimate=cost(2 * rows.size * rows.shape[1], 12 * rows.size),
        name="middle",
    )(*context, *out_parts, rows, vectors)


def middle_back_kernel(terms, parts, owner, *refs):
    term_refs, out_refs = refs[:terms], refs[terms : terms + parts]
    context_refs = refs[terms + parts : terms + 2 * parts]
    middle_ref, cotangent_ref, vector_ref, grad_ref, sum_ref = refs[
        terms + 2 * parts : terms + 2 * parts + 5
    ]
    head_refs = refs[terms + 2 * parts + 5 : terms + 3 * parts + 5]
    block_refs = refs[terms + 3 * parts + 5 : -1]
    found_ref = refs[-1]
    first = pl.program_id(0) == 0
    last = pl.program_id(0) == pl.num_programs(0) - 1
    count, own, width = block_refs[0].shape
    grad_normed = total([ref[...].astype(F32) for ref in term_refs])
    unit, inverse = norm_parts(middle_ref[...])
    cotangent = cotangent_ref[...].astype(F32)
    grad = cotangent + norm_back(grad_normed, unit, inverse, vector_ref[1:2, :])
    grad_ref[...] = grad
    low = grad.astype(BF16)
    for head_ref, out_ref in zip(head_refs, out_refs):
        head_ref[...] = matmul(low, out_ref[...], NN).astype(BF16)
    sums = [
        jnp.sum(value, axis=0, keepdims=True)
        for value in (grad_normed * unit, grad_normed, grad, cotangent)
    ]
    sums = jnp.concatenate(sums, axis=0)

    @pl.when(first)
    def _():
        sum_ref[...] = jnp.zeros_like(sum_ref)
        found_ref[...] = jnp.zeros_like(found_ref)

    sum_ref[...] += sums
    for k, context_ref in enumerate(context_refs):
        found_ref[:, k * width : (k + 1) * width] += matmul(low, context_ref[...], TN)

    @pl.when(last)
    def _():
        for k, block_ref in enumerate(block_refs):
            for p in range(count):
                at = pl.ds(pl.multiple_of(owner[p] * own, own), own)
                block_ref[p] = found_ref[at, k * width : (k + 1) * width].astype(BF16)


def middle_back(terms, out_parts, context, middle, cotangent, vectors, owner):
    rows, features = middle.shape
    width = out_parts[0].shape[1]
    parts = len(out_parts)
    count = owner.shape[0]
    sums = jax.ShapeDtypeStruct((4, features), F32)
    head = jax.ShapeDtypeStruct((rows, width), BF16)
    blocks = jax.ShapeDtypeStruct((count, features // count, width), BF16)
    found = pl.pallas_call(
        functools.partial(middle_back_kernel, len(terms), parts),
        grid=(rows // TILE,),
        out_shape=[like(middle), sums] + [head] * parts + [blocks] * parts,
        in_specs=[in_smem()]
        + [tiled_spec(value) for value in terms]
        + [whole_spec(value) for value in out_parts]
        + [tiled_spec(value) for value in context]
        + [tiled_spec(middle), tiled_spec(cotangent), whole_spec(vectors)],
        out_specs=[tiled_spec(middle), whole_spec(sums)]
        + [tiled_spec(head)] * parts
        + [whole_spec(blocks)] * parts,
        scratch_shapes=[pltpu.VMEM((features, width * parts), F32)],
        compiler_params=limit(62),
        cost_estimate=cost(4 * middle.size * features, 20 * middle.size),
        name="middle_back",
    )(owner, *terms, *out_parts, *context, middle, cotangent, vectors)
    return found[0], found[1], found[2 : 2 + parts], found[2 + parts :]


def qkv_grads_kernel(parts, terms, owner_a, owner_b, *refs):
    unit_refs, term_refs = refs[:parts], refs[parts : parts + terms]
    grad_ref, weight_ref, *block_refs, late_ref, sum_ref = refs[parts + terms : parts + terms + 8]
    *row_refs, raw_ref = refs[parts + terms + 8 :]
    half, own, split = block_refs[0].shape
    width = weight_ref.shape[1]
    rest = width - split
    near = unit_refs[0].shape[0]
    step = 256
    sums = jnp.sum(grad_ref[...].astype(F32), axis=0, keepdims=True)
    sum_ref[...] = sums
    for i in range(weight_ref.shape[0] // step):
        at = slice(step * i, step * (i + 1))
        raw = total(
            [
                matmul(ref[:, at], grad_ref[near * k : near * (k + 1), :], TN)
                for k, ref in enumerate(unit_refs)
            ]
        )
        weight = weight_ref[at, :].astype(F32)
        raw_ref[at, :] = raw.astype(BF16)
        for row, value in enumerate((raw * weight, weight * sums)):
            lanes = total([value[:, 128 * c : 128 * (c + 1)] for c in range(width // 128)])
            for b in range(step // 128):
                turned = lanes[128 * b : 128 * (b + 1)].T
                found = jnp.sum(turned, axis=0, keepdims=True)
                start = step * i + 128 * b
                late_ref[row : row + 1, start : start + 128] = found
    for p in range(2 * half):
        first_ref, last_ref = block_refs[p // half], block_refs[2 + p // half]
        at = pl.ds(pl.multiple_of(owner_a[p] * own, own), own)
        first_ref[p % half] = raw_ref[at, :split]
        at = pl.ds(pl.multiple_of(owner_b[p] * own, own), own)
        last_ref[p % half, :, :rest] = raw_ref[at, split:]
        found = total([ref[p].astype(F32) for ref in term_refs])
        last_ref[p % half, :, rest:] = found.astype(BF16)
    for k, ref in enumerate(row_refs):

        def tile(i, carry, k=k, ref=ref):
            at = pl.ds(pl.multiple_of(i * TILE + k * near, TILE), TILE)
            to = pl.ds(pl.multiple_of(i * TILE, TILE), TILE)
            ref[to, :] = matmul(grad_ref[at, :], weight_ref[...], NT).astype(BF16)
            return carry

        lax.fori_loop(0, near // TILE, tile, 0)


def qkv_grads(unit, out_terms, grad_qkv, weight, owner_a, owner_b, split):
    features, width = weight.shape
    count, own, more = out_terms[0].shape
    first = jax.ShapeDtypeStruct((count // 2, own, split), BF16)
    last = jax.ShapeDtypeStruct((count // 2, own, width - split + more), BF16)
    return pl.pallas_call(
        functools.partial(qkv_grads_kernel, len(unit), len(out_terms)),
        grid=(1,),
        out_shape=[
            first,
            first,
            last,
            last,
            jax.ShapeDtypeStruct((2, features), F32),
            jax.ShapeDtypeStruct((1, width), F32),
        ]
        + [like(value) for value in unit],
        in_specs=[in_smem()] * 2 + [in_vmem()] * (len(unit) + len(out_terms) + 2),
        out_specs=[whole_spec(value) for value in (first, first, last, last)]
        + [pl.BlockSpec((2, features), lambda i: (0, 0)), pl.BlockSpec((1, width), lambda i: (0, 0))]
        + [whole_spec(value) for value in unit],
        scratch_shapes=[pltpu.VMEM((features, width), BF16)],
        compiler_params=limit(32),
        cost_estimate=cost(4 * grad_qkv.size * features, 4 * grad_qkv.size + 8 * weight.size),
        name="qkv_grads",
    )(owner_a, owner_b, *unit, *out_terms, grad_qkv, weight)


def input_back_kernel(terms, *refs):
    *term_refs, first_ref, last_ref = refs[:terms]
    rows_ref, middle_ref, vector_ref, out_ref = refs[terms:]
    half = jnp.where(pl.program_id(0) == 0, first_ref[...], last_ref[...])
    grad_normed = total([ref[...].astype(F32) for ref in term_refs]) + half.astype(F32)
    unit, inverse = norm_parts(rows_ref[...].astype(F32))
    grad = norm_back(grad_normed, unit, inverse, vector_ref[0:1, :])
    out_ref[...] = (middle_ref[...] + grad).astype(BF16)


def input_back(terms, rows, grad_middle, vectors):
    tile = rows.shape[0] // 2
    return pl.pallas_call(
        functools.partial(input_back_kernel, len(terms)),
        grid=(2,),
        out_shape=like(rows),
        in_specs=[tiled_spec(value, tile) for value in terms[:-2]]
        + [whole_spec(value) for value in terms[-2:]]
        + [tiled_spec(rows, tile), tiled_spec(grad_middle, tile), whole_spec(vectors)],
        out_specs=tiled_spec(rows, tile),
        compiler_params=limit(62),
        cost_estimate=cost(20 * rows.size, 14 * rows.size),
        name="input_back",
    )(*terms, rows, grad_middle, vectors)


def per_device(
    tokens,
    output_cotangent,
    lengths,
    block_place,
    random_blocks,
    qkv_weight,
    out_weight,
    up_weight,
    down_weight,
    vectors,
    hidden_bias,
):
    ways = lax.axis_size("tensor")
    spread_ways = lax.axis_size("dp")
    position = lax.axis_index("tensor")
    index = lax.axis_index("dp") * ways + position
    near = tokens.shape[0]
    rows = near * ways
    features = tokens.shape[1]
    width = qkv_weight.shape[2]
    heads = width // HEAD_DIM
    units = up_weight.shape[1]
    own = features // spread_ways
    piece = vectors.shape[1]
    unit_piece = hidden_bias.shape[1]

    def quarters(value):
        return [value[k * near : (k + 1) * near] for k in range(ways)]

    small = jnp.zeros((8, features), F32)
    small = lax.dynamic_update_slice(small, vectors, (0, index * piece))
    small_hidden = jnp.zeros((1, units * ways), F32)
    small_hidden = lax.dynamic_update_slice(small_hidden, hidden_bias, (0, index * unit_piece))
    packed = jnp.concatenate([small.reshape(-1), small_hidden.reshape(-1)])
    packed = summed_everywhere(packed, ("tensor",))

    unit_near = unit_rows(tokens)
    unit_near, packed = together(unit_near, packed)
    unit_far = far(unit_near, "tensor")

    bits = bits_of("dp")
    order_a = bits[::-1]
    order_b = bits[:1] + bits[:0:-1]
    owner_a = block_owners("dp", order_a)
    owner_b = block_owners("dp", order_b)
    split = 2 * width
    qkv_flat = qkv_weight.reshape(own, 3 * width)
    first_blocks = doubled(qkv_flat[:, :split], "dp", order_a)
    last_flat = jnp.concatenate([qkv_flat[:, split:], out_weight], axis=1)
    last_blocks = doubled(last_flat, "dp", order_b)
    packed = summed_everywhere(packed, ("dp",))
    feed_flat = jnp.concatenate([up_weight, down_weight], axis=1)
    cotangent_near, unit_far = together(output_cotangent, unit_far)
    feed_flat, first_blocks, last_blocks, _here, packed = together(
        feed_flat, first_blocks, last_blocks, unit_far, packed
    )
    feed_full = lax.all_gather(feed_flat, "dp", axis=0, tiled=True)
    cotangent_far = far(cotangent_near, "tensor")
    unit_parts = gathered_parts(unit_near, unit_far, "tensor")

    vectors_full = packed[: 8 * features].reshape(8, features)
    hidden_full = packed[8 * features :]
    bias_query = lax.dynamic_slice_in_dim(vectors_full[6], position * width, width)
    bias_value = lax.dynamic_slice_in_dim(vectors_full[7], position * width, width)
    bias_qkv = jnp.concatenate([bias_query, jnp.zeros_like(bias_query), bias_value])[None]
    bias_hidden = lax.dynamic_slice_in_dim(hidden_full, position * units, units)[None]
    norm_one = vectors_full[:2]
    norm_two = jnp.stack([vectors_full[4], vectors_full[2], vectors_full[3]])

    placed = block_place[0].reshape(ways, -1)
    order = position ^ jnp.arange(ways, dtype=jnp.int32)
    chosen_rows = order[:, None, None] == jnp.arange(ways, dtype=jnp.int32)[None, :, None]
    place = jnp.sum(jnp.where(chosen_rows, placed[None], 0), axis=1).reshape(-1)
    tables = attention_tables(lengths[0], place, random_blocks[0])

    qkv, qkv_full, out_group = project(
        unit_parts, first_blocks, last_blocks, owner_a, owner_b, norm_one, bias_qkv
    )
    context, log_totals = attend(qkv, tables, heads)
    out_far = far(out_group, "tensor")
    context, out_far, cotangent_far = together(context, out_far, cotangent_far)
    grad_parts = gathered_parts(output_cotangent, cotangent_far, "tensor")

    out_parts = gathered_parts(out_group, out_far, "tensor")
    context_near = exchanged_parts(quarters(context), "tensor")
    middle, normed_two = middle_rows(context_near, out_parts, tokens, norm_two)

    half = ways // 2
    normed_far = far(normed_two, "tensor")
    normed_parts = gathered_parts(normed_two, normed_far, "tensor")
    near_back, near_out, stacks = feed(
        normed_parts[:half], grad_parts[:half], feed_full, bias_hidden, (), 0, ways
    )
    normed_far, *stacks = together(normed_far, *stacks)
    normed_parts = gathered_parts(normed_two, normed_far, "tensor")
    far_back, far_out, stacks = feed(
        normed_parts[half:], grad_parts[half:], feed_full, bias_hidden, stacks, half, ways
    )
    back_parts, feed_parts = near_back + far_back, near_out + far_out
    back_terms, far_sum = summed_halves(back_parts, "tensor")
    back_terms.append(far(far_sum, "tensor"))
    feed_sums, sum_hidden = feed_grads(stacks)
    feed_weight_grads = lax.psum_scatter(feed_sums, "dp", scatter_dimension=0, tiled=True)
    feed_weight_grads = feed_weight_grads.astype(F32)
    *back_terms, sum_hidden = together(*back_terms, sum_hidden)

    grad_middle, sums_two, grad_heads, out_blocks = middle_back(
        back_terms, out_parts, context_near, middle, output_cotangent, norm_two, owner_b
    )
    grad_heads = exchanged_parts(grad_heads, "tensor")
    grad_context = jnp.concatenate(grad_heads, axis=0)

    out_terms, out_far = summed_halves(out_blocks, "tensor")
    feed_terms, feed_far = summed_halves(feed_parts, "tensor")
    early, late_rows = feed_far[: near // 2], feed_far[near // 2 :]
    grad_context, out_far, early = together(grad_context, out_far, early)
    out_terms.append(far(out_far, "tensor"))
    early = far(early, "tensor")
    grad_qkv = attend_back(qkv, grad_context, log_totals, tables, heads)
    grad_qkv, early, late_rows, *out_terms = together(grad_qkv, early, late_rows, *out_terms)
    late_rows = far(late_rows, "tensor")
    first_keep, first_send, last_keep, last_send, late, sum_qkv, *back_parts = qkv_grads(
        unit_parts, out_terms, grad_qkv, qkv_full, owner_a, owner_b, split
    )
    near_rows, far_rows = back_parts[:half], back_parts[half:]
    head_sums = lax.dynamic_update_slice(
        jnp.zeros((3, features), F32), sum_qkv.reshape(3, width), (0, position * width)
    )
    hidden_sums = lax.dynamic_update_slice(
        jnp.zeros((1, units * ways), F32), sum_hidden, (0, position * units)
    )
    packed = jnp.concatenate(
        [late.reshape(-1), sums_two.reshape(-1), head_sums.reshape(-1), hidden_sums.reshape(-1)]
    )
    far_sum = added(far_rows[0], swapped(far_rows[1], "tensor", 1))
    packed, far_sum, first_keep, last_keep, *near_rows = together(
        packed, far_sum, first_keep, last_keep, *near_rows
    )
    far_first = far(far_sum[: near // 2], "tensor")
    far_last = far(far_sum[near // 2 :], "tensor")
    first_keep, first_send = halved(first_keep, first_send, "dp", order_a)
    last_keep, last_send = halved(last_keep, last_send, "dp", order_b)
    first_send, last_send, far_first = together(first_send, last_send, far_first)
    while first_send.shape[0] > 1:
        first_keep, first_send = halved(first_keep, first_send, "dp", order_a)
        last_keep, last_send = halved(last_keep, last_send, "dp", order_b)
    first_send, last_send, far_last = together(first_send, last_send, far_last)
    near_terms = [near_rows[0], swapped(near_rows[1], "tensor", 1), far_first, far_last]
    first_raw = halved(first_keep, first_send, "dp", order_a)[0][0].astype(F32)
    last_raw = halved(last_keep, last_send, "dp", order_b)[0][0].astype(F32)
    out_weight_grad = last_raw[:, width:]
    last_raw = last_raw[:, :width]
    input_grad = input_back(near_terms, tokens, grad_middle, norm_one)
    feed_terms.append(jnp.concatenate([early, late_rows], axis=0))
    output = total([term.astype(F32) for term in feed_terms]) + middle + vectors_full[5]
    output = output.astype(BF16)

    packed = summed_everywhere(packed, ("tensor", "dp"))
    by_feature = packed[: 9 * features].reshape(9, features)
    hidden_sums = packed[9 * features :]
    vectors_grad = lax.dynamic_slice_in_dim(by_feature, index * piece, piece, axis=1)
    vectors_grad = jnp.concatenate([vectors_grad[:7], vectors_grad[8:]], axis=0)
    hidden_bias_grad = lax.dynamic_slice_in_dim(hidden_sums, index * unit_piece, unit_piece)

    sum_qkv = lax.dynamic_slice_in_dim(by_feature[6:], position * width, width, axis=1)
    mine = lax.dynamic_slice_in_dim(norm_one, lax.axis_index("dp") * own, own, axis=1)
    raw = jnp.concatenate([first_raw, last_raw], axis=1).reshape(own, 3, width)
    qkv_weight_grad = mine[0][:, None, None] * raw + mine[1][:, None, None] * sum_qkv
    return (
        output,
        input_grad,
        qkv_weight_grad,
        out_weight_grad,
        feed_weight_grads[:, :units],
        feed_weight_grads[:, units:],
        vectors_grad,
        hidden_bias_grad[None, :],
    )


def solution(mesh):
    placed = (
        P(("dp", "tensor"), None),
        P(("dp", "tensor"), None),
        P("dp"),
        P("dp", None),
        P("dp", "tensor", None, None),
        P("dp", None, "tensor"),
        P("dp", "tensor"),
        P("dp", "tensor"),
        P("dp", "tensor"),
        P(None, ("dp", "tensor")),
        P(None, ("dp", "tensor")),
    )
    return jax.shard_map(
        per_device,
        mesh=mesh,
        in_specs=placed,
        out_specs=(
            P(("dp", "tensor"), None),
            P(("dp", "tensor"), None),
            P("dp", None, "tensor"),
            P("dp", "tensor"),
            P("dp", "tensor"),
            P("dp", "tensor"),
            P(None, ("dp", "tensor")),
            P(None, ("dp", "tensor")),
        ),
        check_vma=False,
    )
```

```python
import functools

import jax
import jax.numpy as jnp
from jax import lax
from jax.experimental import pallas as pl
from jax.experimental.pallas import tpu as pltpu
from jax.sharding import PartitionSpec as P

HEAD_DIM = 64
BLOCK = 64
PAIR = 2 * HEAD_DIM
SLOTS = 8
CHUNK = 512
EPS = 1e-05
NEGATIVE = -1e30
F32 = jnp.float32
BF16 = jnp.bfloat16
NT = (((1,), (1,)), ((), ()))
NN = (((1,), (0,)), ((), ()))
TN = (((0,), (0,)), ((), ()))


def matmul(left, right, dims):
    return lax.dot_general(left, right, dims, preferred_element_type=F32)


def swapped(value, axis, bit):
    count = lax.axis_size(axis)
    return lax.ppermute(value, axis, [(i, i ^ bit) for i in range(count)])


def bits_of(axis):
    count = lax.axis_size(axis)
    return [1 << b for b in range(count.bit_length() - 1)]


def together(*values):
    return lax.optimization_barrier(values)


def far(value, axis):
    return swapped(value, axis, bits_of(axis)[-1])


def gathered_parts(value, far_value, axis):
    bits = bits_of(axis)
    parts = {0: value, bits[-1]: far_value}
    for bit in reversed(bits[:-1]):
        parts.update({k | bit: swapped(p, axis, bit) for k, p in list(parts.items())})
    return [parts[k] for k in range(len(parts))]


def summed_halves(parts, axis):
    left = dict(enumerate(parts))
    terms = [parts[0]]
    for bit in bits_of(axis)[: len(parts).bit_length() - 2]:
        kept = {}
        for k in sorted(left, reverse=True):
            if k & bit == 0:
                arrived = swapped(left[k | bit], axis, bit)
                if k == 0:
                    terms.append(arrived)
                    kept[k] = None
                else:
                    kept[k] = added(left[k], arrived)
        left = kept
    return terms, left[len(parts) // 2]


def added(left, right):
    return (left.astype(F32) + right.astype(F32)).astype(BF16)


def doubled(value, axis, order):
    blocks = value[None]
    for bit in order:
        blocks = jnp.concatenate([blocks, swapped(blocks, axis, bit)], axis=0)
    return blocks


def halved(keep, send, axis, order):
    half = send.shape[0]
    arrived = swapped(send, axis, order[half.bit_length() - 1])
    rest = half // 2
    return added(keep[: half - rest], arrived[: half - rest]), added(
        keep[half - rest :], arrived[half - rest :]
    )


def block_owners(axis, order):
    count = lax.axis_size(axis)
    device = [sum(bit for b, bit in enumerate(order) if p >> b & 1) for p in range(count)]
    return lax.axis_index(axis) ^ jnp.asarray(device, jnp.int32)


def exchanged_parts(parts, axis):
    return [p if k == 0 else swapped(p, axis, k) for k, p in enumerate(parts)]


def summed_everywhere(value, axes):
    size = value.shape[0]
    value = jnp.pad(value, (0, -size % 1024)).reshape(-1, 128)
    for axis in axes:
        for bit in bits_of(axis):
            value = value + swapped(value, axis, bit)
    return value.reshape(-1)[:size]


def sent_and_summed(value, axis):
    count = lax.axis_size(axis)
    blocks = value.reshape(count, value.shape[0] // count, *value.shape[1:])
    arrived = lax.all_to_all(blocks, axis, 0, 0, tiled=True)
    return jnp.sum(arrived.astype(F32), axis=0)


def attention_facts(length, position, placing, chosen):
    head = jnp.stack([length, position]).astype(jnp.int32)
    return jnp.concatenate([head, placing.reshape(-1), chosen.reshape(-1)])


class Blocks:
    def __init__(self, facts, stored, limits, heads, quarters):
        self.facts, self.stored, self.limits = facts, stored, limits
        self.heads, self.quarters = heads, quarters
        self.count = stored.shape[0]
        self.length = facts[0]
        self.last = (self.length + BLOCK - 1) // BLOCK - 1
        self.last_rows = self.length - BLOCK * self.last

    def find(self):
        per = self.count // self.quarters
        for quarter in range(self.quarters):
            start = (self.facts[1] ^ quarter) * per
            for n in range(per):
                number = self.facts[2 + start + n]
                self.stored[number] = quarter * per + n
                rows = self.length - BLOCK * number
                self.limits[quarter * per + n] = jnp.clip(rows, 0, BLOCK)

    def item(self, number):
        last = self.last
        alive = number != last
        before, behind = number - 1, number + 1
        common = [0, last, before, number, jnp.minimum(behind, self.count - 1)]
        good = [
            alive,
            alive,
            alive & (before > 0) & (before < last),
            alive & (number < last),
            alive & (behind < last),
        ]
        places = [self.stored[block] for block in common]
        lane = lax.broadcasted_iota(jnp.int32, (1, self.heads * HEAD_DIM), 1)
        added_scores = [jnp.where(flag, 0.0, NEGATIVE).astype(F32) for flag in good]
        drawn = [
            [
                self.facts[2 + self.count + (h * self.count + number) * 3 + s]
                for h in range(self.heads)
            ]
            for s in range(3)
        ]
        random = []
        for s in range(3):
            random.append([self.stored[block] for block in drawn[s]])
            row = jnp.zeros((1, self.heads * HEAD_DIM), F32)
            for h, block in enumerate(drawn[s]):
                fresh = alive & (block > 0) & (block < last) & (jnp.abs(block - number) > 1)
                for other in range(s):
                    fresh = fresh & (block != drawn[other][h])
                score = jnp.where(fresh, 0.0, NEGATIVE).astype(F32)
                row = jnp.where(lane // HEAD_DIM == h, score, row)
            added_scores.append(row)
        return places, random, added_scores


def block_rows(index):
    return pl.ds(pl.multiple_of(index * BLOCK, BLOCK), BLOCK)


def spread(rows, heads):
    lane = lax.broadcasted_iota(jnp.int32, (1, heads * HEAD_DIM), 1)
    zero = jnp.zeros_like(rows)
    return jnp.concatenate(
        [jnp.where(lane // HEAD_DIM == h, rows, zero) for h in range(heads)], axis=0
    )


def collapse(full, heads):
    lane = lax.broadcasted_iota(jnp.int32, (1, PAIR), 1)
    pieces = []
    for pair in range(heads // 2):
        cols = slice(PAIR * pair, PAIR * (pair + 1))
        even = full[2 * pair * HEAD_DIM : (2 * pair + 1) * HEAD_DIM, cols]
        odd = full[(2 * pair + 1) * HEAD_DIM : (2 * pair + 2) * HEAD_DIM, cols]
        pieces.append(jnp.where(lane < HEAD_DIM, even, odd))
    return jnp.concatenate(pieces, axis=1)


def gathered_keys(ref, start, places, random, heads):
    width = heads * HEAD_DIM
    lane = lax.broadcasted_iota(jnp.int32, (1, PAIR), 1)
    parts = [ref[block_rows(place), start : start + width] for place in places]
    for drawn in random:
        pieces = []
        for pair in range(heads // 2):
            cols = slice(start + PAIR * pair, start + PAIR * (pair + 1))
            even = ref[block_rows(drawn[2 * pair]), cols]
            odd = ref[block_rows(drawn[2 * pair + 1]), cols]
            pieces.append(jnp.where(lane < HEAD_DIM, even, odd))
        parts.append(jnp.concatenate(pieces, axis=1))
    return jnp.concatenate(parts, axis=0)


def slot(value, index):
    return value[BLOCK * index : BLOCK * (index + 1)]


def biased(scores, bias, last_rows):
    row = lax.broadcasted_iota(jnp.int32, (BLOCK, 1), 0)
    parts = [slot(scores, s) + bias[s] for s in range(SLOTS)]
    parts[1] = jnp.where(row < last_rows, parts[1], NEGATIVE)
    return parts


def total(parts):
    return functools.reduce(jnp.add, parts)


def attend_body(heads, blocks, qkv_ref, out_ref, log_ref, keep_ref):
    count = blocks.count
    stored, limits = blocks.stored, blocks.limits
    width = heads * HEAD_DIM
    scale = jnp.asarray(HEAD_DIM**-0.5, BF16)

    def item(number):
        places, random, scores = blocks.item(number)
        here = block_rows(places[3])
        queries = spread(qkv_ref[here, :width] * scale, heads)
        keys = gathered_keys(qkv_ref, width, places, random, heads)
        parts = biased(matmul(keys, queries, NT), scores, blocks.last_rows)
        top = jnp.max(functools.reduce(jnp.maximum, parts), axis=0, keepdims=True)
        weights = [jnp.exp(p - top) for p in parts]
        row_total = jnp.sum(total(weights), axis=0, keepdims=True)
        inverse = 1.0 / row_total
        probs = jnp.concatenate([(p * inverse).astype(BF16) for p in weights], axis=0)
        values = gathered_keys(qkv_ref, 2 * width, places, random, heads)
        out_ref[here, :] = collapse(matmul(probs, values, TN), heads).astype(BF16)
        log_ref[pl.ds(number, 1), :] = top + jnp.log(row_total)

    def step(group, carry):
        for part in range(10):
            item(1 + group * 10 + part)
        return carry

    lax.fori_loop(0, (count - 1) // 10, step, 0)
    for number in range(1 + (count - 1) // 10 * 10, count):
        item(number)

    row = lax.broadcasted_iota(jnp.int32, (BLOCK, 1), 0)
    per = CHUNK // BLOCK
    chunks = count // per

    def chunk_rows(chunk):
        return pl.ds(pl.multiple_of(chunk * CHUNK, CHUNK), CHUNK)

    numbers = [0, blocks.last]
    rows_of = [block_rows(stored[number]) for number in numbers]
    queries = [spread(qkv_ref[at, :width] * scale, heads) for at in rows_of]

    def scores(chunk, tops):
        at = chunk_rows(chunk)
        keys = qkv_ref[at, width : 2 * width]
        found = []
        for end in range(2):
            raw = matmul(keys, queries[end], NT)
            parts = [
                jnp.where(row < limits[chunk * per + s], slot(raw, s), NEGATIVE)
                for s in range(per)
            ]
            keep_ref[end, at, :] = jnp.concatenate(parts, axis=0)
            found.append(jnp.maximum(tops[end], functools.reduce(jnp.maximum, parts)))
        return tuple(found)

    tops = lax.fori_loop(0, chunks, scores, (jnp.full((BLOCK, width), NEGATIVE, F32),) * 2)
    tops = [jnp.max(top, axis=0, keepdims=True) for top in tops]

    def exponents(chunk, totals):
        at = chunk_rows(chunk)
        found = []
        for end in range(2):
            weights = jnp.exp(keep_ref[end, at, :] - tops[end])
            keep_ref[end, at, :] = weights
            found.append(totals[end] + total([slot(weights, s) for s in range(per)]))
        return tuple(found)

    totals = lax.fori_loop(0, chunks, exponents, (jnp.zeros((BLOCK, width), F32),) * 2)
    totals = [jnp.sum(found, axis=0, keepdims=True) for found in totals]
    inverses = [1.0 / found for found in totals]

    def contexts(chunk, sums):
        at = chunk_rows(chunk)
        values = qkv_ref[at, 2 * width :]
        return tuple(
            sums[end] + matmul((keep_ref[end, at, :] * inverses[end]).astype(BF16), values, TN)
            for end in range(2)
        )

    sums = lax.fori_loop(0, chunks, contexts, (jnp.zeros((width, width), F32),) * 2)
    for end in range(2):
        out_ref[rows_of[end], :] = collapse(sums[end], heads).astype(BF16)
        log_ref[pl.ds(numbers[end], 1), :] = tops[end] + jnp.log(totals[end])


def attend_back_body(
    heads,
    blocks,
    qkv_ref,
    grad_ref,
    log_ref,
    out_ref,
    keys_acc,
    values_acc,
    probs_ref,
    inner_ref,
):
    count = blocks.count
    stored, limits = blocks.stored, blocks.limits
    width = heads * HEAD_DIM
    scale = jnp.asarray(HEAD_DIM**-0.5, BF16)
    lane = lax.broadcasted_iota(jnp.int32, (1, PAIR), 1)
    keys_acc[...] = jnp.zeros_like(keys_acc)
    values_acc[...] = jnp.zeros_like(values_acc)

    def accumulate(acc, value, places, random):
        for s in range(5):
            acc[block_rows(places[s]), :] += slot(value, s)
        for s in range(3):
            for h in range(heads):
                cols = slice(PAIR * (h // 2), PAIR * (h // 2 + 1))
                mine = (lane < HEAD_DIM) == (h % 2 == 0)
                term = jnp.where(mine, slot(value, 5 + s)[:, cols], 0.0)
                acc[block_rows(random[s][h]), cols] += term

    def item(number):
        places, random, scores = blocks.item(number)
        here = block_rows(places[3])
        queries = spread(qkv_ref[here, :width] * scale, heads)
        grads = spread(grad_ref[here, :], heads)
        keys = gathered_keys(qkv_ref, width, places, random, heads)
        values = gathered_keys(qkv_ref, 2 * width, places, random, heads)
        log_total = log_ref[pl.ds(number, 1), :]
        parts = biased(matmul(keys, queries, NT), scores, blocks.last_rows)
        probs = [jnp.exp(p - log_total) for p in parts]
        found = matmul(values, grads, NT)
        found = [slot(found, s) for s in range(SLOTS)]
        inner = total([p * d for p, d in zip(probs, found)])
        inner = jnp.sum(inner, axis=0, keepdims=True)
        grad_scores = jnp.concatenate(
            [(p * (d - inner)).astype(BF16) for p, d in zip(probs, found)], axis=0
        )
        probs_low = jnp.concatenate([p.astype(BF16) for p in probs], axis=0)
        accumulate(values_acc, matmul(probs_low, grads, NN), places, random)
        accumulate(keys_acc, matmul(grad_scores, queries, NN), places, random)
        grad_queries = collapse(matmul(grad_scores, keys, TN), heads) * HEAD_DIM**-0.5
        out_ref[here, :width] = grad_queries.astype(BF16)

    def step(group, carry):
        for part in range(6):
            item(1 + group * 6 + part)
        return carry

    lax.fori_loop(0, (count - 1) // 6, step, 0)
    for number in range(1 + (count - 1) // 6 * 6, count):
        item(number)

    row = lax.broadcasted_iota(jnp.int32, (BLOCK, 1), 0)
    per = CHUNK // BLOCK
    chunks = count // per

    def chunk_rows(chunk):
        return pl.ds(pl.multiple_of(chunk * CHUNK, CHUNK), CHUNK)

    numbers = [0, blocks.last]
    rows_of = [block_rows(stored[number]) for number in numbers]
    queries = [spread(qkv_ref[at, :width] * scale, heads) for at in rows_of]
    grads = [spread(grad_ref[at, :], heads) for at in rows_of]
    log_rows = [log_ref[pl.ds(number, 1), :] for number in numbers]

    def first(chunk, inners):
        at = chunk_rows(chunk)
        keys = qkv_ref[at, width : 2 * width]
        values = qkv_ref[at, 2 * width :]
        sums = []
        for end in range(2):
            scores = matmul(keys, queries[end], NT)
            parts = [
                jnp.where(row < limits[chunk * per + s], slot(scores, s), NEGATIVE)
                for s in range(per)
            ]
            probs = jnp.exp(jnp.concatenate(parts, axis=0) - log_rows[end])
            found = matmul(values, grads[end], NT)
            probs_ref[end, at, :] = probs
            inner_ref[end, at, :] = found
            both = probs * found
            sums.append(inners[end] + total([slot(both, s) for s in range(per)]))
        return tuple(sums)

    inners = lax.fori_loop(0, chunks, first, (jnp.zeros((BLOCK, width), F32),) * 2)
    inners = [jnp.sum(inner, axis=0, keepdims=True) for inner in inners]

    def second(chunk, sums):
        at = chunk_rows(chunk)
        keys = qkv_ref[at, width : 2 * width]
        found, to_values, to_keys = [], values_acc[at, :], keys_acc[at, :]
        for end in range(2):
            probs = probs_ref[end, at, :]
            grad_scores = (probs * (inner_ref[end, at, :] - inners[end])).astype(BF16)
            to_values = to_values + matmul(probs.astype(BF16), grads[end], NN)
            to_keys = to_keys + matmul(grad_scores, queries[end], NN)
            found.append(sums[end] + matmul(grad_scores, keys, TN))
        out_ref[at, width : 2 * width] = to_keys.astype(BF16)
        out_ref[at, 2 * width :] = to_values.astype(BF16)
        return tuple(found)

    sums = lax.fori_loop(0, chunks, second, (jnp.zeros((width, width), F32),) * 2)
    for end in range(2):
        grad_queries = collapse(sums[end], heads) * HEAD_DIM**-0.5
        out_ref[rows_of[end], :width] = grad_queries.astype(BF16)


def in_smem():
    return pl.BlockSpec(memory_space=pltpu.SMEM)


def in_vmem():
    return pl.BlockSpec(memory_space=pltpu.VMEM)


def project_attend_kernel(heads, parts, owner_a, owner_b, facts, *refs):
    unit_refs = refs[:parts]
    first_ref, last_ref, norm_ref, bias_ref = refs[parts : parts + 4]
    *quarter_refs, kept_ref, weight_out_ref, log_ref = refs[parts + 4 : 2 * parts + 7]
    qkv_ref, weight_ref, out_ref, keep_ref, stored, limits, sems = refs[2 * parts + 7 :]
    blocks = Blocks(facts, stored, limits, heads, parts)
    blocks.find()
    count, own, split = first_ref.shape
    near = unit_refs[0].shape[0]
    rest = weight_ref.shape[1] - split
    for p in range(count):
        at = pl.ds(pl.multiple_of(owner_a[p] * own, own), own)
        weight_ref[at, :split] = first_ref[p]
        at = pl.ds(pl.multiple_of(owner_b[p] * own, own), own)
        weight_ref[at, split:] = last_ref[p, :, :rest]
    copies = [pltpu.make_async_copy(weight_ref, weight_out_ref, sems.at[0])]
    copies[0].start()
    for k, ref in enumerate(unit_refs):
        normed = ref[...].astype(F32) * norm_ref[0:1, :] + norm_ref[1:2, :]
        found = matmul(normed.astype(BF16), weight_ref[...], NN) + bias_ref[...]
        qkv_ref[near * k : near * (k + 1), :] = found.astype(BF16)
    copies.append(pltpu.make_async_copy(qkv_ref, kept_ref, sems.at[1]))
    copies[1].start()
    attend_body(heads, blocks, qkv_ref, out_ref, log_ref, keep_ref)
    for k, ref in enumerate(quarter_refs):
        part = out_ref.at[near * k : near * (k + 1), :]
        copies.append(pltpu.make_async_copy(part, ref, sems.at[2 + k]))
        copies[-1].start()
    for copy in copies:
        copy.wait()


def in_hbm():
    return pl.BlockSpec(memory_space=pltpu.HBM)


def project_attend(unit, first, last, owner_a, owner_b, norm, bias, facts, heads):
    rows = sum(value.shape[0] for value in unit)
    features = unit[0].shape[1]
    width = heads * HEAD_DIM
    log_shape = jax.ShapeDtypeStruct((rows // BLOCK, width), F32)
    quarter = [jax.ShapeDtypeStruct((value.shape[0], width), BF16) for value in unit]
    qkv = jax.ShapeDtypeStruct((rows, 3 * width), BF16)
    weight = jax.ShapeDtypeStruct((features, 3 * width), BF16)
    found = pl.pallas_call(
        functools.partial(project_attend_kernel, heads, len(unit)),
        grid=(1,),
        out_shape=[*quarter, qkv, weight, log_shape],
        in_specs=[in_smem()] * 3 + [in_vmem()] * (len(unit) + 4),
        out_specs=[in_hbm()] * (len(unit) + 2)
        + [pl.BlockSpec(log_shape.shape, lambda i: (0, 0))],
        scratch_shapes=[
            pltpu.VMEM(qkv.shape, BF16),
            pltpu.VMEM(weight.shape, BF16),
            pltpu.VMEM((rows, width), BF16),
            pltpu.VMEM((2, rows, width), F32),
            pltpu.SMEM((rows // BLOCK,), jnp.int32),
            pltpu.SMEM((rows // BLOCK,), jnp.int32),
            pltpu.SemaphoreType.DMA((len(unit) + 2,)),
        ],
        compiler_params=pltpu.CompilerParams(vmem_limit_bytes=56 << 20),
        cost_estimate=pl.CostEstimate(
            flops=20 * rows * CHUNK * width,
            bytes_accessed=20 * rows * width,
            transcendentals=rows * CHUNK * width // HEAD_DIM,
        ),
        name="project_attend",
    )(owner_a, owner_b, facts, *unit, first, last, norm, bias)
    return found[: len(unit)], *found[len(unit) :]


def place_kernel(owner, blocks_ref, out_ref):
    count, own, _ = blocks_ref.shape
    width = out_ref.shape[1]
    for p in range(count):
        at = pl.ds(pl.multiple_of(owner[p] * own, own), own)
        out_ref[at, :] = blocks_ref[p, :, -width:]


def placed_rows(blocks, owner, width):
    out = jax.ShapeDtypeStruct((blocks.shape[0] * blocks.shape[1], width), blocks.dtype)
    return pl.pallas_call(
        place_kernel,
        grid=(1,),
        out_shape=out,
        in_specs=[in_smem(), in_vmem()],
        out_specs=pl.BlockSpec(out.shape, lambda i: (0, 0)),
        name="placed_rows",
    )(owner, blocks)


def attend_back_kernel(heads, parts, owner_a, owner_b, facts, *refs):
    qkv_ref, log_ref, weight_ref = refs[:3]
    part_refs, unit_refs = refs[3 : 3 + parts], refs[3 + parts : 3 + 2 * parts]
    outs = refs[3 + 2 * parts :]
    block_outs, row_outs, late_ref, sum_ref = outs[:4], outs[4 : 4 + parts], *outs[4 + parts :][:2]
    grads_ref, grad_ref, keys_acc, values_acc, probs_ref, inner_ref = outs[6 + parts :][:6]
    raw_ref, *block_refs, rows_ref, stored, limits, sems = outs[12 + parts :]
    blocks = Blocks(facts, stored, limits, heads, parts)
    blocks.find()
    half, own, split = block_refs[0].shape
    width = weight_ref.shape[1]
    near = unit_refs[0].shape[0]
    step = 2 * TILE
    for k, ref in enumerate(part_refs):
        grads_ref[near * k : near * (k + 1), :] = ref[...]
    attend_back_body(
        heads,
        blocks,
        qkv_ref,
        grads_ref,
        log_ref,
        grad_ref,
        keys_acc,
        values_acc,
        probs_ref,
        inner_ref,
    )
    copies = []

    def leave(source, target):
        copies.append(pltpu.make_async_copy(source, target, sems.at[len(copies)]))
        copies[-1].start()

    sums = jnp.sum(grad_ref[...].astype(F32), axis=0, keepdims=True)
    sum_ref[...] = sums
    for i in range(weight_ref.shape[0] // step):
        at = slice(step * i, step * (i + 1))
        raw = total(
            [
                matmul(ref[:, at], grad_ref[near * k : near * (k + 1), :], TN)
                for k, ref in enumerate(unit_refs)
            ]
        )
        weight = weight_ref[at, :].astype(F32)
        raw_ref[at, :] = raw.astype(BF16)
        for row, value in enumerate((raw * weight, weight * sums)):
            lanes = total([value[:, 128 * c : 128 * (c + 1)] for c in range(width // 128)])
            for b in range(step // 128):
                turned = lanes[128 * b : 128 * (b + 1)].T
                found = jnp.sum(turned, axis=0, keepdims=True)
                start = step * i + 128 * b
                late_ref[row : row + 1, start : start + 128] = found
    for p in range(2 * half):
        at = pl.ds(pl.multiple_of(owner_a[p] * own, own), own)
        block_refs[p // half][p % half] = raw_ref[at, :split]
        at = pl.ds(pl.multiple_of(owner_b[p] * own, own), own)
        block_refs[2 + p // half][p % half] = raw_ref[at, split:]
    for source, target in zip(block_refs, block_outs):
        leave(source, target)
    for k in range(parts - 1, -1, -1):
        at = slice(near * k, near * (k + 1))
        rows_ref[at, :] = matmul(grad_ref[at, :], weight_ref[...], NT).astype(BF16)
        leave(rows_ref.at[at, :], row_outs[k])
    for copy in copies:
        copy.wait()


def attend_back(
    qkv, grad_context, log_totals, unit, weight, owner_a, owner_b, split, facts, heads
):
    rows, width = qkv.shape[0], heads * HEAD_DIM
    features = weight.shape[0]
    count = owner_a.shape[0]
    own = features // count
    first = jax.ShapeDtypeStruct((count // 2, own, split), BF16)
    last = jax.ShapeDtypeStruct((count // 2, own, 3 * width - split), BF16)
    small = [
        jax.ShapeDtypeStruct((2, features), F32),
        jax.ShapeDtypeStruct((1, 3 * width), F32),
    ]
    blocks = [first, first, last, last]
    return pl.pallas_call(
        functools.partial(attend_back_kernel, heads, len(unit)),
        grid=(1,),
        out_shape=[*blocks, *[like(value) for value in unit], *small],
        in_specs=[in_smem()] * 3 + [in_vmem()] * (3 + 2 * len(unit)),
        out_specs=[in_hbm()] * (4 + len(unit))
        + [pl.BlockSpec(value.shape, lambda i: (0, 0)) for value in small],
        scratch_shapes=[
            pltpu.VMEM((rows, width), BF16),
            pltpu.VMEM(qkv.shape, BF16),
            pltpu.VMEM((rows, width), F32),
            pltpu.VMEM((rows, width), F32),
            pltpu.VMEM((2, rows, width), F32),
            pltpu.VMEM((2, rows, width), F32),
            pltpu.VMEM(weight.shape, BF16),
            *[pltpu.VMEM(value.shape, BF16) for value in blocks],
            pltpu.VMEM((rows, features), BF16),
            pltpu.SMEM((rows // BLOCK,), jnp.int32),
            pltpu.SMEM((rows // BLOCK,), jnp.int32),
            pltpu.SemaphoreType.DMA((4 + len(unit),)),
        ],
        compiler_params=pltpu.CompilerParams(vmem_limit_bytes=53 << 20),
        cost_estimate=pl.CostEstimate(
            flops=40 * rows * CHUNK * width,
            bytes_accessed=40 * rows * width,
            transcendentals=rows * CHUNK * width // HEAD_DIM,
        ),
        name="attend_back",
    )(
        owner_a,
        owner_b,
        facts,
        qkv,
        log_totals,
        weight,
        *grad_context,
        *unit,
    )


TILE = 256


def gelu_and_slope(pre):
    scale = (2.0 / 3.141592653589793) ** 0.5
    square = pre * pre
    bent = jnp.tanh(scale * pre * (1.0 + 0.044715 * square))
    half = 0.5 + 0.5 * bent
    slope = half + (0.5 * scale) * pre * (1.0 - bent * bent) * (1.0 + 0.134145 * square)
    return pre * half, slope


def pick(refs):
    per = pl.num_programs(0) // len(refs)
    value = refs[0][...]
    for k, ref in enumerate(refs[1:], 1):
        value = jnp.where(pl.program_id(0) >= k * per, ref[...], value)
    return value


def put(refs, value):
    per = pl.num_programs(0) // len(refs)
    for k, ref in enumerate(refs):
        ref[...] = jnp.where(pl.program_id(0) // per == k, value, ref[...])


def feed_kernel(quarters, taken, *refs):
    normed = pick(refs[:quarters])
    grads = pick(refs[quarters : 2 * quarters])
    weight_ref, bias_ref = refs[2 * quarters : 2 * quarters + 2]
    results = refs[2 * quarters + 2 + taken :]
    units = bias_ref.shape[1]
    up = weight_ref[:, :units]
    down = weight_ref[:, units:]
    active, slope = gelu_and_slope(matmul(normed, up, NN) + bias_ref[...])
    active = active.astype(BF16)
    grad_hidden = (matmul(grads, down, NN) * slope).astype(BF16)
    put(results[:quarters], matmul(grad_hidden, up, NT).astype(BF16))
    put(results[quarters : 2 * quarters], matmul(active, down, NT).astype(BF16))
    for ref, value in zip(results[2 * quarters :], (normed, grad_hidden, grads, active)):
        ref[...] = value


def tile_specs(arrays):
    def spec(k, value):
        tiles = value.shape[0] // TILE
        return pl.BlockSpec(
            (TILE, value.shape[1]), lambda i: (jnp.clip(i - k * tiles, 0, tiles - 1), 0)
        )

    return [spec(k, value) for k, value in enumerate(arrays)]


def feed(normed, grads, weights, bias, stacks, start, quarters):
    rows, features = normed[0].shape
    units = bias.shape[1]
    here = len(normed)
    tiles = rows // TILE
    stacked = [jax.ShapeDtypeStruct((rows * quarters, n), BF16) for n in (features, units) * 2]
    found = pl.pallas_call(
        functools.partial(feed_kernel, here, len(stacks)),
        grid=(here * tiles,),
        out_shape=[like(value) for value in normed] * 2 + stacked,
        in_specs=tile_specs(normed)
        + tile_specs(grads)
        + [in_vmem(), whole_spec(bias)]
        + [pl.BlockSpec(memory_space=pl.ANY)] * len(stacks),
        out_specs=tile_specs(normed) * 2
        + [
            pl.BlockSpec((TILE, value.shape[1]), lambda i: (i + start * tiles, 0))
            for value in stacked
        ],
        input_output_aliases={2 * here + 2 + n: 2 * here + n for n in range(len(stacks))},
        compiler_params=limit(56),
        cost_estimate=pl.CostEstimate(
            flops=8 * here * rows * features * units,
            bytes_accessed=16 * here * rows * features + 4 * features * units,
            transcendentals=here * rows * units,
        ),
        name="feed",
    )(*normed, *grads, weights, bias, *stacks)
    return found[:here], found[here : 2 * here], found[2 * here :]


def feed_grads_kernel(normed_ref, grad_ref, grads_ref, active_ref, out_ref, sum_ref, acc_ref):
    units = sum_ref.shape[1]
    grad_hidden = grad_ref[...]

    @pl.when(pl.program_id(0) == 0)
    def _():
        acc_ref[...] = jnp.zeros_like(acc_ref)
        sum_ref[...] = jnp.zeros_like(sum_ref)

    acc_ref[:, :units] += matmul(normed_ref[...], grad_hidden, TN)
    acc_ref[:, units:] += matmul(grads_ref[...], active_ref[...], TN)
    sum_ref[...] += jnp.sum(grad_hidden.astype(F32), axis=0, keepdims=True)

    @pl.when(pl.program_id(0) == pl.num_programs(0) - 1)
    def _():
        out_ref[...] = acc_ref[...].astype(BF16)


def feed_grads(stacks):
    rows, features = stacks[0].shape
    units = stacks[1].shape[1]
    sums = jax.ShapeDtypeStruct((features, 2 * units), BF16)
    hidden = jax.ShapeDtypeStruct((1, units), F32)
    return pl.pallas_call(
        feed_grads_kernel,
        grid=(rows // (2 * TILE),),
        out_shape=[sums, hidden],
        in_specs=[tiled_spec(value, 2 * TILE) for value in stacks],
        out_specs=[whole_spec(sums), whole_spec(hidden)],
        scratch_shapes=[pltpu.VMEM(sums.shape, F32)],
        compiler_params=limit(62),
        cost_estimate=cost(4 * rows * features * units, 8 * rows * features),
        name="feed_grads",
    )(*stacks)


def norm_parts(rows):
    centred = rows - jnp.mean(rows, axis=-1, keepdims=True)
    inverse = lax.rsqrt(jnp.mean(centred * centred, axis=-1, keepdims=True) + EPS)
    return centred * inverse, inverse


def norm_back(grad_normed, unit, inverse, gain):
    grad_unit = grad_normed * gain
    return inverse * (
        grad_unit
        - jnp.mean(grad_unit, axis=-1, keepdims=True)
        - unit * jnp.mean(grad_unit * unit, axis=-1, keepdims=True)
    )


def whole_spec(value):
    return pl.BlockSpec(value.shape, lambda i: (0,) * value.ndim)


def tiled_spec(value, tile=TILE):
    return pl.BlockSpec((tile, value.shape[1]), lambda i: (i, 0))


def like(value, dtype=None):
    return jax.ShapeDtypeStruct(value.shape, dtype or value.dtype)


def limit(mebibytes):
    return pltpu.CompilerParams(vmem_limit_bytes=mebibytes << 20)


def cost(flops, moved):
    return pl.CostEstimate(flops=flops, bytes_accessed=moved, transcendentals=0)


def unit_kernel(rows_ref, unit_ref):
    unit_ref[...] = norm_parts(rows_ref[...].astype(F32))[0].astype(BF16)


def unit_rows(rows):
    return pl.pallas_call(
        unit_kernel,
        grid=(rows.shape[0] // TILE,),
        out_shape=like(rows),
        in_specs=[tiled_spec(rows)],
        out_specs=tiled_spec(rows),
        compiler_params=limit(62),
        cost_estimate=cost(8 * rows.size, 4 * rows.size),
        name="unit",
    )(rows)


def middle_kernel(parts, *refs):
    context_refs, out_refs = refs[:parts], refs[parts : 2 * parts]
    rows_ref, vector_ref, middle_ref, normed_ref = refs[2 * parts :]
    middle = rows_ref[...].astype(F32) + vector_ref[0:1, :]
    for context_ref, out_ref in zip(context_refs, out_refs):
        middle += matmul(context_ref[...], out_ref[...], NT)
    middle_ref[...] = middle.astype(BF16)
    unit = norm_parts(middle)[0]
    normed_ref[...] = (unit * vector_ref[1:2, :] + vector_ref[2:3, :]).astype(BF16)


def middle_rows(context, out_parts, rows, vectors):
    return pl.pallas_call(
        functools.partial(middle_kernel, len(context)),
        grid=(rows.shape[0] // TILE,),
        out_shape=[like(rows), like(rows)],
        in_specs=[tiled_spec(value) for value in context]
        + [whole_spec(value) for value in out_parts]
        + [tiled_spec(rows), whole_spec(vectors)],
        out_specs=[tiled_spec(rows), tiled_spec(rows)],
        compiler_params=limit(62),
        cost_estimate=cost(2 * rows.size * rows.shape[1], 12 * rows.size),
        name="middle",
    )(*context, *out_parts, rows, vectors)


def middle_back_kernel(terms, parts, owner, *refs):
    term_refs, out_refs = refs[:terms], refs[terms : terms + parts]
    context_refs = refs[terms + parts : terms + 2 * parts]
    middle_ref, cotangent_ref, vector_ref, grad_ref, sum_ref = refs[
        terms + 2 * parts : terms + 2 * parts + 5
    ]
    head_refs = refs[terms + 2 * parts + 5 : terms + 3 * parts + 5]
    block_refs = refs[terms + 3 * parts + 5 : -1]
    found_ref = refs[-1]
    first = pl.program_id(0) == 0
    last = pl.program_id(0) == pl.num_programs(0) - 1
    count, own, width = block_refs[0].shape
    grad_normed = total([ref[...].astype(F32) for ref in term_refs])
    unit, inverse = norm_parts(middle_ref[...].astype(F32))
    cotangent = cotangent_ref[...].astype(F32)
    grad = cotangent + norm_back(grad_normed, unit, inverse, vector_ref[1:2, :])
    low = grad.astype(BF16)
    grad_ref[...] = low
    for head_ref, out_ref in zip(head_refs, out_refs):
        head_ref[...] = matmul(low, out_ref[...], NN).astype(BF16)
    sums = [
        jnp.sum(value, axis=0, keepdims=True)
        for value in (grad_normed * unit, grad_normed, grad, cotangent)
    ]
    sums = jnp.concatenate(sums, axis=0)

    @pl.when(first)
    def _():
        sum_ref[...] = jnp.zeros_like(sum_ref)
        found_ref[...] = jnp.zeros_like(found_ref)

    sum_ref[...] += sums
    for k, context_ref in enumerate(context_refs):
        found_ref[:, k * width : (k + 1) * width] += matmul(low, context_ref[...], TN)

    @pl.when(last)
    def _():
        for k, block_ref in enumerate(block_refs):
            for p in range(count):
                at = pl.ds(pl.multiple_of(owner[p] * own, own), own)
                block_ref[p] = found_ref[at, k * width : (k + 1) * width].astype(BF16)


def middle_back(terms, out_parts, context, middle, cotangent, vectors, owner):
    rows, features = middle.shape
    width = out_parts[0].shape[1]
    parts = len(out_parts)
    count = owner.shape[0]
    sums = jax.ShapeDtypeStruct((4, features), F32)
    head = jax.ShapeDtypeStruct((rows, width), BF16)
    blocks = jax.ShapeDtypeStruct((count, features // count, width), BF16)
    found = pl.pallas_call(
        functools.partial(middle_back_kernel, len(terms), parts),
        grid=(rows // TILE,),
        out_shape=[like(middle), sums] + [head] * parts + [blocks] * parts,
        in_specs=[in_smem()]
        + [tiled_spec(value) for value in terms]
        + [whole_spec(value) for value in out_parts]
        + [tiled_spec(value) for value in context]
        + [tiled_spec(middle), tiled_spec(cotangent), whole_spec(vectors)],
        out_specs=[tiled_spec(middle), whole_spec(sums)]
        + [tiled_spec(head)] * parts
        + [whole_spec(blocks)] * parts,
        scratch_shapes=[pltpu.VMEM((features, width * parts), F32)],
        compiler_params=limit(62),
        cost_estimate=cost(4 * middle.size * features, 20 * middle.size),
        name="middle_back",
    )(owner, *terms, *out_parts, *context, middle, cotangent, vectors)
    return found[0], found[1], found[2 : 2 + parts], found[2 + parts :]


def input_back_kernel(terms, *refs):
    *term_refs, first_ref, last_ref = refs[:terms]
    rows_ref, middle_ref, vector_ref, out_ref = refs[terms:]
    half = jnp.where(pl.program_id(0) == 0, first_ref[...], last_ref[...])
    grad_normed = total([ref[...].astype(F32) for ref in term_refs]) + half.astype(F32)
    unit, inverse = norm_parts(rows_ref[...].astype(F32))
    grad = norm_back(grad_normed, unit, inverse, vector_ref[0:1, :])
    out_ref[...] = (middle_ref[...].astype(F32) + grad).astype(BF16)


def input_back(terms, rows, grad_middle, vectors):
    tile = rows.shape[0] // 2
    return pl.pallas_call(
        functools.partial(input_back_kernel, len(terms)),
        grid=(2,),
        out_shape=like(rows),
        in_specs=[tiled_spec(value, tile) for value in terms[:-2]]
        + [whole_spec(value) for value in terms[-2:]]
        + [tiled_spec(rows, tile), tiled_spec(grad_middle, tile), whole_spec(vectors)],
        out_specs=tiled_spec(rows, tile),
        compiler_params=limit(62),
        cost_estimate=cost(20 * rows.size, 14 * rows.size),
        name="input_back",
    )(*terms, rows, grad_middle, vectors)


def per_device(
    tokens,
    output_cotangent,
    lengths,
    block_place,
    random_blocks,
    qkv_weight,
    out_weight,
    up_weight,
    down_weight,
    vectors,
    hidden_bias,
):
    ways = lax.axis_size("tensor")
    spread_ways = lax.axis_size("dp")
    position = lax.axis_index("tensor")
    index = lax.axis_index("dp") * ways + position
    near = tokens.shape[0]
    rows = near * ways
    features = tokens.shape[1]
    width = qkv_weight.shape[2]
    heads = width // HEAD_DIM
    units = up_weight.shape[1]
    own = features // spread_ways
    piece = vectors.shape[1]
    unit_piece = hidden_bias.shape[1]

    small = jnp.zeros((8, features), F32)
    small = lax.dynamic_update_slice(small, vectors, (0, index * piece))
    small_hidden = jnp.zeros((1, units * ways), F32)
    small_hidden = lax.dynamic_update_slice(small_hidden, hidden_bias, (0, index * unit_piece))
    packed = jnp.concatenate([small.reshape(-1), small_hidden.reshape(-1)])
    packed = summed_everywhere(packed, ("tensor",))

    unit_near = unit_rows(tokens)
    unit_near, packed = together(unit_near, packed)
    unit_far = far(unit_near, "tensor")

    facts = attention_facts(lengths[0], position, block_place, random_blocks)

    bits = bits_of("dp")
    order_a = bits[::-1]
    order_b = bits[:1] + bits[:0:-1]
    owner_a = block_owners("dp", order_a)
    owner_b = block_owners("dp", order_b)
    split = 2 * width
    qkv_flat = qkv_weight.reshape(own, 3 * width)
    first_blocks = doubled(qkv_flat[:, :split], "dp", order_a)
    last_flat = jnp.concatenate([qkv_flat[:, split:], out_weight], axis=1)
    last_blocks = doubled(last_flat, "dp", order_b)
    packed = summed_everywhere(packed, ("dp",))
    feed_flat = jnp.concatenate([up_weight, down_weight], axis=1)
    first_going, last_going = output_cotangent[: near // 2], output_cotangent[near // 2 :]
    first_going, unit_far = together(first_going, unit_far)
    cotangent_first = far(first_going, "tensor")
    feed_flat, first_blocks, last_blocks, cotangent_first, packed = together(
        feed_flat, first_blocks, last_blocks, cotangent_first, packed
    )
    feed_full = lax.all_gather(feed_flat, "dp", axis=0, tiled=True)
    unit_parts = gathered_parts(unit_near, unit_far, "tensor")

    vectors_full = packed[: 8 * features].reshape(8, features)
    hidden_full = packed[8 * features :]
    bias_query = lax.dynamic_slice_in_dim(vectors_full[6], position * width, width)
    bias_value = lax.dynamic_slice_in_dim(vectors_full[7], position * width, width)
    bias_qkv = jnp.concatenate([bias_query, jnp.zeros_like(bias_query), bias_value])[None]
    bias_hidden = lax.dynamic_slice_in_dim(hidden_full, position * units, units)[None]
    norm_one = vectors_full[:2]
    norm_two = jnp.stack([vectors_full[4], vectors_full[2], vectors_full[3]])


    out_group = placed_rows(last_blocks, owner_b, width)
    out_far = far(out_group, "tensor")
    last_going, out_group = together(last_going, out_group)
    cotangent_last = far(last_going, "tensor")
    *context, qkv, qkv_full, log_totals = project_attend(
        unit_parts,
        first_blocks,
        last_blocks,
        owner_a,
        owner_b,
        norm_one,
        bias_qkv,
        facts,
        heads,
    )
    context = context[0]
    *context, out_far, cotangent_last = together(*context, out_far, cotangent_last)
    cotangent_far = jnp.concatenate([cotangent_first, cotangent_last], axis=0)
    grad_parts = gathered_parts(output_cotangent, cotangent_far, "tensor")

    out_parts = gathered_parts(out_group, out_far, "tensor")
    context_near = exchanged_parts(context, "tensor")
    middle, normed_two = middle_rows(context_near, out_parts, tokens, norm_two)

    half = ways // 2
    normed_far = far(normed_two, "tensor")
    normed_parts = gathered_parts(normed_two, normed_far, "tensor")
    near_back, near_out, stacks = feed(
        normed_parts[:half], grad_parts[:half], feed_full, bias_hidden, (), 0, ways
    )
    normed_far, *stacks = together(normed_far, *stacks)
    normed_parts = gathered_parts(normed_two, normed_far, "tensor")
    far_back, far_out, stacks = feed(
        normed_parts[half:], grad_parts[half:], feed_full, bias_hidden, stacks, half, ways
    )
    back_parts, feed_parts = near_back + far_back, near_out + far_out
    back_terms, far_sum = summed_halves(back_parts, "tensor")
    back_terms.append(far(far_sum, "tensor"))
    feed_sums, sum_hidden = feed_grads(stacks)
    feed_terms, feed_far = summed_halves(feed_parts, "tensor")
    early, late_rows = feed_far[: near // 2], feed_far[near // 2 :]
    *back_terms, feed_sums, early = together(*back_terms, feed_sums, early)
    early = far(early, "tensor")
    feed_weight_grads = lax.psum_scatter(feed_sums, "dp", scatter_dimension=0, tiled=True)
    feed_weight_grads = feed_weight_grads.astype(F32)

    grad_middle, sums_two, grad_heads, out_blocks = middle_back(
        back_terms, out_parts, context_near, middle, output_cotangent, norm_two, owner_b
    )
    grad_context = exchanged_parts(grad_heads, "tensor")

    *out_blocks, early = together(*out_blocks, early)
    out_terms, out_far = summed_halves(out_blocks, "tensor")
    *grad_context, out_far, late_rows = together(*grad_context, out_far, late_rows)
    out_terms.append(far(out_far, "tensor"))
    late_rows = far(late_rows, "tensor")
    first_keep, first_send, last_keep, last_send, *back_parts, late, sum_qkv = attend_back(
        qkv,
        grad_context,
        log_totals,
        unit_parts,
        qkv_full,
        owner_a,
        owner_b,
        split,
        facts,
        heads,
    )
    first_send, last_send, late, late_rows, *rest = together(
        first_send, last_send, late, late_rows, *out_terms, *back_parts
    )
    out_terms, back_parts = rest[: len(out_terms)], rest[len(out_terms) :]
    near_rows, far_rows = back_parts[:half], back_parts[half:]
    feed_terms.append(jnp.concatenate([early, late_rows], axis=0))
    output = total([term.astype(F32) for term in (*feed_terms, middle)]) + vectors_full[5]
    output = output.astype(BF16)
    out_sums = total([term.astype(F32) for term in out_terms]).astype(BF16)
    last_keep = jnp.concatenate([last_keep, out_sums[: spread_ways // 2]], axis=2)
    last_send = jnp.concatenate([last_send, out_sums[spread_ways // 2 :]], axis=2)
    head_sums = lax.dynamic_update_slice(
        jnp.zeros((3, features), F32), sum_qkv.reshape(3, width), (0, position * width)
    )
    hidden_sums = lax.dynamic_update_slice(
        jnp.zeros((1, units * ways), F32), sum_hidden, (0, position * units)
    )
    packed = jnp.concatenate(
        [late.reshape(-1), sums_two.reshape(-1), head_sums.reshape(-1), hidden_sums.reshape(-1)]
    )
    packed = summed_everywhere(packed, ("tensor",))
    far_sum = added(far_rows[0], swapped(far_rows[1], "tensor", 1))
    packed, far_sum, first_keep, last_keep, *near_rows = together(
        packed, far_sum, first_keep, last_keep, *near_rows
    )
    far_first = far(far_sum[: near // 2], "tensor")
    far_last = far(far_sum[near // 2 :], "tensor")
    first_keep, first_send = halved(first_keep, first_send, "dp", order_a)
    last_keep, last_send = halved(last_keep, last_send, "dp", order_b)
    first_send, last_send, far_first = together(first_send, last_send, far_first)
    while first_send.shape[0] > 1:
        first_keep, first_send = halved(first_keep, first_send, "dp", order_a)
        last_keep, last_send = halved(last_keep, last_send, "dp", order_b)
    first_send, last_send, far_last, feed_weight_grads, output = together(
        first_send, last_send, far_last, feed_weight_grads, output
    )
    near_terms = [near_rows[0], swapped(near_rows[1], "tensor", 1), far_first, far_last]
    input_grad = input_back(near_terms, tokens, grad_middle, norm_one)
    first_keep, last_keep, input_grad = together(first_keep, last_keep, input_grad)
    first_raw = halved(first_keep, first_send, "dp", order_a)[0][0].astype(F32)
    last_raw = halved(last_keep, last_send, "dp", order_b)[0][0].astype(F32)
    out_weight_grad = last_raw[:, width:]
    last_raw = last_raw[:, :width]

    packed = summed_everywhere(packed, ("dp",))
    by_feature = packed[: 9 * features].reshape(9, features)
    hidden_sums = packed[9 * features :]
    vectors_grad = lax.dynamic_slice_in_dim(by_feature, index * piece, piece, axis=1)
    vectors_grad = jnp.concatenate([vectors_grad[:7], vectors_grad[8:]], axis=0)
    hidden_bias_grad = lax.dynamic_slice_in_dim(hidden_sums, index * unit_piece, unit_piece)

    sum_qkv = lax.dynamic_slice_in_dim(by_feature[6:], position * width, width, axis=1)
    mine = lax.dynamic_slice_in_dim(norm_one, lax.axis_index("dp") * own, own, axis=1)
    raw = jnp.concatenate([first_raw, last_raw], axis=1).reshape(own, 3, width)
    qkv_weight_grad = mine[0][:, None, None] * raw + mine[1][:, None, None] * sum_qkv
    return (
        output,
        input_grad,
        qkv_weight_grad,
        out_weight_grad,
        feed_weight_grads[:, :units],
        feed_weight_grads[:, units:],
        vectors_grad,
        hidden_bias_grad[None, :],
    )


def solution(mesh):
    placed = (
        P(("dp", "tensor"), None),
        P(("dp", "tensor"), None),
        P("dp"),
        P("dp", None),
        P("dp", "tensor", None, None),
        P("dp", None, "tensor"),
        P("dp", "tensor"),
        P("dp", "tensor"),
        P("dp", "tensor"),
        P(None, ("dp", "tensor")),
        P(None, ("dp", "tensor")),
    )
    return jax.shard_map(
        per_device,
        mesh=mesh,
        in_specs=placed,
        out_specs=(
            P(("dp", "tensor"), None),
            P(("dp", "tensor"), None),
            P("dp", None, "tensor"),
            P("dp", "tensor"),
            P("dp", "tensor"),
            P("dp", "tensor"),
            P(None, ("dp", "tensor")),
            P(None, ("dp", "tensor")),
        ),
        check_vma=False,
    )
```

```python
import functools

import jax
import jax.numpy as jnp
from jax import lax
from jax.experimental import pallas as pl
from jax.experimental.pallas import tpu as pltpu
from jax.sharding import PartitionSpec as P

HEAD_DIM = 64
BLOCK = 64
PAIR = 2 * HEAD_DIM
SLOTS = 8
CHUNK = 512
EPS = 1e-05
NEGATIVE = -1e30
F32 = jnp.float32
BF16 = jnp.bfloat16
NT = (((1,), (1,)), ((), ()))
NN = (((1,), (0,)), ((), ()))
TN = (((0,), (0,)), ((), ()))


def matmul(left, right, dims):
    return lax.dot_general(left, right, dims, preferred_element_type=F32)


def swapped(value, axis, bit):
    count = lax.axis_size(axis)
    return lax.ppermute(value, axis, [(i, i ^ bit) for i in range(count)])


def bits_of(axis):
    count = lax.axis_size(axis)
    return [1 << b for b in range(count.bit_length() - 1)]


def together(*values):
    return lax.optimization_barrier(values)


def far(value, axis):
    return swapped(value, axis, bits_of(axis)[-1])


def gathered_parts(value, far_value, axis):
    bits = bits_of(axis)
    parts = {0: value, bits[-1]: far_value}
    for bit in reversed(bits[:-1]):
        parts.update({k | bit: swapped(p, axis, bit) for k, p in list(parts.items())})
    return [parts[k] for k in range(len(parts))]


def summed_halves(parts, axis):
    left = dict(enumerate(parts))
    terms = [parts[0]]
    for bit in bits_of(axis)[: len(parts).bit_length() - 2]:
        kept = {}
        for k in sorted(left, reverse=True):
            if k & bit == 0:
                arrived = swapped(left[k | bit], axis, bit)
                if k == 0:
                    terms.append(arrived)
                    kept[k] = None
                else:
                    kept[k] = added(left[k], arrived)
        left = kept
    return terms, left[len(parts) // 2]


def added(left, right):
    return (left.astype(F32) + right.astype(F32)).astype(BF16)


def doubled(value, axis, order):
    blocks = value[None]
    for bit in order:
        blocks = jnp.concatenate([blocks, swapped(blocks, axis, bit)], axis=0)
    return blocks


def halved(keep, send, axis, order):
    half = send.shape[0]
    arrived = swapped(send, axis, order[half.bit_length() - 1])
    rest = half // 2
    return added(keep[: half - rest], arrived[: half - rest]), added(
        keep[half - rest :], arrived[half - rest :]
    )


def block_owners(axis, order):
    count = lax.axis_size(axis)
    device = [sum(bit for b, bit in enumerate(order) if p >> b & 1) for p in range(count)]
    return lax.axis_index(axis) ^ jnp.asarray(device, jnp.int32)


def exchanged_parts(parts, axis):
    return [p if k == 0 else swapped(p, axis, k) for k, p in enumerate(parts)]


def summed_everywhere(value, axes):
    size = value.shape[0]
    value = jnp.pad(value, (0, -size % 1024)).reshape(-1, 128)
    for axis in axes:
        if lax.axis_size(axis) <= 4:
            value = total([value] + [swapped(value, axis, k) for k in range(1, lax.axis_size(axis))])
        else:
            for bit in bits_of(axis):
                value = value + swapped(value, axis, bit)
    return value.reshape(-1)[:size]


def sent_and_summed(value, axis):
    count = lax.axis_size(axis)
    blocks = value.reshape(count, value.shape[0] // count, *value.shape[1:])
    arrived = lax.all_to_all(blocks, axis, 0, 0, tiled=True)
    return jnp.sum(arrived.astype(F32), axis=0)


def attention_facts(length, position, placing, chosen):
    head = jnp.stack([length, position]).astype(jnp.int32)
    return jnp.concatenate([head, placing.reshape(-1), chosen.reshape(-1)])


class Blocks:
    def __init__(self, facts, stored, limits, heads, quarters):
        self.facts, self.stored, self.limits = facts, stored, limits
        self.heads, self.quarters = heads, quarters
        self.count = stored.shape[0]
        self.length = facts[0]
        self.last = (self.length + BLOCK - 1) // BLOCK - 1
        self.last_rows = self.length - BLOCK * self.last

    def find(self):
        per = self.count // self.quarters
        for quarter in range(self.quarters):
            start = (self.facts[1] ^ quarter) * per
            for n in range(per):
                number = self.facts[2 + start + n]
                self.stored[number] = quarter * per + n
                rows = self.length - BLOCK * number
                self.limits[quarter * per + n] = jnp.clip(rows, 0, BLOCK)

    def item(self, number):
        last = self.last
        alive = number != last
        before, behind = number - 1, number + 1
        common = [0, last, before, number, jnp.minimum(behind, self.count - 1)]
        good = [
            alive,
            alive,
            alive & (before > 0) & (before < last),
            alive & (number < last),
            alive & (behind < last),
        ]
        places = [self.stored[block] for block in common]
        lane = lax.broadcasted_iota(jnp.int32, (1, self.heads * HEAD_DIM), 1)
        added_scores = [jnp.where(flag, 0.0, NEGATIVE).astype(F32) for flag in good]
        drawn = [
            [
                self.facts[2 + self.count + (h * self.count + number) * 3 + s]
                for h in range(self.heads)
            ]
            for s in range(3)
        ]
        random = []
        for s in range(3):
            random.append([self.stored[block] for block in drawn[s]])
            row = jnp.zeros((1, self.heads * HEAD_DIM), F32)
            for h, block in enumerate(drawn[s]):
                fresh = alive & (block > 0) & (block < last) & (jnp.abs(block - number) > 1)
                for other in range(s):
                    fresh = fresh & (block != drawn[other][h])
                score = jnp.where(fresh, 0.0, NEGATIVE).astype(F32)
                row = jnp.where(lane // HEAD_DIM == h, score, row)
            added_scores.append(row)
        return places, random, added_scores


def block_rows(index):
    return pl.ds(pl.multiple_of(index * BLOCK, BLOCK), BLOCK)


def spread(rows, heads):
    lane = lax.broadcasted_iota(jnp.int32, (1, heads * HEAD_DIM), 1)
    zero = jnp.zeros_like(rows)
    return jnp.concatenate(
        [jnp.where(lane // HEAD_DIM == h, rows, zero) for h in range(heads)], axis=0
    )


def collapse(full, heads):
    lane = lax.broadcasted_iota(jnp.int32, (1, PAIR), 1)
    pieces = []
    for pair in range(heads // 2):
        cols = slice(PAIR * pair, PAIR * (pair + 1))
        even = full[2 * pair * HEAD_DIM : (2 * pair + 1) * HEAD_DIM, cols]
        odd = full[(2 * pair + 1) * HEAD_DIM : (2 * pair + 2) * HEAD_DIM, cols]
        pieces.append(jnp.where(lane < HEAD_DIM, even, odd))
    return jnp.concatenate(pieces, axis=1)


def gathered_keys(ref, start, places, random, heads):
    width = heads * HEAD_DIM
    lane = lax.broadcasted_iota(jnp.int32, (1, PAIR), 1)
    parts = [ref[block_rows(place), start : start + width] for place in places]
    for drawn in random:
        pieces = []
        for pair in range(heads // 2):
            cols = slice(start + PAIR * pair, start + PAIR * (pair + 1))
            even = ref[block_rows(drawn[2 * pair]), cols]
            odd = ref[block_rows(drawn[2 * pair + 1]), cols]
            pieces.append(jnp.where(lane < HEAD_DIM, even, odd))
        parts.append(jnp.concatenate(pieces, axis=1))
    return jnp.concatenate(parts, axis=0)


def slot(value, index):
    return value[BLOCK * index : BLOCK * (index + 1)]


def biased(scores, bias, last_rows):
    row = lax.broadcasted_iota(jnp.int32, (BLOCK, 1), 0)
    parts = [slot(scores, s) + bias[s] for s in range(SLOTS)]
    parts[1] = jnp.where(row < last_rows, parts[1], NEGATIVE)
    return parts


def total(parts):
    return functools.reduce(jnp.add, parts)


def attend_body(heads, blocks, qkv_ref, out_ref, log_ref, keep_ref):
    count = blocks.count
    stored, limits = blocks.stored, blocks.limits
    width = heads * HEAD_DIM
    scale = jnp.asarray(HEAD_DIM**-0.5, BF16)

    def item(number):
        places, random, scores = blocks.item(number)
        here = block_rows(places[3])
        queries = spread(qkv_ref[here, :width] * scale, heads)
        keys = gathered_keys(qkv_ref, width, places, random, heads)
        parts = biased(matmul(keys, queries, NT), scores, blocks.last_rows)
        top = jnp.max(functools.reduce(jnp.maximum, parts), axis=0, keepdims=True)
        weights = [jnp.exp(p - top) for p in parts]
        row_total = jnp.sum(total(weights), axis=0, keepdims=True)
        inverse = 1.0 / row_total
        probs = jnp.concatenate([(p * inverse).astype(BF16) for p in weights], axis=0)
        values = gathered_keys(qkv_ref, 2 * width, places, random, heads)
        out_ref[here, :] = collapse(matmul(probs, values, TN), heads).astype(BF16)
        log_ref[pl.ds(number, 1), :] = top + jnp.log(row_total)

    def step(group, carry):
        for part in range(10):
            item(1 + group * 10 + part)
        return carry

    lax.fori_loop(0, (count - 1) // 10, step, 0)
    for number in range(1 + (count - 1) // 10 * 10, count):
        item(number)

    row = lax.broadcasted_iota(jnp.int32, (BLOCK, 1), 0)
    per = CHUNK // BLOCK
    chunks = count // per

    def chunk_rows(chunk):
        return pl.ds(pl.multiple_of(chunk * CHUNK, CHUNK), CHUNK)

    numbers = [0, blocks.last]
    rows_of = [block_rows(stored[number]) for number in numbers]
    queries = [spread(qkv_ref[at, :width] * scale, heads) for at in rows_of]

    def scores(chunk, tops):
        at = chunk_rows(chunk)
        keys = qkv_ref[at, width : 2 * width]
        found = []
        for end in range(2):
            raw = matmul(keys, queries[end], NT)
            parts = [
                jnp.where(row < limits[chunk * per + s], slot(raw, s), NEGATIVE)
                for s in range(per)
            ]
            keep_ref[end, at, :] = jnp.concatenate(parts, axis=0)
            found.append(jnp.maximum(tops[end], functools.reduce(jnp.maximum, parts)))
        return tuple(found)

    tops = lax.fori_loop(0, chunks, scores, (jnp.full((BLOCK, width), NEGATIVE, F32),) * 2)
    tops = [jnp.max(top, axis=0, keepdims=True) for top in tops]

    def exponents(chunk, totals):
        at = chunk_rows(chunk)
        found = []
        for end in range(2):
            weights = jnp.exp(keep_ref[end, at, :] - tops[end])
            keep_ref[end, at, :] = weights
            found.append(totals[end] + total([slot(weights, s) for s in range(per)]))
        return tuple(found)

    totals = lax.fori_loop(0, chunks, exponents, (jnp.zeros((BLOCK, width), F32),) * 2)
    totals = [jnp.sum(found, axis=0, keepdims=True) for found in totals]
    inverses = [1.0 / found for found in totals]

    def contexts(chunk, sums):
        at = chunk_rows(chunk)
        values = qkv_ref[at, 2 * width :]
        return tuple(
            sums[end] + matmul((keep_ref[end, at, :] * inverses[end]).astype(BF16), values, TN)
            for end in range(2)
        )

    sums = lax.fori_loop(0, chunks, contexts, (jnp.zeros((width, width), F32),) * 2)
    for end in range(2):
        out_ref[rows_of[end], :] = collapse(sums[end], heads).astype(BF16)
        log_ref[pl.ds(numbers[end], 1), :] = tops[end] + jnp.log(totals[end])


def attend_back_body(
    heads,
    blocks,
    qkv_ref,
    grad_ref,
    log_ref,
    out_ref,
    keys_acc,
    values_acc,
    probs_ref,
    inner_ref,
):
    count = blocks.count
    stored, limits = blocks.stored, blocks.limits
    width = heads * HEAD_DIM
    scale = jnp.asarray(HEAD_DIM**-0.5, BF16)
    lane = lax.broadcasted_iota(jnp.int32, (1, PAIR), 1)
    keys_acc[...] = jnp.zeros_like(keys_acc)
    values_acc[...] = jnp.zeros_like(values_acc)

    def accumulate(acc, value, places, random):
        for s in range(5):
            acc[block_rows(places[s]), :] += slot(value, s)
        for s in range(3):
            for h in range(heads):
                cols = slice(PAIR * (h // 2), PAIR * (h // 2 + 1))
                mine = (lane < HEAD_DIM) == (h % 2 == 0)
                term = jnp.where(mine, slot(value, 5 + s)[:, cols], 0.0)
                acc[block_rows(random[s][h]), cols] += term

    def item(number):
        places, random, scores = blocks.item(number)
        here = block_rows(places[3])
        queries = spread(qkv_ref[here, :width] * scale, heads)
        grads = spread(grad_ref[here, :], heads)
        keys = gathered_keys(qkv_ref, width, places, random, heads)
        values = gathered_keys(qkv_ref, 2 * width, places, random, heads)
        log_total = log_ref[pl.ds(number, 1), :]
        parts = biased(matmul(keys, queries, NT), scores, blocks.last_rows)
        probs = [jnp.exp(p - log_total) for p in parts]
        found = matmul(values, grads, NT)
        found = [slot(found, s) for s in range(SLOTS)]
        inner = total([p * d for p, d in zip(probs, found)])
        inner = jnp.sum(inner, axis=0, keepdims=True)
        grad_scores = jnp.concatenate(
            [(p * (d - inner)).astype(BF16) for p, d in zip(probs, found)], axis=0
        )
        probs_low = jnp.concatenate([p.astype(BF16) for p in probs], axis=0)
        accumulate(values_acc, matmul(probs_low, grads, NN), places, random)
        accumulate(keys_acc, matmul(grad_scores, queries, NN), places, random)
        grad_queries = collapse(matmul(grad_scores, keys, TN), heads) * HEAD_DIM**-0.5
        out_ref[here, :width] = grad_queries.astype(BF16)

    def step(group, carry):
        for part in range(6):
            item(1 + group * 6 + part)
        return carry

    lax.fori_loop(0, (count - 1) // 6, step, 0)
    for number in range(1 + (count - 1) // 6 * 6, count):
        item(number)

    row = lax.broadcasted_iota(jnp.int32, (BLOCK, 1), 0)
    per = CHUNK // BLOCK
    chunks = count // per

    def chunk_rows(chunk):
        return pl.ds(pl.multiple_of(chunk * CHUNK, CHUNK), CHUNK)

    numbers = [0, blocks.last]
    rows_of = [block_rows(stored[number]) for number in numbers]
    queries = [spread(qkv_ref[at, :width] * scale, heads) for at in rows_of]
    grads = [spread(grad_ref[at, :], heads) for at in rows_of]
    log_rows = [log_ref[pl.ds(number, 1), :] for number in numbers]

    def first(chunk, inners):
        at = chunk_rows(chunk)
        keys = qkv_ref[at, width : 2 * width]
        values = qkv_ref[at, 2 * width :]
        sums = []
        for end in range(2):
            scores = matmul(keys, queries[end], NT)
            parts = [
                jnp.where(row < limits[chunk * per + s], slot(scores, s), NEGATIVE)
                for s in range(per)
            ]
            probs = jnp.exp(jnp.concatenate(parts, axis=0) - log_rows[end])
            found = matmul(values, grads[end], NT)
            probs_ref[end, at, :] = probs
            inner_ref[end, at, :] = found
            both = probs * found
            sums.append(inners[end] + total([slot(both, s) for s in range(per)]))
        return tuple(sums)

    inners = lax.fori_loop(0, chunks, first, (jnp.zeros((BLOCK, width), F32),) * 2)
    inners = [jnp.sum(inner, axis=0, keepdims=True) for inner in inners]

    def second(chunk, sums):
        at = chunk_rows(chunk)
        keys = qkv_ref[at, width : 2 * width]
        found, to_values, to_keys = [], values_acc[at, :], keys_acc[at, :]
        for end in range(2):
            probs = probs_ref[end, at, :]
            grad_scores = (probs * (inner_ref[end, at, :] - inners[end])).astype(BF16)
            to_values = to_values + matmul(probs.astype(BF16), grads[end], NN)
            to_keys = to_keys + matmul(grad_scores, queries[end], NN)
            found.append(sums[end] + matmul(grad_scores, keys, TN))
        out_ref[at, width : 2 * width] = to_keys.astype(BF16)
        out_ref[at, 2 * width :] = to_values.astype(BF16)
        return tuple(found)

    sums = lax.fori_loop(0, chunks, second, (jnp.zeros((width, width), F32),) * 2)
    for end in range(2):
        grad_queries = collapse(sums[end], heads) * HEAD_DIM**-0.5
        out_ref[rows_of[end], :width] = grad_queries.astype(BF16)


def in_smem():
    return pl.BlockSpec(memory_space=pltpu.SMEM)


def in_vmem():
    return pl.BlockSpec(memory_space=pltpu.VMEM)


def project_attend_kernel(heads, parts, owner_a, owner_b, facts, *refs):
    unit_refs = refs[:parts]
    first_ref, last_ref, norm_ref, bias_ref = refs[parts : parts + 4]
    *quarter_refs, kept_ref, weight_out_ref, log_ref = refs[parts + 4 : 2 * parts + 7]
    qkv_ref, weight_ref, out_ref, keep_ref, stored, limits, sems = refs[2 * parts + 7 :]
    blocks = Blocks(facts, stored, limits, heads, parts)
    blocks.find()
    count, own, split = first_ref.shape
    near = unit_refs[0].shape[0]
    rest = weight_ref.shape[1] - split
    for p in range(count):
        at = pl.ds(pl.multiple_of(owner_a[p] * own, own), own)
        weight_ref[at, :split] = first_ref[p]
        at = pl.ds(pl.multiple_of(owner_b[p] * own, own), own)
        weight_ref[at, split:] = last_ref[p, :, :rest]
    copies = [pltpu.make_async_copy(weight_ref, weight_out_ref, sems.at[0])]
    copies[0].start()
    for k, ref in enumerate(unit_refs):
        normed = ref[...].astype(F32) * norm_ref[0:1, :] + norm_ref[1:2, :]
        found = matmul(normed.astype(BF16), weight_ref[...], NN) + bias_ref[...]
        qkv_ref[near * k : near * (k + 1), :] = found.astype(BF16)
    copies.append(pltpu.make_async_copy(qkv_ref, kept_ref, sems.at[1]))
    copies[1].start()
    attend_body(heads, blocks, qkv_ref, out_ref, log_ref, keep_ref)
    for k, ref in enumerate(quarter_refs):
        part = out_ref.at[near * k : near * (k + 1), :]
        copies.append(pltpu.make_async_copy(part, ref, sems.at[2 + k]))
        copies[-1].start()
    for copy in copies:
        copy.wait()


def in_hbm():
    return pl.BlockSpec(memory_space=pltpu.HBM)


def project_attend(unit, first, last, owner_a, owner_b, norm, bias, facts, heads):
    rows = sum(value.shape[0] for value in unit)
    features = unit[0].shape[1]
    width = heads * HEAD_DIM
    log_shape = jax.ShapeDtypeStruct((rows // BLOCK, width), F32)
    quarter = [jax.ShapeDtypeStruct((value.shape[0], width), BF16) for value in unit]
    qkv = jax.ShapeDtypeStruct((rows, 3 * width), BF16)
    weight = jax.ShapeDtypeStruct((features, 3 * width), BF16)
    found = pl.pallas_call(
        functools.partial(project_attend_kernel, heads, len(unit)),
        grid=(1,),
        out_shape=[*quarter, qkv, weight, log_shape],
        in_specs=[in_smem()] * 3 + [in_vmem()] * (len(unit) + 4),
        out_specs=[in_hbm()] * (len(unit) + 2)
        + [pl.BlockSpec(log_shape.shape, lambda i: (0, 0))],
        scratch_shapes=[
            pltpu.VMEM(qkv.shape, BF16),
            pltpu.VMEM(weight.shape, BF16),
            pltpu.VMEM((rows, width), BF16),
            pltpu.VMEM((2, rows, width), F32),
            pltpu.SMEM((rows // BLOCK,), jnp.int32),
            pltpu.SMEM((rows // BLOCK,), jnp.int32),
            pltpu.SemaphoreType.DMA((len(unit) + 2,)),
        ],
        compiler_params=pltpu.CompilerParams(vmem_limit_bytes=56 << 20),
        cost_estimate=pl.CostEstimate(
            flops=20 * rows * CHUNK * width,
            bytes_accessed=20 * rows * width,
            transcendentals=rows * CHUNK * width // HEAD_DIM,
        ),
        name="project_attend",
    )(owner_a, owner_b, facts, *unit, first, last, norm, bias)
    return found[: len(unit)], *found[len(unit) :]


def place_kernel(owner, blocks_ref, out_ref):
    count, own, _ = blocks_ref.shape
    width = out_ref.shape[1]
    for p in range(count):
        at = pl.ds(pl.multiple_of(owner[p] * own, own), own)
        out_ref[at, :] = blocks_ref[p, :, -width:]


def placed_rows(blocks, owner, width):
    out = jax.ShapeDtypeStruct((blocks.shape[0] * blocks.shape[1], width), blocks.dtype)
    return pl.pallas_call(
        place_kernel,
        grid=(1,),
        out_shape=out,
        in_specs=[in_smem(), in_vmem()],
        out_specs=pl.BlockSpec(out.shape, lambda i: (0, 0)),
        name="placed_rows",
    )(owner, blocks)


def attend_back_kernel(heads, parts, owner_a, owner_b, facts, *refs):
    qkv_ref, log_ref, weight_ref = refs[:3]
    part_refs, unit_refs = refs[3 : 3 + parts], refs[3 + parts : 3 + 2 * parts]
    outs = refs[3 + 2 * parts :]
    block_outs, row_outs, late_ref, sum_ref = outs[:4], outs[4 : 4 + parts], *outs[4 + parts :][:2]
    grads_ref, grad_ref, keys_acc, values_acc, probs_ref, inner_ref = outs[6 + parts :][:6]
    raw_ref, *block_refs, rows_ref, stored, limits, sems = outs[12 + parts :]
    blocks = Blocks(facts, stored, limits, heads, parts)
    blocks.find()
    half, own, split = block_refs[0].shape
    width = weight_ref.shape[1]
    near = unit_refs[0].shape[0]
    step = 2 * TILE
    for k, ref in enumerate(part_refs):
        grads_ref[near * k : near * (k + 1), :] = ref[...]
    attend_back_body(
        heads,
        blocks,
        qkv_ref,
        grads_ref,
        log_ref,
        grad_ref,
        keys_acc,
        values_acc,
        probs_ref,
        inner_ref,
    )
    copies = []

    def leave(source, target):
        copies.append(pltpu.make_async_copy(source, target, sems.at[len(copies)]))
        copies[-1].start()

    sums = jnp.sum(grad_ref[...].astype(F32), axis=0, keepdims=True)
    sum_ref[...] = sums
    for i in range(weight_ref.shape[0] // step):
        at = slice(step * i, step * (i + 1))
        raw = total(
            [
                matmul(ref[:, at], grad_ref[near * k : near * (k + 1), :], TN)
                for k, ref in enumerate(unit_refs)
            ]
        )
        weight = weight_ref[at, :].astype(F32)
        raw_ref[at, :] = raw.astype(BF16)
        for row, value in enumerate((raw * weight, weight * sums)):
            lanes = total([value[:, 128 * c : 128 * (c + 1)] for c in range(width // 128)])
            for b in range(step // 128):
                turned = lanes[128 * b : 128 * (b + 1)].T
                found = jnp.sum(turned, axis=0, keepdims=True)
                start = step * i + 128 * b
                late_ref[row : row + 1, start : start + 128] = found
    for p in range(2 * half):
        at = pl.ds(pl.multiple_of(owner_a[p] * own, own), own)
        block_refs[p // half][p % half] = raw_ref[at, :split]
        at = pl.ds(pl.multiple_of(owner_b[p] * own, own), own)
        block_refs[2 + p // half][p % half] = raw_ref[at, split:]
    for source, target in zip(block_refs, block_outs):
        leave(source, target)
    for k in range(parts - 1, -1, -1):
        at = slice(near * k, near * (k + 1))
        rows_ref[at, :] = matmul(grad_ref[at, :], weight_ref[...], NT).astype(BF16)
        leave(rows_ref.at[at, :], row_outs[k])
    for copy in copies:
        copy.wait()


def attend_back(
    qkv, grad_context, log_totals, unit, weight, owner_a, owner_b, split, facts, heads
):
    rows, width = qkv.shape[0], heads * HEAD_DIM
    features = weight.shape[0]
    count = owner_a.shape[0]
    own = features // count
    first = jax.ShapeDtypeStruct((count // 2, own, split), BF16)
    last = jax.ShapeDtypeStruct((count // 2, own, 3 * width - split), BF16)
    small = [
        jax.ShapeDtypeStruct((2, features), F32),
        jax.ShapeDtypeStruct((1, 3 * width), F32),
    ]
    blocks = [first, first, last, last]
    return pl.pallas_call(
        functools.partial(attend_back_kernel, heads, len(unit)),
        grid=(1,),
        out_shape=[*blocks, *[like(value) for value in unit], *small],
        in_specs=[in_smem()] * 3 + [in_vmem()] * (3 + 2 * len(unit)),
        out_specs=[in_hbm()] * (4 + len(unit))
        + [pl.BlockSpec(value.shape, lambda i: (0, 0)) for value in small],
        scratch_shapes=[
            pltpu.VMEM((rows, width), BF16),
            pltpu.VMEM(qkv.shape, BF16),
            pltpu.VMEM((rows, width), F32),
            pltpu.VMEM((rows, width), F32),
            pltpu.VMEM((2, rows, width), F32),
            pltpu.VMEM((2, rows, width), F32),
            pltpu.VMEM(weight.shape, BF16),
            *[pltpu.VMEM(value.shape, BF16) for value in blocks],
            pltpu.VMEM((rows, features), BF16),
            pltpu.SMEM((rows // BLOCK,), jnp.int32),
            pltpu.SMEM((rows // BLOCK,), jnp.int32),
            pltpu.SemaphoreType.DMA((4 + len(unit),)),
        ],
        compiler_params=pltpu.CompilerParams(vmem_limit_bytes=53 << 20),
        cost_estimate=pl.CostEstimate(
            flops=40 * rows * CHUNK * width,
            bytes_accessed=40 * rows * width,
            transcendentals=rows * CHUNK * width // HEAD_DIM,
        ),
        name="attend_back",
    )(
        owner_a,
        owner_b,
        facts,
        qkv,
        log_totals,
        weight,
        *grad_context,
        *unit,
    )


TILE = 256


def gelu_and_slope(pre):
    scale = (2.0 / 3.141592653589793) ** 0.5
    square = pre * pre
    bent = jnp.tanh(scale * pre * (1.0 + 0.044715 * square))
    half = 0.5 + 0.5 * bent
    slope = half + (0.5 * scale) * pre * (1.0 - bent * bent) * (1.0 + 0.134145 * square)
    return pre * half, slope


def pick(refs):
    per = pl.num_programs(0) // len(refs)
    value = refs[0][...]
    for k, ref in enumerate(refs[1:], 1):
        value = jnp.where(pl.program_id(0) >= k * per, ref[...], value)
    return value


def put(refs, value):
    per = pl.num_programs(0) // len(refs)
    for k, ref in enumerate(refs):
        ref[...] = jnp.where(pl.program_id(0) // per == k, value, ref[...])


def feed_kernel(quarters, taken, *refs):
    normed = pick(refs[:quarters])
    grads = pick(refs[quarters : 2 * quarters])
    weight_ref, bias_ref = refs[2 * quarters : 2 * quarters + 2]
    results = refs[2 * quarters + 2 + taken :]
    units = bias_ref.shape[1]
    up = weight_ref[:, :units]
    down = weight_ref[:, units:]
    active, slope = gelu_and_slope(matmul(normed, up, NN) + bias_ref[...])
    active = active.astype(BF16)
    grad_hidden = (matmul(grads, down, NN) * slope).astype(BF16)
    put(results[:quarters], matmul(grad_hidden, up, NT).astype(BF16))
    put(results[quarters : 2 * quarters], matmul(active, down, NT).astype(BF16))
    for ref, value in zip(results[2 * quarters :], (normed, grad_hidden, grads, active)):
        ref[...] = value


def tile_specs(arrays):
    def spec(k, value):
        tiles = value.shape[0] // TILE
        return pl.BlockSpec(
            (TILE, value.shape[1]), lambda i: (jnp.clip(i - k * tiles, 0, tiles - 1), 0)
        )

    return [spec(k, value) for k, value in enumerate(arrays)]


def feed(normed, grads, weights, bias, stacks, start, quarters):
    rows, features = normed[0].shape
    units = bias.shape[1]
    here = len(normed)
    tiles = rows // TILE
    stacked = [jax.ShapeDtypeStruct((rows * quarters, n), BF16) for n in (features, units) * 2]
    found = pl.pallas_call(
        functools.partial(feed_kernel, here, len(stacks)),
        grid=(here * tiles,),
        out_shape=[like(value) for value in normed] * 2 + stacked,
        in_specs=tile_specs(normed)
        + tile_specs(grads)
        + [in_vmem(), whole_spec(bias)]
        + [pl.BlockSpec(memory_space=pl.ANY)] * len(stacks),
        out_specs=tile_specs(normed) * 2
        + [
            pl.BlockSpec((TILE, value.shape[1]), lambda i: (i + start * tiles, 0))
            for value in stacked
        ],
        input_output_aliases={2 * here + 2 + n: 2 * here + n for n in range(len(stacks))},
        compiler_params=limit(56),
        cost_estimate=pl.CostEstimate(
            flops=8 * here * rows * features * units,
            bytes_accessed=16 * here * rows * features + 4 * features * units,
            transcendentals=here * rows * units,
        ),
        name="feed",
    )(*normed, *grads, weights, bias, *stacks)
    return found[:here], found[here : 2 * here], found[2 * here :]


def feed_grads_kernel(normed_ref, grad_ref, grads_ref, active_ref, out_ref, sum_ref, acc_ref):
    units = sum_ref.shape[1]
    grad_hidden = grad_ref[...]

    @pl.when(pl.program_id(0) == 0)
    def _():
        acc_ref[...] = jnp.zeros_like(acc_ref)
        sum_ref[...] = jnp.zeros_like(sum_ref)

    acc_ref[:, :units] += matmul(normed_ref[...], grad_hidden, TN)
    acc_ref[:, units:] += matmul(grads_ref[...], active_ref[...], TN)
    sum_ref[...] += jnp.sum(grad_hidden.astype(F32), axis=0, keepdims=True)

    @pl.when(pl.program_id(0) == pl.num_programs(0) - 1)
    def _():
        out_ref[...] = acc_ref[...].astype(BF16)


def feed_grads(stacks):
    rows, features = stacks[0].shape
    units = stacks[1].shape[1]
    sums = jax.ShapeDtypeStruct((features, 2 * units), BF16)
    hidden = jax.ShapeDtypeStruct((1, units), F32)
    return pl.pallas_call(
        feed_grads_kernel,
        grid=(rows // (2 * TILE),),
        out_shape=[sums, hidden],
        in_specs=[tiled_spec(value, 2 * TILE) for value in stacks],
        out_specs=[whole_spec(sums), whole_spec(hidden)],
        scratch_shapes=[pltpu.VMEM(sums.shape, F32)],
        compiler_params=limit(62),
        cost_estimate=cost(4 * rows * features * units, 8 * rows * features),
        name="feed_grads",
    )(*stacks)


def norm_parts(rows):
    centred = rows - jnp.mean(rows, axis=-1, keepdims=True)
    inverse = lax.rsqrt(jnp.mean(centred * centred, axis=-1, keepdims=True) + EPS)
    return centred * inverse, inverse


def norm_back(grad_normed, unit, inverse, gain):
    grad_unit = grad_normed * gain
    return inverse * (
        grad_unit
        - jnp.mean(grad_unit, axis=-1, keepdims=True)
        - unit * jnp.mean(grad_unit * unit, axis=-1, keepdims=True)
    )


def whole_spec(value):
    return pl.BlockSpec(value.shape, lambda i: (0,) * value.ndim)


def tiled_spec(value, tile=TILE):
    return pl.BlockSpec((tile, value.shape[1]), lambda i: (i, 0))


def like(value, dtype=None):
    return jax.ShapeDtypeStruct(value.shape, dtype or value.dtype)


def limit(mebibytes):
    return pltpu.CompilerParams(vmem_limit_bytes=mebibytes << 20)


def cost(flops, moved):
    return pl.CostEstimate(flops=flops, bytes_accessed=moved, transcendentals=0)


def unit_kernel(rows_ref, unit_ref):
    unit_ref[...] = norm_parts(rows_ref[...].astype(F32))[0].astype(BF16)


def unit_rows(rows):
    return pl.pallas_call(
        unit_kernel,
        grid=(rows.shape[0] // TILE,),
        out_shape=like(rows),
        in_specs=[tiled_spec(rows)],
        out_specs=tiled_spec(rows),
        compiler_params=limit(62),
        cost_estimate=cost(8 * rows.size, 4 * rows.size),
        name="unit",
    )(rows)


def middle_kernel(parts, *refs):
    context_refs, out_refs = refs[:parts], refs[parts : 2 * parts]
    rows_ref, vector_ref, middle_ref, normed_ref = refs[2 * parts :]
    middle = rows_ref[...].astype(F32) + vector_ref[0:1, :]
    for context_ref, out_ref in zip(context_refs, out_refs):
        middle += matmul(context_ref[...], out_ref[...], NT)
    middle_ref[...] = middle.astype(BF16)
    unit = norm_parts(middle)[0]
    normed_ref[...] = (unit * vector_ref[1:2, :] + vector_ref[2:3, :]).astype(BF16)


def middle_rows(context, out_parts, rows, vectors):
    return pl.pallas_call(
        functools.partial(middle_kernel, len(context)),
        grid=(rows.shape[0] // TILE,),
        out_shape=[like(rows), like(rows)],
        in_specs=[tiled_spec(value) for value in context]
        + [whole_spec(value) for value in out_parts]
        + [tiled_spec(rows), whole_spec(vectors)],
        out_specs=[tiled_spec(rows), tiled_spec(rows)],
        compiler_params=limit(62),
        cost_estimate=cost(2 * rows.size * rows.shape[1], 12 * rows.size),
        name="middle",
    )(*context, *out_parts, rows, vectors)


def middle_back_kernel(terms, parts, owner, *refs):
    term_refs, out_refs = refs[:terms], refs[terms : terms + parts]
    context_refs = refs[terms + parts : terms + 2 * parts]
    middle_ref, cotangent_ref, vector_ref, grad_ref, sum_ref = refs[
        terms + 2 * parts : terms + 2 * parts + 5
    ]
    head_refs = refs[terms + 2 * parts + 5 : terms + 3 * parts + 5]
    block_refs = refs[terms + 3 * parts + 5 : -1]
    found_ref = refs[-1]
    first = pl.program_id(0) == 0
    last = pl.program_id(0) == pl.num_programs(0) - 1
    count, own, width = block_refs[0].shape
    grad_normed = total([ref[...].astype(F32) for ref in term_refs])
    unit, inverse = norm_parts(middle_ref[...].astype(F32))
    cotangent = cotangent_ref[...].astype(F32)
    grad = cotangent + norm_back(grad_normed, unit, inverse, vector_ref[1:2, :])
    low = grad.astype(BF16)
    grad_ref[...] = low
    for head_ref, out_ref in zip(head_refs, out_refs):
        head_ref[...] = matmul(low, out_ref[...], NN).astype(BF16)
    sums = [
        jnp.sum(value, axis=0, keepdims=True)
        for value in (grad_normed * unit, grad_normed, grad, cotangent)
    ]
    sums = jnp.concatenate(sums, axis=0)

    @pl.when(first)
    def _():
        sum_ref[...] = jnp.zeros_like(sum_ref)
        found_ref[...] = jnp.zeros_like(found_ref)

    sum_ref[...] += sums
    for k, context_ref in enumerate(context_refs):
        found_ref[:, k * width : (k + 1) * width] += matmul(low, context_ref[...], TN)

    @pl.when(last)
    def _():
        for k, block_ref in enumerate(block_refs):
            for p in range(count):
                at = pl.ds(pl.multiple_of(owner[p] * own, own), own)
                block_ref[p] = found_ref[at, k * width : (k + 1) * width].astype(BF16)


def middle_back(terms, out_parts, context, middle, cotangent, vectors, owner):
    rows, features = middle.shape
    width = out_parts[0].shape[1]
    parts = len(out_parts)
    count = owner.shape[0]
    sums = jax.ShapeDtypeStruct((4, features), F32)
    head = jax.ShapeDtypeStruct((rows, width), BF16)
    blocks = jax.ShapeDtypeStruct((count, features // count, width), BF16)
    found = pl.pallas_call(
        functools.partial(middle_back_kernel, len(terms), parts),
        grid=(rows // TILE,),
        out_shape=[like(middle), sums] + [head] * parts + [blocks] * parts,
        in_specs=[in_smem()]
        + [tiled_spec(value) for value in terms]
        + [whole_spec(value) for value in out_parts]
        + [tiled_spec(value) for value in context]
        + [tiled_spec(middle), tiled_spec(cotangent), whole_spec(vectors)],
        out_specs=[tiled_spec(middle), whole_spec(sums)]
        + [tiled_spec(head)] * parts
        + [whole_spec(blocks)] * parts,
        scratch_shapes=[pltpu.VMEM((features, width * parts), F32)],
        compiler_params=limit(62),
        cost_estimate=cost(4 * middle.size * features, 20 * middle.size),
        name="middle_back",
    )(owner, *terms, *out_parts, *context, middle, cotangent, vectors)
    return found[0], found[1], found[2 : 2 + parts], found[2 + parts :]


def input_back_kernel(terms, *refs):
    *term_refs, first_ref, last_ref = refs[:terms]
    rows_ref, middle_ref, vector_ref, out_ref = refs[terms:]
    half = jnp.where(pl.program_id(0) == 0, first_ref[...], last_ref[...])
    grad_normed = total([ref[...].astype(F32) for ref in term_refs]) + half.astype(F32)
    unit, inverse = norm_parts(rows_ref[...].astype(F32))
    grad = norm_back(grad_normed, unit, inverse, vector_ref[0:1, :])
    out_ref[...] = (middle_ref[...].astype(F32) + grad).astype(BF16)


def input_back(terms, rows, grad_middle, vectors):
    tile = rows.shape[0] // 2
    return pl.pallas_call(
        functools.partial(input_back_kernel, len(terms)),
        grid=(2,),
        out_shape=like(rows),
        in_specs=[tiled_spec(value, tile) for value in terms[:-2]]
        + [whole_spec(value) for value in terms[-2:]]
        + [tiled_spec(rows, tile), tiled_spec(grad_middle, tile), whole_spec(vectors)],
        out_specs=tiled_spec(rows, tile),
        compiler_params=limit(62),
        cost_estimate=cost(20 * rows.size, 14 * rows.size),
        name="input_back",
    )(*terms, rows, grad_middle, vectors)


def per_device(
    tokens,
    output_cotangent,
    lengths,
    block_place,
    random_blocks,
    qkv_weight,
    out_weight,
    up_weight,
    down_weight,
    vectors,
    hidden_bias,
):
    ways = lax.axis_size("tensor")
    spread_ways = lax.axis_size("dp")
    position = lax.axis_index("tensor")
    index = lax.axis_index("dp") * ways + position
    near = tokens.shape[0]
    rows = near * ways
    features = tokens.shape[1]
    width = qkv_weight.shape[2]
    heads = width // HEAD_DIM
    units = up_weight.shape[1]
    own = features // spread_ways
    piece = vectors.shape[1]
    unit_piece = hidden_bias.shape[1]

    small = jnp.zeros((8, features), F32)
    small = lax.dynamic_update_slice(small, vectors, (0, index * piece))
    small_hidden = jnp.zeros((1, units * ways), F32)
    small_hidden = lax.dynamic_update_slice(small_hidden, hidden_bias, (0, index * unit_piece))
    packed = jnp.concatenate([small.reshape(-1), small_hidden.reshape(-1)])
    packed = summed_everywhere(packed, ("tensor",))

    unit_near = unit_rows(tokens)
    unit_near, packed = together(unit_near, packed)
    unit_far = far(unit_near, "tensor")

    facts = attention_facts(lengths[0], position, block_place, random_blocks)

    bits = bits_of("dp")
    order_a = bits[::-1]
    order_b = bits[:1] + bits[:0:-1]
    owner_a = block_owners("dp", order_a)
    owner_b = block_owners("dp", order_b)
    split = 2 * width
    qkv_flat = qkv_weight.reshape(own, 3 * width)
    first_blocks = doubled(qkv_flat[:, :split], "dp", order_a)
    last_flat = jnp.concatenate([qkv_flat[:, split:], out_weight], axis=1)
    last_blocks = doubled(last_flat, "dp", order_b)
    packed = summed_everywhere(packed, ("dp",))
    feed_flat = jnp.concatenate([up_weight, down_weight], axis=1)
    first_going, last_going = output_cotangent[: near // 2], output_cotangent[near // 2 :]
    first_going, unit_far = together(first_going, unit_far)
    cotangent_first = far(first_going, "tensor")
    feed_flat, first_blocks, last_blocks, cotangent_first, packed = together(
        feed_flat, first_blocks, last_blocks, cotangent_first, packed
    )
    feed_full = lax.all_gather(feed_flat, "dp", axis=0, tiled=True)
    unit_parts = gathered_parts(unit_near, unit_far, "tensor")

    vectors_full = packed[: 8 * features].reshape(8, features)
    hidden_full = packed[8 * features :]
    bias_query = lax.dynamic_slice_in_dim(vectors_full[6], position * width, width)
    bias_value = lax.dynamic_slice_in_dim(vectors_full[7], position * width, width)
    bias_qkv = jnp.concatenate([bias_query, jnp.zeros_like(bias_query), bias_value])[None]
    bias_hidden = lax.dynamic_slice_in_dim(hidden_full, position * units, units)[None]
    norm_one = vectors_full[:2]
    norm_two = jnp.stack([vectors_full[4], vectors_full[2], vectors_full[3]])


    out_group = placed_rows(last_blocks, owner_b, width)
    out_far = far(out_group, "tensor")
    last_going, out_group = together(last_going, out_group)
    cotangent_last = far(last_going, "tensor")
    *context, qkv, qkv_full, log_totals = project_attend(
        unit_parts,
        first_blocks,
        last_blocks,
        owner_a,
        owner_b,
        norm_one,
        bias_qkv,
        facts,
        heads,
    )
    context = context[0]
    *context, out_far, cotangent_last = together(*context, out_far, cotangent_last)
    cotangent_far = jnp.concatenate([cotangent_first, cotangent_last], axis=0)
    grad_parts = gathered_parts(output_cotangent, cotangent_far, "tensor")

    out_parts = gathered_parts(out_group, out_far, "tensor")
    context_near = exchanged_parts(context, "tensor")
    middle, normed_two = middle_rows(context_near, out_parts, tokens, norm_two)

    half = ways // 2
    normed_far = far(normed_two, "tensor")
    normed_parts = gathered_parts(normed_two, normed_far, "tensor")
    near_back, near_out, stacks = feed(
        normed_parts[:half], grad_parts[:half], feed_full, bias_hidden, (), 0, ways
    )
    normed_far, *stacks = together(normed_far, *stacks)
    normed_parts = gathered_parts(normed_two, normed_far, "tensor")
    far_back, far_out, stacks = feed(
        normed_parts[half:], grad_parts[half:], feed_full, bias_hidden, stacks, half, ways
    )
    back_parts, feed_parts = near_back + far_back, near_out + far_out
    back_terms, far_sum = summed_halves(back_parts, "tensor")
    back_terms.append(far(far_sum, "tensor"))
    feed_sums, sum_hidden = feed_grads(stacks)
    feed_terms, feed_far = summed_halves(feed_parts, "tensor")
    early, late_rows = feed_far[: near // 2], feed_far[near // 2 :]
    feed_weight_grads = lax.psum_scatter(feed_sums, "dp", scatter_dimension=0, tiled=True)
    feed_weight_grads = feed_weight_grads.astype(F32)
    *back_terms, sum_hidden, early = together(*back_terms, sum_hidden, early)
    early = far(early, "tensor")

    grad_middle, sums_two, grad_heads, out_blocks = middle_back(
        back_terms, out_parts, context_near, middle, output_cotangent, norm_two, owner_b
    )
    grad_context = exchanged_parts(grad_heads, "tensor")

    *out_blocks, early = together(*out_blocks, early)
    out_terms, out_far = summed_halves(out_blocks, "tensor")
    *grad_context, out_far, late_rows = together(*grad_context, out_far, late_rows)
    out_terms.append(far(out_far, "tensor"))
    late_rows = far(late_rows, "tensor")
    first_keep, first_send, last_keep, last_send, *back_parts, late, sum_qkv = attend_back(
        qkv,
        grad_context,
        log_totals,
        unit_parts,
        qkv_full,
        owner_a,
        owner_b,
        split,
        facts,
        heads,
    )
    first_send, last_send, late, late_rows, *rest = together(
        first_send, last_send, late, late_rows, *out_terms, *back_parts
    )
    out_terms, back_parts = rest[: len(out_terms)], rest[len(out_terms) :]
    near_rows, far_rows = back_parts[:half], back_parts[half:]
    feed_terms.append(jnp.concatenate([early, late_rows], axis=0))
    output = total([term.astype(F32) for term in (*feed_terms, middle)]) + vectors_full[5]
    output = output.astype(BF16)
    out_sums = total([term.astype(F32) for term in out_terms]).astype(BF16)
    last_keep = jnp.concatenate([last_keep, out_sums[: spread_ways // 2]], axis=2)
    last_send = jnp.concatenate([last_send, out_sums[spread_ways // 2 :]], axis=2)
    head_sums = lax.dynamic_update_slice(
        jnp.zeros((3, features), F32), sum_qkv.reshape(3, width), (0, position * width)
    )
    hidden_sums = lax.dynamic_update_slice(
        jnp.zeros((1, units * ways), F32), sum_hidden, (0, position * units)
    )
    packed = jnp.concatenate(
        [late.reshape(-1), sums_two.reshape(-1), head_sums.reshape(-1), hidden_sums.reshape(-1)]
    )
    packed = summed_everywhere(packed, ("tensor",))
    far_sum = added(far_rows[0], swapped(far_rows[1], "tensor", 1))
    far_sum, first_keep, last_keep, *near_rows = together(
        far_sum, first_keep, last_keep, *near_rows
    )
    far_first = far(far_sum[: near // 2], "tensor")
    far_last = far(far_sum[near // 2 :], "tensor")
    first_keep, first_send = halved(first_keep, first_send, "dp", order_a)
    last_keep, last_send = halved(last_keep, last_send, "dp", order_b)
    first_send, last_send, far_first = together(first_send, last_send, far_first)
    while first_send.shape[0] > 1:
        first_keep, first_send = halved(first_keep, first_send, "dp", order_a)
        last_keep, last_send = halved(last_keep, last_send, "dp", order_b)
    first_send, last_send, far_last, output = together(first_send, last_send, far_last, output)
    near_terms = [near_rows[0], swapped(near_rows[1], "tensor", 1), far_first, far_last]
    input_grad = input_back(near_terms, tokens, grad_middle, norm_one)
    first_keep, last_keep, input_grad, packed = together(
        first_keep, last_keep, input_grad, packed
    )
    first_raw = halved(first_keep, first_send, "dp", order_a)[0][0].astype(F32)
    last_raw = halved(last_keep, last_send, "dp", order_b)[0][0].astype(F32)
    out_weight_grad = last_raw[:, width:]
    last_raw = last_raw[:, :width]

    packed = summed_everywhere(packed, ("dp",))
    by_feature = packed[: 9 * features].reshape(9, features)
    hidden_sums = packed[9 * features :]
    vectors_grad = lax.dynamic_slice_in_dim(by_feature, index * piece, piece, axis=1)
    vectors_grad = jnp.concatenate([vectors_grad[:7], vectors_grad[8:]], axis=0)
    hidden_bias_grad = lax.dynamic_slice_in_dim(hidden_sums, index * unit_piece, unit_piece)

    sum_qkv = lax.dynamic_slice_in_dim(by_feature[6:], position * width, width, axis=1)
    mine = lax.dynamic_slice_in_dim(norm_one, lax.axis_index("dp") * own, own, axis=1)
    raw = jnp.concatenate([first_raw, last_raw], axis=1).reshape(own, 3, width)
    qkv_weight_grad = mine[0][:, None, None] * raw + mine[1][:, None, None] * sum_qkv
    return (
        output,
        input_grad,
        qkv_weight_grad,
        out_weight_grad,
        feed_weight_grads[:, :units],
        feed_weight_grads[:, units:],
        vectors_grad,
        hidden_bias_grad[None, :],
    )


def solution(mesh):
    placed = (
        P(("dp", "tensor"), None),
        P(("dp", "tensor"), None),
        P("dp"),
        P("dp", None),
        P("dp", "tensor", None, None),
        P("dp", None, "tensor"),
        P("dp", "tensor"),
        P("dp", "tensor"),
        P("dp", "tensor"),
        P(None, ("dp", "tensor")),
        P(None, ("dp", "tensor")),
    )
    return jax.shard_map(
        per_device,
        mesh=mesh,
        in_specs=placed,
        out_specs=(
            P(("dp", "tensor"), None),
            P(("dp", "tensor"), None),
            P("dp", None, "tensor"),
            P("dp", "tensor"),
            P("dp", "tensor"),
            P("dp", "tensor"),
            P(None, ("dp", "tensor")),
            P(None, ("dp", "tensor")),
        ),
        check_vma=False,
    )
```

```python
import functools

import jax
import jax.numpy as jnp
from jax import lax
from jax.experimental import pallas as pl
from jax.experimental.pallas import tpu as pltpu
from jax.sharding import PartitionSpec as P

HEAD_DIM = 64
BLOCK = 64
PAIR = 2 * HEAD_DIM
SLOTS = 8
CHUNK = 512
EPS = 1e-05
NEGATIVE = -1e30
F32 = jnp.float32
BF16 = jnp.bfloat16
NT = (((1,), (1,)), ((), ()))
NN = (((1,), (0,)), ((), ()))
TN = (((0,), (0,)), ((), ()))


def matmul(left, right, dims):
    return lax.dot_general(left, right, dims, preferred_element_type=F32)


def swapped(value, axis, bit):
    count = lax.axis_size(axis)
    return lax.ppermute(value, axis, [(i, i ^ bit) for i in range(count)])


def bits_of(axis):
    count = lax.axis_size(axis)
    return [1 << b for b in range(count.bit_length() - 1)]


def together(*values):
    return lax.optimization_barrier(values)


def far(value, axis):
    return swapped(value, axis, bits_of(axis)[-1])


def gathered_parts(value, far_value, axis):
    bits = bits_of(axis)
    parts = {0: value, bits[-1]: far_value}
    for bit in reversed(bits[:-1]):
        parts.update({k | bit: swapped(p, axis, bit) for k, p in list(parts.items())})
    return [parts[k] for k in range(len(parts))]


def summed_halves(parts, axis):
    left = dict(enumerate(parts))
    terms = [parts[0]]
    for bit in bits_of(axis)[: len(parts).bit_length() - 2]:
        kept = {}
        for k in sorted(left, reverse=True):
            if k & bit == 0:
                arrived = swapped(left[k | bit], axis, bit)
                if k == 0:
                    terms.append(arrived)
                    kept[k] = None
                else:
                    kept[k] = added(left[k], arrived)
        left = kept
    return terms, left[len(parts) // 2]


def added(left, right):
    return (left.astype(F32) + right.astype(F32)).astype(BF16)


def doubled(value, axis, order):
    blocks = value[None]
    for bit in order:
        blocks = jnp.concatenate([blocks, swapped(blocks, axis, bit)], axis=0)
    return blocks


def halved(keep, send, axis, order):
    half = send.shape[0]
    arrived = swapped(send, axis, order[half.bit_length() - 1])
    rest = half // 2
    return added(keep[: half - rest], arrived[: half - rest]), added(
        keep[half - rest :], arrived[half - rest :]
    )


def block_owners(axis, order):
    count = lax.axis_size(axis)
    device = [sum(bit for b, bit in enumerate(order) if p >> b & 1) for p in range(count)]
    return lax.axis_index(axis) ^ jnp.asarray(device, jnp.int32)


def exchanged_parts(parts, axis):
    return [p if k == 0 else swapped(p, axis, k) for k, p in enumerate(parts)]


def summed_everywhere(value, axes, direct=False):
    size = value.shape[0]
    value = jnp.pad(value, (0, -size % 1024)).reshape(-1, 128)
    for axis in axes:
        if direct:
            value = total([value] + [swapped(value, axis, k) for k in range(1, lax.axis_size(axis))])
        else:
            for bit in bits_of(axis):
                value = value + swapped(value, axis, bit)
    return value.reshape(-1)[:size]


def sent_and_summed(value, axis):
    count = lax.axis_size(axis)
    blocks = value.reshape(count, value.shape[0] // count, *value.shape[1:])
    arrived = lax.all_to_all(blocks, axis, 0, 0, tiled=True)
    return jnp.sum(arrived.astype(F32), axis=0)


def attention_facts(length, position, placing, chosen):
    head = jnp.stack([length, position]).astype(jnp.int32)
    return jnp.concatenate([head, placing.reshape(-1), chosen.reshape(-1)])


class Blocks:
    def __init__(self, facts, stored, limits, heads, quarters):
        self.facts, self.stored, self.limits = facts, stored, limits
        self.heads, self.quarters = heads, quarters
        self.count = stored.shape[0]
        self.length = facts[0]
        self.last = (self.length + BLOCK - 1) // BLOCK - 1
        self.last_rows = self.length - BLOCK * self.last

    def find(self):
        per = self.count // self.quarters
        for quarter in range(self.quarters):
            start = (self.facts[1] ^ quarter) * per
            for n in range(per):
                number = self.facts[2 + start + n]
                self.stored[number] = quarter * per + n
                rows = self.length - BLOCK * number
                self.limits[quarter * per + n] = jnp.clip(rows, 0, BLOCK)

    def item(self, number):
        last = self.last
        alive = number != last
        before, behind = number - 1, number + 1
        common = [0, last, before, number, jnp.minimum(behind, self.count - 1)]
        good = [
            alive,
            alive,
            alive & (before > 0) & (before < last),
            alive & (number < last),
            alive & (behind < last),
        ]
        places = [self.stored[block] for block in common]
        lane = lax.broadcasted_iota(jnp.int32, (1, self.heads * HEAD_DIM), 1)
        added_scores = [jnp.where(flag, 0.0, NEGATIVE).astype(F32) for flag in good]
        drawn = [
            [
                self.facts[2 + self.count + (h * self.count + number) * 3 + s]
                for h in range(self.heads)
            ]
            for s in range(3)
        ]
        random = []
        for s in range(3):
            random.append([self.stored[block] for block in drawn[s]])
            row = jnp.zeros((1, self.heads * HEAD_DIM), F32)
            for h, block in enumerate(drawn[s]):
                fresh = alive & (block > 0) & (block < last) & (jnp.abs(block - number) > 1)
                for other in range(s):
                    fresh = fresh & (block != drawn[other][h])
                score = jnp.where(fresh, 0.0, NEGATIVE).astype(F32)
                row = jnp.where(lane // HEAD_DIM == h, score, row)
            added_scores.append(row)
        return places, random, added_scores


def block_rows(index):
    return pl.ds(pl.multiple_of(index * BLOCK, BLOCK), BLOCK)


def spread(rows, heads):
    lane = lax.broadcasted_iota(jnp.int32, (1, heads * HEAD_DIM), 1)
    zero = jnp.zeros_like(rows)
    return jnp.concatenate(
        [jnp.where(lane // HEAD_DIM == h, rows, zero) for h in range(heads)], axis=0
    )


def collapse(full, heads):
    lane = lax.broadcasted_iota(jnp.int32, (1, PAIR), 1)
    pieces = []
    for pair in range(heads // 2):
        cols = slice(PAIR * pair, PAIR * (pair + 1))
        even = full[2 * pair * HEAD_DIM : (2 * pair + 1) * HEAD_DIM, cols]
        odd = full[(2 * pair + 1) * HEAD_DIM : (2 * pair + 2) * HEAD_DIM, cols]
        pieces.append(jnp.where(lane < HEAD_DIM, even, odd))
    return jnp.concatenate(pieces, axis=1)


def gathered_keys(ref, start, places, random, heads):
    width = heads * HEAD_DIM
    lane = lax.broadcasted_iota(jnp.int32, (1, PAIR), 1)
    parts = [ref[block_rows(place), start : start + width] for place in places]
    for drawn in random:
        pieces = []
        for pair in range(heads // 2):
            cols = slice(start + PAIR * pair, start + PAIR * (pair + 1))
            even = ref[block_rows(drawn[2 * pair]), cols]
            odd = ref[block_rows(drawn[2 * pair + 1]), cols]
            pieces.append(jnp.where(lane < HEAD_DIM, even, odd))
        parts.append(jnp.concatenate(pieces, axis=1))
    return jnp.concatenate(parts, axis=0)


def slot(value, index):
    return value[BLOCK * index : BLOCK * (index + 1)]


def biased(scores, bias, last_rows):
    row = lax.broadcasted_iota(jnp.int32, (BLOCK, 1), 0)
    parts = [slot(scores, s) + bias[s] for s in range(SLOTS)]
    parts[1] = jnp.where(row < last_rows, parts[1], NEGATIVE)
    return parts


def total(parts):
    return functools.reduce(jnp.add, parts)


def attend_body(heads, blocks, qkv_ref, out_ref, log_ref, keep_ref):
    count = blocks.count
    stored, limits = blocks.stored, blocks.limits
    width = heads * HEAD_DIM
    scale = jnp.asarray(HEAD_DIM**-0.5, BF16)

    def item(number):
        places, random, scores = blocks.item(number)
        here = block_rows(places[3])
        queries = spread(qkv_ref[here, :width] * scale, heads)
        keys = gathered_keys(qkv_ref, width, places, random, heads)
        parts = biased(matmul(keys, queries, NT), scores, blocks.last_rows)
        top = jnp.max(functools.reduce(jnp.maximum, parts), axis=0, keepdims=True)
        weights = [jnp.exp(p - top) for p in parts]
        row_total = jnp.sum(total(weights), axis=0, keepdims=True)
        inverse = 1.0 / row_total
        probs = jnp.concatenate([(p * inverse).astype(BF16) for p in weights], axis=0)
        values = gathered_keys(qkv_ref, 2 * width, places, random, heads)
        out_ref[here, :] = collapse(matmul(probs, values, TN), heads).astype(BF16)
        log_ref[pl.ds(number, 1), :] = top + jnp.log(row_total)

    def step(group, carry):
        for part in range(10):
            item(1 + group * 10 + part)
        return carry

    lax.fori_loop(0, (count - 1) // 10, step, 0)
    for number in range(1 + (count - 1) // 10 * 10, count):
        item(number)

    row = lax.broadcasted_iota(jnp.int32, (BLOCK, 1), 0)
    per = CHUNK // BLOCK
    chunks = count // per

    def chunk_rows(chunk):
        return pl.ds(pl.multiple_of(chunk * CHUNK, CHUNK), CHUNK)

    numbers = [0, blocks.last]
    rows_of = [block_rows(stored[number]) for number in numbers]
    queries = [spread(qkv_ref[at, :width] * scale, heads) for at in rows_of]

    def scores(chunk, tops):
        at = chunk_rows(chunk)
        keys = qkv_ref[at, width : 2 * width]
        found = []
        for end in range(2):
            raw = matmul(keys, queries[end], NT)
            parts = [
                jnp.where(row < limits[chunk * per + s], slot(raw, s), NEGATIVE)
                for s in range(per)
            ]
            keep_ref[end, at, :] = jnp.concatenate(parts, axis=0)
            found.append(jnp.maximum(tops[end], functools.reduce(jnp.maximum, parts)))
        return tuple(found)

    tops = lax.fori_loop(0, chunks, scores, (jnp.full((BLOCK, width), NEGATIVE, F32),) * 2)
    tops = [jnp.max(top, axis=0, keepdims=True) for top in tops]

    def exponents(chunk, totals):
        at = chunk_rows(chunk)
        found = []
        for end in range(2):
            weights = jnp.exp(keep_ref[end, at, :] - tops[end])
            keep_ref[end, at, :] = weights
            found.append(totals[end] + total([slot(weights, s) for s in range(per)]))
        return tuple(found)

    totals = lax.fori_loop(0, chunks, exponents, (jnp.zeros((BLOCK, width), F32),) * 2)
    totals = [jnp.sum(found, axis=0, keepdims=True) for found in totals]
    inverses = [1.0 / found for found in totals]

    def contexts(chunk, sums):
        at = chunk_rows(chunk)
        values = qkv_ref[at, 2 * width :]
        return tuple(
            sums[end] + matmul((keep_ref[end, at, :] * inverses[end]).astype(BF16), values, TN)
            for end in range(2)
        )

    sums = lax.fori_loop(0, chunks, contexts, (jnp.zeros((width, width), F32),) * 2)
    for end in range(2):
        out_ref[rows_of[end], :] = collapse(sums[end], heads).astype(BF16)
        log_ref[pl.ds(numbers[end], 1), :] = tops[end] + jnp.log(totals[end])


def attend_back_body(
    heads,
    blocks,
    qkv_ref,
    grad_ref,
    log_ref,
    out_ref,
    keys_acc,
    values_acc,
    probs_ref,
    inner_ref,
):
    count = blocks.count
    stored, limits = blocks.stored, blocks.limits
    width = heads * HEAD_DIM
    scale = jnp.asarray(HEAD_DIM**-0.5, BF16)
    lane = lax.broadcasted_iota(jnp.int32, (1, PAIR), 1)
    keys_acc[...] = jnp.zeros_like(keys_acc)
    values_acc[...] = jnp.zeros_like(values_acc)

    def accumulate(acc, value, places, random):
        for s in range(5):
            acc[block_rows(places[s]), :] += slot(value, s)
        for s in range(3):
            for h in range(heads):
                cols = slice(PAIR * (h // 2), PAIR * (h // 2 + 1))
                mine = (lane < HEAD_DIM) == (h % 2 == 0)
                term = jnp.where(mine, slot(value, 5 + s)[:, cols], 0.0)
                acc[block_rows(random[s][h]), cols] += term

    def item(number):
        places, random, scores = blocks.item(number)
        here = block_rows(places[3])
        queries = spread(qkv_ref[here, :width] * scale, heads)
        grads = spread(grad_ref[here, :], heads)
        keys = gathered_keys(qkv_ref, width, places, random, heads)
        values = gathered_keys(qkv_ref, 2 * width, places, random, heads)
        log_total = log_ref[pl.ds(number, 1), :]
        parts = biased(matmul(keys, queries, NT), scores, blocks.last_rows)
        probs = [jnp.exp(p - log_total) for p in parts]
        found = matmul(values, grads, NT)
        found = [slot(found, s) for s in range(SLOTS)]
        inner = total([p * d for p, d in zip(probs, found)])
        inner = jnp.sum(inner, axis=0, keepdims=True)
        grad_scores = jnp.concatenate(
            [(p * (d - inner)).astype(BF16) for p, d in zip(probs, found)], axis=0
        )
        probs_low = jnp.concatenate([p.astype(BF16) for p in probs], axis=0)
        accumulate(values_acc, matmul(probs_low, grads, NN), places, random)
        accumulate(keys_acc, matmul(grad_scores, queries, NN), places, random)
        grad_queries = collapse(matmul(grad_scores, keys, TN), heads) * HEAD_DIM**-0.5
        out_ref[here, :width] = grad_queries.astype(BF16)

    def step(group, carry):
        for part in range(6):
            item(1 + group * 6 + part)
        return carry

    lax.fori_loop(0, (count - 1) // 6, step, 0)
    for number in range(1 + (count - 1) // 6 * 6, count):
        item(number)

    row = lax.broadcasted_iota(jnp.int32, (BLOCK, 1), 0)
    per = CHUNK // BLOCK
    chunks = count // per

    def chunk_rows(chunk):
        return pl.ds(pl.multiple_of(chunk * CHUNK, CHUNK), CHUNK)

    numbers = [0, blocks.last]
    rows_of = [block_rows(stored[number]) for number in numbers]
    queries = [spread(qkv_ref[at, :width] * scale, heads) for at in rows_of]
    grads = [spread(grad_ref[at, :], heads) for at in rows_of]
    log_rows = [log_ref[pl.ds(number, 1), :] for number in numbers]

    def first(chunk, inners):
        at = chunk_rows(chunk)
        keys = qkv_ref[at, width : 2 * width]
        values = qkv_ref[at, 2 * width :]
        sums = []
        for end in range(2):
            scores = matmul(keys, queries[end], NT)
            parts = [
                jnp.where(row < limits[chunk * per + s], slot(scores, s), NEGATIVE)
                for s in range(per)
            ]
            probs = jnp.exp(jnp.concatenate(parts, axis=0) - log_rows[end])
            found = matmul(values, grads[end], NT)
            probs_ref[end, at, :] = probs
            inner_ref[end, at, :] = found
            both = probs * found
            sums.append(inners[end] + total([slot(both, s) for s in range(per)]))
        return tuple(sums)

    inners = lax.fori_loop(0, chunks, first, (jnp.zeros((BLOCK, width), F32),) * 2)
    inners = [jnp.sum(inner, axis=0, keepdims=True) for inner in inners]

    def second(chunk, sums):
        at = chunk_rows(chunk)
        keys = qkv_ref[at, width : 2 * width]
        found, to_values, to_keys = [], values_acc[at, :], keys_acc[at, :]
        for end in range(2):
            probs = probs_ref[end, at, :]
            grad_scores = (probs * (inner_ref[end, at, :] - inners[end])).astype(BF16)
            to_values = to_values + matmul(probs.astype(BF16), grads[end], NN)
            to_keys = to_keys + matmul(grad_scores, queries[end], NN)
            found.append(sums[end] + matmul(grad_scores, keys, TN))
        out_ref[at, width : 2 * width] = to_keys.astype(BF16)
        out_ref[at, 2 * width :] = to_values.astype(BF16)
        return tuple(found)

    sums = lax.fori_loop(0, chunks, second, (jnp.zeros((width, width), F32),) * 2)
    for end in range(2):
        grad_queries = collapse(sums[end], heads) * HEAD_DIM**-0.5
        out_ref[rows_of[end], :width] = grad_queries.astype(BF16)


def in_smem():
    return pl.BlockSpec(memory_space=pltpu.SMEM)


def in_vmem():
    return pl.BlockSpec(memory_space=pltpu.VMEM)


def project_attend_kernel(heads, parts, owner_a, owner_b, facts, *refs):
    unit_refs = refs[:parts]
    first_ref, last_ref, norm_ref, bias_ref = refs[parts : parts + 4]
    *quarter_refs, kept_ref, weight_out_ref, log_ref = refs[parts + 4 : 2 * parts + 7]
    qkv_ref, weight_ref, out_ref, keep_ref, stored, limits, sems = refs[2 * parts + 7 :]
    blocks = Blocks(facts, stored, limits, heads, parts)
    blocks.find()
    count, own, split = first_ref.shape
    near = unit_refs[0].shape[0]
    rest = weight_ref.shape[1] - split
    for p in range(count):
        at = pl.ds(pl.multiple_of(owner_a[p] * own, own), own)
        weight_ref[at, :split] = first_ref[p]
        at = pl.ds(pl.multiple_of(owner_b[p] * own, own), own)
        weight_ref[at, split:] = last_ref[p, :, :rest]
    copies = [pltpu.make_async_copy(weight_ref, weight_out_ref, sems.at[0])]
    copies[0].start()
    for k, ref in enumerate(unit_refs):
        normed = ref[...].astype(F32) * norm_ref[0:1, :] + norm_ref[1:2, :]
        found = matmul(normed.astype(BF16), weight_ref[...], NN) + bias_ref[...]
        qkv_ref[near * k : near * (k + 1), :] = found.astype(BF16)
    copies.append(pltpu.make_async_copy(qkv_ref, kept_ref, sems.at[1]))
    copies[1].start()
    attend_body(heads, blocks, qkv_ref, out_ref, log_ref, keep_ref)
    for k, ref in enumerate(quarter_refs):
        part = out_ref.at[near * k : near * (k + 1), :]
        copies.append(pltpu.make_async_copy(part, ref, sems.at[2 + k]))
        copies[-1].start()
    for copy in copies:
        copy.wait()


def in_hbm():
    return pl.BlockSpec(memory_space=pltpu.HBM)


def project_attend(unit, first, last, owner_a, owner_b, norm, bias, facts, heads):
    rows = sum(value.shape[0] for value in unit)
    features = unit[0].shape[1]
    width = heads * HEAD_DIM
    log_shape = jax.ShapeDtypeStruct((rows // BLOCK, width), F32)
    quarter = [jax.ShapeDtypeStruct((value.shape[0], width), BF16) for value in unit]
    qkv = jax.ShapeDtypeStruct((rows, 3 * width), BF16)
    weight = jax.ShapeDtypeStruct((features, 3 * width), BF16)
    found = pl.pallas_call(
        functools.partial(project_attend_kernel, heads, len(unit)),
        grid=(1,),
        out_shape=[*quarter, qkv, weight, log_shape],
        in_specs=[in_smem()] * 3 + [in_vmem()] * (len(unit) + 4),
        out_specs=[in_hbm()] * (len(unit) + 2)
        + [pl.BlockSpec(log_shape.shape, lambda i: (0, 0))],
        scratch_shapes=[
            pltpu.VMEM(qkv.shape, BF16),
            pltpu.VMEM(weight.shape, BF16),
            pltpu.VMEM((rows, width), BF16),
            pltpu.VMEM((2, rows, width), F32),
            pltpu.SMEM((rows // BLOCK,), jnp.int32),
            pltpu.SMEM((rows // BLOCK,), jnp.int32),
            pltpu.SemaphoreType.DMA((len(unit) + 2,)),
        ],
        compiler_params=pltpu.CompilerParams(vmem_limit_bytes=56 << 20),
        cost_estimate=pl.CostEstimate(
            flops=20 * rows * CHUNK * width,
            bytes_accessed=20 * rows * width,
            transcendentals=rows * CHUNK * width // HEAD_DIM,
        ),
        name="project_attend",
    )(owner_a, owner_b, facts, *unit, first, last, norm, bias)
    return found[: len(unit)], *found[len(unit) :]


def place_kernel(owner, blocks_ref, out_ref):
    count, own, _ = blocks_ref.shape
    width = out_ref.shape[1]
    for p in range(count):
        at = pl.ds(pl.multiple_of(owner[p] * own, own), own)
        out_ref[at, :] = blocks_ref[p, :, -width:]


def placed_rows(blocks, owner, width):
    out = jax.ShapeDtypeStruct((blocks.shape[0] * blocks.shape[1], width), blocks.dtype)
    return pl.pallas_call(
        place_kernel,
        grid=(1,),
        out_shape=out,
        in_specs=[in_smem(), in_vmem()],
        out_specs=pl.BlockSpec(out.shape, lambda i: (0, 0)),
        name="placed_rows",
    )(owner, blocks)


def attend_back_kernel(heads, parts, owner_a, owner_b, facts, *refs):
    qkv_ref, log_ref, weight_ref = refs[:3]
    part_refs, unit_refs = refs[3 : 3 + parts], refs[3 + parts : 3 + 2 * parts]
    outs = refs[3 + 2 * parts :]
    block_outs, row_outs, late_ref, sum_ref = outs[:4], outs[4 : 4 + parts], *outs[4 + parts :][:2]
    grads_ref, grad_ref, keys_acc, values_acc, probs_ref, inner_ref = outs[6 + parts :][:6]
    raw_ref, *block_refs, rows_ref, stored, limits, sems = outs[12 + parts :]
    blocks = Blocks(facts, stored, limits, heads, parts)
    blocks.find()
    half, own, split = block_refs[0].shape
    width = weight_ref.shape[1]
    near = unit_refs[0].shape[0]
    step = 2 * TILE
    for k, ref in enumerate(part_refs):
        grads_ref[near * k : near * (k + 1), :] = ref[...]
    attend_back_body(
        heads,
        blocks,
        qkv_ref,
        grads_ref,
        log_ref,
        grad_ref,
        keys_acc,
        values_acc,
        probs_ref,
        inner_ref,
    )
    copies = []

    def leave(source, target):
        copies.append(pltpu.make_async_copy(source, target, sems.at[len(copies)]))
        copies[-1].start()

    sums = jnp.sum(grad_ref[...].astype(F32), axis=0, keepdims=True)
    sum_ref[...] = sums
    for i in range(weight_ref.shape[0] // step):
        at = slice(step * i, step * (i + 1))
        raw = total(
            [
                matmul(ref[:, at], grad_ref[near * k : near * (k + 1), :], TN)
                for k, ref in enumerate(unit_refs)
            ]
        )
        weight = weight_ref[at, :].astype(F32)
        raw_ref[at, :] = raw.astype(BF16)
        for row, value in enumerate((raw * weight, weight * sums)):
            lanes = total([value[:, 128 * c : 128 * (c + 1)] for c in range(width // 128)])
            for b in range(step // 128):
                turned = lanes[128 * b : 128 * (b + 1)].T
                found = jnp.sum(turned, axis=0, keepdims=True)
                start = step * i + 128 * b
                late_ref[row : row + 1, start : start + 128] = found
    for p in range(2 * half):
        at = pl.ds(pl.multiple_of(owner_a[p] * own, own), own)
        block_refs[p // half][p % half] = raw_ref[at, :split]
        at = pl.ds(pl.multiple_of(owner_b[p] * own, own), own)
        block_refs[2 + p // half][p % half] = raw_ref[at, split:]
    for source, target in zip(block_refs, block_outs):
        leave(source, target)
    for k in range(parts - 1, -1, -1):
        at = slice(near * k, near * (k + 1))
        rows_ref[at, :] = matmul(grad_ref[at, :], weight_ref[...], NT).astype(BF16)
        leave(rows_ref.at[at, :], row_outs[k])
    for copy in copies:
        copy.wait()


def attend_back(
    qkv, grad_context, log_totals, unit, weight, owner_a, owner_b, split, facts, heads
):
    rows, width = qkv.shape[0], heads * HEAD_DIM
    features = weight.shape[0]
    count = owner_a.shape[0]
    own = features // count
    first = jax.ShapeDtypeStruct((count // 2, own, split), BF16)
    last = jax.ShapeDtypeStruct((count // 2, own, 3 * width - split), BF16)
    small = [
        jax.ShapeDtypeStruct((2, features), F32),
        jax.ShapeDtypeStruct((1, 3 * width), F32),
    ]
    blocks = [first, first, last, last]
    return pl.pallas_call(
        functools.partial(attend_back_kernel, heads, len(unit)),
        grid=(1,),
        out_shape=[*blocks, *[like(value) for value in unit], *small],
        in_specs=[in_smem()] * 3 + [in_vmem()] * (3 + 2 * len(unit)),
        out_specs=[in_hbm()] * (4 + len(unit))
        + [pl.BlockSpec(value.shape, lambda i: (0, 0)) for value in small],
        scratch_shapes=[
            pltpu.VMEM((rows, width), BF16),
            pltpu.VMEM(qkv.shape, BF16),
            pltpu.VMEM((rows, width), F32),
            pltpu.VMEM((rows, width), F32),
            pltpu.VMEM((2, rows, width), F32),
            pltpu.VMEM((2, rows, width), F32),
            pltpu.VMEM(weight.shape, BF16),
            *[pltpu.VMEM(value.shape, BF16) for value in blocks],
            pltpu.VMEM((rows, features), BF16),
            pltpu.SMEM((rows // BLOCK,), jnp.int32),
            pltpu.SMEM((rows // BLOCK,), jnp.int32),
            pltpu.SemaphoreType.DMA((4 + len(unit),)),
        ],
        compiler_params=pltpu.CompilerParams(vmem_limit_bytes=53 << 20),
        cost_estimate=pl.CostEstimate(
            flops=40 * rows * CHUNK * width,
            bytes_accessed=40 * rows * width,
            transcendentals=rows * CHUNK * width // HEAD_DIM,
        ),
        name="attend_back",
    )(
        owner_a,
        owner_b,
        facts,
        qkv,
        log_totals,
        weight,
        *grad_context,
        *unit,
    )


TILE = 256


def gelu_and_slope(pre):
    scale = (2.0 / 3.141592653589793) ** 0.5
    square = pre * pre
    bent = jnp.tanh(scale * pre * (1.0 + 0.044715 * square))
    half = 0.5 + 0.5 * bent
    slope = half + (0.5 * scale) * pre * (1.0 - bent * bent) * (1.0 + 0.134145 * square)
    return pre * half, slope


def pick(refs):
    per = pl.num_programs(0) // len(refs)
    value = refs[0][...]
    for k, ref in enumerate(refs[1:], 1):
        value = jnp.where(pl.program_id(0) >= k * per, ref[...], value)
    return value


def put(refs, value):
    per = pl.num_programs(0) // len(refs)
    for k, ref in enumerate(refs):
        ref[...] = jnp.where(pl.program_id(0) // per == k, value, ref[...])


def feed_kernel(quarters, taken, *refs):
    normed = pick(refs[:quarters])
    grads = pick(refs[quarters : 2 * quarters])
    weight_ref, bias_ref = refs[2 * quarters : 2 * quarters + 2]
    results = refs[2 * quarters + 2 + taken :]
    units = bias_ref.shape[1]
    up = weight_ref[:, :units]
    down = weight_ref[:, units:]
    active, slope = gelu_and_slope(matmul(normed, up, NN) + bias_ref[...])
    active = active.astype(BF16)
    grad_hidden = (matmul(grads, down, NN) * slope).astype(BF16)
    put(results[:quarters], matmul(grad_hidden, up, NT).astype(BF16))
    put(results[quarters : 2 * quarters], matmul(active, down, NT).astype(BF16))
    for ref, value in zip(results[2 * quarters :], (normed, grad_hidden, grads, active)):
        ref[...] = value


def tile_specs(arrays):
    def spec(k, value):
        tiles = value.shape[0] // TILE
        return pl.BlockSpec(
            (TILE, value.shape[1]), lambda i: (jnp.clip(i - k * tiles, 0, tiles - 1), 0)
        )

    return [spec(k, value) for k, value in enumerate(arrays)]


def feed(normed, grads, weights, bias, stacks, start, quarters):
    rows, features = normed[0].shape
    units = bias.shape[1]
    here = len(normed)
    tiles = rows // TILE
    stacked = [jax.ShapeDtypeStruct((rows * quarters, n), BF16) for n in (features, units) * 2]
    found = pl.pallas_call(
        functools.partial(feed_kernel, here, len(stacks)),
        grid=(here * tiles,),
        out_shape=[like(value) for value in normed] * 2 + stacked,
        in_specs=tile_specs(normed)
        + tile_specs(grads)
        + [in_vmem(), whole_spec(bias)]
        + [pl.BlockSpec(memory_space=pl.ANY)] * len(stacks),
        out_specs=tile_specs(normed) * 2
        + [
            pl.BlockSpec((TILE, value.shape[1]), lambda i: (i + start * tiles, 0))
            for value in stacked
        ],
        input_output_aliases={2 * here + 2 + n: 2 * here + n for n in range(len(stacks))},
        compiler_params=limit(56),
        cost_estimate=pl.CostEstimate(
            flops=8 * here * rows * features * units,
            bytes_accessed=16 * here * rows * features + 4 * features * units,
            transcendentals=here * rows * units,
        ),
        name="feed",
    )(*normed, *grads, weights, bias, *stacks)
    return found[:here], found[here : 2 * here], found[2 * here :]


def feed_grads_kernel(normed_ref, grad_ref, grads_ref, active_ref, out_ref, sum_ref, acc_ref):
    units = sum_ref.shape[1]
    grad_hidden = grad_ref[...]

    @pl.when(pl.program_id(0) == 0)
    def _():
        acc_ref[...] = jnp.zeros_like(acc_ref)
        sum_ref[...] = jnp.zeros_like(sum_ref)

    acc_ref[:, :units] += matmul(normed_ref[...], grad_hidden, TN)
    acc_ref[:, units:] += matmul(grads_ref[...], active_ref[...], TN)
    sum_ref[...] += jnp.sum(grad_hidden.astype(F32), axis=0, keepdims=True)

    @pl.when(pl.program_id(0) == pl.num_programs(0) - 1)
    def _():
        out_ref[...] = acc_ref[...].astype(BF16)


def feed_grads(stacks):
    rows, features = stacks[0].shape
    units = stacks[1].shape[1]
    sums = jax.ShapeDtypeStruct((features, 2 * units), BF16)
    hidden = jax.ShapeDtypeStruct((1, units), F32)
    return pl.pallas_call(
        feed_grads_kernel,
        grid=(rows // (2 * TILE),),
        out_shape=[sums, hidden],
        in_specs=[tiled_spec(value, 2 * TILE) for value in stacks],
        out_specs=[whole_spec(sums), whole_spec(hidden)],
        scratch_shapes=[pltpu.VMEM(sums.shape, F32)],
        compiler_params=limit(62),
        cost_estimate=cost(4 * rows * features * units, 8 * rows * features),
        name="feed_grads",
    )(*stacks)


def norm_parts(rows):
    centred = rows - jnp.mean(rows, axis=-1, keepdims=True)
    inverse = lax.rsqrt(jnp.mean(centred * centred, axis=-1, keepdims=True) + EPS)
    return centred * inverse, inverse


def norm_back(grad_normed, unit, inverse, gain):
    grad_unit = grad_normed * gain
    return inverse * (
        grad_unit
        - jnp.mean(grad_unit, axis=-1, keepdims=True)
        - unit * jnp.mean(grad_unit * unit, axis=-1, keepdims=True)
    )


def whole_spec(value):
    return pl.BlockSpec(value.shape, lambda i: (0,) * value.ndim)


def tiled_spec(value, tile=TILE):
    return pl.BlockSpec((tile, value.shape[1]), lambda i: (i, 0))


def like(value, dtype=None):
    return jax.ShapeDtypeStruct(value.shape, dtype or value.dtype)


def limit(mebibytes):
    return pltpu.CompilerParams(vmem_limit_bytes=mebibytes << 20)


def cost(flops, moved):
    return pl.CostEstimate(flops=flops, bytes_accessed=moved, transcendentals=0)


def unit_kernel(rows_ref, unit_ref):
    unit_ref[...] = norm_parts(rows_ref[...].astype(F32))[0].astype(BF16)


def unit_rows(rows):
    return pl.pallas_call(
        unit_kernel,
        grid=(rows.shape[0] // TILE,),
        out_shape=like(rows),
        in_specs=[tiled_spec(rows)],
        out_specs=tiled_spec(rows),
        compiler_params=limit(62),
        cost_estimate=cost(8 * rows.size, 4 * rows.size),
        name="unit",
    )(rows)


def middle_kernel(parts, *refs):
    context_refs, out_refs = refs[:parts], refs[parts : 2 * parts]
    rows_ref, vector_ref, middle_ref, normed_ref = refs[2 * parts :]
    middle = rows_ref[...].astype(F32) + vector_ref[0:1, :]
    for context_ref, out_ref in zip(context_refs, out_refs):
        middle += matmul(context_ref[...], out_ref[...], NT)
    middle_ref[...] = middle.astype(BF16)
    unit = norm_parts(middle)[0]
    normed_ref[...] = (unit * vector_ref[1:2, :] + vector_ref[2:3, :]).astype(BF16)


def middle_rows(context, out_parts, rows, vectors):
    return pl.pallas_call(
        functools.partial(middle_kernel, len(context)),
        grid=(rows.shape[0] // TILE,),
        out_shape=[like(rows), like(rows)],
        in_specs=[tiled_spec(value) for value in context]
        + [whole_spec(value) for value in out_parts]
        + [tiled_spec(rows), whole_spec(vectors)],
        out_specs=[tiled_spec(rows), tiled_spec(rows)],
        compiler_params=limit(62),
        cost_estimate=cost(2 * rows.size * rows.shape[1], 12 * rows.size),
        name="middle",
    )(*context, *out_parts, rows, vectors)


def middle_back_kernel(terms, parts, owner, *refs):
    term_refs, out_refs = refs[:terms], refs[terms : terms + parts]
    context_refs = refs[terms + parts : terms + 2 * parts]
    middle_ref, cotangent_ref, vector_ref, grad_ref, sum_ref = refs[
        terms + 2 * parts : terms + 2 * parts + 5
    ]
    head_refs = refs[terms + 2 * parts + 5 : terms + 3 * parts + 5]
    block_refs = refs[terms + 3 * parts + 5 : -1]
    found_ref = refs[-1]
    first = pl.program_id(0) == 0
    last = pl.program_id(0) == pl.num_programs(0) - 1
    count, own, width = block_refs[0].shape
    grad_normed = total([ref[...].astype(F32) for ref in term_refs])
    unit, inverse = norm_parts(middle_ref[...].astype(F32))
    cotangent = cotangent_ref[...].astype(F32)
    grad = cotangent + norm_back(grad_normed, unit, inverse, vector_ref[1:2, :])
    low = grad.astype(BF16)
    grad_ref[...] = low
    for head_ref, out_ref in zip(head_refs, out_refs):
        head_ref[...] = matmul(low, out_ref[...], NN).astype(BF16)
    sums = [
        jnp.sum(value, axis=0, keepdims=True)
        for value in (grad_normed * unit, grad_normed, grad, cotangent)
    ]
    sums = jnp.concatenate(sums, axis=0)

    @pl.when(first)
    def _():
        sum_ref[...] = jnp.zeros_like(sum_ref)
        found_ref[...] = jnp.zeros_like(found_ref)

    sum_ref[...] += sums
    for k, context_ref in enumerate(context_refs):
        found_ref[:, k * width : (k + 1) * width] += matmul(low, context_ref[...], TN)

    @pl.when(last)
    def _():
        for k, block_ref in enumerate(block_refs):
            for p in range(count):
                at = pl.ds(pl.multiple_of(owner[p] * own, own), own)
                block_ref[p] = found_ref[at, k * width : (k + 1) * width].astype(BF16)


def middle_back(terms, out_parts, context, middle, cotangent, vectors, owner):
    rows, features = middle.shape
    width = out_parts[0].shape[1]
    parts = len(out_parts)
    count = owner.shape[0]
    sums = jax.ShapeDtypeStruct((4, features), F32)
    head = jax.ShapeDtypeStruct((rows, width), BF16)
    blocks = jax.ShapeDtypeStruct((count, features // count, width), BF16)
    found = pl.pallas_call(
        functools.partial(middle_back_kernel, len(terms), parts),
        grid=(rows // TILE,),
        out_shape=[like(middle), sums] + [head] * parts + [blocks] * parts,
        in_specs=[in_smem()]
        + [tiled_spec(value) for value in terms]
        + [whole_spec(value) for value in out_parts]
        + [tiled_spec(value) for value in context]
        + [tiled_spec(middle), tiled_spec(cotangent), whole_spec(vectors)],
        out_specs=[tiled_spec(middle), whole_spec(sums)]
        + [tiled_spec(head)] * parts
        + [whole_spec(blocks)] * parts,
        scratch_shapes=[pltpu.VMEM((features, width * parts), F32)],
        compiler_params=limit(62),
        cost_estimate=cost(4 * middle.size * features, 20 * middle.size),
        name="middle_back",
    )(owner, *terms, *out_parts, *context, middle, cotangent, vectors)
    return found[0], found[1], found[2 : 2 + parts], found[2 + parts :]


def input_back_kernel(terms, *refs):
    *term_refs, first_ref, last_ref = refs[:terms]
    rows_ref, middle_ref, vector_ref, out_ref = refs[terms:]
    half = jnp.where(pl.program_id(0) == 0, first_ref[...], last_ref[...])
    grad_normed = total([ref[...].astype(F32) for ref in term_refs]) + half.astype(F32)
    unit, inverse = norm_parts(rows_ref[...].astype(F32))
    grad = norm_back(grad_normed, unit, inverse, vector_ref[0:1, :])
    out_ref[...] = (middle_ref[...].astype(F32) + grad).astype(BF16)


def input_back(terms, rows, grad_middle, vectors):
    tile = rows.shape[0] // 2
    return pl.pallas_call(
        functools.partial(input_back_kernel, len(terms)),
        grid=(2,),
        out_shape=like(rows),
        in_specs=[tiled_spec(value, tile) for value in terms[:-2]]
        + [whole_spec(value) for value in terms[-2:]]
        + [tiled_spec(rows, tile), tiled_spec(grad_middle, tile), whole_spec(vectors)],
        out_specs=tiled_spec(rows, tile),
        compiler_params=limit(62),
        cost_estimate=cost(20 * rows.size, 14 * rows.size),
        name="input_back",
    )(*terms, rows, grad_middle, vectors)


def per_device(
    tokens,
    output_cotangent,
    lengths,
    block_place,
    random_blocks,
    qkv_weight,
    out_weight,
    up_weight,
    down_weight,
    vectors,
    hidden_bias,
):
    ways = lax.axis_size("tensor")
    spread_ways = lax.axis_size("dp")
    position = lax.axis_index("tensor")
    index = lax.axis_index("dp") * ways + position
    near = tokens.shape[0]
    rows = near * ways
    features = tokens.shape[1]
    width = qkv_weight.shape[2]
    heads = width // HEAD_DIM
    units = up_weight.shape[1]
    own = features // spread_ways
    piece = vectors.shape[1]
    unit_piece = hidden_bias.shape[1]

    small = jnp.zeros((8, features), F32)
    small = lax.dynamic_update_slice(small, vectors, (0, index * piece))
    small_hidden = jnp.zeros((1, units * ways), F32)
    small_hidden = lax.dynamic_update_slice(small_hidden, hidden_bias, (0, index * unit_piece))
    packed = jnp.concatenate([small.reshape(-1), small_hidden.reshape(-1)])
    packed = summed_everywhere(packed, ("tensor",))

    unit_near = unit_rows(tokens)
    unit_near, packed = together(unit_near, packed)
    unit_far = far(unit_near, "tensor")

    facts = attention_facts(lengths[0], position, block_place, random_blocks)

    bits = bits_of("dp")
    order_a = bits[::-1]
    order_b = bits[:1] + bits[:0:-1]
    owner_a = block_owners("dp", order_a)
    owner_b = block_owners("dp", order_b)
    split = 2 * width
    qkv_flat = qkv_weight.reshape(own, 3 * width)
    first_blocks = doubled(qkv_flat[:, :split], "dp", order_a)
    last_flat = jnp.concatenate([qkv_flat[:, split:], out_weight], axis=1)
    last_blocks = doubled(last_flat, "dp", order_b)
    packed = summed_everywhere(packed, ("dp",))
    feed_flat = jnp.concatenate([up_weight, down_weight], axis=1)
    first_going, last_going = output_cotangent[: near // 2], output_cotangent[near // 2 :]
    first_going, unit_far = together(first_going, unit_far)
    cotangent_first = far(first_going, "tensor")
    feed_flat, first_blocks, last_blocks, packed, unit_far = together(
        feed_flat, first_blocks, last_blocks, packed, unit_far
    )
    feed_full = lax.all_gather(feed_flat, "dp", axis=0, tiled=True)
    unit_parts = gathered_parts(unit_near, unit_far, "tensor")

    vectors_full = packed[: 8 * features].reshape(8, features)
    hidden_full = packed[8 * features :]
    bias_query = lax.dynamic_slice_in_dim(vectors_full[6], position * width, width)
    bias_value = lax.dynamic_slice_in_dim(vectors_full[7], position * width, width)
    bias_qkv = jnp.concatenate([bias_query, jnp.zeros_like(bias_query), bias_value])[None]
    bias_hidden = lax.dynamic_slice_in_dim(hidden_full, position * units, units)[None]
    norm_one = vectors_full[:2]
    norm_two = jnp.stack([vectors_full[4], vectors_full[2], vectors_full[3]])


    last_blocks, cotangent_first = together(last_blocks, cotangent_first)
    out_group = placed_rows(last_blocks, owner_b, width)
    out_far = far(out_group, "tensor")
    last_going, out_group = together(last_going, out_group)
    cotangent_last = far(last_going, "tensor")
    *context, qkv, qkv_full, log_totals = project_attend(
        unit_parts,
        first_blocks,
        last_blocks,
        owner_a,
        owner_b,
        norm_one,
        bias_qkv,
        facts,
        heads,
    )
    context = context[0]
    *context, out_far, cotangent_last = together(*context, out_far, cotangent_last)
    cotangent_far = jnp.concatenate([cotangent_first, cotangent_last], axis=0)
    grad_parts = gathered_parts(output_cotangent, cotangent_far, "tensor")

    out_parts = gathered_parts(out_group, out_far, "tensor")
    context_near = exchanged_parts(context, "tensor")
    middle, normed_two = middle_rows(context_near, out_parts, tokens, norm_two)

    half = ways // 2
    normed_far = far(normed_two, "tensor")
    normed_parts = gathered_parts(normed_two, normed_far, "tensor")
    near_back, near_out, stacks = feed(
        normed_parts[:half], grad_parts[:half], feed_full, bias_hidden, (), 0, ways
    )
    normed_far, *stacks = together(normed_far, *stacks)
    normed_parts = gathered_parts(normed_two, normed_far, "tensor")
    far_back, far_out, stacks = feed(
        normed_parts[half:], grad_parts[half:], feed_full, bias_hidden, stacks, half, ways
    )
    back_parts, feed_parts = near_back + far_back, near_out + far_out
    back_terms, far_sum = summed_halves(back_parts, "tensor")
    back_terms.append(far(far_sum, "tensor"))
    feed_sums, sum_hidden = feed_grads(stacks)
    feed_terms, feed_far = summed_halves(feed_parts, "tensor")
    early, late_rows = feed_far[: near // 2], feed_far[near // 2 :]
    feed_weight_grads = lax.psum_scatter(feed_sums, "dp", scatter_dimension=0, tiled=True)
    feed_weight_grads = feed_weight_grads.astype(F32)
    *back_terms, sum_hidden, early = together(*back_terms, sum_hidden, early)
    early = far(early, "tensor")

    grad_middle, sums_two, grad_heads, out_blocks = middle_back(
        back_terms, out_parts, context_near, middle, output_cotangent, norm_two, owner_b
    )
    grad_context = exchanged_parts(grad_heads, "tensor")

    *out_blocks, early = together(*out_blocks, early)
    out_terms, out_far = summed_halves(out_blocks, "tensor")
    *grad_context, out_far, late_rows = together(*grad_context, out_far, late_rows)
    out_terms.append(far(out_far, "tensor"))
    late_rows = far(late_rows, "tensor")
    first_keep, first_send, last_keep, last_send, *back_parts, late, sum_qkv = attend_back(
        qkv,
        grad_context,
        log_totals,
        unit_parts,
        qkv_full,
        owner_a,
        owner_b,
        split,
        facts,
        heads,
    )
    first_send, last_send, late, late_rows, *rest = together(
        first_send, last_send, late, late_rows, *out_terms, *back_parts
    )
    out_terms, back_parts = rest[: len(out_terms)], rest[len(out_terms) :]
    near_rows, far_rows = back_parts[:half], back_parts[half:]
    feed_terms.append(jnp.concatenate([early, late_rows], axis=0))
    output = total([term.astype(F32) for term in (*feed_terms, middle)]) + vectors_full[5]
    output = output.astype(BF16)
    out_sums = total([term.astype(F32) for term in out_terms]).astype(BF16)
    last_keep = jnp.concatenate([last_keep, out_sums[: spread_ways // 2]], axis=2)
    last_send = jnp.concatenate([last_send, out_sums[spread_ways // 2 :]], axis=2)
    head_sums = lax.dynamic_update_slice(
        jnp.zeros((3, features), F32), sum_qkv.reshape(3, width), (0, position * width)
    )
    hidden_sums = lax.dynamic_update_slice(
        jnp.zeros((1, units * ways), F32), sum_hidden, (0, position * units)
    )
    packed = jnp.concatenate(
        [late.reshape(-1), sums_two.reshape(-1), head_sums.reshape(-1), hidden_sums.reshape(-1)]
    )
    packed = summed_everywhere(packed, ("dp",))
    far_sum = added(far_rows[0], swapped(far_rows[1], "tensor", 1))
    far_sum, first_keep, last_keep, *near_rows = together(
        far_sum, first_keep, last_keep, *near_rows
    )
    far_first = far(far_sum[: near // 2], "tensor")
    far_last = far(far_sum[near // 2 :], "tensor")
    first_keep, first_send = halved(first_keep, first_send, "dp", order_a)
    last_keep, last_send = halved(last_keep, last_send, "dp", order_b)
    first_send, last_send, far_first = together(first_send, last_send, far_first)
    while first_send.shape[0] > 1:
        first_keep, first_send = halved(first_keep, first_send, "dp", order_a)
        last_keep, last_send = halved(last_keep, last_send, "dp", order_b)
    first_send, last_send, far_last, output = together(first_send, last_send, far_last, output)
    near_terms = [near_rows[0], swapped(near_rows[1], "tensor", 1), far_first, far_last]
    input_grad = input_back(near_terms, tokens, grad_middle, norm_one)
    first_keep, last_keep, input_grad, packed = together(
        first_keep, last_keep, input_grad, packed
    )
    first_raw = halved(first_keep, first_send, "dp", order_a)[0][0].astype(F32)
    last_raw = halved(last_keep, last_send, "dp", order_b)[0][0].astype(F32)
    out_weight_grad = last_raw[:, width:]
    last_raw = last_raw[:, :width]

    packed = summed_everywhere(packed, ("tensor",), direct=True)
    by_feature = packed[: 9 * features].reshape(9, features)
    hidden_sums = packed[9 * features :]
    vectors_grad = lax.dynamic_slice_in_dim(by_feature, index * piece, piece, axis=1)
    vectors_grad = jnp.concatenate([vectors_grad[:7], vectors_grad[8:]], axis=0)
    hidden_bias_grad = lax.dynamic_slice_in_dim(hidden_sums, index * unit_piece, unit_piece)

    sum_qkv = lax.dynamic_slice_in_dim(by_feature[6:], position * width, width, axis=1)
    mine = lax.dynamic_slice_in_dim(norm_one, lax.axis_index("dp") * own, own, axis=1)
    raw = jnp.concatenate([first_raw, last_raw], axis=1).reshape(own, 3, width)
    qkv_weight_grad = mine[0][:, None, None] * raw + mine[1][:, None, None] * sum_qkv
    return (
        output,
        input_grad,
        qkv_weight_grad,
        out_weight_grad,
        feed_weight_grads[:, :units],
        feed_weight_grads[:, units:],
        vectors_grad,
        hidden_bias_grad[None, :],
    )


def solution(mesh):
    placed = (
        P(("dp", "tensor"), None),
        P(("dp", "tensor"), None),
        P("dp"),
        P("dp", None),
        P("dp", "tensor", None, None),
        P("dp", None, "tensor"),
        P("dp", "tensor"),
        P("dp", "tensor"),
        P("dp", "tensor"),
        P(None, ("dp", "tensor")),
        P(None, ("dp", "tensor")),
    )
    return jax.shard_map(
        per_device,
        mesh=mesh,
        in_specs=placed,
        out_specs=(
            P(("dp", "tensor"), None),
            P(("dp", "tensor"), None),
            P("dp", None, "tensor"),
            P("dp", "tensor"),
            P("dp", "tensor"),
            P("dp", "tensor"),
            P(None, ("dp", "tensor")),
            P(None, ("dp", "tensor")),
        ),
        check_vma=False,
    )
```

```python
import functools

import jax
import jax.numpy as jnp
from jax import lax
from jax.experimental import pallas as pl
from jax.experimental.pallas import tpu as pltpu
from jax.sharding import PartitionSpec as P

HEAD_DIM = 64
BLOCK = 64
PAIR = 2 * HEAD_DIM
SLOTS = 8
CHUNK = 512
EPS = 1e-05
NEGATIVE = -1e30
F32 = jnp.float32
BF16 = jnp.bfloat16
NT = (((1,), (1,)), ((), ()))
NN = (((1,), (0,)), ((), ()))
TN = (((0,), (0,)), ((), ()))


def matmul(left, right, dims):
    return lax.dot_general(left, right, dims, preferred_element_type=F32)


def swapped(value, axis, bit):
    count = lax.axis_size(axis)
    return lax.ppermute(value, axis, [(i, i ^ bit) for i in range(count)])


def bits_of(axis):
    count = lax.axis_size(axis)
    return [1 << b for b in range(count.bit_length() - 1)]


def together(*values):
    return lax.optimization_barrier(values)


def far(value, axis):
    return swapped(value, axis, bits_of(axis)[-1])


def gathered_parts(value, far_value, axis):
    bits = bits_of(axis)
    parts = {0: value, bits[-1]: far_value}
    for bit in reversed(bits[:-1]):
        parts.update({k | bit: swapped(p, axis, bit) for k, p in list(parts.items())})
    return [parts[k] for k in range(len(parts))]


def summed_halves(parts, axis):
    left = dict(enumerate(parts))
    terms = [parts[0]]
    for bit in bits_of(axis)[: len(parts).bit_length() - 2]:
        kept = {}
        for k in sorted(left, reverse=True):
            if k & bit == 0:
                arrived = swapped(left[k | bit], axis, bit)
                if k == 0:
                    terms.append(arrived)
                    kept[k] = None
                else:
                    kept[k] = added(left[k], arrived)
        left = kept
    return terms, left[len(parts) // 2]


def added(left, right):
    return (left.astype(F32) + right.astype(F32)).astype(BF16)


def doubled(value, axis, order):
    blocks = value[None]
    for bit in order:
        blocks = jnp.concatenate([blocks, swapped(blocks, axis, bit)], axis=0)
    return blocks


def halved(keep, send, axis, order):
    half = send.shape[0]
    arrived = swapped(send, axis, order[half.bit_length() - 1])
    rest = half // 2
    return added(keep[: half - rest], arrived[: half - rest]), added(
        keep[half - rest :], arrived[half - rest :]
    )


def block_owners(axis, order):
    count = lax.axis_size(axis)
    device = [sum(bit for b, bit in enumerate(order) if p >> b & 1) for p in range(count)]
    return lax.axis_index(axis) ^ jnp.asarray(device, jnp.int32)


def exchanged_parts(parts, axis):
    return [p if k == 0 else swapped(p, axis, k) for k, p in enumerate(parts)]


def summed_everywhere(value, axes, direct=False):
    size = value.shape[0]
    value = jnp.pad(value, (0, -size % 1024)).reshape(-1, 128)
    for axis in axes:
        if direct:
            value = total([value] + [swapped(value, axis, k) for k in range(1, lax.axis_size(axis))])
        else:
            for bit in bits_of(axis):
                value = value + swapped(value, axis, bit)
    return value.reshape(-1)[:size]


def sent_and_summed(value, axis):
    count = lax.axis_size(axis)
    blocks = value.reshape(count, value.shape[0] // count, *value.shape[1:])
    arrived = lax.all_to_all(blocks, axis, 0, 0, tiled=True)
    return jnp.sum(arrived.astype(F32), axis=0)


def attention_facts(length, position, placing, chosen):
    head = jnp.stack([length, position]).astype(jnp.int32)
    return jnp.concatenate([head, placing.reshape(-1), chosen.reshape(-1)])


class Blocks:
    def __init__(self, facts, stored, limits, heads, quarters):
        self.facts, self.stored, self.limits = facts, stored, limits
        self.heads, self.quarters = heads, quarters
        self.count = stored.shape[0]
        self.length = facts[0]
        self.last = (self.length + BLOCK - 1) // BLOCK - 1
        self.last_rows = self.length - BLOCK * self.last

    def find(self):
        per = self.count // self.quarters
        for quarter in range(self.quarters):
            start = (self.facts[1] ^ quarter) * per
            for n in range(per):
                number = self.facts[2 + start + n]
                self.stored[number] = quarter * per + n
                rows = self.length - BLOCK * number
                self.limits[quarter * per + n] = jnp.clip(rows, 0, BLOCK)

    def item(self, number):
        last = self.last
        alive = number != last
        before, behind = number - 1, number + 1
        common = [0, last, before, number, jnp.minimum(behind, self.count - 1)]
        good = [
            alive,
            alive,
            alive & (before > 0) & (before < last),
            alive & (number < last),
            alive & (behind < last),
        ]
        places = [self.stored[block] for block in common]
        lane = lax.broadcasted_iota(jnp.int32, (1, self.heads * HEAD_DIM), 1)
        added_scores = [jnp.where(flag, 0.0, NEGATIVE).astype(F32) for flag in good]
        drawn = [
            [
                self.facts[2 + self.count + (h * self.count + number) * 3 + s]
                for h in range(self.heads)
            ]
            for s in range(3)
        ]
        random = []
        for s in range(3):
            random.append([self.stored[block] for block in drawn[s]])
            row = jnp.zeros((1, self.heads * HEAD_DIM), F32)
            for h, block in enumerate(drawn[s]):
                fresh = alive & (block > 0) & (block < last) & (jnp.abs(block - number) > 1)
                for other in range(s):
                    fresh = fresh & (block != drawn[other][h])
                score = jnp.where(fresh, 0.0, NEGATIVE).astype(F32)
                row = jnp.where(lane // HEAD_DIM == h, score, row)
            added_scores.append(row)
        return places, random, added_scores


def block_rows(index):
    return pl.ds(pl.multiple_of(index * BLOCK, BLOCK), BLOCK)


def spread(rows, heads):
    lane = lax.broadcasted_iota(jnp.int32, (1, heads * HEAD_DIM), 1)
    zero = jnp.zeros_like(rows)
    return jnp.concatenate(
        [jnp.where(lane // HEAD_DIM == h, rows, zero) for h in range(heads)], axis=0
    )


def collapse(full, heads):
    lane = lax.broadcasted_iota(jnp.int32, (1, PAIR), 1)
    pieces = []
    for pair in range(heads // 2):
        cols = slice(PAIR * pair, PAIR * (pair + 1))
        even = full[2 * pair * HEAD_DIM : (2 * pair + 1) * HEAD_DIM, cols]
        odd = full[(2 * pair + 1) * HEAD_DIM : (2 * pair + 2) * HEAD_DIM, cols]
        pieces.append(jnp.where(lane < HEAD_DIM, even, odd))
    return jnp.concatenate(pieces, axis=1)


def gathered_keys(ref, start, places, random, heads):
    width = heads * HEAD_DIM
    lane = lax.broadcasted_iota(jnp.int32, (1, PAIR), 1)
    parts = [ref[block_rows(place), start : start + width] for place in places]
    for drawn in random:
        pieces = []
        for pair in range(heads // 2):
            cols = slice(start + PAIR * pair, start + PAIR * (pair + 1))
            even = ref[block_rows(drawn[2 * pair]), cols]
            odd = ref[block_rows(drawn[2 * pair + 1]), cols]
            pieces.append(jnp.where(lane < HEAD_DIM, even, odd))
        parts.append(jnp.concatenate(pieces, axis=1))
    return jnp.concatenate(parts, axis=0)


def slot(value, index):
    return value[BLOCK * index : BLOCK * (index + 1)]


def biased(scores, bias, last_rows):
    row = lax.broadcasted_iota(jnp.int32, (BLOCK, 1), 0)
    parts = [slot(scores, s) + bias[s] for s in range(SLOTS)]
    parts[1] = jnp.where(row < last_rows, parts[1], NEGATIVE)
    return parts


def total(parts):
    return functools.reduce(jnp.add, parts)


def attend_body(heads, blocks, qkv_ref, out_ref, log_ref, keep_ref):
    count = blocks.count
    stored, limits = blocks.stored, blocks.limits
    width = heads * HEAD_DIM
    scale = jnp.asarray(HEAD_DIM**-0.5, BF16)

    def item(number):
        places, random, scores = blocks.item(number)
        here = block_rows(places[3])
        queries = spread(qkv_ref[here, :width] * scale, heads)
        keys = gathered_keys(qkv_ref, width, places, random, heads)
        parts = biased(matmul(keys, queries, NT), scores, blocks.last_rows)
        top = jnp.max(functools.reduce(jnp.maximum, parts), axis=0, keepdims=True)
        weights = [jnp.exp(p - top) for p in parts]
        row_total = jnp.sum(total(weights), axis=0, keepdims=True)
        inverse = 1.0 / row_total
        probs = jnp.concatenate([(p * inverse).astype(BF16) for p in weights], axis=0)
        values = gathered_keys(qkv_ref, 2 * width, places, random, heads)
        out_ref[here, :] = collapse(matmul(probs, values, TN), heads).astype(BF16)
        log_ref[pl.ds(number, 1), :] = top + jnp.log(row_total)

    def step(group, carry):
        for part in range(10):
            item(1 + group * 10 + part)
        return carry

    lax.fori_loop(0, (count - 1) // 10, step, 0)
    for number in range(1 + (count - 1) // 10 * 10, count):
        item(number)

    row = lax.broadcasted_iota(jnp.int32, (BLOCK, 1), 0)
    per = CHUNK // BLOCK
    chunks = count // per

    def chunk_rows(chunk):
        return pl.ds(pl.multiple_of(chunk * CHUNK, CHUNK), CHUNK)

    numbers = [0, blocks.last]
    rows_of = [block_rows(stored[number]) for number in numbers]
    queries = [spread(qkv_ref[at, :width] * scale, heads) for at in rows_of]

    def scores(chunk, tops):
        at = chunk_rows(chunk)
        keys = qkv_ref[at, width : 2 * width]
        found = []
        for end in range(2):
            raw = matmul(keys, queries[end], NT)
            parts = [
                jnp.where(row < limits[chunk * per + s], slot(raw, s), NEGATIVE)
                for s in range(per)
            ]
            keep_ref[end, at, :] = jnp.concatenate(parts, axis=0)
            found.append(jnp.maximum(tops[end], functools.reduce(jnp.maximum, parts)))
        return tuple(found)

    tops = lax.fori_loop(0, chunks, scores, (jnp.full((BLOCK, width), NEGATIVE, F32),) * 2)
    tops = [jnp.max(top, axis=0, keepdims=True) for top in tops]

    def exponents(chunk, totals):
        at = chunk_rows(chunk)
        found = []
        for end in range(2):
            weights = jnp.exp(keep_ref[end, at, :] - tops[end])
            keep_ref[end, at, :] = weights
            found.append(totals[end] + total([slot(weights, s) for s in range(per)]))
        return tuple(found)

    totals = lax.fori_loop(0, chunks, exponents, (jnp.zeros((BLOCK, width), F32),) * 2)
    totals = [jnp.sum(found, axis=0, keepdims=True) for found in totals]
    inverses = [1.0 / found for found in totals]

    def contexts(chunk, sums):
        at = chunk_rows(chunk)
        values = qkv_ref[at, 2 * width :]
        return tuple(
            sums[end] + matmul((keep_ref[end, at, :] * inverses[end]).astype(BF16), values, TN)
            for end in range(2)
        )

    sums = lax.fori_loop(0, chunks, contexts, (jnp.zeros((width, width), F32),) * 2)
    for end in range(2):
        out_ref[rows_of[end], :] = collapse(sums[end], heads).astype(BF16)
        log_ref[pl.ds(numbers[end], 1), :] = tops[end] + jnp.log(totals[end])


def attend_back_body(
    heads,
    blocks,
    qkv_ref,
    grad_ref,
    log_ref,
    out_ref,
    keys_acc,
    values_acc,
    probs_ref,
    inner_ref,
):
    count = blocks.count
    stored, limits = blocks.stored, blocks.limits
    width = heads * HEAD_DIM
    scale = jnp.asarray(HEAD_DIM**-0.5, BF16)
    lane = lax.broadcasted_iota(jnp.int32, (1, PAIR), 1)
    keys_acc[...] = jnp.zeros_like(keys_acc)
    values_acc[...] = jnp.zeros_like(values_acc)

    def accumulate(acc, value, places, random):
        for s in range(5):
            acc[block_rows(places[s]), :] += slot(value, s)
        for s in range(3):
            for h in range(heads):
                cols = slice(PAIR * (h // 2), PAIR * (h // 2 + 1))
                mine = (lane < HEAD_DIM) == (h % 2 == 0)
                term = jnp.where(mine, slot(value, 5 + s)[:, cols], 0.0)
                acc[block_rows(random[s][h]), cols] += term

    def item(number):
        places, random, scores = blocks.item(number)
        here = block_rows(places[3])
        queries = spread(qkv_ref[here, :width] * scale, heads)
        grads = spread(grad_ref[here, :], heads)
        keys = gathered_keys(qkv_ref, width, places, random, heads)
        values = gathered_keys(qkv_ref, 2 * width, places, random, heads)
        log_total = log_ref[pl.ds(number, 1), :]
        parts = biased(matmul(keys, queries, NT), scores, blocks.last_rows)
        probs = [jnp.exp(p - log_total) for p in parts]
        found = matmul(values, grads, NT)
        found = [slot(found, s) for s in range(SLOTS)]
        inner = total([p * d for p, d in zip(probs, found)])
        inner = jnp.sum(inner, axis=0, keepdims=True)
        grad_scores = jnp.concatenate(
            [(p * (d - inner)).astype(BF16) for p, d in zip(probs, found)], axis=0
        )
        probs_low = jnp.concatenate([p.astype(BF16) for p in probs], axis=0)
        accumulate(values_acc, matmul(probs_low, grads, NN), places, random)
        accumulate(keys_acc, matmul(grad_scores, queries, NN), places, random)
        grad_queries = collapse(matmul(grad_scores, keys, TN), heads) * HEAD_DIM**-0.5
        out_ref[here, :width] = grad_queries.astype(BF16)

    def step(group, carry):
        for part in range(6):
            item(1 + group * 6 + part)
        return carry

    lax.fori_loop(0, (count - 1) // 6, step, 0)
    for number in range(1 + (count - 1) // 6 * 6, count):
        item(number)

    row = lax.broadcasted_iota(jnp.int32, (BLOCK, 1), 0)
    per = CHUNK // BLOCK
    chunks = count // per

    def chunk_rows(chunk):
        return pl.ds(pl.multiple_of(chunk * CHUNK, CHUNK), CHUNK)

    numbers = [0, blocks.last]
    rows_of = [block_rows(stored[number]) for number in numbers]
    queries = [spread(qkv_ref[at, :width] * scale, heads) for at in rows_of]
    grads = [spread(grad_ref[at, :], heads) for at in rows_of]
    log_rows = [log_ref[pl.ds(number, 1), :] for number in numbers]

    def first(chunk, inners):
        at = chunk_rows(chunk)
        keys = qkv_ref[at, width : 2 * width]
        values = qkv_ref[at, 2 * width :]
        sums = []
        for end in range(2):
            scores = matmul(keys, queries[end], NT)
            parts = [
                jnp.where(row < limits[chunk * per + s], slot(scores, s), NEGATIVE)
                for s in range(per)
            ]
            probs = jnp.exp(jnp.concatenate(parts, axis=0) - log_rows[end])
            found = matmul(values, grads[end], NT)
            probs_ref[end, at, :] = probs
            inner_ref[end, at, :] = found
            both = probs * found
            sums.append(inners[end] + total([slot(both, s) for s in range(per)]))
        return tuple(sums)

    inners = lax.fori_loop(0, chunks, first, (jnp.zeros((BLOCK, width), F32),) * 2)
    inners = [jnp.sum(inner, axis=0, keepdims=True) for inner in inners]

    def second(chunk, sums):
        at = chunk_rows(chunk)
        keys = qkv_ref[at, width : 2 * width]
        found, to_values, to_keys = [], values_acc[at, :], keys_acc[at, :]
        for end in range(2):
            probs = probs_ref[end, at, :]
            grad_scores = (probs * (inner_ref[end, at, :] - inners[end])).astype(BF16)
            to_values = to_values + matmul(probs.astype(BF16), grads[end], NN)
            to_keys = to_keys + matmul(grad_scores, queries[end], NN)
            found.append(sums[end] + matmul(grad_scores, keys, TN))
        out_ref[at, width : 2 * width] = to_keys.astype(BF16)
        out_ref[at, 2 * width :] = to_values.astype(BF16)
        return tuple(found)

    sums = lax.fori_loop(0, chunks, second, (jnp.zeros((width, width), F32),) * 2)
    for end in range(2):
        grad_queries = collapse(sums[end], heads) * HEAD_DIM**-0.5
        out_ref[rows_of[end], :width] = grad_queries.astype(BF16)


def in_smem():
    return pl.BlockSpec(memory_space=pltpu.SMEM)


def in_vmem():
    return pl.BlockSpec(memory_space=pltpu.VMEM)


def project_attend_kernel(heads, parts, owner_a, owner_b, facts, *refs):
    unit_refs = refs[:parts]
    first_ref, last_ref, norm_ref, bias_ref = refs[parts : parts + 4]
    *quarter_refs, kept_ref, weight_out_ref, log_ref = refs[parts + 4 : 2 * parts + 7]
    qkv_ref, weight_ref, out_ref, keep_ref, stored, limits, sems = refs[2 * parts + 7 :]
    blocks = Blocks(facts, stored, limits, heads, parts)
    blocks.find()
    count, own, split = first_ref.shape
    near = unit_refs[0].shape[0]
    rest = weight_ref.shape[1] - split
    for p in range(count):
        at = pl.ds(pl.multiple_of(owner_a[p] * own, own), own)
        weight_ref[at, :split] = first_ref[p]
        at = pl.ds(pl.multiple_of(owner_b[p] * own, own), own)
        weight_ref[at, split:] = last_ref[p, :, :rest]
    copies = [pltpu.make_async_copy(weight_ref, weight_out_ref, sems.at[0])]
    copies[0].start()
    for k, ref in enumerate(unit_refs):
        normed = ref[...].astype(F32) * norm_ref[0:1, :] + norm_ref[1:2, :]
        found = matmul(normed.astype(BF16), weight_ref[...], NN) + bias_ref[...]
        qkv_ref[near * k : near * (k + 1), :] = found.astype(BF16)
    copies.append(pltpu.make_async_copy(qkv_ref, kept_ref, sems.at[1]))
    copies[1].start()
    attend_body(heads, blocks, qkv_ref, out_ref, log_ref, keep_ref)
    for k, ref in enumerate(quarter_refs):
        part = out_ref.at[near * k : near * (k + 1), :]
        copies.append(pltpu.make_async_copy(part, ref, sems.at[2 + k]))
        copies[-1].start()
    for copy in copies:
        copy.wait()


def in_hbm():
    return pl.BlockSpec(memory_space=pltpu.HBM)


def project_attend(unit, first, last, owner_a, owner_b, norm, bias, facts, heads):
    rows = sum(value.shape[0] for value in unit)
    features = unit[0].shape[1]
    width = heads * HEAD_DIM
    log_shape = jax.ShapeDtypeStruct((rows // BLOCK, width), F32)
    quarter = [jax.ShapeDtypeStruct((value.shape[0], width), BF16) for value in unit]
    qkv = jax.ShapeDtypeStruct((rows, 3 * width), BF16)
    weight = jax.ShapeDtypeStruct((features, 3 * width), BF16)
    found = pl.pallas_call(
        functools.partial(project_attend_kernel, heads, len(unit)),
        grid=(1,),
        out_shape=[*quarter, qkv, weight, log_shape],
        in_specs=[in_smem()] * 3 + [in_vmem()] * (len(unit) + 4),
        out_specs=[in_hbm()] * (len(unit) + 2)
        + [pl.BlockSpec(log_shape.shape, lambda i: (0, 0))],
        scratch_shapes=[
            pltpu.VMEM(qkv.shape, BF16),
            pltpu.VMEM(weight.shape, BF16),
            pltpu.VMEM((rows, width), BF16),
            pltpu.VMEM((2, rows, width), F32),
            pltpu.SMEM((rows // BLOCK,), jnp.int32),
            pltpu.SMEM((rows // BLOCK,), jnp.int32),
            pltpu.SemaphoreType.DMA((len(unit) + 2,)),
        ],
        compiler_params=pltpu.CompilerParams(vmem_limit_bytes=56 << 20),
        cost_estimate=pl.CostEstimate(
            flops=20 * rows * CHUNK * width,
            bytes_accessed=20 * rows * width,
            transcendentals=rows * CHUNK * width // HEAD_DIM,
        ),
        name="project_attend",
    )(owner_a, owner_b, facts, *unit, first, last, norm, bias)
    return found[: len(unit)], *found[len(unit) :]


def place_kernel(owner, blocks_ref, out_ref):
    count, own, _ = blocks_ref.shape
    width = out_ref.shape[1]
    for p in range(count):
        at = pl.ds(pl.multiple_of(owner[p] * own, own), own)
        out_ref[at, :] = blocks_ref[p, :, -width:]


def placed_rows(blocks, owner, width):
    out = jax.ShapeDtypeStruct((blocks.shape[0] * blocks.shape[1], width), blocks.dtype)
    return pl.pallas_call(
        place_kernel,
        grid=(1,),
        out_shape=out,
        in_specs=[in_smem(), in_vmem()],
        out_specs=pl.BlockSpec(out.shape, lambda i: (0, 0)),
        name="placed_rows",
    )(owner, blocks)


def attend_back_kernel(heads, parts, owner_a, owner_b, facts, *refs):
    qkv_ref, log_ref, weight_ref = refs[:3]
    part_refs, unit_refs = refs[3 : 3 + parts], refs[3 + parts : 3 + 2 * parts]
    outs = refs[3 + 2 * parts :]
    block_outs, row_outs, late_ref, sum_ref = outs[:4], outs[4 : 4 + parts], *outs[4 + parts :][:2]
    grads_ref, grad_ref, keys_acc, values_acc, probs_ref, inner_ref = outs[6 + parts :][:6]
    raw_ref, *block_refs, rows_ref, stored, limits, sems = outs[12 + parts :]
    blocks = Blocks(facts, stored, limits, heads, parts)
    blocks.find()
    half, own, split = block_refs[0].shape
    width = weight_ref.shape[1]
    near = unit_refs[0].shape[0]
    step = 2 * TILE
    for k, ref in enumerate(part_refs):
        grads_ref[near * k : near * (k + 1), :] = ref[...]
    attend_back_body(
        heads,
        blocks,
        qkv_ref,
        grads_ref,
        log_ref,
        grad_ref,
        keys_acc,
        values_acc,
        probs_ref,
        inner_ref,
    )
    copies = []

    def leave(source, target):
        copies.append(pltpu.make_async_copy(source, target, sems.at[len(copies)]))
        copies[-1].start()

    sums = jnp.sum(grad_ref[...].astype(F32), axis=0, keepdims=True)
    sum_ref[...] = sums
    for i in range(weight_ref.shape[0] // step):
        at = slice(step * i, step * (i + 1))
        raw = total(
            [
                matmul(ref[:, at], grad_ref[near * k : near * (k + 1), :], TN)
                for k, ref in enumerate(unit_refs)
            ]
        )
        weight = weight_ref[at, :].astype(F32)
        raw_ref[at, :] = raw.astype(BF16)
        for row, value in enumerate((raw * weight, weight * sums)):
            lanes = total([value[:, 128 * c : 128 * (c + 1)] for c in range(width // 128)])
            for b in range(step // 128):
                turned = lanes[128 * b : 128 * (b + 1)].T
                found = jnp.sum(turned, axis=0, keepdims=True)
                start = step * i + 128 * b
                late_ref[row : row + 1, start : start + 128] = found
    for p in range(2 * half):
        at = pl.ds(pl.multiple_of(owner_a[p] * own, own), own)
        block_refs[p // half][p % half] = raw_ref[at, :split]
        at = pl.ds(pl.multiple_of(owner_b[p] * own, own), own)
        block_refs[2 + p // half][p % half] = raw_ref[at, split:]
    for source, target in zip(block_refs, block_outs):
        leave(source, target)
    for k in range(parts - 1, -1, -1):
        at = slice(near * k, near * (k + 1))
        rows_ref[at, :] = matmul(grad_ref[at, :], weight_ref[...], NT).astype(BF16)
        leave(rows_ref.at[at, :], row_outs[k])
    for copy in copies:
        copy.wait()


def attend_back(
    qkv, grad_context, log_totals, unit, weight, owner_a, owner_b, split, facts, heads
):
    rows, width = qkv.shape[0], heads * HEAD_DIM
    features = weight.shape[0]
    count = owner_a.shape[0]
    own = features // count
    first = jax.ShapeDtypeStruct((count // 2, own, split), BF16)
    last = jax.ShapeDtypeStruct((count // 2, own, 3 * width - split), BF16)
    small = [
        jax.ShapeDtypeStruct((2, features), F32),
        jax.ShapeDtypeStruct((1, 3 * width), F32),
    ]
    blocks = [first, first, last, last]
    return pl.pallas_call(
        functools.partial(attend_back_kernel, heads, len(unit)),
        grid=(1,),
        out_shape=[*blocks, *[like(value) for value in unit], *small],
        in_specs=[in_smem()] * 3 + [in_vmem()] * (3 + 2 * len(unit)),
        out_specs=[in_hbm()] * (4 + len(unit))
        + [pl.BlockSpec(value.shape, lambda i: (0, 0)) for value in small],
        scratch_shapes=[
            pltpu.VMEM((rows, width), BF16),
            pltpu.VMEM(qkv.shape, BF16),
            pltpu.VMEM((rows, width), F32),
            pltpu.VMEM((rows, width), F32),
            pltpu.VMEM((2, rows, width), F32),
            pltpu.VMEM((2, rows, width), F32),
            pltpu.VMEM(weight.shape, BF16),
            *[pltpu.VMEM(value.shape, BF16) for value in blocks],
            pltpu.VMEM((rows, features), BF16),
            pltpu.SMEM((rows // BLOCK,), jnp.int32),
            pltpu.SMEM((rows // BLOCK,), jnp.int32),
            pltpu.SemaphoreType.DMA((4 + len(unit),)),
        ],
        compiler_params=pltpu.CompilerParams(vmem_limit_bytes=53 << 20),
        cost_estimate=pl.CostEstimate(
            flops=40 * rows * CHUNK * width,
            bytes_accessed=40 * rows * width,
            transcendentals=rows * CHUNK * width // HEAD_DIM,
        ),
        name="attend_back",
    )(
        owner_a,
        owner_b,
        facts,
        qkv,
        log_totals,
        weight,
        *grad_context,
        *unit,
    )


TILE = 256


def gelu_and_slope(pre):
    scale = (2.0 / 3.141592653589793) ** 0.5
    square = pre * pre
    bent = jnp.tanh(scale * pre * (1.0 + 0.044715 * square))
    half = 0.5 + 0.5 * bent
    slope = half + (0.5 * scale) * pre * (1.0 - bent * bent) * (1.0 + 0.134145 * square)
    return pre * half, slope


def pick(refs):
    per = pl.num_programs(0) // len(refs)
    value = refs[0][...]
    for k, ref in enumerate(refs[1:], 1):
        value = jnp.where(pl.program_id(0) >= k * per, ref[...], value)
    return value


def put(refs, value):
    per = pl.num_programs(0) // len(refs)
    for k, ref in enumerate(refs):
        ref[...] = jnp.where(pl.program_id(0) // per == k, value, ref[...])


def feed_kernel(quarters, taken, *refs):
    normed = pick(refs[:quarters])
    grads = pick(refs[quarters : 2 * quarters])
    weight_ref, bias_ref = refs[2 * quarters : 2 * quarters + 2]
    results = refs[2 * quarters + 2 + taken :]
    units = bias_ref.shape[1]
    up = weight_ref[:, :units]
    down = weight_ref[:, units:]
    active, slope = gelu_and_slope(matmul(normed, up, NN) + bias_ref[...])
    active = active.astype(BF16)
    grad_hidden = (matmul(grads, down, NN) * slope).astype(BF16)
    put(results[:quarters], matmul(grad_hidden, up, NT).astype(BF16))
    put(results[quarters : 2 * quarters], matmul(active, down, NT).astype(BF16))
    for ref, value in zip(results[2 * quarters :], (normed, grad_hidden, grads, active)):
        ref[...] = value


def tile_specs(arrays):
    def spec(k, value):
        tiles = value.shape[0] // TILE
        return pl.BlockSpec(
            (TILE, value.shape[1]), lambda i: (jnp.clip(i - k * tiles, 0, tiles - 1), 0)
        )

    return [spec(k, value) for k, value in enumerate(arrays)]


def feed(normed, grads, weights, bias, stacks, start, quarters):
    rows, features = normed[0].shape
    units = bias.shape[1]
    here = len(normed)
    tiles = rows // TILE
    stacked = [jax.ShapeDtypeStruct((rows * quarters, n), BF16) for n in (features, units) * 2]
    found = pl.pallas_call(
        functools.partial(feed_kernel, here, len(stacks)),
        grid=(here * tiles,),
        out_shape=[like(value) for value in normed] * 2 + stacked,
        in_specs=tile_specs(normed)
        + tile_specs(grads)
        + [in_vmem(), whole_spec(bias)]
        + [pl.BlockSpec(memory_space=pl.ANY)] * len(stacks),
        out_specs=tile_specs(normed) * 2
        + [
            pl.BlockSpec((TILE, value.shape[1]), lambda i: (i + start * tiles, 0))
            for value in stacked
        ],
        input_output_aliases={2 * here + 2 + n: 2 * here + n for n in range(len(stacks))},
        compiler_params=limit(56),
        cost_estimate=pl.CostEstimate(
            flops=8 * here * rows * features * units,
            bytes_accessed=16 * here * rows * features + 4 * features * units,
            transcendentals=here * rows * units,
        ),
        name="feed",
    )(*normed, *grads, weights, bias, *stacks)
    return found[:here], found[here : 2 * here], found[2 * here :]


def feed_grads_kernel(normed_ref, grad_ref, grads_ref, active_ref, out_ref, sum_ref, acc_ref):
    units = sum_ref.shape[1]
    grad_hidden = grad_ref[...]

    @pl.when(pl.program_id(0) == 0)
    def _():
        acc_ref[...] = jnp.zeros_like(acc_ref)
        sum_ref[...] = jnp.zeros_like(sum_ref)

    acc_ref[:, :units] += matmul(normed_ref[...], grad_hidden, TN)
    acc_ref[:, units:] += matmul(grads_ref[...], active_ref[...], TN)
    sum_ref[...] += jnp.sum(grad_hidden.astype(F32), axis=0, keepdims=True)

    @pl.when(pl.program_id(0) == pl.num_programs(0) - 1)
    def _():
        out_ref[...] = acc_ref[...].astype(BF16)


def feed_grads(stacks):
    rows, features = stacks[0].shape
    units = stacks[1].shape[1]
    sums = jax.ShapeDtypeStruct((features, 2 * units), BF16)
    hidden = jax.ShapeDtypeStruct((1, units), F32)
    return pl.pallas_call(
        feed_grads_kernel,
        grid=(rows // (2 * TILE),),
        out_shape=[sums, hidden],
        in_specs=[tiled_spec(value, 2 * TILE) for value in stacks],
        out_specs=[whole_spec(sums), whole_spec(hidden)],
        scratch_shapes=[pltpu.VMEM(sums.shape, F32)],
        compiler_params=limit(62),
        cost_estimate=cost(4 * rows * features * units, 8 * rows * features),
        name="feed_grads",
    )(*stacks)


def norm_parts(rows):
    centred = rows - jnp.mean(rows, axis=-1, keepdims=True)
    inverse = lax.rsqrt(jnp.mean(centred * centred, axis=-1, keepdims=True) + EPS)
    return centred * inverse, inverse


def norm_back(grad_normed, unit, inverse, gain):
    grad_unit = grad_normed * gain
    return inverse * (
        grad_unit
        - jnp.mean(grad_unit, axis=-1, keepdims=True)
        - unit * jnp.mean(grad_unit * unit, axis=-1, keepdims=True)
    )


def whole_spec(value):
    return pl.BlockSpec(value.shape, lambda i: (0,) * value.ndim)


def tiled_spec(value, tile=TILE):
    return pl.BlockSpec((tile, value.shape[1]), lambda i: (i, 0))


def like(value, dtype=None):
    return jax.ShapeDtypeStruct(value.shape, dtype or value.dtype)


def limit(mebibytes):
    return pltpu.CompilerParams(vmem_limit_bytes=mebibytes << 20)


def cost(flops, moved):
    return pl.CostEstimate(flops=flops, bytes_accessed=moved, transcendentals=0)


def unit_kernel(rows_ref, unit_ref):
    unit_ref[...] = norm_parts(rows_ref[...].astype(F32))[0].astype(BF16)


def unit_rows(rows):
    return pl.pallas_call(
        unit_kernel,
        grid=(rows.shape[0] // TILE,),
        out_shape=like(rows),
        in_specs=[tiled_spec(rows)],
        out_specs=tiled_spec(rows),
        compiler_params=limit(62),
        cost_estimate=cost(8 * rows.size, 4 * rows.size),
        name="unit",
    )(rows)


def middle_kernel(parts, *refs):
    context_refs, out_refs = refs[:parts], refs[parts : 2 * parts]
    rows_ref, vector_ref, middle_ref, normed_ref = refs[2 * parts :]
    middle = rows_ref[...].astype(F32) + vector_ref[0:1, :]
    for context_ref, out_ref in zip(context_refs, out_refs):
        middle += matmul(context_ref[...], out_ref[...], NT)
    middle_ref[...] = middle.astype(BF16)
    unit = norm_parts(middle)[0]
    normed_ref[...] = (unit * vector_ref[1:2, :] + vector_ref[2:3, :]).astype(BF16)


def middle_rows(context, out_parts, rows, vectors):
    return pl.pallas_call(
        functools.partial(middle_kernel, len(context)),
        grid=(rows.shape[0] // TILE,),
        out_shape=[like(rows), like(rows)],
        in_specs=[tiled_spec(value) for value in context]
        + [whole_spec(value) for value in out_parts]
        + [tiled_spec(rows), whole_spec(vectors)],
        out_specs=[tiled_spec(rows), tiled_spec(rows)],
        compiler_params=limit(62),
        cost_estimate=cost(2 * rows.size * rows.shape[1], 12 * rows.size),
        name="middle",
    )(*context, *out_parts, rows, vectors)


def middle_back_kernel(terms, parts, owner, *refs):
    term_refs, out_refs = refs[:terms], refs[terms : terms + parts]
    context_refs = refs[terms + parts : terms + 2 * parts]
    middle_ref, cotangent_ref, vector_ref, grad_ref, sum_ref = refs[
        terms + 2 * parts : terms + 2 * parts + 5
    ]
    head_refs = refs[terms + 2 * parts + 5 : terms + 3 * parts + 5]
    block_refs = refs[terms + 3 * parts + 5 : -1]
    found_ref = refs[-1]
    first = pl.program_id(0) == 0
    last = pl.program_id(0) == pl.num_programs(0) - 1
    count, own, width = block_refs[0].shape
    grad_normed = total([ref[...].astype(F32) for ref in term_refs])
    unit, inverse = norm_parts(middle_ref[...].astype(F32))
    cotangent = cotangent_ref[...].astype(F32)
    grad = cotangent + norm_back(grad_normed, unit, inverse, vector_ref[1:2, :])
    low = grad.astype(BF16)
    grad_ref[...] = low
    for head_ref, out_ref in zip(head_refs, out_refs):
        head_ref[...] = matmul(low, out_ref[...], NN).astype(BF16)
    sums = [
        jnp.sum(value, axis=0, keepdims=True)
        for value in (grad_normed * unit, grad_normed, grad, cotangent)
    ]
    sums = jnp.concatenate(sums, axis=0)

    @pl.when(first)
    def _():
        sum_ref[...] = jnp.zeros_like(sum_ref)
        found_ref[...] = jnp.zeros_like(found_ref)

    sum_ref[...] += sums
    for k, context_ref in enumerate(context_refs):
        found_ref[:, k * width : (k + 1) * width] += matmul(low, context_ref[...], TN)

    @pl.when(last)
    def _():
        for k, block_ref in enumerate(block_refs):
            for p in range(count):
                at = pl.ds(pl.multiple_of(owner[p] * own, own), own)
                block_ref[p] = found_ref[at, k * width : (k + 1) * width].astype(BF16)


def middle_back(terms, out_parts, context, middle, cotangent, vectors, owner):
    rows, features = middle.shape
    width = out_parts[0].shape[1]
    parts = len(out_parts)
    count = owner.shape[0]
    sums = jax.ShapeDtypeStruct((4, features), F32)
    head = jax.ShapeDtypeStruct((rows, width), BF16)
    blocks = jax.ShapeDtypeStruct((count, features // count, width), BF16)
    found = pl.pallas_call(
        functools.partial(middle_back_kernel, len(terms), parts),
        grid=(rows // TILE,),
        out_shape=[like(middle), sums] + [head] * parts + [blocks] * parts,
        in_specs=[in_smem()]
        + [tiled_spec(value) for value in terms]
        + [whole_spec(value) for value in out_parts]
        + [tiled_spec(value) for value in context]
        + [tiled_spec(middle), tiled_spec(cotangent), whole_spec(vectors)],
        out_specs=[tiled_spec(middle), whole_spec(sums)]
        + [tiled_spec(head)] * parts
        + [whole_spec(blocks)] * parts,
        scratch_shapes=[pltpu.VMEM((features, width * parts), F32)],
        compiler_params=limit(62),
        cost_estimate=cost(4 * middle.size * features, 20 * middle.size),
        name="middle_back",
    )(owner, *terms, *out_parts, *context, middle, cotangent, vectors)
    return found[0], found[1], found[2 : 2 + parts], found[2 + parts :]


def input_back_kernel(terms, *refs):
    *term_refs, first_ref, last_ref = refs[:terms]
    rows_ref, middle_ref, vector_ref, out_ref = refs[terms:]
    half = jnp.where(pl.program_id(0) == 0, first_ref[...], last_ref[...])
    grad_normed = total([ref[...].astype(F32) for ref in term_refs]) + half.astype(F32)
    unit, inverse = norm_parts(rows_ref[...].astype(F32))
    grad = norm_back(grad_normed, unit, inverse, vector_ref[0:1, :])
    out_ref[...] = (middle_ref[...].astype(F32) + grad).astype(BF16)


def input_back(terms, rows, grad_middle, vectors):
    tile = rows.shape[0] // 2
    return pl.pallas_call(
        functools.partial(input_back_kernel, len(terms)),
        grid=(2,),
        out_shape=like(rows),
        in_specs=[tiled_spec(value, tile) for value in terms[:-2]]
        + [whole_spec(value) for value in terms[-2:]]
        + [tiled_spec(rows, tile), tiled_spec(grad_middle, tile), whole_spec(vectors)],
        out_specs=tiled_spec(rows, tile),
        compiler_params=limit(62),
        cost_estimate=cost(20 * rows.size, 14 * rows.size),
        name="input_back",
    )(*terms, rows, grad_middle, vectors)


def per_device(
    tokens,
    output_cotangent,
    lengths,
    block_place,
    random_blocks,
    qkv_weight,
    out_weight,
    up_weight,
    down_weight,
    vectors,
    hidden_bias,
):
    ways = lax.axis_size("tensor")
    spread_ways = lax.axis_size("dp")
    position = lax.axis_index("tensor")
    index = lax.axis_index("dp") * ways + position
    near = tokens.shape[0]
    rows = near * ways
    features = tokens.shape[1]
    width = qkv_weight.shape[2]
    heads = width // HEAD_DIM
    units = up_weight.shape[1]
    own = features // spread_ways
    piece = vectors.shape[1]
    unit_piece = hidden_bias.shape[1]

    small = jnp.zeros((8, features), F32)
    small = lax.dynamic_update_slice(small, vectors, (0, index * piece))
    small_hidden = jnp.zeros((1, units * ways), F32)
    small_hidden = lax.dynamic_update_slice(small_hidden, hidden_bias, (0, index * unit_piece))
    packed = jnp.concatenate([small.reshape(-1), small_hidden.reshape(-1)])
    packed = summed_everywhere(packed, ("tensor",))

    unit_near = unit_rows(tokens)
    unit_near, packed = together(unit_near, packed)
    unit_far = far(unit_near, "tensor")

    facts = attention_facts(lengths[0], position, block_place, random_blocks)

    bits = bits_of("dp")
    order_a = bits[::-1]
    order_b = bits[:1] + bits[:0:-1]
    owner_a = block_owners("dp", order_a)
    owner_b = block_owners("dp", order_b)
    split = 2 * width
    qkv_flat = qkv_weight.reshape(own, 3 * width)
    first_blocks = doubled(qkv_flat[:, :split], "dp", order_a)
    last_flat = jnp.concatenate([qkv_flat[:, split:], out_weight], axis=1)
    last_blocks = doubled(last_flat, "dp", order_b)
    packed = summed_everywhere(packed, ("dp",))
    feed_flat = jnp.concatenate([up_weight, down_weight], axis=1)
    piece_rows = near // 4
    first_going, next_going = output_cotangent[:piece_rows], output_cotangent[piece_rows:]
    next_going, last_going = next_going[:piece_rows], next_going[piece_rows:]
    first_going, unit_far = together(first_going, unit_far)
    cotangent_first = far(first_going, "tensor")
    feed_flat, first_blocks, last_blocks, packed, cotangent_first, next_going = together(
        feed_flat, first_blocks, last_blocks, packed, cotangent_first, next_going
    )
    cotangent_next = far(next_going, "tensor")
    feed_full = lax.all_gather(feed_flat, "dp", axis=0, tiled=True)
    unit_parts = gathered_parts(unit_near, unit_far, "tensor")

    vectors_full = packed[: 8 * features].reshape(8, features)
    hidden_full = packed[8 * features :]
    bias_query = lax.dynamic_slice_in_dim(vectors_full[6], position * width, width)
    bias_value = lax.dynamic_slice_in_dim(vectors_full[7], position * width, width)
    bias_qkv = jnp.concatenate([bias_query, jnp.zeros_like(bias_query), bias_value])[None]
    bias_hidden = lax.dynamic_slice_in_dim(hidden_full, position * units, units)[None]
    norm_one = vectors_full[:2]
    norm_two = jnp.stack([vectors_full[4], vectors_full[2], vectors_full[3]])


    last_blocks, cotangent_next = together(last_blocks, cotangent_next)
    out_group = placed_rows(last_blocks, owner_b, width)
    out_far = far(out_group, "tensor")
    last_going, out_group = together(last_going, out_group)
    cotangent_last = far(last_going, "tensor")
    *context, qkv, qkv_full, log_totals = project_attend(
        unit_parts,
        first_blocks,
        last_blocks,
        owner_a,
        owner_b,
        norm_one,
        bias_qkv,
        facts,
        heads,
    )
    context = context[0]
    *context, out_far, cotangent_last = together(*context, out_far, cotangent_last)
    cotangent_far = jnp.concatenate([cotangent_first, cotangent_next, cotangent_last], axis=0)
    grad_parts = gathered_parts(output_cotangent, cotangent_far, "tensor")

    out_parts = gathered_parts(out_group, out_far, "tensor")
    context_near = exchanged_parts(context, "tensor")
    middle, normed_two = middle_rows(context_near, out_parts, tokens, norm_two)

    half = ways // 2
    normed_far = far(normed_two, "tensor")
    normed_parts = gathered_parts(normed_two, normed_far, "tensor")
    near_back, near_out, stacks = feed(
        normed_parts[:half], grad_parts[:half], feed_full, bias_hidden, (), 0, ways
    )
    normed_far, *stacks = together(normed_far, *stacks)
    normed_parts = gathered_parts(normed_two, normed_far, "tensor")
    far_back, far_out, stacks = feed(
        normed_parts[half:], grad_parts[half:], feed_full, bias_hidden, stacks, half, ways
    )
    back_parts, feed_parts = near_back + far_back, near_out + far_out
    back_terms, far_sum = summed_halves(back_parts, "tensor")
    back_terms.append(far(far_sum, "tensor"))
    feed_sums, sum_hidden = feed_grads(stacks)
    feed_terms, feed_far = summed_halves(feed_parts, "tensor")
    early, late_rows = feed_far[: near // 2], feed_far[near // 2 :]
    feed_weight_grads = lax.psum_scatter(feed_sums, "dp", scatter_dimension=0, tiled=True)
    feed_weight_grads = feed_weight_grads.astype(F32)
    *back_terms, sum_hidden, early = together(*back_terms, sum_hidden, early)
    early = far(early, "tensor")

    grad_middle, sums_two, grad_heads, out_blocks = middle_back(
        back_terms, out_parts, context_near, middle, output_cotangent, norm_two, owner_b
    )
    grad_context = exchanged_parts(grad_heads, "tensor")

    *out_blocks, early = together(*out_blocks, early)
    out_terms, out_far = summed_halves(out_blocks, "tensor")
    *grad_context, out_far, late_rows = together(*grad_context, out_far, late_rows)
    out_terms.append(far(out_far, "tensor"))
    late_rows = far(late_rows, "tensor")
    first_keep, first_send, last_keep, last_send, *back_parts, late, sum_qkv = attend_back(
        qkv,
        grad_context,
        log_totals,
        unit_parts,
        qkv_full,
        owner_a,
        owner_b,
        split,
        facts,
        heads,
    )
    first_send, last_send, late, late_rows, *rest = together(
        first_send, last_send, late, late_rows, *out_terms, *back_parts
    )
    out_terms, back_parts = rest[: len(out_terms)], rest[len(out_terms) :]
    near_rows, far_rows = back_parts[:half], back_parts[half:]
    feed_terms.append(jnp.concatenate([early, late_rows], axis=0))
    output = total([term.astype(F32) for term in (*feed_terms, middle)]) + vectors_full[5]
    output = output.astype(BF16)
    out_sums = total([term.astype(F32) for term in out_terms]).astype(BF16)
    last_keep = jnp.concatenate([last_keep, out_sums[: spread_ways // 2]], axis=2)
    last_send = jnp.concatenate([last_send, out_sums[spread_ways // 2 :]], axis=2)
    head_sums = lax.dynamic_update_slice(
        jnp.zeros((3, features), F32), sum_qkv.reshape(3, width), (0, position * width)
    )
    hidden_sums = lax.dynamic_update_slice(
        jnp.zeros((1, units * ways), F32), sum_hidden, (0, position * units)
    )
    packed = jnp.concatenate(
        [late.reshape(-1), sums_two.reshape(-1), head_sums.reshape(-1), hidden_sums.reshape(-1)]
    )
    packed = summed_everywhere(packed, ("dp",))
    far_sum = added(far_rows[0], swapped(far_rows[1], "tensor", 1))
    far_sum, first_keep, last_keep, *near_rows = together(
        far_sum, first_keep, last_keep, *near_rows
    )
    far_first = far(far_sum[: near // 2], "tensor")
    far_last = far(far_sum[near // 2 :], "tensor")
    first_keep, first_send = halved(first_keep, first_send, "dp", order_a)
    last_keep, last_send = halved(last_keep, last_send, "dp", order_b)
    first_send, last_send, far_first = together(first_send, last_send, far_first)
    while first_send.shape[0] > 1:
        first_keep, first_send = halved(first_keep, first_send, "dp", order_a)
        last_keep, last_send = halved(last_keep, last_send, "dp", order_b)
    first_send, last_send, far_last, output = together(first_send, last_send, far_last, output)
    near_terms = [near_rows[0], swapped(near_rows[1], "tensor", 1), far_first, far_last]
    input_grad = input_back(near_terms, tokens, grad_middle, norm_one)
    first_keep, last_keep, input_grad, packed = together(
        first_keep, last_keep, input_grad, packed
    )
    first_raw = halved(first_keep, first_send, "dp", order_a)[0][0].astype(F32)
    last_raw = halved(last_keep, last_send, "dp", order_b)[0][0].astype(F32)
    out_weight_grad = last_raw[:, width:]
    last_raw = last_raw[:, :width]

    packed = summed_everywhere(packed, ("tensor",), direct=True)
    by_feature = packed[: 9 * features].reshape(9, features)
    hidden_sums = packed[9 * features :]
    vectors_grad = lax.dynamic_slice_in_dim(by_feature, index * piece, piece, axis=1)
    vectors_grad = jnp.concatenate([vectors_grad[:7], vectors_grad[8:]], axis=0)
    hidden_bias_grad = lax.dynamic_slice_in_dim(hidden_sums, index * unit_piece, unit_piece)

    sum_qkv = lax.dynamic_slice_in_dim(by_feature[6:], position * width, width, axis=1)
    mine = lax.dynamic_slice_in_dim(norm_one, lax.axis_index("dp") * own, own, axis=1)
    raw = jnp.concatenate([first_raw, last_raw], axis=1).reshape(own, 3, width)
    qkv_weight_grad = mine[0][:, None, None] * raw + mine[1][:, None, None] * sum_qkv
    return (
        output,
        input_grad,
        qkv_weight_grad,
        out_weight_grad,
        feed_weight_grads[:, :units],
        feed_weight_grads[:, units:],
        vectors_grad,
        hidden_bias_grad[None, :],
    )


def solution(mesh):
    placed = (
        P(("dp", "tensor"), None),
        P(("dp", "tensor"), None),
        P("dp"),
        P("dp", None),
        P("dp", "tensor", None, None),
        P("dp", None, "tensor"),
        P("dp", "tensor"),
        P("dp", "tensor"),
        P("dp", "tensor"),
        P(None, ("dp", "tensor")),
        P(None, ("dp", "tensor")),
    )
    return jax.shard_map(
        per_device,
        mesh=mesh,
        in_specs=placed,
        out_specs=(
            P(("dp", "tensor"), None),
            P(("dp", "tensor"), None),
            P("dp", None, "tensor"),
            P("dp", "tensor"),
            P("dp", "tensor"),
            P("dp", "tensor"),
            P(None, ("dp", "tensor")),
            P(None, ("dp", "tensor")),
        ),
        check_vma=False,
    )
```

```python
import functools

import jax
import jax.numpy as jnp
from jax import lax
from jax.experimental import pallas as pl
from jax.experimental.pallas import tpu as pltpu
from jax.sharding import PartitionSpec as P

HEAD_DIM = 64
BLOCK = 64
PAIR = 2 * HEAD_DIM
SLOTS = 8
CHUNK = 512
EPS = 1e-05
NEGATIVE = -1e30
F32 = jnp.float32
BF16 = jnp.bfloat16
NT = (((1,), (1,)), ((), ()))
NN = (((1,), (0,)), ((), ()))
TN = (((0,), (0,)), ((), ()))


def matmul(left, right, dims):
    return lax.dot_general(left, right, dims, preferred_element_type=F32)


def swapped(value, axis, bit):
    count = lax.axis_size(axis)
    return lax.ppermute(value, axis, [(i, i ^ bit) for i in range(count)])


def bits_of(axis):
    count = lax.axis_size(axis)
    return [1 << b for b in range(count.bit_length() - 1)]


def together(*values):
    return lax.optimization_barrier(values)


def far(value, axis):
    return swapped(value, axis, bits_of(axis)[-1])


def gathered_parts(value, far_value, axis):
    bits = bits_of(axis)
    parts = {0: value, bits[-1]: far_value}
    for bit in reversed(bits[:-1]):
        parts.update({k | bit: swapped(p, axis, bit) for k, p in list(parts.items())})
    return [parts[k] for k in range(len(parts))]


def summed_halves(parts, axis):
    left = dict(enumerate(parts))
    terms = [parts[0]]
    for bit in bits_of(axis)[: len(parts).bit_length() - 2]:
        kept = {}
        for k in sorted(left, reverse=True):
            if k & bit == 0:
                arrived = swapped(left[k | bit], axis, bit)
                if k == 0:
                    terms.append(arrived)
                    kept[k] = None
                else:
                    kept[k] = added(left[k], arrived)
        left = kept
    return terms, left[len(parts) // 2]


def added(left, right):
    return (left.astype(F32) + right.astype(F32)).astype(BF16)


def doubled(value, axis, order):
    blocks = value[None]
    for bit in order:
        blocks = jnp.concatenate([blocks, swapped(blocks, axis, bit)], axis=0)
    return blocks


def halved(keep, send, axis, order):
    half = send.shape[0]
    arrived = swapped(send, axis, order[half.bit_length() - 1])
    rest = half // 2
    return added(keep[: half - rest], arrived[: half - rest]), added(
        keep[half - rest :], arrived[half - rest :]
    )


def block_owners(axis, order):
    count = lax.axis_size(axis)
    device = [sum(bit for b, bit in enumerate(order) if p >> b & 1) for p in range(count)]
    return lax.axis_index(axis) ^ jnp.asarray(device, jnp.int32)


def exchanged_parts(parts, axis):
    return [p if k == 0 else swapped(p, axis, k) for k, p in enumerate(parts)]


def summed_everywhere(value, axes, direct=False):
    size = value.shape[0]
    value = jnp.pad(value, (0, -size % 1024)).reshape(-1, 128)
    for axis in axes:
        if direct:
            value = total([value] + [swapped(value, axis, k) for k in range(1, lax.axis_size(axis))])
        else:
            for bit in bits_of(axis):
                value = value + swapped(value, axis, bit)
    return value.reshape(-1)[:size]


def sent_and_summed(value, axis):
    count = lax.axis_size(axis)
    blocks = value.reshape(count, value.shape[0] // count, *value.shape[1:])
    arrived = lax.all_to_all(blocks, axis, 0, 0, tiled=True)
    return jnp.sum(arrived.astype(F32), axis=0)


def attention_facts(length, position, placing, chosen):
    head = jnp.stack([length, position]).astype(jnp.int32)
    return jnp.concatenate([head, placing.reshape(-1), chosen.reshape(-1)])


class Blocks:
    def __init__(self, facts, stored, limits, heads, quarters):
        self.facts, self.stored, self.limits = facts, stored, limits
        self.heads, self.quarters = heads, quarters
        self.count = stored.shape[0]
        self.length = facts[0]
        self.last = (self.length + BLOCK - 1) // BLOCK - 1
        self.last_rows = self.length - BLOCK * self.last

    def find(self):
        per = self.count // self.quarters
        for quarter in range(self.quarters):
            start = (self.facts[1] ^ quarter) * per
            for n in range(per):
                number = self.facts[2 + start + n]
                self.stored[number] = quarter * per + n
                rows = self.length - BLOCK * number
                self.limits[quarter * per + n] = jnp.clip(rows, 0, BLOCK)

    def item(self, number):
        last = self.last
        alive = number != last
        before, behind = number - 1, number + 1
        common = [0, last, before, number, jnp.minimum(behind, self.count - 1)]
        good = [
            alive,
            alive,
            alive & (before > 0) & (before < last),
            alive & (number < last),
            alive & (behind < last),
        ]
        places = [self.stored[block] for block in common]
        lane = lax.broadcasted_iota(jnp.int32, (1, self.heads * HEAD_DIM), 1)
        added_scores = [jnp.where(flag, 0.0, NEGATIVE).astype(F32) for flag in good]
        drawn = [
            [
                self.facts[2 + self.count + (h * self.count + number) * 3 + s]
                for h in range(self.heads)
            ]
            for s in range(3)
        ]
        random = []
        for s in range(3):
            random.append([self.stored[block] for block in drawn[s]])
            row = jnp.zeros((1, self.heads * HEAD_DIM), F32)
            for h, block in enumerate(drawn[s]):
                fresh = alive & (block > 0) & (block < last) & (jnp.abs(block - number) > 1)
                for other in range(s):
                    fresh = fresh & (block != drawn[other][h])
                score = jnp.where(fresh, 0.0, NEGATIVE).astype(F32)
                row = jnp.where(lane // HEAD_DIM == h, score, row)
            added_scores.append(row)
        return places, random, added_scores


def block_rows(index):
    return pl.ds(pl.multiple_of(index * BLOCK, BLOCK), BLOCK)


def spread(rows, heads):
    lane = lax.broadcasted_iota(jnp.int32, (1, heads * HEAD_DIM), 1)
    zero = jnp.zeros_like(rows)
    return jnp.concatenate(
        [jnp.where(lane // HEAD_DIM == h, rows, zero) for h in range(heads)], axis=0
    )


def collapse(full, heads):
    lane = lax.broadcasted_iota(jnp.int32, (1, PAIR), 1)
    pieces = []
    for pair in range(heads // 2):
        cols = slice(PAIR * pair, PAIR * (pair + 1))
        even = full[2 * pair * HEAD_DIM : (2 * pair + 1) * HEAD_DIM, cols]
        odd = full[(2 * pair + 1) * HEAD_DIM : (2 * pair + 2) * HEAD_DIM, cols]
        pieces.append(jnp.where(lane < HEAD_DIM, even, odd))
    return jnp.concatenate(pieces, axis=1)


def gathered_keys(ref, start, places, random, heads):
    width = heads * HEAD_DIM
    lane = lax.broadcasted_iota(jnp.int32, (1, PAIR), 1)
    parts = [ref[block_rows(place), start : start + width] for place in places]
    for drawn in random:
        pieces = []
        for pair in range(heads // 2):
            cols = slice(start + PAIR * pair, start + PAIR * (pair + 1))
            even = ref[block_rows(drawn[2 * pair]), cols]
            odd = ref[block_rows(drawn[2 * pair + 1]), cols]
            pieces.append(jnp.where(lane < HEAD_DIM, even, odd))
        parts.append(jnp.concatenate(pieces, axis=1))
    return jnp.concatenate(parts, axis=0)


def slot(value, index):
    return value[BLOCK * index : BLOCK * (index + 1)]


def biased(scores, bias, last_rows):
    row = lax.broadcasted_iota(jnp.int32, (BLOCK, 1), 0)
    parts = [slot(scores, s) + bias[s] for s in range(SLOTS)]
    parts[1] = jnp.where(row < last_rows, parts[1], NEGATIVE)
    return parts


def total(parts):
    return functools.reduce(jnp.add, parts)


def attend_body(heads, blocks, qkv_ref, out_ref, log_ref, keep_ref):
    count = blocks.count
    stored, limits = blocks.stored, blocks.limits
    width = heads * HEAD_DIM
    scale = jnp.asarray(HEAD_DIM**-0.5, BF16)

    def item(number):
        places, random, scores = blocks.item(number)
        here = block_rows(places[3])
        queries = spread(qkv_ref[here, :width] * scale, heads)
        keys = gathered_keys(qkv_ref, width, places, random, heads)
        parts = biased(matmul(keys, queries, NT), scores, blocks.last_rows)
        top = jnp.max(functools.reduce(jnp.maximum, parts), axis=0, keepdims=True)
        weights = [jnp.exp(p - top) for p in parts]
        row_total = jnp.sum(total(weights), axis=0, keepdims=True)
        inverse = 1.0 / row_total
        probs = jnp.concatenate([(p * inverse).astype(BF16) for p in weights], axis=0)
        values = gathered_keys(qkv_ref, 2 * width, places, random, heads)
        out_ref[here, :] = collapse(matmul(probs, values, TN), heads).astype(BF16)
        log_ref[pl.ds(number, 1), :] = top + jnp.log(row_total)

    def step(group, carry):
        for part in range(10):
            item(1 + group * 10 + part)
        return carry

    lax.fori_loop(0, (count - 1) // 10, step, 0)
    for number in range(1 + (count - 1) // 10 * 10, count):
        item(number)

    row = lax.broadcasted_iota(jnp.int32, (BLOCK, 1), 0)
    per = CHUNK // BLOCK
    chunks = count // per

    def chunk_rows(chunk):
        return pl.ds(pl.multiple_of(chunk * CHUNK, CHUNK), CHUNK)

    numbers = [0, blocks.last]
    rows_of = [block_rows(stored[number]) for number in numbers]
    queries = [spread(qkv_ref[at, :width] * scale, heads) for at in rows_of]

    def scores(chunk, tops):
        at = chunk_rows(chunk)
        keys = qkv_ref[at, width : 2 * width]
        found = []
        for end in range(2):
            raw = matmul(keys, queries[end], NT)
            parts = [
                jnp.where(row < limits[chunk * per + s], slot(raw, s), NEGATIVE)
                for s in range(per)
            ]
            keep_ref[end, at, :] = jnp.concatenate(parts, axis=0)
            found.append(jnp.maximum(tops[end], functools.reduce(jnp.maximum, parts)))
        return tuple(found)

    tops = lax.fori_loop(0, chunks, scores, (jnp.full((BLOCK, width), NEGATIVE, F32),) * 2)
    tops = [jnp.max(top, axis=0, keepdims=True) for top in tops]

    def exponents(chunk, totals):
        at = chunk_rows(chunk)
        found = []
        for end in range(2):
            weights = jnp.exp(keep_ref[end, at, :] - tops[end])
            keep_ref[end, at, :] = weights
            found.append(totals[end] + total([slot(weights, s) for s in range(per)]))
        return tuple(found)

    totals = lax.fori_loop(0, chunks, exponents, (jnp.zeros((BLOCK, width), F32),) * 2)
    totals = [jnp.sum(found, axis=0, keepdims=True) for found in totals]
    inverses = [1.0 / found for found in totals]

    def contexts(chunk, sums):
        at = chunk_rows(chunk)
        values = qkv_ref[at, 2 * width :]
        return tuple(
            sums[end] + matmul((keep_ref[end, at, :] * inverses[end]).astype(BF16), values, TN)
            for end in range(2)
        )

    sums = lax.fori_loop(0, chunks, contexts, (jnp.zeros((width, width), F32),) * 2)
    for end in range(2):
        out_ref[rows_of[end], :] = collapse(sums[end], heads).astype(BF16)
        log_ref[pl.ds(numbers[end], 1), :] = tops[end] + jnp.log(totals[end])


def attend_back_body(
    heads,
    blocks,
    qkv_ref,
    grad_ref,
    log_ref,
    out_ref,
    keys_acc,
    values_acc,
    probs_ref,
    inner_ref,
):
    count = blocks.count
    stored, limits = blocks.stored, blocks.limits
    width = heads * HEAD_DIM
    scale = jnp.asarray(HEAD_DIM**-0.5, BF16)
    lane = lax.broadcasted_iota(jnp.int32, (1, PAIR), 1)
    keys_acc[...] = jnp.zeros_like(keys_acc)
    values_acc[...] = jnp.zeros_like(values_acc)

    def accumulate(acc, value, places, random):
        for s in range(5):
            acc[block_rows(places[s]), :] += slot(value, s)
        for s in range(3):
            for h in range(heads):
                cols = slice(PAIR * (h // 2), PAIR * (h // 2 + 1))
                mine = (lane < HEAD_DIM) == (h % 2 == 0)
                term = jnp.where(mine, slot(value, 5 + s)[:, cols], 0.0)
                acc[block_rows(random[s][h]), cols] += term

    def item(number):
        places, random, scores = blocks.item(number)
        here = block_rows(places[3])
        queries = spread(qkv_ref[here, :width] * scale, heads)
        grads = spread(grad_ref[here, :], heads)
        keys = gathered_keys(qkv_ref, width, places, random, heads)
        values = gathered_keys(qkv_ref, 2 * width, places, random, heads)
        log_total = log_ref[pl.ds(number, 1), :]
        parts = biased(matmul(keys, queries, NT), scores, blocks.last_rows)
        probs = [jnp.exp(p - log_total) for p in parts]
        found = matmul(values, grads, NT)
        found = [slot(found, s) for s in range(SLOTS)]
        inner = total([p * d for p, d in zip(probs, found)])
        inner = jnp.sum(inner, axis=0, keepdims=True)
        grad_scores = jnp.concatenate(
            [(p * (d - inner)).astype(BF16) for p, d in zip(probs, found)], axis=0
        )
        probs_low = jnp.concatenate([p.astype(BF16) for p in probs], axis=0)
        accumulate(values_acc, matmul(probs_low, grads, NN), places, random)
        accumulate(keys_acc, matmul(grad_scores, queries, NN), places, random)
        grad_queries = collapse(matmul(grad_scores, keys, TN), heads) * HEAD_DIM**-0.5
        out_ref[here, :width] = grad_queries.astype(BF16)

    def step(group, carry):
        for part in range(6):
            item(1 + group * 6 + part)
        return carry

    lax.fori_loop(0, (count - 1) // 6, step, 0)
    for number in range(1 + (count - 1) // 6 * 6, count):
        item(number)

    row = lax.broadcasted_iota(jnp.int32, (BLOCK, 1), 0)
    per = CHUNK // BLOCK
    chunks = count // per

    def chunk_rows(chunk):
        return pl.ds(pl.multiple_of(chunk * CHUNK, CHUNK), CHUNK)

    numbers = [0, blocks.last]
    rows_of = [block_rows(stored[number]) for number in numbers]
    queries = [spread(qkv_ref[at, :width] * scale, heads) for at in rows_of]
    grads = [spread(grad_ref[at, :], heads) for at in rows_of]
    log_rows = [log_ref[pl.ds(number, 1), :] for number in numbers]

    def first(chunk, inners):
        at = chunk_rows(chunk)
        keys = qkv_ref[at, width : 2 * width]
        values = qkv_ref[at, 2 * width :]
        sums = []
        for end in range(2):
            scores = matmul(keys, queries[end], NT)
            parts = [
                jnp.where(row < limits[chunk * per + s], slot(scores, s), NEGATIVE)
                for s in range(per)
            ]
            probs = jnp.exp(jnp.concatenate(parts, axis=0) - log_rows[end])
            found = matmul(values, grads[end], NT)
            probs_ref[end, at, :] = probs
            inner_ref[end, at, :] = found
            both = probs * found
            sums.append(inners[end] + total([slot(both, s) for s in range(per)]))
        return tuple(sums)

    inners = lax.fori_loop(0, chunks, first, (jnp.zeros((BLOCK, width), F32),) * 2)
    inners = [jnp.sum(inner, axis=0, keepdims=True) for inner in inners]

    def second(chunk, sums):
        at = chunk_rows(chunk)
        keys = qkv_ref[at, width : 2 * width]
        found, to_values, to_keys = [], values_acc[at, :], keys_acc[at, :]
        for end in range(2):
            probs = probs_ref[end, at, :]
            grad_scores = (probs * (inner_ref[end, at, :] - inners[end])).astype(BF16)
            to_values = to_values + matmul(probs.astype(BF16), grads[end], NN)
            to_keys = to_keys + matmul(grad_scores, queries[end], NN)
            found.append(sums[end] + matmul(grad_scores, keys, TN))
        out_ref[at, width : 2 * width] = to_keys.astype(BF16)
        out_ref[at, 2 * width :] = to_values.astype(BF16)
        return tuple(found)

    sums = lax.fori_loop(0, chunks, second, (jnp.zeros((width, width), F32),) * 2)
    for end in range(2):
        grad_queries = collapse(sums[end], heads) * HEAD_DIM**-0.5
        out_ref[rows_of[end], :width] = grad_queries.astype(BF16)


def in_smem():
    return pl.BlockSpec(memory_space=pltpu.SMEM)


def in_vmem():
    return pl.BlockSpec(memory_space=pltpu.VMEM)


def project_attend_kernel(heads, parts, owner_a, owner_b, facts, *refs):
    unit_refs = refs[:parts]
    first_ref, last_ref, norm_ref, bias_ref = refs[parts : parts + 4]
    *quarter_refs, kept_ref, weight_out_ref, log_ref = refs[parts + 4 : 2 * parts + 7]
    qkv_ref, weight_ref, out_ref, keep_ref, stored, limits, sems = refs[2 * parts + 7 :]
    blocks = Blocks(facts, stored, limits, heads, parts)
    blocks.find()
    count, own, split = first_ref.shape
    near = unit_refs[0].shape[0]
    rest = weight_ref.shape[1] - split
    for p in range(count):
        at = pl.ds(pl.multiple_of(owner_a[p] * own, own), own)
        weight_ref[at, :split] = first_ref[p]
        at = pl.ds(pl.multiple_of(owner_b[p] * own, own), own)
        weight_ref[at, split:] = last_ref[p, :, :rest]
    copies = [pltpu.make_async_copy(weight_ref, weight_out_ref, sems.at[0])]
    copies[0].start()
    for k, ref in enumerate(unit_refs):
        normed = ref[...].astype(F32) * norm_ref[0:1, :] + norm_ref[1:2, :]
        found = matmul(normed.astype(BF16), weight_ref[...], NN) + bias_ref[...]
        qkv_ref[near * k : near * (k + 1), :] = found.astype(BF16)
    copies.append(pltpu.make_async_copy(qkv_ref, kept_ref, sems.at[1]))
    copies[1].start()
    attend_body(heads, blocks, qkv_ref, out_ref, log_ref, keep_ref)
    for k, ref in enumerate(quarter_refs):
        part = out_ref.at[near * k : near * (k + 1), :]
        copies.append(pltpu.make_async_copy(part, ref, sems.at[2 + k]))
        copies[-1].start()
    for copy in copies:
        copy.wait()


def in_hbm():
    return pl.BlockSpec(memory_space=pltpu.HBM)


def project_attend(unit, first, last, owner_a, owner_b, norm, bias, facts, heads):
    rows = sum(value.shape[0] for value in unit)
    features = unit[0].shape[1]
    width = heads * HEAD_DIM
    log_shape = jax.ShapeDtypeStruct((rows // BLOCK, width), F32)
    quarter = [jax.ShapeDtypeStruct((value.shape[0], width), BF16) for value in unit]
    qkv = jax.ShapeDtypeStruct((rows, 3 * width), BF16)
    weight = jax.ShapeDtypeStruct((features, 3 * width), BF16)
    found = pl.pallas_call(
        functools.partial(project_attend_kernel, heads, len(unit)),
        grid=(1,),
        out_shape=[*quarter, qkv, weight, log_shape],
        in_specs=[in_smem()] * 3 + [in_vmem()] * (len(unit) + 4),
        out_specs=[in_hbm()] * (len(unit) + 2)
        + [pl.BlockSpec(log_shape.shape, lambda i: (0, 0))],
        scratch_shapes=[
            pltpu.VMEM(qkv.shape, BF16),
            pltpu.VMEM(weight.shape, BF16),
            pltpu.VMEM((rows, width), BF16),
            pltpu.VMEM((2, rows, width), F32),
            pltpu.SMEM((rows // BLOCK,), jnp.int32),
            pltpu.SMEM((rows // BLOCK,), jnp.int32),
            pltpu.SemaphoreType.DMA((len(unit) + 2,)),
        ],
        compiler_params=pltpu.CompilerParams(vmem_limit_bytes=56 << 20),
        cost_estimate=pl.CostEstimate(
            flops=20 * rows * CHUNK * width,
            bytes_accessed=20 * rows * width,
            transcendentals=rows * CHUNK * width // HEAD_DIM,
        ),
        name="project_attend",
    )(owner_a, owner_b, facts, *unit, first, last, norm, bias)
    return found[: len(unit)], *found[len(unit) :]


def place_kernel(owner, blocks_ref, out_ref):
    count, own, _ = blocks_ref.shape
    width = out_ref.shape[1]
    for p in range(count):
        at = pl.ds(pl.multiple_of(owner[p] * own, own), own)
        out_ref[at, :] = blocks_ref[p, :, -width:]


def placed_rows(blocks, owner, width):
    out = jax.ShapeDtypeStruct((blocks.shape[0] * blocks.shape[1], width), blocks.dtype)
    return pl.pallas_call(
        place_kernel,
        grid=(1,),
        out_shape=out,
        in_specs=[in_smem(), in_vmem()],
        out_specs=pl.BlockSpec(out.shape, lambda i: (0, 0)),
        name="placed_rows",
    )(owner, blocks)


def attend_back_kernel(heads, parts, owner_a, owner_b, facts, *refs):
    qkv_ref, log_ref, weight_ref = refs[:3]
    part_refs, unit_refs = refs[3 : 3 + parts], refs[3 + parts : 3 + 2 * parts]
    outs = refs[3 + 2 * parts :]
    block_outs, row_outs, late_ref, sum_ref = outs[:4], outs[4 : 4 + parts], *outs[4 + parts :][:2]
    grads_ref, grad_ref, keys_acc, values_acc, probs_ref, inner_ref = outs[6 + parts :][:6]
    raw_ref, *block_refs, rows_ref, stored, limits, sems = outs[12 + parts :]
    blocks = Blocks(facts, stored, limits, heads, parts)
    blocks.find()
    half, own, split = block_refs[0].shape
    width = weight_ref.shape[1]
    near = unit_refs[0].shape[0]
    step = 2 * TILE
    for k, ref in enumerate(part_refs):
        grads_ref[near * k : near * (k + 1), :] = ref[...]
    attend_back_body(
        heads,
        blocks,
        qkv_ref,
        grads_ref,
        log_ref,
        grad_ref,
        keys_acc,
        values_acc,
        probs_ref,
        inner_ref,
    )
    copies = []

    def leave(source, target):
        copies.append(pltpu.make_async_copy(source, target, sems.at[len(copies)]))
        copies[-1].start()

    sums = jnp.sum(grad_ref[...].astype(F32), axis=0, keepdims=True)
    sum_ref[...] = sums
    for i in range(weight_ref.shape[0] // step):
        at = slice(step * i, step * (i + 1))
        raw = total(
            [
                matmul(ref[:, at], grad_ref[near * k : near * (k + 1), :], TN)
                for k, ref in enumerate(unit_refs)
            ]
        )
        weight = weight_ref[at, :].astype(F32)
        raw_ref[at, :] = raw.astype(BF16)
        for row, value in enumerate((raw * weight, weight * sums)):
            lanes = total([value[:, 128 * c : 128 * (c + 1)] for c in range(width // 128)])
            for b in range(step // 128):
                turned = lanes[128 * b : 128 * (b + 1)].T
                found = jnp.sum(turned, axis=0, keepdims=True)
                start = step * i + 128 * b
                late_ref[row : row + 1, start : start + 128] = found
    for p in range(2 * half):
        at = pl.ds(pl.multiple_of(owner_a[p] * own, own), own)
        block_refs[p // half][p % half] = raw_ref[at, :split]
        at = pl.ds(pl.multiple_of(owner_b[p] * own, own), own)
        block_refs[2 + p // half][p % half] = raw_ref[at, split:]
    for source, target in zip(block_refs, block_outs):
        leave(source, target)
    for k in range(parts - 1, -1, -1):
        at = slice(near * k, near * (k + 1))
        rows_ref[at, :] = matmul(grad_ref[at, :], weight_ref[...], NT).astype(BF16)
        leave(rows_ref.at[at, :], row_outs[k])
    for copy in copies:
        copy.wait()


def attend_back(
    qkv, grad_context, log_totals, unit, weight, owner_a, owner_b, split, facts, heads
):
    rows, width = qkv.shape[0], heads * HEAD_DIM
    features = weight.shape[0]
    count = owner_a.shape[0]
    own = features // count
    first = jax.ShapeDtypeStruct((count // 2, own, split), BF16)
    last = jax.ShapeDtypeStruct((count // 2, own, 3 * width - split), BF16)
    small = [
        jax.ShapeDtypeStruct((2, features), F32),
        jax.ShapeDtypeStruct((1, 3 * width), F32),
    ]
    blocks = [first, first, last, last]
    return pl.pallas_call(
        functools.partial(attend_back_kernel, heads, len(unit)),
        grid=(1,),
        out_shape=[*blocks, *[like(value) for value in unit], *small],
        in_specs=[in_smem()] * 3 + [in_vmem()] * (3 + 2 * len(unit)),
        out_specs=[in_hbm()] * (4 + len(unit))
        + [pl.BlockSpec(value.shape, lambda i: (0, 0)) for value in small],
        scratch_shapes=[
            pltpu.VMEM((rows, width), BF16),
            pltpu.VMEM(qkv.shape, BF16),
            pltpu.VMEM((rows, width), F32),
            pltpu.VMEM((rows, width), F32),
            pltpu.VMEM((2, rows, width), F32),
            pltpu.VMEM((2, rows, width), F32),
            pltpu.VMEM(weight.shape, BF16),
            *[pltpu.VMEM(value.shape, BF16) for value in blocks],
            pltpu.VMEM((rows, features), BF16),
            pltpu.SMEM((rows // BLOCK,), jnp.int32),
            pltpu.SMEM((rows // BLOCK,), jnp.int32),
            pltpu.SemaphoreType.DMA((4 + len(unit),)),
        ],
        compiler_params=pltpu.CompilerParams(vmem_limit_bytes=53 << 20),
        cost_estimate=pl.CostEstimate(
            flops=40 * rows * CHUNK * width,
            bytes_accessed=40 * rows * width,
            transcendentals=rows * CHUNK * width // HEAD_DIM,
        ),
        name="attend_back",
    )(
        owner_a,
        owner_b,
        facts,
        qkv,
        log_totals,
        weight,
        *grad_context,
        *unit,
    )


TILE = 256


def gelu_and_slope(pre):
    scale = (2.0 / 3.141592653589793) ** 0.5
    square = pre * pre
    bent = jnp.tanh(scale * pre * (1.0 + 0.044715 * square))
    half = 0.5 + 0.5 * bent
    slope = half + (0.5 * scale) * pre * (1.0 - bent * bent) * (1.0 + 0.134145 * square)
    return pre * half, slope


def pick(refs):
    per = pl.num_programs(0) // len(refs)
    value = refs[0][...]
    for k, ref in enumerate(refs[1:], 1):
        value = jnp.where(pl.program_id(0) >= k * per, ref[...], value)
    return value


def put(refs, value):
    per = pl.num_programs(0) // len(refs)
    for k, ref in enumerate(refs):
        ref[...] = jnp.where(pl.program_id(0) // per == k, value, ref[...])


def feed_kernel(quarters, taken, *refs):
    normed = pick(refs[:quarters])
    grads = pick(refs[quarters : 2 * quarters])
    weight_ref, bias_ref = refs[2 * quarters : 2 * quarters + 2]
    results = refs[2 * quarters + 2 + taken :]
    units = bias_ref.shape[1]
    up = weight_ref[:, :units]
    down = weight_ref[:, units:]
    active, slope = gelu_and_slope(matmul(normed, up, NN) + bias_ref[...])
    active = active.astype(BF16)
    grad_hidden = (matmul(grads, down, NN) * slope).astype(BF16)
    put(results[:quarters], matmul(grad_hidden, up, NT).astype(BF16))
    put(results[quarters : 2 * quarters], matmul(active, down, NT).astype(BF16))
    for ref, value in zip(results[2 * quarters :], (normed, grad_hidden, grads, active)):
        ref[...] = value


def tile_specs(arrays):
    def spec(k, value):
        tiles = value.shape[0] // TILE
        return pl.BlockSpec(
            (TILE, value.shape[1]), lambda i: (jnp.clip(i - k * tiles, 0, tiles - 1), 0)
        )

    return [spec(k, value) for k, value in enumerate(arrays)]


def feed(normed, grads, weights, bias, stacks, start, quarters):
    rows, features = normed[0].shape
    units = bias.shape[1]
    here = len(normed)
    tiles = rows // TILE
    stacked = [jax.ShapeDtypeStruct((rows * quarters, n), BF16) for n in (features, units) * 2]
    found = pl.pallas_call(
        functools.partial(feed_kernel, here, len(stacks)),
        grid=(here * tiles,),
        out_shape=[like(value) for value in normed] * 2 + stacked,
        in_specs=tile_specs(normed)
        + tile_specs(grads)
        + [in_vmem(), whole_spec(bias)]
        + [pl.BlockSpec(memory_space=pl.ANY)] * len(stacks),
        out_specs=tile_specs(normed) * 2
        + [
            pl.BlockSpec((TILE, value.shape[1]), lambda i: (i + start * tiles, 0))
            for value in stacked
        ],
        input_output_aliases={2 * here + 2 + n: 2 * here + n for n in range(len(stacks))},
        compiler_params=limit(56),
        cost_estimate=pl.CostEstimate(
            flops=8 * here * rows * features * units,
            bytes_accessed=16 * here * rows * features + 4 * features * units,
            transcendentals=here * rows * units,
        ),
        name="feed",
    )(*normed, *grads, weights, bias, *stacks)
    return found[:here], found[here : 2 * here], found[2 * here :]


def feed_grads_kernel(normed_ref, grad_ref, grads_ref, active_ref, out_ref, sum_ref, acc_ref):
    units = sum_ref.shape[1]
    grad_hidden = grad_ref[...]

    @pl.when(pl.program_id(0) == 0)
    def _():
        acc_ref[...] = jnp.zeros_like(acc_ref)
        sum_ref[...] = jnp.zeros_like(sum_ref)

    acc_ref[:, :units] += matmul(normed_ref[...], grad_hidden, TN)
    acc_ref[:, units:] += matmul(grads_ref[...], active_ref[...], TN)
    sum_ref[...] += jnp.sum(grad_hidden.astype(F32), axis=0, keepdims=True)

    @pl.when(pl.program_id(0) == pl.num_programs(0) - 1)
    def _():
        out_ref[...] = acc_ref[...].astype(BF16)


def feed_grads(stacks):
    rows, features = stacks[0].shape
    units = stacks[1].shape[1]
    sums = jax.ShapeDtypeStruct((features, 2 * units), BF16)
    hidden = jax.ShapeDtypeStruct((1, units), F32)
    return pl.pallas_call(
        feed_grads_kernel,
        grid=(rows // (2 * TILE),),
        out_shape=[sums, hidden],
        in_specs=[tiled_spec(value, 2 * TILE) for value in stacks],
        out_specs=[whole_spec(sums), whole_spec(hidden)],
        scratch_shapes=[pltpu.VMEM(sums.shape, F32)],
        compiler_params=limit(62),
        cost_estimate=cost(4 * rows * features * units, 8 * rows * features),
        name="feed_grads",
    )(*stacks)


def norm_parts(rows):
    centred = rows - jnp.mean(rows, axis=-1, keepdims=True)
    inverse = lax.rsqrt(jnp.mean(centred * centred, axis=-1, keepdims=True) + EPS)
    return centred * inverse, inverse


def norm_back(grad_normed, unit, inverse, gain):
    grad_unit = grad_normed * gain
    return inverse * (
        grad_unit
        - jnp.mean(grad_unit, axis=-1, keepdims=True)
        - unit * jnp.mean(grad_unit * unit, axis=-1, keepdims=True)
    )


def whole_spec(value):
    return pl.BlockSpec(value.shape, lambda i: (0,) * value.ndim)


def tiled_spec(value, tile=TILE):
    return pl.BlockSpec((tile, value.shape[1]), lambda i: (i, 0))


def like(value, dtype=None):
    return jax.ShapeDtypeStruct(value.shape, dtype or value.dtype)


def limit(mebibytes):
    return pltpu.CompilerParams(vmem_limit_bytes=mebibytes << 20)


def cost(flops, moved):
    return pl.CostEstimate(flops=flops, bytes_accessed=moved, transcendentals=0)


def unit_kernel(rows_ref, unit_ref):
    unit_ref[...] = norm_parts(rows_ref[...].astype(F32))[0].astype(BF16)


def unit_rows(rows):
    return pl.pallas_call(
        unit_kernel,
        grid=(rows.shape[0] // TILE,),
        out_shape=like(rows),
        in_specs=[tiled_spec(rows)],
        out_specs=tiled_spec(rows),
        compiler_params=limit(62),
        cost_estimate=cost(8 * rows.size, 4 * rows.size),
        name="unit",
    )(rows)


def middle_kernel(parts, *refs):
    context_refs, out_refs = refs[:parts], refs[parts : 2 * parts]
    rows_ref, vector_ref, middle_ref, normed_ref = refs[2 * parts :]
    middle = rows_ref[...].astype(F32) + vector_ref[0:1, :]
    for context_ref, out_ref in zip(context_refs, out_refs):
        middle += matmul(context_ref[...], out_ref[...], NT)
    middle_ref[...] = middle.astype(BF16)
    unit = norm_parts(middle)[0]
    normed_ref[...] = (unit * vector_ref[1:2, :] + vector_ref[2:3, :]).astype(BF16)


def middle_rows(context, out_parts, rows, vectors):
    return pl.pallas_call(
        functools.partial(middle_kernel, len(context)),
        grid=(rows.shape[0] // TILE,),
        out_shape=[like(rows), like(rows)],
        in_specs=[tiled_spec(value) for value in context]
        + [whole_spec(value) for value in out_parts]
        + [tiled_spec(rows), whole_spec(vectors)],
        out_specs=[tiled_spec(rows), tiled_spec(rows)],
        compiler_params=limit(62),
        cost_estimate=cost(2 * rows.size * rows.shape[1], 12 * rows.size),
        name="middle",
    )(*context, *out_parts, rows, vectors)


def middle_back_kernel(terms, parts, owner, *refs):
    term_refs, out_refs = refs[:terms], refs[terms : terms + parts]
    context_refs = refs[terms + parts : terms + 2 * parts]
    middle_ref, cotangent_ref, vector_ref, grad_ref, sum_ref = refs[
        terms + 2 * parts : terms + 2 * parts + 5
    ]
    head_refs = refs[terms + 2 * parts + 5 : terms + 3 * parts + 5]
    block_refs = refs[terms + 3 * parts + 5 : -1]
    found_ref = refs[-1]
    first = pl.program_id(0) == 0
    last = pl.program_id(0) == pl.num_programs(0) - 1
    count, own, width = block_refs[0].shape
    grad_normed = total([ref[...].astype(F32) for ref in term_refs])
    unit, inverse = norm_parts(middle_ref[...].astype(F32))
    cotangent = cotangent_ref[...].astype(F32)
    grad = cotangent + norm_back(grad_normed, unit, inverse, vector_ref[1:2, :])
    low = grad.astype(BF16)
    grad_ref[...] = low
    for head_ref, out_ref in zip(head_refs, out_refs):
        head_ref[...] = matmul(low, out_ref[...], NN).astype(BF16)
    sums = [
        jnp.sum(value, axis=0, keepdims=True)
        for value in (grad_normed * unit, grad_normed, grad, cotangent)
    ]
    sums = jnp.concatenate(sums, axis=0)

    @pl.when(first)
    def _():
        sum_ref[...] = jnp.zeros_like(sum_ref)
        found_ref[...] = jnp.zeros_like(found_ref)

    sum_ref[...] += sums
    for k, context_ref in enumerate(context_refs):
        found_ref[:, k * width : (k + 1) * width] += matmul(low, context_ref[...], TN)

    @pl.when(last)
    def _():
        for k, block_ref in enumerate(block_refs):
            for p in range(count):
                at = pl.ds(pl.multiple_of(owner[p] * own, own), own)
                block_ref[p] = found_ref[at, k * width : (k + 1) * width].astype(BF16)


def middle_back(terms, out_parts, context, middle, cotangent, vectors, owner):
    rows, features = middle.shape
    width = out_parts[0].shape[1]
    parts = len(out_parts)
    count = owner.shape[0]
    sums = jax.ShapeDtypeStruct((4, features), F32)
    head = jax.ShapeDtypeStruct((rows, width), BF16)
    blocks = jax.ShapeDtypeStruct((count, features // count, width), BF16)
    found = pl.pallas_call(
        functools.partial(middle_back_kernel, len(terms), parts),
        grid=(rows // TILE,),
        out_shape=[like(middle), sums] + [head] * parts + [blocks] * parts,
        in_specs=[in_smem()]
        + [tiled_spec(value) for value in terms]
        + [whole_spec(value) for value in out_parts]
        + [tiled_spec(value) for value in context]
        + [tiled_spec(middle), tiled_spec(cotangent), whole_spec(vectors)],
        out_specs=[tiled_spec(middle), whole_spec(sums)]
        + [tiled_spec(head)] * parts
        + [whole_spec(blocks)] * parts,
        scratch_shapes=[pltpu.VMEM((features, width * parts), F32)],
        compiler_params=limit(62),
        cost_estimate=cost(4 * middle.size * features, 20 * middle.size),
        name="middle_back",
    )(owner, *terms, *out_parts, *context, middle, cotangent, vectors)
    return found[0], found[1], found[2 : 2 + parts], found[2 + parts :]


def input_back_kernel(terms, *refs):
    *term_refs, first_ref, last_ref = refs[:terms]
    rows_ref, middle_ref, vector_ref, out_ref = refs[terms:]
    half = jnp.where(pl.program_id(0) == 0, first_ref[...], last_ref[...])
    grad_normed = total([ref[...].astype(F32) for ref in term_refs]) + half.astype(F32)
    unit, inverse = norm_parts(rows_ref[...].astype(F32))
    grad = norm_back(grad_normed, unit, inverse, vector_ref[0:1, :])
    out_ref[...] = (middle_ref[...].astype(F32) + grad).astype(BF16)


def input_back(terms, rows, grad_middle, vectors):
    tile = rows.shape[0] // 2
    return pl.pallas_call(
        functools.partial(input_back_kernel, len(terms)),
        grid=(2,),
        out_shape=like(rows),
        in_specs=[tiled_spec(value, tile) for value in terms[:-2]]
        + [whole_spec(value) for value in terms[-2:]]
        + [tiled_spec(rows, tile), tiled_spec(grad_middle, tile), whole_spec(vectors)],
        out_specs=tiled_spec(rows, tile),
        compiler_params=limit(62),
        cost_estimate=cost(20 * rows.size, 14 * rows.size),
        name="input_back",
    )(*terms, rows, grad_middle, vectors)


def per_device(
    tokens,
    output_cotangent,
    lengths,
    block_place,
    random_blocks,
    qkv_weight,
    out_weight,
    up_weight,
    down_weight,
    vectors,
    hidden_bias,
):
    ways = lax.axis_size("tensor")
    spread_ways = lax.axis_size("dp")
    position = lax.axis_index("tensor")
    index = lax.axis_index("dp") * ways + position
    near = tokens.shape[0]
    rows = near * ways
    features = tokens.shape[1]
    width = qkv_weight.shape[2]
    heads = width // HEAD_DIM
    units = up_weight.shape[1]
    own = features // spread_ways
    piece = vectors.shape[1]
    unit_piece = hidden_bias.shape[1]

    small = jnp.zeros((8, features), F32)
    small = lax.dynamic_update_slice(small, vectors, (0, index * piece))
    small_hidden = jnp.zeros((1, units * ways), F32)
    small_hidden = lax.dynamic_update_slice(small_hidden, hidden_bias, (0, index * unit_piece))
    packed = jnp.concatenate([small.reshape(-1), small_hidden.reshape(-1)])
    packed = summed_everywhere(packed, ("tensor",))

    unit_near = unit_rows(tokens)
    unit_near, packed = together(unit_near, packed)
    unit_far = far(unit_near, "tensor")

    facts = attention_facts(lengths[0], position, block_place, random_blocks)

    bits = bits_of("dp")
    order_a = bits[::-1]
    order_b = bits[-1:] + bits[:1] + bits[-2:0:-1]
    owner_a = block_owners("dp", order_a)
    owner_b = block_owners("dp", order_b)
    split = 2 * width
    qkv_flat = qkv_weight.reshape(own, 3 * width)
    first_blocks = doubled(qkv_flat[:, :split], "dp", order_a)
    last_flat = jnp.concatenate([qkv_flat[:, split:], out_weight], axis=1)
    last_blocks = doubled(last_flat, "dp", order_b)
    packed = summed_everywhere(packed, ("dp",))
    feed_flat = jnp.concatenate([up_weight, down_weight], axis=1)
    piece_rows = near // 4
    first_going, next_going = output_cotangent[:piece_rows], output_cotangent[piece_rows:]
    next_going, last_going = next_going[:piece_rows], next_going[piece_rows:]
    first_going, unit_far = together(first_going, unit_far)
    cotangent_first = far(first_going, "tensor")
    feed_flat, first_blocks, last_blocks, packed, cotangent_first, next_going = together(
        feed_flat, first_blocks, last_blocks, packed, cotangent_first, next_going
    )
    cotangent_next = far(next_going, "tensor")
    feed_full = lax.all_gather(feed_flat, "dp", axis=0, tiled=True)
    unit_parts = gathered_parts(unit_near, unit_far, "tensor")

    vectors_full = packed[: 8 * features].reshape(8, features)
    hidden_full = packed[8 * features :]
    bias_query = lax.dynamic_slice_in_dim(vectors_full[6], position * width, width)
    bias_value = lax.dynamic_slice_in_dim(vectors_full[7], position * width, width)
    bias_qkv = jnp.concatenate([bias_query, jnp.zeros_like(bias_query), bias_value])[None]
    bias_hidden = lax.dynamic_slice_in_dim(hidden_full, position * units, units)[None]
    norm_one = vectors_full[:2]
    norm_two = jnp.stack([vectors_full[4], vectors_full[2], vectors_full[3]])


    last_blocks, cotangent_next = together(last_blocks, cotangent_next)
    out_group = placed_rows(last_blocks, owner_b, width)
    out_far = far(out_group, "tensor")
    last_going, out_group = together(last_going, out_group)
    cotangent_last = far(last_going, "tensor")
    *context, qkv, qkv_full, log_totals = project_attend(
        unit_parts,
        first_blocks,
        last_blocks,
        owner_a,
        owner_b,
        norm_one,
        bias_qkv,
        facts,
        heads,
    )
    context = context[0]
    *context, out_far, cotangent_last = together(*context, out_far, cotangent_last)
    cotangent_far = jnp.concatenate([cotangent_first, cotangent_next, cotangent_last], axis=0)
    grad_parts = gathered_parts(output_cotangent, cotangent_far, "tensor")

    out_parts = gathered_parts(out_group, out_far, "tensor")
    context_near = exchanged_parts(context, "tensor")
    middle, normed_two = middle_rows(context_near, out_parts, tokens, norm_two)

    half = ways // 2
    normed_far = far(normed_two, "tensor")
    normed_parts = gathered_parts(normed_two, normed_far, "tensor")
    near_back, near_out, stacks = feed(
        normed_parts[:half], grad_parts[:half], feed_full, bias_hidden, (), 0, ways
    )
    normed_far, *stacks = together(normed_far, *stacks)
    normed_parts = gathered_parts(normed_two, normed_far, "tensor")
    far_back, far_out, stacks = feed(
        normed_parts[half:], grad_parts[half:], feed_full, bias_hidden, stacks, half, ways
    )
    back_parts, feed_parts = near_back + far_back, near_out + far_out
    back_terms, far_sum = summed_halves(back_parts, "tensor")
    back_terms.append(far(far_sum, "tensor"))
    feed_sums, sum_hidden = feed_grads(stacks)
    feed_terms, feed_far = summed_halves(feed_parts, "tensor")
    early, late_rows = feed_far[: near // 2], feed_far[near // 2 :]
    feed_weight_grads = lax.psum_scatter(feed_sums, "dp", scatter_dimension=0, tiled=True)
    feed_weight_grads = feed_weight_grads.astype(F32)
    *back_terms, sum_hidden, early = together(*back_terms, sum_hidden, early)
    early = far(early, "tensor")

    grad_middle, sums_two, grad_heads, out_blocks = middle_back(
        back_terms, out_parts, context_near, middle, output_cotangent, norm_two, owner_b
    )
    grad_context = exchanged_parts(grad_heads, "tensor")

    *out_blocks, early = together(*out_blocks, early)
    out_terms, out_far = summed_halves(out_blocks, "tensor")
    *grad_context, out_far, late_rows = together(*grad_context, out_far, late_rows)
    out_terms.append(far(out_far, "tensor"))
    late_rows = far(late_rows, "tensor")
    first_keep, first_send, last_keep, last_send, *back_parts, late, sum_qkv = attend_back(
        qkv,
        grad_context,
        log_totals,
        unit_parts,
        qkv_full,
        owner_a,
        owner_b,
        split,
        facts,
        heads,
    )
    first_send, last_send, late, late_rows, *rest = together(
        first_send, last_send, late, late_rows, *out_terms, *back_parts
    )
    out_terms, back_parts = rest[: len(out_terms)], rest[len(out_terms) :]
    near_rows, far_rows = back_parts[:half], back_parts[half:]
    feed_terms.append(jnp.concatenate([early, late_rows], axis=0))
    output = total([term.astype(F32) for term in (*feed_terms, middle)]) + vectors_full[5]
    output = output.astype(BF16)
    out_sums = total([term.astype(F32) for term in out_terms]).astype(BF16)
    last_keep = jnp.concatenate([last_keep, out_sums[: spread_ways // 2]], axis=2)
    last_send = jnp.concatenate([last_send, out_sums[spread_ways // 2 :]], axis=2)
    head_sums = lax.dynamic_update_slice(
        jnp.zeros((3, features), F32), sum_qkv.reshape(3, width), (0, position * width)
    )
    hidden_sums = lax.dynamic_update_slice(
        jnp.zeros((1, units * ways), F32), sum_hidden, (0, position * units)
    )
    packed = jnp.concatenate(
        [late.reshape(-1), sums_two.reshape(-1), head_sums.reshape(-1), hidden_sums.reshape(-1)]
    )
    packed = summed_everywhere(packed, ("dp",))
    far_sum = added(far_rows[0], swapped(far_rows[1], "tensor", 1))
    far_sum, first_keep, last_keep, *near_rows = together(
        far_sum, first_keep, last_keep, *near_rows
    )
    far_first = far(far_sum[: near // 2], "tensor")
    far_last = far(far_sum[near // 2 :], "tensor")
    first_keep, first_send = halved(first_keep, first_send, "dp", order_a)
    last_keep, last_send = halved(last_keep, last_send, "dp", order_b)
    first_send, last_send, far_first = together(first_send, last_send, far_first)
    while first_send.shape[0] > 1:
        first_keep, first_send = halved(first_keep, first_send, "dp", order_a)
        last_keep, last_send = halved(last_keep, last_send, "dp", order_b)
    first_send, last_send, far_last, output = together(first_send, last_send, far_last, output)
    near_terms = [near_rows[0], swapped(near_rows[1], "tensor", 1), far_first, far_last]
    input_grad = input_back(near_terms, tokens, grad_middle, norm_one)
    first_keep, last_keep, input_grad, packed = together(
        first_keep, last_keep, input_grad, packed
    )
    first_raw = halved(first_keep, first_send, "dp", order_a)[0][0].astype(F32)
    last_raw = halved(last_keep, last_send, "dp", order_b)[0][0].astype(F32)
    out_weight_grad = last_raw[:, width:]
    last_raw = last_raw[:, :width]

    packed = summed_everywhere(packed, ("tensor",), direct=True)
    by_feature = packed[: 9 * features].reshape(9, features)
    hidden_sums = packed[9 * features :]
    vectors_grad = lax.dynamic_slice_in_dim(by_feature, index * piece, piece, axis=1)
    vectors_grad = jnp.concatenate([vectors_grad[:7], vectors_grad[8:]], axis=0)
    hidden_bias_grad = lax.dynamic_slice_in_dim(hidden_sums, index * unit_piece, unit_piece)

    sum_qkv = lax.dynamic_slice_in_dim(by_feature[6:], position * width, width, axis=1)
    mine = lax.dynamic_slice_in_dim(norm_one, lax.axis_index("dp") * own, own, axis=1)
    raw = jnp.concatenate([first_raw, last_raw], axis=1).reshape(own, 3, width)
    qkv_weight_grad = mine[0][:, None, None] * raw + mine[1][:, None, None] * sum_qkv
    return (
        output,
        input_grad,
        qkv_weight_grad,
        out_weight_grad,
        feed_weight_grads[:, :units],
        feed_weight_grads[:, units:],
        vectors_grad,
        hidden_bias_grad[None, :],
    )


def solution(mesh):
    placed = (
        P(("dp", "tensor"), None),
        P(("dp", "tensor"), None),
        P("dp"),
        P("dp", None),
        P("dp", "tensor", None, None),
        P("dp", None, "tensor"),
        P("dp", "tensor"),
        P("dp", "tensor"),
        P("dp", "tensor"),
        P(None, ("dp", "tensor")),
        P(None, ("dp", "tensor")),
    )
    return jax.shard_map(
        per_device,
        mesh=mesh,
        in_specs=placed,
        out_specs=(
            P(("dp", "tensor"), None),
            P(("dp", "tensor"), None),
            P("dp", None, "tensor"),
            P("dp", "tensor"),
            P("dp", "tensor"),
            P("dp", "tensor"),
            P(None, ("dp", "tensor")),
            P(None, ("dp", "tensor")),
        ),
        check_vma=False,
    )
```

```python
import functools

import jax
import jax.numpy as jnp
from jax import lax
from jax.experimental import pallas as pl
from jax.experimental.pallas import tpu as pltpu
from jax.sharding import PartitionSpec as P

HEAD_DIM = 64
BLOCK = 64
PAIR = 2 * HEAD_DIM
SLOTS = 8
CHUNK = 512
EPS = 1e-05
NEGATIVE = -1e30
F32 = jnp.float32
BF16 = jnp.bfloat16
NT = (((1,), (1,)), ((), ()))
NN = (((1,), (0,)), ((), ()))
TN = (((0,), (0,)), ((), ()))


def matmul(left, right, dims):
    return lax.dot_general(left, right, dims, preferred_element_type=F32)


def swapped(value, axis, bit):
    count = lax.axis_size(axis)
    return lax.ppermute(value, axis, [(i, i ^ bit) for i in range(count)])


def bits_of(axis):
    count = lax.axis_size(axis)
    return [1 << b for b in range(count.bit_length() - 1)]


def together(*values):
    return lax.optimization_barrier(values)


def far(value, axis):
    return swapped(value, axis, bits_of(axis)[-1])


def gathered_parts(value, far_value, axis):
    bits = bits_of(axis)
    parts = {0: value, bits[-1]: far_value}
    for bit in reversed(bits[:-1]):
        parts.update({k | bit: swapped(p, axis, bit) for k, p in list(parts.items())})
    return [parts[k] for k in range(len(parts))]


def summed_halves(parts, axis):
    left = dict(enumerate(parts))
    terms = [parts[0]]
    for bit in bits_of(axis)[: len(parts).bit_length() - 2]:
        kept = {}
        for k in sorted(left, reverse=True):
            if k & bit == 0:
                arrived = swapped(left[k | bit], axis, bit)
                if k == 0:
                    terms.append(arrived)
                    kept[k] = None
                else:
                    kept[k] = added(left[k], arrived)
        left = kept
    return terms, left[len(parts) // 2]


def added(left, right):
    return (left.astype(F32) + right.astype(F32)).astype(BF16)


def doubled(value, axis, order):
    blocks = value[None]
    for bit in order:
        blocks = jnp.concatenate([blocks, swapped(blocks, axis, bit)], axis=0)
    return blocks


def halved(keep, send, axis, order):
    half = send.shape[0]
    arrived = swapped(send, axis, order[half.bit_length() - 1])
    rest = half // 2
    return added(keep[: half - rest], arrived[: half - rest]), added(
        keep[half - rest :], arrived[half - rest :]
    )


def block_owners(axis, order):
    count = lax.axis_size(axis)
    device = [sum(bit for b, bit in enumerate(order) if p >> b & 1) for p in range(count)]
    return lax.axis_index(axis) ^ jnp.asarray(device, jnp.int32)


def exchanged_parts(parts, axis):
    return [p if k == 0 else swapped(p, axis, k) for k, p in enumerate(parts)]


def summed_everywhere(value, axes, direct=False):
    size = value.shape[0]
    value = jnp.pad(value, (0, -size % 1024)).reshape(-1, 128)
    for axis in axes:
        if direct:
            value = total([value] + [swapped(value, axis, k) for k in range(1, lax.axis_size(axis))])
        else:
            for bit in bits_of(axis):
                value = value + swapped(value, axis, bit)
    return value.reshape(-1)[:size]


def sent_and_summed(value, axis):
    count = lax.axis_size(axis)
    blocks = value.reshape(count, value.shape[0] // count, *value.shape[1:])
    arrived = lax.all_to_all(blocks, axis, 0, 0, tiled=True)
    return jnp.sum(arrived.astype(F32), axis=0)


def attention_facts(length, position, placing, chosen):
    head = jnp.stack([length, position]).astype(jnp.int32)
    return jnp.concatenate([head, placing.reshape(-1), chosen.reshape(-1)])


class Blocks:
    def __init__(self, facts, stored, limits, heads, quarters):
        self.facts, self.stored, self.limits = facts, stored, limits
        self.heads, self.quarters = heads, quarters
        self.count = stored.shape[0]
        self.length = facts[0]
        self.last = (self.length + BLOCK - 1) // BLOCK - 1
        self.last_rows = self.length - BLOCK * self.last

    def find(self):
        per = self.count // self.quarters
        for quarter in range(self.quarters):
            start = (self.facts[1] ^ quarter) * per
            for n in range(per):
                number = self.facts[2 + start + n]
                self.stored[number] = quarter * per + n
                rows = self.length - BLOCK * number
                self.limits[quarter * per + n] = jnp.clip(rows, 0, BLOCK)

    def item(self, number):
        last = self.last
        alive = number != last
        before, behind = number - 1, number + 1
        common = [0, last, before, number, jnp.minimum(behind, self.count - 1)]
        good = [
            alive,
            alive,
            alive & (before > 0) & (before < last),
            alive & (number < last),
            alive & (behind < last),
        ]
        places = [self.stored[block] for block in common]
        lane = lax.broadcasted_iota(jnp.int32, (1, self.heads * HEAD_DIM), 1)
        added_scores = [jnp.where(flag, 0.0, NEGATIVE).astype(F32) for flag in good]
        drawn = [
            [
                self.facts[2 + self.count + (h * self.count + number) * 3 + s]
                for h in range(self.heads)
            ]
            for s in range(3)
        ]
        random = []
        for s in range(3):
            random.append([self.stored[block] for block in drawn[s]])
            row = jnp.zeros((1, self.heads * HEAD_DIM), F32)
            for h, block in enumerate(drawn[s]):
                fresh = alive & (block > 0) & (block < last) & (jnp.abs(block - number) > 1)
                for other in range(s):
                    fresh = fresh & (block != drawn[other][h])
                score = jnp.where(fresh, 0.0, NEGATIVE).astype(F32)
                row = jnp.where(lane // HEAD_DIM == h, score, row)
            added_scores.append(row)
        return places, random, added_scores


def block_rows(index):
    return pl.ds(pl.multiple_of(index * BLOCK, BLOCK), BLOCK)


def spread(rows, heads):
    lane = lax.broadcasted_iota(jnp.int32, (1, heads * HEAD_DIM), 1)
    zero = jnp.zeros_like(rows)
    return jnp.concatenate(
        [jnp.where(lane // HEAD_DIM == h, rows, zero) for h in range(heads)], axis=0
    )


def collapse(full, heads):
    lane = lax.broadcasted_iota(jnp.int32, (1, PAIR), 1)
    pieces = []
    for pair in range(heads // 2):
        cols = slice(PAIR * pair, PAIR * (pair + 1))
        even = full[2 * pair * HEAD_DIM : (2 * pair + 1) * HEAD_DIM, cols]
        odd = full[(2 * pair + 1) * HEAD_DIM : (2 * pair + 2) * HEAD_DIM, cols]
        pieces.append(jnp.where(lane < HEAD_DIM, even, odd))
    return jnp.concatenate(pieces, axis=1)


def gathered_keys(ref, start, places, random, heads):
    width = heads * HEAD_DIM
    lane = lax.broadcasted_iota(jnp.int32, (1, PAIR), 1)
    parts = [ref[block_rows(place), start : start + width] for place in places]
    for drawn in random:
        pieces = []
        for pair in range(heads // 2):
            cols = slice(start + PAIR * pair, start + PAIR * (pair + 1))
            even = ref[block_rows(drawn[2 * pair]), cols]
            odd = ref[block_rows(drawn[2 * pair + 1]), cols]
            pieces.append(jnp.where(lane < HEAD_DIM, even, odd))
        parts.append(jnp.concatenate(pieces, axis=1))
    return jnp.concatenate(parts, axis=0)


def slot(value, index):
    return value[BLOCK * index : BLOCK * (index + 1)]


def biased(scores, bias, last_rows):
    row = lax.broadcasted_iota(jnp.int32, (BLOCK, 1), 0)
    parts = [slot(scores, s) + bias[s] for s in range(SLOTS)]
    parts[1] = jnp.where(row < last_rows, parts[1], NEGATIVE)
    return parts


def total(parts):
    return functools.reduce(jnp.add, parts)


def attend_body(heads, blocks, qkv_ref, out_ref, log_ref, keep_ref):
    count = blocks.count
    stored, limits = blocks.stored, blocks.limits
    width = heads * HEAD_DIM
    scale = jnp.asarray(HEAD_DIM**-0.5, BF16)

    def item(number):
        places, random, scores = blocks.item(number)
        here = block_rows(places[3])
        queries = spread(qkv_ref[here, :width] * scale, heads)
        keys = gathered_keys(qkv_ref, width, places, random, heads)
        parts = biased(matmul(keys, queries, NT), scores, blocks.last_rows)
        top = jnp.max(functools.reduce(jnp.maximum, parts), axis=0, keepdims=True)
        weights = [jnp.exp(p - top) for p in parts]
        row_total = jnp.sum(total(weights), axis=0, keepdims=True)
        inverse = 1.0 / row_total
        probs = jnp.concatenate([(p * inverse).astype(BF16) for p in weights], axis=0)
        values = gathered_keys(qkv_ref, 2 * width, places, random, heads)
        out_ref[here, :] = collapse(matmul(probs, values, TN), heads).astype(BF16)
        log_ref[pl.ds(number, 1), :] = top + jnp.log(row_total)

    def step(group, carry):
        for part in range(10):
            item(1 + group * 10 + part)
        return carry

    lax.fori_loop(0, (count - 1) // 10, step, 0)
    for number in range(1 + (count - 1) // 10 * 10, count):
        item(number)

    row = lax.broadcasted_iota(jnp.int32, (BLOCK, 1), 0)
    per = CHUNK // BLOCK
    chunks = count // per

    def chunk_rows(chunk):
        return pl.ds(pl.multiple_of(chunk * CHUNK, CHUNK), CHUNK)

    numbers = [0, blocks.last]
    rows_of = [block_rows(stored[number]) for number in numbers]
    queries = [spread(qkv_ref[at, :width] * scale, heads) for at in rows_of]

    def scores(chunk, tops):
        at = chunk_rows(chunk)
        keys = qkv_ref[at, width : 2 * width]
        found = []
        for end in range(2):
            raw = matmul(keys, queries[end], NT)
            parts = [
                jnp.where(row < limits[chunk * per + s], slot(raw, s), NEGATIVE)
                for s in range(per)
            ]
            keep_ref[end, at, :] = jnp.concatenate(parts, axis=0)
            found.append(jnp.maximum(tops[end], functools.reduce(jnp.maximum, parts)))
        return tuple(found)

    tops = lax.fori_loop(0, chunks, scores, (jnp.full((BLOCK, width), NEGATIVE, F32),) * 2)
    tops = [jnp.max(top, axis=0, keepdims=True) for top in tops]

    def exponents(chunk, totals):
        at = chunk_rows(chunk)
        found = []
        for end in range(2):
            weights = jnp.exp(keep_ref[end, at, :] - tops[end])
            keep_ref[end, at, :] = weights
            found.append(totals[end] + total([slot(weights, s) for s in range(per)]))
        return tuple(found)

    totals = lax.fori_loop(0, chunks, exponents, (jnp.zeros((BLOCK, width), F32),) * 2)
    totals = [jnp.sum(found, axis=0, keepdims=True) for found in totals]
    inverses = [1.0 / found for found in totals]

    def contexts(chunk, sums):
        at = chunk_rows(chunk)
        values = qkv_ref[at, 2 * width :]
        return tuple(
            sums[end] + matmul((keep_ref[end, at, :] * inverses[end]).astype(BF16), values, TN)
            for end in range(2)
        )

    sums = lax.fori_loop(0, chunks, contexts, (jnp.zeros((width, width), F32),) * 2)
    for end in range(2):
        out_ref[rows_of[end], :] = collapse(sums[end], heads).astype(BF16)
        log_ref[pl.ds(numbers[end], 1), :] = tops[end] + jnp.log(totals[end])


def attend_back_body(
    heads,
    blocks,
    qkv_ref,
    grad_ref,
    log_ref,
    out_ref,
    keys_acc,
    values_acc,
    probs_ref,
    inner_ref,
):
    count = blocks.count
    stored, limits = blocks.stored, blocks.limits
    width = heads * HEAD_DIM
    scale = jnp.asarray(HEAD_DIM**-0.5, BF16)
    lane = lax.broadcasted_iota(jnp.int32, (1, PAIR), 1)
    keys_acc[...] = jnp.zeros_like(keys_acc)
    values_acc[...] = jnp.zeros_like(values_acc)

    def accumulate(acc, value, places, random):
        for s in range(5):
            acc[block_rows(places[s]), :] += slot(value, s)
        for s in range(3):
            for h in range(heads):
                cols = slice(PAIR * (h // 2), PAIR * (h // 2 + 1))
                mine = (lane < HEAD_DIM) == (h % 2 == 0)
                term = jnp.where(mine, slot(value, 5 + s)[:, cols], 0.0)
                acc[block_rows(random[s][h]), cols] += term

    def item(number):
        places, random, scores = blocks.item(number)
        here = block_rows(places[3])
        queries = spread(qkv_ref[here, :width] * scale, heads)
        grads = spread(grad_ref[here, :], heads)
        keys = gathered_keys(qkv_ref, width, places, random, heads)
        values = gathered_keys(qkv_ref, 2 * width, places, random, heads)
        log_total = log_ref[pl.ds(number, 1), :]
        parts = biased(matmul(keys, queries, NT), scores, blocks.last_rows)
        probs = [jnp.exp(p - log_total) for p in parts]
        found = matmul(values, grads, NT)
        found = [slot(found, s) for s in range(SLOTS)]
        inner = total([p * d for p, d in zip(probs, found)])
        inner = jnp.sum(inner, axis=0, keepdims=True)
        grad_scores = jnp.concatenate(
            [(p * (d - inner)).astype(BF16) for p, d in zip(probs, found)], axis=0
        )
        probs_low = jnp.concatenate([p.astype(BF16) for p in probs], axis=0)
        accumulate(values_acc, matmul(probs_low, grads, NN), places, random)
        accumulate(keys_acc, matmul(grad_scores, queries, NN), places, random)
        grad_queries = collapse(matmul(grad_scores, keys, TN), heads) * HEAD_DIM**-0.5
        out_ref[here, :width] = grad_queries.astype(BF16)

    def step(group, carry):
        for part in range(6):
            item(1 + group * 6 + part)
        return carry

    lax.fori_loop(0, (count - 1) // 6, step, 0)
    for number in range(1 + (count - 1) // 6 * 6, count):
        item(number)

    row = lax.broadcasted_iota(jnp.int32, (BLOCK, 1), 0)
    per = CHUNK // BLOCK
    chunks = count // per

    def chunk_rows(chunk):
        return pl.ds(pl.multiple_of(chunk * CHUNK, CHUNK), CHUNK)

    numbers = [0, blocks.last]
    rows_of = [block_rows(stored[number]) for number in numbers]
    queries = [spread(qkv_ref[at, :width] * scale, heads) for at in rows_of]
    grads = [spread(grad_ref[at, :], heads) for at in rows_of]
    log_rows = [log_ref[pl.ds(number, 1), :] for number in numbers]

    def first(chunk, inners):
        at = chunk_rows(chunk)
        keys = qkv_ref[at, width : 2 * width]
        values = qkv_ref[at, 2 * width :]
        sums = []
        for end in range(2):
            scores = matmul(keys, queries[end], NT)
            parts = [
                jnp.where(row < limits[chunk * per + s], slot(scores, s), NEGATIVE)
                for s in range(per)
            ]
            probs = jnp.exp(jnp.concatenate(parts, axis=0) - log_rows[end])
            found = matmul(values, grads[end], NT)
            probs_ref[end, at, :] = probs
            inner_ref[end, at, :] = found
            both = probs * found
            sums.append(inners[end] + total([slot(both, s) for s in range(per)]))
        return tuple(sums)

    inners = lax.fori_loop(0, chunks, first, (jnp.zeros((BLOCK, width), F32),) * 2)
    inners = [jnp.sum(inner, axis=0, keepdims=True) for inner in inners]

    def second(chunk, sums):
        at = chunk_rows(chunk)
        keys = qkv_ref[at, width : 2 * width]
        found, to_values, to_keys = [], values_acc[at, :], keys_acc[at, :]
        for end in range(2):
            probs = probs_ref[end, at, :]
            grad_scores = (probs * (inner_ref[end, at, :] - inners[end])).astype(BF16)
            to_values = to_values + matmul(probs.astype(BF16), grads[end], NN)
            to_keys = to_keys + matmul(grad_scores, queries[end], NN)
            found.append(sums[end] + matmul(grad_scores, keys, TN))
        out_ref[at, width : 2 * width] = to_keys.astype(BF16)
        out_ref[at, 2 * width :] = to_values.astype(BF16)
        return tuple(found)

    sums = lax.fori_loop(0, chunks, second, (jnp.zeros((width, width), F32),) * 2)
    for end in range(2):
        grad_queries = collapse(sums[end], heads) * HEAD_DIM**-0.5
        out_ref[rows_of[end], :width] = grad_queries.astype(BF16)


def in_smem():
    return pl.BlockSpec(memory_space=pltpu.SMEM)


def in_vmem():
    return pl.BlockSpec(memory_space=pltpu.VMEM)


def project_attend_kernel(heads, parts, owner_a, owner_b, facts, *refs):
    unit_refs = refs[:parts]
    first_ref, last_ref, norm_ref, bias_ref = refs[parts : parts + 4]
    *quarter_refs, kept_ref, weight_out_ref, log_ref = refs[parts + 4 : 2 * parts + 7]
    qkv_ref, weight_ref, out_ref, keep_ref, stored, limits, sems = refs[2 * parts + 7 :]
    blocks = Blocks(facts, stored, limits, heads, parts)
    blocks.find()
    count, own, split = first_ref.shape
    near = unit_refs[0].shape[0]
    rest = weight_ref.shape[1] - split
    for p in range(count):
        at = pl.ds(pl.multiple_of(owner_a[p] * own, own), own)
        weight_ref[at, :split] = first_ref[p]
        at = pl.ds(pl.multiple_of(owner_b[p] * own, own), own)
        weight_ref[at, split:] = last_ref[p, :, :rest]
    copies = [pltpu.make_async_copy(weight_ref, weight_out_ref, sems.at[0])]
    copies[0].start()
    for k, ref in enumerate(unit_refs):
        normed = ref[...].astype(F32) * norm_ref[0:1, :] + norm_ref[1:2, :]
        found = matmul(normed.astype(BF16), weight_ref[...], NN) + bias_ref[...]
        qkv_ref[near * k : near * (k + 1), :] = found.astype(BF16)
    copies.append(pltpu.make_async_copy(qkv_ref, kept_ref, sems.at[1]))
    copies[1].start()
    attend_body(heads, blocks, qkv_ref, out_ref, log_ref, keep_ref)
    for k, ref in enumerate(quarter_refs):
        part = out_ref.at[near * k : near * (k + 1), :]
        copies.append(pltpu.make_async_copy(part, ref, sems.at[2 + k]))
        copies[-1].start()
    for copy in copies:
        copy.wait()


def in_hbm():
    return pl.BlockSpec(memory_space=pltpu.HBM)


def project_attend(unit, first, last, owner_a, owner_b, norm, bias, facts, heads):
    rows = sum(value.shape[0] for value in unit)
    features = unit[0].shape[1]
    width = heads * HEAD_DIM
    log_shape = jax.ShapeDtypeStruct((rows // BLOCK, width), F32)
    quarter = [jax.ShapeDtypeStruct((value.shape[0], width), BF16) for value in unit]
    qkv = jax.ShapeDtypeStruct((rows, 3 * width), BF16)
    weight = jax.ShapeDtypeStruct((features, 3 * width), BF16)
    found = pl.pallas_call(
        functools.partial(project_attend_kernel, heads, len(unit)),
        grid=(1,),
        out_shape=[*quarter, qkv, weight, log_shape],
        in_specs=[in_smem()] * 3 + [in_vmem()] * (len(unit) + 4),
        out_specs=[in_hbm()] * (len(unit) + 2)
        + [pl.BlockSpec(log_shape.shape, lambda i: (0, 0))],
        scratch_shapes=[
            pltpu.VMEM(qkv.shape, BF16),
            pltpu.VMEM(weight.shape, BF16),
            pltpu.VMEM((rows, width), BF16),
            pltpu.VMEM((2, rows, width), F32),
            pltpu.SMEM((rows // BLOCK,), jnp.int32),
            pltpu.SMEM((rows // BLOCK,), jnp.int32),
            pltpu.SemaphoreType.DMA((len(unit) + 2,)),
        ],
        compiler_params=pltpu.CompilerParams(vmem_limit_bytes=56 << 20),
        cost_estimate=pl.CostEstimate(
            flops=20 * rows * CHUNK * width,
            bytes_accessed=20 * rows * width,
            transcendentals=rows * CHUNK * width // HEAD_DIM,
        ),
        name="project_attend",
    )(owner_a, owner_b, facts, *unit, first, last, norm, bias)
    return found[: len(unit)], *found[len(unit) :]


def place_kernel(owner, blocks_ref, out_ref):
    count, own, _ = blocks_ref.shape
    width = out_ref.shape[1]
    for p in range(count):
        at = pl.ds(pl.multiple_of(owner[p] * own, own), own)
        out_ref[at, :] = blocks_ref[p, :, -width:]


def placed_rows(blocks, owner, width):
    out = jax.ShapeDtypeStruct((blocks.shape[0] * blocks.shape[1], width), blocks.dtype)
    return pl.pallas_call(
        place_kernel,
        grid=(1,),
        out_shape=out,
        in_specs=[in_smem(), in_vmem()],
        out_specs=pl.BlockSpec(out.shape, lambda i: (0, 0)),
        name="placed_rows",
    )(owner, blocks)


def attend_back_kernel(heads, parts, owner_a, owner_b, facts, *refs):
    qkv_ref, log_ref, weight_ref = refs[:3]
    part_refs, unit_refs = refs[3 : 3 + parts], refs[3 + parts : 3 + 2 * parts]
    outs = refs[3 + 2 * parts :]
    block_outs, row_outs, late_ref, sum_ref = outs[:4], outs[4 : 4 + parts], *outs[4 + parts :][:2]
    grads_ref, grad_ref, keys_acc, values_acc, probs_ref, inner_ref = outs[6 + parts :][:6]
    raw_ref, *block_refs, rows_ref, stored, limits, sems = outs[12 + parts :]
    blocks = Blocks(facts, stored, limits, heads, parts)
    blocks.find()
    half, own, split = block_refs[0].shape
    width = weight_ref.shape[1]
    near = unit_refs[0].shape[0]
    step = 2 * TILE
    for k, ref in enumerate(part_refs):
        grads_ref[near * k : near * (k + 1), :] = ref[...]
    attend_back_body(
        heads,
        blocks,
        qkv_ref,
        grads_ref,
        log_ref,
        grad_ref,
        keys_acc,
        values_acc,
        probs_ref,
        inner_ref,
    )
    copies = []

    def leave(source, target):
        copies.append(pltpu.make_async_copy(source, target, sems.at[len(copies)]))
        copies[-1].start()

    sums = jnp.sum(grad_ref[...].astype(F32), axis=0, keepdims=True)
    sum_ref[...] = sums
    for i in range(weight_ref.shape[0] // step):
        at = slice(step * i, step * (i + 1))
        raw = total(
            [
                matmul(ref[:, at], grad_ref[near * k : near * (k + 1), :], TN)
                for k, ref in enumerate(unit_refs)
            ]
        )
        weight = weight_ref[at, :].astype(F32)
        raw_ref[at, :] = raw.astype(BF16)
        for row, value in enumerate((raw * weight, weight * sums)):
            lanes = total([value[:, 128 * c : 128 * (c + 1)] for c in range(width // 128)])
            for b in range(step // 128):
                turned = lanes[128 * b : 128 * (b + 1)].T
                found = jnp.sum(turned, axis=0, keepdims=True)
                start = step * i + 128 * b
                late_ref[row : row + 1, start : start + 128] = found
    for p in range(2 * half):
        at = pl.ds(pl.multiple_of(owner_a[p] * own, own), own)
        block_refs[p // half][p % half] = raw_ref[at, :split]
        at = pl.ds(pl.multiple_of(owner_b[p] * own, own), own)
        block_refs[2 + p // half][p % half] = raw_ref[at, split:]
    for source, target in zip(block_refs, block_outs):
        leave(source, target)
    for k in range(parts - 1, -1, -1):
        at = slice(near * k, near * (k + 1))
        rows_ref[at, :] = matmul(grad_ref[at, :], weight_ref[...], NT).astype(BF16)
        leave(rows_ref.at[at, :], row_outs[k])
    for copy in copies:
        copy.wait()


def attend_back(
    qkv, grad_context, log_totals, unit, weight, owner_a, owner_b, split, facts, heads
):
    rows, width = qkv.shape[0], heads * HEAD_DIM
    features = weight.shape[0]
    count = owner_a.shape[0]
    own = features // count
    first = jax.ShapeDtypeStruct((count // 2, own, split), BF16)
    last = jax.ShapeDtypeStruct((count // 2, own, 3 * width - split), BF16)
    small = [
        jax.ShapeDtypeStruct((2, features), F32),
        jax.ShapeDtypeStruct((1, 3 * width), F32),
    ]
    blocks = [first, first, last, last]
    return pl.pallas_call(
        functools.partial(attend_back_kernel, heads, len(unit)),
        grid=(1,),
        out_shape=[*blocks, *[like(value) for value in unit], *small],
        in_specs=[in_smem()] * 3 + [in_vmem()] * (3 + 2 * len(unit)),
        out_specs=[in_hbm()] * (4 + len(unit))
        + [pl.BlockSpec(value.shape, lambda i: (0, 0)) for value in small],
        scratch_shapes=[
            pltpu.VMEM((rows, width), BF16),
            pltpu.VMEM(qkv.shape, BF16),
            pltpu.VMEM((rows, width), F32),
            pltpu.VMEM((rows, width), F32),
            pltpu.VMEM((2, rows, width), F32),
            pltpu.VMEM((2, rows, width), F32),
            pltpu.VMEM(weight.shape, BF16),
            *[pltpu.VMEM(value.shape, BF16) for value in blocks],
            pltpu.VMEM((rows, features), BF16),
            pltpu.SMEM((rows // BLOCK,), jnp.int32),
            pltpu.SMEM((rows // BLOCK,), jnp.int32),
            pltpu.SemaphoreType.DMA((4 + len(unit),)),
        ],
        compiler_params=pltpu.CompilerParams(vmem_limit_bytes=53 << 20),
        cost_estimate=pl.CostEstimate(
            flops=40 * rows * CHUNK * width,
            bytes_accessed=40 * rows * width,
            transcendentals=rows * CHUNK * width // HEAD_DIM,
        ),
        name="attend_back",
    )(
        owner_a,
        owner_b,
        facts,
        qkv,
        log_totals,
        weight,
        *grad_context,
        *unit,
    )


TILE = 256


def gelu_and_slope(pre):
    scale = (2.0 / 3.141592653589793) ** 0.5
    square = pre * pre
    bent = jnp.tanh(scale * pre * (1.0 + 0.044715 * square))
    half = 0.5 + 0.5 * bent
    slope = half + (0.5 * scale) * pre * (1.0 - bent * bent) * (1.0 + 0.134145 * square)
    return pre * half, slope


def pick(refs):
    per = pl.num_programs(0) // len(refs)
    value = refs[0][...]
    for k, ref in enumerate(refs[1:], 1):
        value = jnp.where(pl.program_id(0) >= k * per, ref[...], value)
    return value


def put(refs, value):
    per = pl.num_programs(0) // len(refs)
    for k, ref in enumerate(refs):
        ref[...] = jnp.where(pl.program_id(0) // per == k, value, ref[...])


def feed_kernel(quarters, taken, *refs):
    normed = pick(refs[:quarters])
    grads = pick(refs[quarters : 2 * quarters])
    weight_ref, bias_ref = refs[2 * quarters : 2 * quarters + 2]
    results = refs[2 * quarters + 2 + taken :]
    units = bias_ref.shape[1]
    up = weight_ref[:, :units]
    down = weight_ref[:, units:]
    active, slope = gelu_and_slope(matmul(normed, up, NN) + bias_ref[...])
    active = active.astype(BF16)
    grad_hidden = (matmul(grads, down, NN) * slope).astype(BF16)
    put(results[:quarters], matmul(grad_hidden, up, NT).astype(BF16))
    put(results[quarters : 2 * quarters], matmul(active, down, NT).astype(BF16))
    for ref, value in zip(results[2 * quarters :], (normed, grad_hidden, grads, active)):
        ref[...] = value


def tile_specs(arrays):
    def spec(k, value):
        tiles = value.shape[0] // TILE
        return pl.BlockSpec(
            (TILE, value.shape[1]), lambda i: (jnp.clip(i - k * tiles, 0, tiles - 1), 0)
        )

    return [spec(k, value) for k, value in enumerate(arrays)]


def feed(normed, grads, weights, bias, stacks, start, quarters):
    rows, features = normed[0].shape
    units = bias.shape[1]
    here = len(normed)
    tiles = rows // TILE
    stacked = [jax.ShapeDtypeStruct((rows * quarters, n), BF16) for n in (features, units) * 2]
    found = pl.pallas_call(
        functools.partial(feed_kernel, here, len(stacks)),
        grid=(here * tiles,),
        out_shape=[like(value) for value in normed] * 2 + stacked,
        in_specs=tile_specs(normed)
        + tile_specs(grads)
        + [in_vmem(), whole_spec(bias)]
        + [pl.BlockSpec(memory_space=pl.ANY)] * len(stacks),
        out_specs=tile_specs(normed) * 2
        + [
            pl.BlockSpec((TILE, value.shape[1]), lambda i: (i + start * tiles, 0))
            for value in stacked
        ],
        input_output_aliases={2 * here + 2 + n: 2 * here + n for n in range(len(stacks))},
        compiler_params=limit(56),
        cost_estimate=pl.CostEstimate(
            flops=8 * here * rows * features * units,
            bytes_accessed=16 * here * rows * features + 4 * features * units,
            transcendentals=here * rows * units,
        ),
        name="feed",
    )(*normed, *grads, weights, bias, *stacks)
    return found[:here], found[here : 2 * here], found[2 * here :]


def feed_grads_kernel(normed_ref, grad_ref, grads_ref, active_ref, out_ref, sum_ref, acc_ref):
    units = sum_ref.shape[1]
    grad_hidden = grad_ref[...]

    @pl.when(pl.program_id(0) == 0)
    def _():
        acc_ref[...] = jnp.zeros_like(acc_ref)
        sum_ref[...] = jnp.zeros_like(sum_ref)

    acc_ref[:, :units] += matmul(normed_ref[...], grad_hidden, TN)
    acc_ref[:, units:] += matmul(grads_ref[...], active_ref[...], TN)
    sum_ref[...] += jnp.sum(grad_hidden.astype(F32), axis=0, keepdims=True)

    @pl.when(pl.program_id(0) == pl.num_programs(0) - 1)
    def _():
        out_ref[...] = acc_ref[...].astype(BF16)


def feed_grads(stacks):
    rows, features = stacks[0].shape
    units = stacks[1].shape[1]
    sums = jax.ShapeDtypeStruct((features, 2 * units), BF16)
    hidden = jax.ShapeDtypeStruct((1, units), F32)
    return pl.pallas_call(
        feed_grads_kernel,
        grid=(rows // (2 * TILE),),
        out_shape=[sums, hidden],
        in_specs=[tiled_spec(value, 2 * TILE) for value in stacks],
        out_specs=[whole_spec(sums), whole_spec(hidden)],
        scratch_shapes=[pltpu.VMEM(sums.shape, F32)],
        compiler_params=limit(62),
        cost_estimate=cost(4 * rows * features * units, 8 * rows * features),
        name="feed_grads",
    )(*stacks)


def norm_parts(rows):
    centred = rows - jnp.mean(rows, axis=-1, keepdims=True)
    inverse = lax.rsqrt(jnp.mean(centred * centred, axis=-1, keepdims=True) + EPS)
    return centred * inverse, inverse


def norm_back(grad_normed, unit, inverse, gain):
    grad_unit = grad_normed * gain
    return inverse * (
        grad_unit
        - jnp.mean(grad_unit, axis=-1, keepdims=True)
        - unit * jnp.mean(grad_unit * unit, axis=-1, keepdims=True)
    )


def whole_spec(value):
    return pl.BlockSpec(value.shape, lambda i: (0,) * value.ndim)


def tiled_spec(value, tile=TILE):
    return pl.BlockSpec((tile, value.shape[1]), lambda i: (i, 0))


def like(value, dtype=None):
    return jax.ShapeDtypeStruct(value.shape, dtype or value.dtype)


def limit(mebibytes):
    return pltpu.CompilerParams(vmem_limit_bytes=mebibytes << 20)


def cost(flops, moved):
    return pl.CostEstimate(flops=flops, bytes_accessed=moved, transcendentals=0)


def unit_kernel(rows_ref, unit_ref):
    unit_ref[...] = norm_parts(rows_ref[...].astype(F32))[0].astype(BF16)


def unit_rows(rows):
    return pl.pallas_call(
        unit_kernel,
        grid=(rows.shape[0] // TILE,),
        out_shape=like(rows),
        in_specs=[tiled_spec(rows)],
        out_specs=tiled_spec(rows),
        compiler_params=limit(62),
        cost_estimate=cost(8 * rows.size, 4 * rows.size),
        name="unit",
    )(rows)


def middle_kernel(parts, *refs):
    context_refs, out_refs = refs[:parts], refs[parts : 2 * parts]
    rows_ref, vector_ref, middle_ref, normed_ref = refs[2 * parts :]
    middle = rows_ref[...].astype(F32) + vector_ref[0:1, :]
    for context_ref, out_ref in zip(context_refs, out_refs):
        middle += matmul(context_ref[...], out_ref[...], NT)
    middle_ref[...] = middle.astype(BF16)
    unit = norm_parts(middle)[0]
    normed_ref[...] = (unit * vector_ref[1:2, :] + vector_ref[2:3, :]).astype(BF16)


def middle_rows(context, out_parts, rows, vectors):
    return pl.pallas_call(
        functools.partial(middle_kernel, len(context)),
        grid=(rows.shape[0] // TILE,),
        out_shape=[like(rows), like(rows)],
        in_specs=[tiled_spec(value) for value in context]
        + [whole_spec(value) for value in out_parts]
        + [tiled_spec(rows), whole_spec(vectors)],
        out_specs=[tiled_spec(rows), tiled_spec(rows)],
        compiler_params=limit(62),
        cost_estimate=cost(2 * rows.size * rows.shape[1], 12 * rows.size),
        name="middle",
    )(*context, *out_parts, rows, vectors)


def middle_back_kernel(terms, parts, owner, *refs):
    term_refs, out_refs = refs[:terms], refs[terms : terms + parts]
    context_refs = refs[terms + parts : terms + 2 * parts]
    middle_ref, cotangent_ref, vector_ref, grad_ref, sum_ref = refs[
        terms + 2 * parts : terms + 2 * parts + 5
    ]
    head_refs = refs[terms + 2 * parts + 5 : terms + 3 * parts + 5]
    block_refs = refs[terms + 3 * parts + 5 : -1]
    found_ref = refs[-1]
    first = pl.program_id(0) == 0
    last = pl.program_id(0) == pl.num_programs(0) - 1
    count, own, width = block_refs[0].shape
    grad_normed = total([ref[...].astype(F32) for ref in term_refs])
    unit, inverse = norm_parts(middle_ref[...].astype(F32))
    cotangent = cotangent_ref[...].astype(F32)
    grad = cotangent + norm_back(grad_normed, unit, inverse, vector_ref[1:2, :])
    low = grad.astype(BF16)
    grad_ref[...] = low
    for head_ref, out_ref in zip(head_refs, out_refs):
        head_ref[...] = matmul(low, out_ref[...], NN).astype(BF16)
    sums = [
        jnp.sum(value, axis=0, keepdims=True)
        for value in (grad_normed * unit, grad_normed, grad, cotangent)
    ]
    sums = jnp.concatenate(sums, axis=0)

    @pl.when(first)
    def _():
        sum_ref[...] = jnp.zeros_like(sum_ref)
        found_ref[...] = jnp.zeros_like(found_ref)

    sum_ref[...] += sums
    for k, context_ref in enumerate(context_refs):
        found_ref[:, k * width : (k + 1) * width] += matmul(low, context_ref[...], TN)

    @pl.when(last)
    def _():
        for k, block_ref in enumerate(block_refs):
            for p in range(count):
                at = pl.ds(pl.multiple_of(owner[p] * own, own), own)
                block_ref[p] = found_ref[at, k * width : (k + 1) * width].astype(BF16)


def middle_back(terms, out_parts, context, middle, cotangent, vectors, owner):
    rows, features = middle.shape
    width = out_parts[0].shape[1]
    parts = len(out_parts)
    count = owner.shape[0]
    sums = jax.ShapeDtypeStruct((4, features), F32)
    head = jax.ShapeDtypeStruct((rows, width), BF16)
    blocks = jax.ShapeDtypeStruct((count, features // count, width), BF16)
    found = pl.pallas_call(
        functools.partial(middle_back_kernel, len(terms), parts),
        grid=(rows // TILE,),
        out_shape=[like(middle), sums] + [head] * parts + [blocks] * parts,
        in_specs=[in_smem()]
        + [tiled_spec(value) for value in terms]
        + [whole_spec(value) for value in out_parts]
        + [tiled_spec(value) for value in context]
        + [tiled_spec(middle), tiled_spec(cotangent), whole_spec(vectors)],
        out_specs=[tiled_spec(middle), whole_spec(sums)]
        + [tiled_spec(head)] * parts
        + [whole_spec(blocks)] * parts,
        scratch_shapes=[pltpu.VMEM((features, width * parts), F32)],
        compiler_params=limit(62),
        cost_estimate=cost(4 * middle.size * features, 20 * middle.size),
        name="middle_back",
    )(owner, *terms, *out_parts, *context, middle, cotangent, vectors)
    return found[0], found[1], found[2 : 2 + parts], found[2 + parts :]


def input_back_kernel(terms, *refs):
    *term_refs, first_ref, last_ref = refs[:terms]
    rows_ref, middle_ref, vector_ref, out_ref = refs[terms:]
    half = jnp.where(pl.program_id(0) == 0, first_ref[...], last_ref[...])
    grad_normed = total([ref[...].astype(F32) for ref in term_refs]) + half.astype(F32)
    unit, inverse = norm_parts(rows_ref[...].astype(F32))
    grad = norm_back(grad_normed, unit, inverse, vector_ref[0:1, :])
    out_ref[...] = (middle_ref[...].astype(F32) + grad).astype(BF16)


def input_back(terms, rows, grad_middle, vectors):
    tile = rows.shape[0] // 2
    return pl.pallas_call(
        functools.partial(input_back_kernel, len(terms)),
        grid=(2,),
        out_shape=like(rows),
        in_specs=[tiled_spec(value, tile) for value in terms[:-2]]
        + [whole_spec(value) for value in terms[-2:]]
        + [tiled_spec(rows, tile), tiled_spec(grad_middle, tile), whole_spec(vectors)],
        out_specs=tiled_spec(rows, tile),
        compiler_params=limit(62),
        cost_estimate=cost(20 * rows.size, 14 * rows.size),
        name="input_back",
    )(*terms, rows, grad_middle, vectors)


def per_device(
    tokens,
    output_cotangent,
    lengths,
    block_place,
    random_blocks,
    qkv_weight,
    out_weight,
    up_weight,
    down_weight,
    vectors,
    hidden_bias,
):
    ways = lax.axis_size("tensor")
    spread_ways = lax.axis_size("dp")
    position = lax.axis_index("tensor")
    index = lax.axis_index("dp") * ways + position
    near = tokens.shape[0]
    rows = near * ways
    features = tokens.shape[1]
    width = qkv_weight.shape[2]
    heads = width // HEAD_DIM
    units = up_weight.shape[1]
    own = features // spread_ways
    piece = vectors.shape[1]
    unit_piece = hidden_bias.shape[1]

    small = jnp.zeros((8, features), F32)
    small = lax.dynamic_update_slice(small, vectors, (0, index * piece))
    small_hidden = jnp.zeros((1, units * ways), F32)
    small_hidden = lax.dynamic_update_slice(small_hidden, hidden_bias, (0, index * unit_piece))
    packed = jnp.concatenate([small.reshape(-1), small_hidden.reshape(-1)])
    packed = summed_everywhere(packed, ("tensor",))

    unit_near = unit_rows(tokens)
    unit_near, packed = together(unit_near, packed)
    unit_far = far(unit_near, "tensor")

    facts = attention_facts(lengths[0], position, block_place, random_blocks)

    bits = bits_of("dp")
    order_a = bits[::-1]
    order_b = bits[-1:] + bits[:1] + bits[-2:0:-1]
    owner_a = block_owners("dp", order_a)
    owner_b = block_owners("dp", order_b)
    split = 2 * width
    qkv_flat = qkv_weight.reshape(own, 3 * width)
    first_blocks = doubled(qkv_flat[:, :split], "dp", order_a)
    last_flat = jnp.concatenate([qkv_flat[:, split:], out_weight], axis=1)
    last_blocks = doubled(last_flat, "dp", order_b)
    packed = summed_everywhere(packed, ("dp",))
    feed_flat = jnp.concatenate([up_weight, down_weight], axis=1)
    first_going = output_cotangent[: near // 8]
    next_going = output_cotangent[near // 8 : near // 2]
    last_going = output_cotangent[near // 2 :]
    first_going, unit_far = together(first_going, unit_far)
    cotangent_first = far(first_going, "tensor")
    feed_flat, first_blocks, last_blocks, packed, cotangent_first, next_going = together(
        feed_flat, first_blocks, last_blocks, packed, cotangent_first, next_going
    )
    cotangent_next = far(next_going, "tensor")
    feed_full = lax.all_gather(feed_flat, "dp", axis=0, tiled=True)
    unit_parts = gathered_parts(unit_near, unit_far, "tensor")

    vectors_full = packed[: 8 * features].reshape(8, features)
    hidden_full = packed[8 * features :]
    bias_query = lax.dynamic_slice_in_dim(vectors_full[6], position * width, width)
    bias_value = lax.dynamic_slice_in_dim(vectors_full[7], position * width, width)
    bias_qkv = jnp.concatenate([bias_query, jnp.zeros_like(bias_query), bias_value])[None]
    bias_hidden = lax.dynamic_slice_in_dim(hidden_full, position * units, units)[None]
    norm_one = vectors_full[:2]
    norm_two = jnp.stack([vectors_full[4], vectors_full[2], vectors_full[3]])


    last_blocks, cotangent_next = together(last_blocks, cotangent_next)
    out_group = placed_rows(last_blocks, owner_b, width)
    out_far = far(out_group, "tensor")
    last_going, out_group = together(last_going, out_group)
    cotangent_last = far(last_going, "tensor")
    *context, qkv, qkv_full, log_totals = project_attend(
        unit_parts,
        first_blocks,
        last_blocks,
        owner_a,
        owner_b,
        norm_one,
        bias_qkv,
        facts,
        heads,
    )
    context = context[0]
    *context, out_far, cotangent_last = together(*context, out_far, cotangent_last)
    cotangent_far = jnp.concatenate([cotangent_first, cotangent_next, cotangent_last], axis=0)
    grad_parts = gathered_parts(output_cotangent, cotangent_far, "tensor")

    out_parts = gathered_parts(out_group, out_far, "tensor")
    context_near = exchanged_parts(context, "tensor")
    middle, normed_two = middle_rows(context_near, out_parts, tokens, norm_two)

    half = ways // 2
    normed_far = far(normed_two, "tensor")
    normed_parts = gathered_parts(normed_two, normed_far, "tensor")
    near_back, near_out, stacks = feed(
        normed_parts[:half], grad_parts[:half], feed_full, bias_hidden, (), 0, ways
    )
    normed_far, *stacks = together(normed_far, *stacks)
    normed_parts = gathered_parts(normed_two, normed_far, "tensor")
    far_back, far_out, stacks = feed(
        normed_parts[half:], grad_parts[half:], feed_full, bias_hidden, stacks, half, ways
    )
    back_parts, feed_parts = near_back + far_back, near_out + far_out
    back_terms, far_sum = summed_halves(back_parts, "tensor")
    back_terms.append(far(far_sum, "tensor"))
    feed_sums, sum_hidden = feed_grads(stacks)
    feed_terms, feed_far = summed_halves(feed_parts, "tensor")
    early, late_rows = feed_far[: near // 2], feed_far[near // 2 :]
    feed_weight_grads = lax.psum_scatter(feed_sums, "dp", scatter_dimension=0, tiled=True)
    feed_weight_grads = feed_weight_grads.astype(F32)
    *back_terms, sum_hidden, early = together(*back_terms, sum_hidden, early)
    early = far(early, "tensor")

    grad_middle, sums_two, grad_heads, out_blocks = middle_back(
        back_terms, out_parts, context_near, middle, output_cotangent, norm_two, owner_b
    )
    grad_context = exchanged_parts(grad_heads, "tensor")

    *out_blocks, early = together(*out_blocks, early)
    out_terms, out_far = summed_halves(out_blocks, "tensor")
    *grad_context, out_far, late_rows = together(*grad_context, out_far, late_rows)
    out_terms.append(far(out_far, "tensor"))
    late_rows = far(late_rows, "tensor")
    first_keep, first_send, last_keep, last_send, *back_parts, late, sum_qkv = attend_back(
        qkv,
        grad_context,
        log_totals,
        unit_parts,
        qkv_full,
        owner_a,
        owner_b,
        split,
        facts,
        heads,
    )
    first_send, last_send, late, late_rows, *rest = together(
        first_send, last_send, late, late_rows, *out_terms, *back_parts
    )
    out_terms, back_parts = rest[: len(out_terms)], rest[len(out_terms) :]
    near_rows, far_rows = back_parts[:half], back_parts[half:]
    feed_terms.append(jnp.concatenate([early, late_rows], axis=0))
    output = total([term.astype(F32) for term in (*feed_terms, middle)]) + vectors_full[5]
    output = output.astype(BF16)
    out_sums = total([term.astype(F32) for term in out_terms]).astype(BF16)
    last_keep = jnp.concatenate([last_keep, out_sums[: spread_ways // 2]], axis=2)
    last_send = jnp.concatenate([last_send, out_sums[spread_ways // 2 :]], axis=2)
    head_sums = lax.dynamic_update_slice(
        jnp.zeros((3, features), F32), sum_qkv.reshape(3, width), (0, position * width)
    )
    hidden_sums = lax.dynamic_update_slice(
        jnp.zeros((1, units * ways), F32), sum_hidden, (0, position * units)
    )
    packed = jnp.concatenate(
        [late.reshape(-1), sums_two.reshape(-1), head_sums.reshape(-1), hidden_sums.reshape(-1)]
    )
    packed = summed_everywhere(packed, ("dp",))
    far_sum = added(far_rows[0], swapped(far_rows[1], "tensor", 1))
    far_sum, first_keep, last_keep, *near_rows = together(
        far_sum, first_keep, last_keep, *near_rows
    )
    far_first = far(far_sum[: near // 2], "tensor")
    far_last = far(far_sum[near // 2 :], "tensor")
    first_keep, first_send = halved(first_keep, first_send, "dp", order_a)
    last_keep, last_send = halved(last_keep, last_send, "dp", order_b)
    first_send, last_send, far_first = together(first_send, last_send, far_first)
    while first_send.shape[0] > 1:
        first_keep, first_send = halved(first_keep, first_send, "dp", order_a)
        last_keep, last_send = halved(last_keep, last_send, "dp", order_b)
    first_send, last_send, far_last, output = together(first_send, last_send, far_last, output)
    near_terms = [near_rows[0], swapped(near_rows[1], "tensor", 1), far_first, far_last]
    input_grad = input_back(near_terms, tokens, grad_middle, norm_one)
    first_keep, last_keep, input_grad, packed = together(
        first_keep, last_keep, input_grad, packed
    )
    first_raw = halved(first_keep, first_send, "dp", order_a)[0][0].astype(F32)
    last_raw = halved(last_keep, last_send, "dp", order_b)[0][0].astype(F32)
    out_weight_grad = last_raw[:, width:]
    last_raw = last_raw[:, :width]

    packed = summed_everywhere(packed, ("tensor",), direct=True)
    by_feature = packed[: 9 * features].reshape(9, features)
    hidden_sums = packed[9 * features :]
    vectors_grad = lax.dynamic_slice_in_dim(by_feature, index * piece, piece, axis=1)
    vectors_grad = jnp.concatenate([vectors_grad[:7], vectors_grad[8:]], axis=0)
    hidden_bias_grad = lax.dynamic_slice_in_dim(hidden_sums, index * unit_piece, unit_piece)

    sum_qkv = lax.dynamic_slice_in_dim(by_feature[6:], position * width, width, axis=1)
    mine = lax.dynamic_slice_in_dim(norm_one, lax.axis_index("dp") * own, own, axis=1)
    raw = jnp.concatenate([first_raw, last_raw], axis=1).reshape(own, 3, width)
    qkv_weight_grad = mine[0][:, None, None] * raw + mine[1][:, None, None] * sum_qkv
    return (
        output,
        input_grad,
        qkv_weight_grad,
        out_weight_grad,
        feed_weight_grads[:, :units],
        feed_weight_grads[:, units:],
        vectors_grad,
        hidden_bias_grad[None, :],
    )


def solution(mesh):
    placed = (
        P(("dp", "tensor"), None),
        P(("dp", "tensor"), None),
        P("dp"),
        P("dp", None),
        P("dp", "tensor", None, None),
        P("dp", None, "tensor"),
        P("dp", "tensor"),
        P("dp", "tensor"),
        P("dp", "tensor"),
        P(None, ("dp", "tensor")),
        P(None, ("dp", "tensor")),
    )
    return jax.shard_map(
        per_device,
        mesh=mesh,
        in_specs=placed,
        out_specs=(
            P(("dp", "tensor"), None),
            P(("dp", "tensor"), None),
            P("dp", None, "tensor"),
            P("dp", "tensor"),
            P("dp", "tensor"),
            P("dp", "tensor"),
            P(None, ("dp", "tensor")),
            P(None, ("dp", "tensor")),
        ),
        check_vma=False,
    )
```

```python
import functools

import jax
import jax.numpy as jnp
from jax import lax
from jax.experimental import pallas as pl
from jax.experimental.pallas import tpu as pltpu
from jax.sharding import PartitionSpec as P

HEAD_DIM = 64
BLOCK = 64
PAIR = 2 * HEAD_DIM
SLOTS = 8
CHUNK = 512
EPS = 1e-05
NEGATIVE = -1e30
F32 = jnp.float32
BF16 = jnp.bfloat16
NT = (((1,), (1,)), ((), ()))
NN = (((1,), (0,)), ((), ()))
TN = (((0,), (0,)), ((), ()))


def matmul(left, right, dims):
    return lax.dot_general(left, right, dims, preferred_element_type=F32)


def swapped(value, axis, bit):
    count = lax.axis_size(axis)
    return lax.ppermute(value, axis, [(i, i ^ bit) for i in range(count)])


def bits_of(axis):
    count = lax.axis_size(axis)
    return [1 << b for b in range(count.bit_length() - 1)]


def together(*values):
    return lax.optimization_barrier(values)


def far(value, axis):
    return swapped(value, axis, bits_of(axis)[-1])


def gathered_parts(value, far_value, axis):
    bits = bits_of(axis)
    parts = {0: value, bits[-1]: far_value}
    for bit in reversed(bits[:-1]):
        parts.update({k | bit: swapped(p, axis, bit) for k, p in list(parts.items())})
    return [parts[k] for k in range(len(parts))]


def summed_halves(parts, axis):
    left = dict(enumerate(parts))
    terms = [parts[0]]
    for bit in bits_of(axis)[: len(parts).bit_length() - 2]:
        kept = {}
        for k in sorted(left, reverse=True):
            if k & bit == 0:
                arrived = swapped(left[k | bit], axis, bit)
                if k == 0:
                    terms.append(arrived)
                    kept[k] = None
                else:
                    kept[k] = added(left[k], arrived)
        left = kept
    return terms, left[len(parts) // 2]


def added(left, right):
    return (left.astype(F32) + right.astype(F32)).astype(BF16)


def doubled(value, axis, order):
    blocks = value[None]
    for bit in order:
        blocks = jnp.concatenate([blocks, swapped(blocks, axis, bit)], axis=0)
    return blocks


def halved(keep, send, axis, order):
    half = send.shape[0]
    arrived = swapped(send, axis, order[half.bit_length() - 1])
    rest = half // 2
    return added(keep[: half - rest], arrived[: half - rest]), added(
        keep[half - rest :], arrived[half - rest :]
    )


def block_owners(axis, order):
    count = lax.axis_size(axis)
    device = [sum(bit for b, bit in enumerate(order) if p >> b & 1) for p in range(count)]
    return lax.axis_index(axis) ^ jnp.asarray(device, jnp.int32)


def exchanged_parts(parts, axis):
    return [p if k == 0 else swapped(p, axis, k) for k, p in enumerate(parts)]


def summed_everywhere(value, axes, direct=False):
    size = value.shape[0]
    value = jnp.pad(value, (0, -size % 1024)).reshape(-1, 128)
    for axis in axes:
        if direct:
            value = total([value] + [swapped(value, axis, k) for k in range(1, lax.axis_size(axis))])
        else:
            for bit in bits_of(axis):
                value = value + swapped(value, axis, bit)
    return value.reshape(-1)[:size]


def sent_and_summed(value, axis):
    count = lax.axis_size(axis)
    blocks = value.reshape(count, value.shape[0] // count, *value.shape[1:])
    arrived = lax.all_to_all(blocks, axis, 0, 0, tiled=True)
    return jnp.sum(arrived.astype(F32), axis=0)


def attention_facts(length, position, placing, chosen):
    head = jnp.stack([length, position]).astype(jnp.int32)
    return jnp.concatenate([head, placing.reshape(-1), chosen.reshape(-1)])


class Blocks:
    def __init__(self, facts, stored, limits, heads, quarters):
        self.facts, self.stored, self.limits = facts, stored, limits
        self.heads, self.quarters = heads, quarters
        self.count = stored.shape[0]
        self.length = facts[0]
        self.last = (self.length + BLOCK - 1) // BLOCK - 1
        self.last_rows = self.length - BLOCK * self.last

    def find(self):
        per = self.count // self.quarters
        for quarter in range(self.quarters):
            start = (self.facts[1] ^ quarter) * per
            for n in range(per):
                number = self.facts[2 + start + n]
                self.stored[number] = quarter * per + n
                rows = self.length - BLOCK * number
                self.limits[quarter * per + n] = jnp.clip(rows, 0, BLOCK)

    def item(self, number):
        last = self.last
        alive = number != last
        before, behind = number - 1, number + 1
        common = [0, last, before, number, jnp.minimum(behind, self.count - 1)]
        good = [
            alive,
            alive,
            alive & (before > 0) & (before < last),
            alive & (number < last),
            alive & (behind < last),
        ]
        places = [self.stored[block] for block in common]
        lane = lax.broadcasted_iota(jnp.int32, (1, self.heads * HEAD_DIM), 1)
        added_scores = [jnp.where(flag, 0.0, NEGATIVE).astype(F32) for flag in good]
        drawn = [
            [
                self.facts[2 + self.count + (h * self.count + number) * 3 + s]
                for h in range(self.heads)
            ]
            for s in range(3)
        ]
        random = []
        for s in range(3):
            random.append([self.stored[block] for block in drawn[s]])
            row = jnp.zeros((1, self.heads * HEAD_DIM), F32)
            for h, block in enumerate(drawn[s]):
                fresh = alive & (block > 0) & (block < last) & (jnp.abs(block - number) > 1)
                for other in range(s):
                    fresh = fresh & (block != drawn[other][h])
                score = jnp.where(fresh, 0.0, NEGATIVE).astype(F32)
                row = jnp.where(lane // HEAD_DIM == h, score, row)
            added_scores.append(row)
        return places, random, added_scores


def block_rows(index):
    return pl.ds(pl.multiple_of(index * BLOCK, BLOCK), BLOCK)


def spread(rows, heads):
    lane = lax.broadcasted_iota(jnp.int32, (1, heads * HEAD_DIM), 1)
    zero = jnp.zeros_like(rows)
    return jnp.concatenate(
        [jnp.where(lane // HEAD_DIM == h, rows, zero) for h in range(heads)], axis=0
    )


def collapse(full, heads):
    lane = lax.broadcasted_iota(jnp.int32, (1, PAIR), 1)
    pieces = []
    for pair in range(heads // 2):
        cols = slice(PAIR * pair, PAIR * (pair + 1))
        even = full[2 * pair * HEAD_DIM : (2 * pair + 1) * HEAD_DIM, cols]
        odd = full[(2 * pair + 1) * HEAD_DIM : (2 * pair + 2) * HEAD_DIM, cols]
        pieces.append(jnp.where(lane < HEAD_DIM, even, odd))
    return jnp.concatenate(pieces, axis=1)


def gathered_keys(ref, start, places, random, heads):
    width = heads * HEAD_DIM
    lane = lax.broadcasted_iota(jnp.int32, (1, PAIR), 1)
    parts = [ref[block_rows(place), start : start + width] for place in places]
    for drawn in random:
        pieces = []
        for pair in range(heads // 2):
            cols = slice(start + PAIR * pair, start + PAIR * (pair + 1))
            even = ref[block_rows(drawn[2 * pair]), cols]
            odd = ref[block_rows(drawn[2 * pair + 1]), cols]
            pieces.append(jnp.where(lane < HEAD_DIM, even, odd))
        parts.append(jnp.concatenate(pieces, axis=1))
    return jnp.concatenate(parts, axis=0)


def slot(value, index):
    return value[BLOCK * index : BLOCK * (index + 1)]


def biased(scores, bias, last_rows):
    row = lax.broadcasted_iota(jnp.int32, (BLOCK, 1), 0)
    parts = [slot(scores, s) + bias[s] for s in range(SLOTS)]
    parts[1] = jnp.where(row < last_rows, parts[1], NEGATIVE)
    return parts


def total(parts):
    return functools.reduce(jnp.add, parts)


def attend_body(heads, blocks, qkv_ref, out_ref, log_ref, keep_ref):
    count = blocks.count
    stored, limits = blocks.stored, blocks.limits
    width = heads * HEAD_DIM
    scale = jnp.asarray(HEAD_DIM**-0.5, BF16)

    def item(number):
        places, random, scores = blocks.item(number)
        here = block_rows(places[3])
        queries = spread(qkv_ref[here, :width] * scale, heads)
        keys = gathered_keys(qkv_ref, width, places, random, heads)
        parts = biased(matmul(keys, queries, NT), scores, blocks.last_rows)
        top = jnp.max(functools.reduce(jnp.maximum, parts), axis=0, keepdims=True)
        weights = [jnp.exp(p - top) for p in parts]
        row_total = jnp.sum(total(weights), axis=0, keepdims=True)
        inverse = 1.0 / row_total
        probs = jnp.concatenate([(p * inverse).astype(BF16) for p in weights], axis=0)
        values = gathered_keys(qkv_ref, 2 * width, places, random, heads)
        out_ref[here, :] = collapse(matmul(probs, values, TN), heads).astype(BF16)
        log_ref[pl.ds(number, 1), :] = top + jnp.log(row_total)

    def step(group, carry):
        for part in range(10):
            item(1 + group * 10 + part)
        return carry

    lax.fori_loop(0, (count - 1) // 10, step, 0)
    for number in range(1 + (count - 1) // 10 * 10, count):
        item(number)

    row = lax.broadcasted_iota(jnp.int32, (BLOCK, 1), 0)
    per = CHUNK // BLOCK
    chunks = count // per

    def chunk_rows(chunk):
        return pl.ds(pl.multiple_of(chunk * CHUNK, CHUNK), CHUNK)

    numbers = [0, blocks.last]
    rows_of = [block_rows(stored[number]) for number in numbers]
    queries = [spread(qkv_ref[at, :width] * scale, heads) for at in rows_of]

    def scores(chunk, tops):
        at = chunk_rows(chunk)
        keys = qkv_ref[at, width : 2 * width]
        found = []
        for end in range(2):
            raw = matmul(keys, queries[end], NT)
            parts = [
                jnp.where(row < limits[chunk * per + s], slot(raw, s), NEGATIVE)
                for s in range(per)
            ]
            keep_ref[end, at, :] = jnp.concatenate(parts, axis=0)
            found.append(jnp.maximum(tops[end], functools.reduce(jnp.maximum, parts)))
        return tuple(found)

    tops = lax.fori_loop(0, chunks, scores, (jnp.full((BLOCK, width), NEGATIVE, F32),) * 2)
    tops = [jnp.max(top, axis=0, keepdims=True) for top in tops]

    def exponents(chunk, totals):
        at = chunk_rows(chunk)
        found = []
        for end in range(2):
            weights = jnp.exp(keep_ref[end, at, :] - tops[end])
            keep_ref[end, at, :] = weights
            found.append(totals[end] + total([slot(weights, s) for s in range(per)]))
        return tuple(found)

    totals = lax.fori_loop(0, chunks, exponents, (jnp.zeros((BLOCK, width), F32),) * 2)
    totals = [jnp.sum(found, axis=0, keepdims=True) for found in totals]
    inverses = [1.0 / found for found in totals]

    def contexts(chunk, sums):
        at = chunk_rows(chunk)
        values = qkv_ref[at, 2 * width :]
        return tuple(
            sums[end] + matmul((keep_ref[end, at, :] * inverses[end]).astype(BF16), values, TN)
            for end in range(2)
        )

    sums = lax.fori_loop(0, chunks, contexts, (jnp.zeros((width, width), F32),) * 2)
    for end in range(2):
        out_ref[rows_of[end], :] = collapse(sums[end], heads).astype(BF16)
        log_ref[pl.ds(numbers[end], 1), :] = tops[end] + jnp.log(totals[end])


def attend_back_body(
    heads,
    blocks,
    qkv_ref,
    grad_ref,
    log_ref,
    out_ref,
    keys_acc,
    values_acc,
    probs_ref,
    inner_ref,
):
    count = blocks.count
    stored, limits = blocks.stored, blocks.limits
    width = heads * HEAD_DIM
    scale = jnp.asarray(HEAD_DIM**-0.5, BF16)
    lane = lax.broadcasted_iota(jnp.int32, (1, PAIR), 1)
    keys_acc[...] = jnp.zeros_like(keys_acc)
    values_acc[...] = jnp.zeros_like(values_acc)

    def accumulate(acc, value, places, random):
        for s in range(5):
            acc[block_rows(places[s]), :] += slot(value, s)
        for s in range(3):
            for h in range(heads):
                cols = slice(PAIR * (h // 2), PAIR * (h // 2 + 1))
                mine = (lane < HEAD_DIM) == (h % 2 == 0)
                term = jnp.where(mine, slot(value, 5 + s)[:, cols], 0.0)
                acc[block_rows(random[s][h]), cols] += term

    def item(number):
        places, random, scores = blocks.item(number)
        here = block_rows(places[3])
        queries = spread(qkv_ref[here, :width] * scale, heads)
        grads = spread(grad_ref[here, :], heads)
        keys = gathered_keys(qkv_ref, width, places, random, heads)
        values = gathered_keys(qkv_ref, 2 * width, places, random, heads)
        log_total = log_ref[pl.ds(number, 1), :]
        parts = biased(matmul(keys, queries, NT), scores, blocks.last_rows)
        probs = [jnp.exp(p - log_total) for p in parts]
        found = matmul(values, grads, NT)
        found = [slot(found, s) for s in range(SLOTS)]
        inner = total([p * d for p, d in zip(probs, found)])
        inner = jnp.sum(inner, axis=0, keepdims=True)
        grad_scores = jnp.concatenate(
            [(p * (d - inner)).astype(BF16) for p, d in zip(probs, found)], axis=0
        )
        probs_low = jnp.concatenate([p.astype(BF16) for p in probs], axis=0)
        accumulate(values_acc, matmul(probs_low, grads, NN), places, random)
        accumulate(keys_acc, matmul(grad_scores, queries, NN), places, random)
        grad_queries = collapse(matmul(grad_scores, keys, TN), heads) * HEAD_DIM**-0.5
        out_ref[here, :width] = grad_queries.astype(BF16)

    def step(group, carry):
        for part in range(10):
            item(1 + group * 10 + part)
        return carry

    lax.fori_loop(0, (count - 1) // 10, step, 0)
    for number in range(1 + (count - 1) // 10 * 10, count):
        item(number)

    row = lax.broadcasted_iota(jnp.int32, (BLOCK, 1), 0)
    per = CHUNK // BLOCK
    chunks = count // per

    def chunk_rows(chunk):
        return pl.ds(pl.multiple_of(chunk * CHUNK, CHUNK), CHUNK)

    numbers = [0, blocks.last]
    rows_of = [block_rows(stored[number]) for number in numbers]
    queries = [spread(qkv_ref[at, :width] * scale, heads) for at in rows_of]
    grads = [spread(grad_ref[at, :], heads) for at in rows_of]
    log_rows = [log_ref[pl.ds(number, 1), :] for number in numbers]

    def first(chunk, inners):
        at = chunk_rows(chunk)
        keys = qkv_ref[at, width : 2 * width]
        values = qkv_ref[at, 2 * width :]
        sums = []
        for end in range(2):
            scores = matmul(keys, queries[end], NT)
            parts = [
                jnp.where(row < limits[chunk * per + s], slot(scores, s), NEGATIVE)
                for s in range(per)
            ]
            probs = jnp.exp(jnp.concatenate(parts, axis=0) - log_rows[end])
            found = matmul(values, grads[end], NT)
            probs_ref[end, at, :] = probs
            inner_ref[end, at, :] = found
            both = probs * found
            sums.append(inners[end] + total([slot(both, s) for s in range(per)]))
        return tuple(sums)

    inners = lax.fori_loop(0, chunks, first, (jnp.zeros((BLOCK, width), F32),) * 2)
    inners = [jnp.sum(inner, axis=0, keepdims=True) for inner in inners]

    def second(chunk, sums):
        at = chunk_rows(chunk)
        keys = qkv_ref[at, width : 2 * width]
        found, to_values, to_keys = [], values_acc[at, :], keys_acc[at, :]
        for end in range(2):
            probs = probs_ref[end, at, :]
            grad_scores = (probs * (inner_ref[end, at, :] - inners[end])).astype(BF16)
            to_values = to_values + matmul(probs.astype(BF16), grads[end], NN)
            to_keys = to_keys + matmul(grad_scores, queries[end], NN)
            found.append(sums[end] + matmul(grad_scores, keys, TN))
        out_ref[at, width : 2 * width] = to_keys.astype(BF16)
        out_ref[at, 2 * width :] = to_values.astype(BF16)
        return tuple(found)

    sums = lax.fori_loop(0, chunks, second, (jnp.zeros((width, width), F32),) * 2)
    for end in range(2):
        grad_queries = collapse(sums[end], heads) * HEAD_DIM**-0.5
        out_ref[rows_of[end], :width] = grad_queries.astype(BF16)


def in_smem():
    return pl.BlockSpec(memory_space=pltpu.SMEM)


def in_vmem():
    return pl.BlockSpec(memory_space=pltpu.VMEM)


def project_attend_kernel(heads, parts, owner_a, owner_b, facts, *refs):
    unit_refs = refs[:parts]
    first_ref, last_ref, norm_ref, bias_ref = refs[parts : parts + 4]
    *quarter_refs, kept_ref, weight_out_ref, log_ref = refs[parts + 4 : 2 * parts + 7]
    qkv_ref, weight_ref, out_ref, keep_ref, stored, limits, sems = refs[2 * parts + 7 :]
    blocks = Blocks(facts, stored, limits, heads, parts)
    blocks.find()
    count, own, split = first_ref.shape
    near = unit_refs[0].shape[0]
    rest = weight_ref.shape[1] - split
    for p in range(count):
        at = pl.ds(pl.multiple_of(owner_a[p] * own, own), own)
        weight_ref[at, :split] = first_ref[p]
        at = pl.ds(pl.multiple_of(owner_b[p] * own, own), own)
        weight_ref[at, split:] = last_ref[p, :, :rest]
    copies = [pltpu.make_async_copy(weight_ref, weight_out_ref, sems.at[0])]
    copies[0].start()
    for k, ref in enumerate(unit_refs):
        normed = ref[...].astype(F32) * norm_ref[0:1, :] + norm_ref[1:2, :]
        found = matmul(normed.astype(BF16), weight_ref[...], NN) + bias_ref[...]
        qkv_ref[near * k : near * (k + 1), :] = found.astype(BF16)
    copies.append(pltpu.make_async_copy(qkv_ref, kept_ref, sems.at[1]))
    copies[1].start()
    attend_body(heads, blocks, qkv_ref, out_ref, log_ref, keep_ref)
    for k, ref in enumerate(quarter_refs):
        part = out_ref.at[near * k : near * (k + 1), :]
        copies.append(pltpu.make_async_copy(part, ref, sems.at[2 + k]))
        copies[-1].start()
    for copy in copies:
        copy.wait()


def in_hbm():
    return pl.BlockSpec(memory_space=pltpu.HBM)


def project_attend(unit, first, last, owner_a, owner_b, norm, bias, facts, heads):
    rows = sum(value.shape[0] for value in unit)
    features = unit[0].shape[1]
    width = heads * HEAD_DIM
    log_shape = jax.ShapeDtypeStruct((rows // BLOCK, width), F32)
    quarter = [jax.ShapeDtypeStruct((value.shape[0], width), BF16) for value in unit]
    qkv = jax.ShapeDtypeStruct((rows, 3 * width), BF16)
    weight = jax.ShapeDtypeStruct((features, 3 * width), BF16)
    found = pl.pallas_call(
        functools.partial(project_attend_kernel, heads, len(unit)),
        grid=(1,),
        out_shape=[*quarter, qkv, weight, log_shape],
        in_specs=[in_smem()] * 3 + [in_vmem()] * (len(unit) + 4),
        out_specs=[in_hbm()] * (len(unit) + 2)
        + [pl.BlockSpec(log_shape.shape, lambda i: (0, 0))],
        scratch_shapes=[
            pltpu.VMEM(qkv.shape, BF16),
            pltpu.VMEM(weight.shape, BF16),
            pltpu.VMEM((rows, width), BF16),
            pltpu.VMEM((2, rows, width), F32),
            pltpu.SMEM((rows // BLOCK,), jnp.int32),
            pltpu.SMEM((rows // BLOCK,), jnp.int32),
            pltpu.SemaphoreType.DMA((len(unit) + 2,)),
        ],
        compiler_params=pltpu.CompilerParams(vmem_limit_bytes=56 << 20),
        cost_estimate=pl.CostEstimate(
            flops=20 * rows * CHUNK * width,
            bytes_accessed=20 * rows * width,
            transcendentals=rows * CHUNK * width // HEAD_DIM,
        ),
        name="project_attend",
    )(owner_a, owner_b, facts, *unit, first, last, norm, bias)
    return found[: len(unit)], *found[len(unit) :]


def place_kernel(owner, blocks_ref, out_ref):
    count, own, _ = blocks_ref.shape
    width = out_ref.shape[1]
    for p in range(count):
        at = pl.ds(pl.multiple_of(owner[p] * own, own), own)
        out_ref[at, :] = blocks_ref[p, :, -width:]


def placed_rows(blocks, owner, width):
    out = jax.ShapeDtypeStruct((blocks.shape[0] * blocks.shape[1], width), blocks.dtype)
    return pl.pallas_call(
        place_kernel,
        grid=(1,),
        out_shape=out,
        in_specs=[in_smem(), in_vmem()],
        out_specs=pl.BlockSpec(out.shape, lambda i: (0, 0)),
        name="placed_rows",
    )(owner, blocks)


def attend_back_kernel(heads, parts, owner_a, owner_b, facts, *refs):
    qkv_ref, log_ref, weight_ref = refs[:3]
    part_refs, unit_refs = refs[3 : 3 + parts], refs[3 + parts : 3 + 2 * parts]
    outs = refs[3 + 2 * parts :]
    block_outs, row_outs, late_ref, sum_ref = outs[:4], outs[4 : 4 + parts], *outs[4 + parts :][:2]
    grads_ref, grad_ref, keys_acc, values_acc, probs_ref, inner_ref = outs[6 + parts :][:6]
    raw_ref, *block_refs, rows_ref, stored, limits, sems = outs[12 + parts :]
    blocks = Blocks(facts, stored, limits, heads, parts)
    blocks.find()
    half, own, split = block_refs[0].shape
    width = weight_ref.shape[1]
    near = unit_refs[0].shape[0]
    step = 2 * TILE
    for k, ref in enumerate(part_refs):
        grads_ref[near * k : near * (k + 1), :] = ref[...]
    attend_back_body(
        heads,
        blocks,
        qkv_ref,
        grads_ref,
        log_ref,
        grad_ref,
        keys_acc,
        values_acc,
        probs_ref,
        inner_ref,
    )
    copies = []

    def leave(source, target):
        copies.append(pltpu.make_async_copy(source, target, sems.at[len(copies)]))
        copies[-1].start()

    sums = jnp.sum(grad_ref[...].astype(F32), axis=0, keepdims=True)
    sum_ref[...] = sums
    for i in range(weight_ref.shape[0] // step):
        at = slice(step * i, step * (i + 1))
        raw = total(
            [
                matmul(ref[:, at], grad_ref[near * k : near * (k + 1), :], TN)
                for k, ref in enumerate(unit_refs)
            ]
        )
        weight = weight_ref[at, :].astype(F32)
        raw_ref[at, :] = raw.astype(BF16)
        for row, value in enumerate((raw * weight, weight * sums)):
            lanes = total([value[:, 128 * c : 128 * (c + 1)] for c in range(width // 128)])
            for b in range(step // 128):
                turned = lanes[128 * b : 128 * (b + 1)].T
                found = jnp.sum(turned, axis=0, keepdims=True)
                start = step * i + 128 * b
                late_ref[row : row + 1, start : start + 128] = found
    for p in range(2 * half):
        at = pl.ds(pl.multiple_of(owner_a[p] * own, own), own)
        block_refs[p // half][p % half] = raw_ref[at, :split]
        at = pl.ds(pl.multiple_of(owner_b[p] * own, own), own)
        block_refs[2 + p // half][p % half] = raw_ref[at, split:]
    for source, target in zip(block_refs, block_outs):
        leave(source, target)
    for k in range(parts - 1, -1, -1):
        at = slice(near * k, near * (k + 1))
        rows_ref[at, :] = matmul(grad_ref[at, :], weight_ref[...], NT).astype(BF16)
        leave(rows_ref.at[at, :], row_outs[k])
    for copy in copies:
        copy.wait()


def attend_back(
    qkv, grad_context, log_totals, unit, weight, owner_a, owner_b, split, facts, heads
):
    rows, width = qkv.shape[0], heads * HEAD_DIM
    features = weight.shape[0]
    count = owner_a.shape[0]
    own = features // count
    first = jax.ShapeDtypeStruct((count // 2, own, split), BF16)
    last = jax.ShapeDtypeStruct((count // 2, own, 3 * width - split), BF16)
    small = [
        jax.ShapeDtypeStruct((2, features), F32),
        jax.ShapeDtypeStruct((1, 3 * width), F32),
    ]
    blocks = [first, first, last, last]
    return pl.pallas_call(
        functools.partial(attend_back_kernel, heads, len(unit)),
        grid=(1,),
        out_shape=[*blocks, *[like(value) for value in unit], *small],
        in_specs=[in_smem()] * 3 + [in_vmem()] * (3 + 2 * len(unit)),
        out_specs=[in_hbm()] * (4 + len(unit))
        + [pl.BlockSpec(value.shape, lambda i: (0, 0)) for value in small],
        scratch_shapes=[
            pltpu.VMEM((rows, width), BF16),
            pltpu.VMEM(qkv.shape, BF16),
            pltpu.VMEM((rows, width), F32),
            pltpu.VMEM((rows, width), F32),
            pltpu.VMEM((2, rows, width), F32),
            pltpu.VMEM((2, rows, width), F32),
            pltpu.VMEM(weight.shape, BF16),
            *[pltpu.VMEM(value.shape, BF16) for value in blocks],
            pltpu.VMEM((rows, features), BF16),
            pltpu.SMEM((rows // BLOCK,), jnp.int32),
            pltpu.SMEM((rows // BLOCK,), jnp.int32),
            pltpu.SemaphoreType.DMA((4 + len(unit),)),
        ],
        compiler_params=pltpu.CompilerParams(vmem_limit_bytes=53 << 20),
        cost_estimate=pl.CostEstimate(
            flops=40 * rows * CHUNK * width,
            bytes_accessed=40 * rows * width,
            transcendentals=rows * CHUNK * width // HEAD_DIM,
        ),
        name="attend_back",
    )(
        owner_a,
        owner_b,
        facts,
        qkv,
        log_totals,
        weight,
        *grad_context,
        *unit,
    )


TILE = 256


def gelu_and_slope(pre):
    scale = (2.0 / 3.141592653589793) ** 0.5
    square = pre * pre
    bent = jnp.tanh(scale * pre * (1.0 + 0.044715 * square))
    half = 0.5 + 0.5 * bent
    slope = half + (0.5 * scale) * pre * (1.0 - bent * bent) * (1.0 + 0.134145 * square)
    return pre * half, slope


def pick(refs):
    per = pl.num_programs(0) // len(refs)
    value = refs[0][...]
    for k, ref in enumerate(refs[1:], 1):
        value = jnp.where(pl.program_id(0) >= k * per, ref[...], value)
    return value


def put(refs, value):
    per = pl.num_programs(0) // len(refs)
    for k, ref in enumerate(refs):
        ref[...] = jnp.where(pl.program_id(0) // per == k, value, ref[...])


def feed_kernel(quarters, taken, *refs):
    normed = pick(refs[:quarters])
    grads = pick(refs[quarters : 2 * quarters])
    weight_ref, bias_ref = refs[2 * quarters : 2 * quarters + 2]
    results = refs[2 * quarters + 2 + taken :]
    units = bias_ref.shape[1]
    up = weight_ref[:, :units]
    down = weight_ref[:, units:]
    active, slope = gelu_and_slope(matmul(normed, up, NN) + bias_ref[...])
    active = active.astype(BF16)
    grad_hidden = (matmul(grads, down, NN) * slope).astype(BF16)
    put(results[:quarters], matmul(grad_hidden, up, NT).astype(BF16))
    put(results[quarters : 2 * quarters], matmul(active, down, NT).astype(BF16))
    for ref, value in zip(results[2 * quarters :], (normed, grad_hidden, grads, active)):
        ref[...] = value


def tile_specs(arrays):
    def spec(k, value):
        tiles = value.shape[0] // TILE
        return pl.BlockSpec(
            (TILE, value.shape[1]), lambda i: (jnp.clip(i - k * tiles, 0, tiles - 1), 0)
        )

    return [spec(k, value) for k, value in enumerate(arrays)]


def feed(normed, grads, weights, bias, stacks, start, quarters):
    rows, features = normed[0].shape
    units = bias.shape[1]
    here = len(normed)
    tiles = rows // TILE
    stacked = [jax.ShapeDtypeStruct((rows * quarters, n), BF16) for n in (features, units) * 2]
    found = pl.pallas_call(
        functools.partial(feed_kernel, here, len(stacks)),
        grid=(here * tiles,),
        out_shape=[like(value) for value in normed] * 2 + stacked,
        in_specs=tile_specs(normed)
        + tile_specs(grads)
        + [in_vmem(), whole_spec(bias)]
        + [pl.BlockSpec(memory_space=pl.ANY)] * len(stacks),
        out_specs=tile_specs(normed) * 2
        + [
            pl.BlockSpec((TILE, value.shape[1]), lambda i: (i + start * tiles, 0))
            for value in stacked
        ],
        input_output_aliases={2 * here + 2 + n: 2 * here + n for n in range(len(stacks))},
        compiler_params=limit(56),
        cost_estimate=pl.CostEstimate(
            flops=8 * here * rows * features * units,
            bytes_accessed=16 * here * rows * features + 4 * features * units,
            transcendentals=here * rows * units,
        ),
        name="feed",
    )(*normed, *grads, weights, bias, *stacks)
    return found[:here], found[here : 2 * here], found[2 * here :]


def feed_grads_kernel(normed_ref, grad_ref, grads_ref, active_ref, out_ref, sum_ref, acc_ref):
    units = sum_ref.shape[1]
    grad_hidden = grad_ref[...]

    @pl.when(pl.program_id(0) == 0)
    def _():
        acc_ref[...] = jnp.zeros_like(acc_ref)
        sum_ref[...] = jnp.zeros_like(sum_ref)

    acc_ref[:, :units] += matmul(normed_ref[...], grad_hidden, TN)
    acc_ref[:, units:] += matmul(grads_ref[...], active_ref[...], TN)
    sum_ref[...] += jnp.sum(grad_hidden.astype(F32), axis=0, keepdims=True)

    @pl.when(pl.program_id(0) == pl.num_programs(0) - 1)
    def _():
        out_ref[...] = acc_ref[...].astype(BF16)


def feed_grads(stacks):
    rows, features = stacks[0].shape
    units = stacks[1].shape[1]
    sums = jax.ShapeDtypeStruct((features, 2 * units), BF16)
    hidden = jax.ShapeDtypeStruct((1, units), F32)
    return pl.pallas_call(
        feed_grads_kernel,
        grid=(rows // (2 * TILE),),
        out_shape=[sums, hidden],
        in_specs=[tiled_spec(value, 2 * TILE) for value in stacks],
        out_specs=[whole_spec(sums), whole_spec(hidden)],
        scratch_shapes=[pltpu.VMEM(sums.shape, F32)],
        compiler_params=limit(62),
        cost_estimate=cost(4 * rows * features * units, 8 * rows * features),
        name="feed_grads",
    )(*stacks)


def norm_parts(rows):
    centred = rows - jnp.mean(rows, axis=-1, keepdims=True)
    inverse = lax.rsqrt(jnp.mean(centred * centred, axis=-1, keepdims=True) + EPS)
    return centred * inverse, inverse


def norm_back(grad_normed, unit, inverse, gain):
    grad_unit = grad_normed * gain
    return inverse * (
        grad_unit
        - jnp.mean(grad_unit, axis=-1, keepdims=True)
        - unit * jnp.mean(grad_unit * unit, axis=-1, keepdims=True)
    )


def whole_spec(value):
    return pl.BlockSpec(value.shape, lambda i: (0,) * value.ndim)


def tiled_spec(value, tile=TILE):
    return pl.BlockSpec((tile, value.shape[1]), lambda i: (i, 0))


def like(value, dtype=None):
    return jax.ShapeDtypeStruct(value.shape, dtype or value.dtype)


def limit(mebibytes):
    return pltpu.CompilerParams(vmem_limit_bytes=mebibytes << 20)


def cost(flops, moved):
    return pl.CostEstimate(flops=flops, bytes_accessed=moved, transcendentals=0)


def unit_kernel(rows_ref, unit_ref):
    unit_ref[...] = norm_parts(rows_ref[...].astype(F32))[0].astype(BF16)


def unit_rows(rows):
    return pl.pallas_call(
        unit_kernel,
        grid=(rows.shape[0] // TILE,),
        out_shape=like(rows),
        in_specs=[tiled_spec(rows)],
        out_specs=tiled_spec(rows),
        compiler_params=limit(62),
        cost_estimate=cost(8 * rows.size, 4 * rows.size),
        name="unit",
    )(rows)


def middle_kernel(parts, *refs):
    context_refs, out_refs = refs[:parts], refs[parts : 2 * parts]
    rows_ref, vector_ref, middle_ref, normed_ref = refs[2 * parts :]
    middle = rows_ref[...].astype(F32) + vector_ref[0:1, :]
    for context_ref, out_ref in zip(context_refs, out_refs):
        middle += matmul(context_ref[...], out_ref[...], NT)
    middle_ref[...] = middle.astype(BF16)
    unit = norm_parts(middle)[0]
    normed_ref[...] = (unit * vector_ref[1:2, :] + vector_ref[2:3, :]).astype(BF16)


def middle_rows(context, out_parts, rows, vectors):
    return pl.pallas_call(
        functools.partial(middle_kernel, len(context)),
        grid=(rows.shape[0] // TILE,),
        out_shape=[like(rows), like(rows)],
        in_specs=[tiled_spec(value) for value in context]
        + [whole_spec(value) for value in out_parts]
        + [tiled_spec(rows), whole_spec(vectors)],
        out_specs=[tiled_spec(rows), tiled_spec(rows)],
        compiler_params=limit(62),
        cost_estimate=cost(2 * rows.size * rows.shape[1], 12 * rows.size),
        name="middle",
    )(*context, *out_parts, rows, vectors)


def middle_back_kernel(terms, parts, owner, *refs):
    term_refs, out_refs = refs[:terms], refs[terms : terms + parts]
    context_refs = refs[terms + parts : terms + 2 * parts]
    middle_ref, cotangent_ref, vector_ref, grad_ref, sum_ref = refs[
        terms + 2 * parts : terms + 2 * parts + 5
    ]
    head_refs = refs[terms + 2 * parts + 5 : terms + 3 * parts + 5]
    block_refs = refs[terms + 3 * parts + 5 : -1]
    found_ref = refs[-1]
    first = pl.program_id(0) == 0
    last = pl.program_id(0) == pl.num_programs(0) - 1
    count, own, width = block_refs[0].shape
    grad_normed = total([ref[...].astype(F32) for ref in term_refs])
    unit, inverse = norm_parts(middle_ref[...].astype(F32))
    cotangent = cotangent_ref[...].astype(F32)
    grad = cotangent + norm_back(grad_normed, unit, inverse, vector_ref[1:2, :])
    low = grad.astype(BF16)
    grad_ref[...] = low
    for head_ref, out_ref in zip(head_refs, out_refs):
        head_ref[...] = matmul(low, out_ref[...], NN).astype(BF16)
    sums = [
        jnp.sum(value, axis=0, keepdims=True)
        for value in (grad_normed * unit, grad_normed, grad, cotangent)
    ]
    sums = jnp.concatenate(sums, axis=0)

    @pl.when(first)
    def _():
        sum_ref[...] = sums
        for k, context_ref in enumerate(context_refs):
            found_ref[:, k * width : (k + 1) * width] = matmul(low, context_ref[...], TN)

    @pl.when(pl.program_id(0) > 0)
    def _():
        sum_ref[...] += sums
        for k, context_ref in enumerate(context_refs):
            found_ref[:, k * width : (k + 1) * width] += matmul(low, context_ref[...], TN)

    @pl.when(last)
    def _():
        for k, block_ref in enumerate(block_refs):
            for p in range(count):
                at = pl.ds(pl.multiple_of(owner[p] * own, own), own)
                block_ref[p] = found_ref[at, k * width : (k + 1) * width].astype(BF16)


def middle_back(terms, out_parts, context, middle, cotangent, vectors, owner):
    rows, features = middle.shape
    width = out_parts[0].shape[1]
    parts = len(out_parts)
    count = owner.shape[0]
    sums = jax.ShapeDtypeStruct((4, features), F32)
    head = jax.ShapeDtypeStruct((rows, width), BF16)
    blocks = jax.ShapeDtypeStruct((count, features // count, width), BF16)
    found = pl.pallas_call(
        functools.partial(middle_back_kernel, len(terms), parts),
        grid=(rows // TILE,),
        out_shape=[like(middle), sums] + [head] * parts + [blocks] * parts,
        in_specs=[in_smem()]
        + [tiled_spec(value) for value in terms]
        + [whole_spec(value) for value in out_parts]
        + [tiled_spec(value) for value in context]
        + [tiled_spec(middle), tiled_spec(cotangent), whole_spec(vectors)],
        out_specs=[tiled_spec(middle), whole_spec(sums)]
        + [tiled_spec(head)] * parts
        + [whole_spec(blocks)] * parts,
        scratch_shapes=[pltpu.VMEM((features, width * parts), F32)],
        compiler_params=limit(62),
        cost_estimate=cost(4 * middle.size * features, 20 * middle.size),
        name="middle_back",
    )(owner, *terms, *out_parts, *context, middle, cotangent, vectors)
    return found[0], found[1], found[2 : 2 + parts], found[2 + parts :]


def input_back_kernel(terms, *refs):
    *term_refs, first_ref, last_ref = refs[:terms]
    rows_ref, middle_ref, vector_ref, out_ref = refs[terms:]
    half = jnp.where(pl.program_id(0) == 0, first_ref[...], last_ref[...])
    grad_normed = total([ref[...].astype(F32) for ref in term_refs]) + half.astype(F32)
    unit, inverse = norm_parts(rows_ref[...].astype(F32))
    grad = norm_back(grad_normed, unit, inverse, vector_ref[0:1, :])
    out_ref[...] = (middle_ref[...].astype(F32) + grad).astype(BF16)


def input_back(terms, rows, grad_middle, vectors):
    tile = rows.shape[0] // 2
    return pl.pallas_call(
        functools.partial(input_back_kernel, len(terms)),
        grid=(2,),
        out_shape=like(rows),
        in_specs=[tiled_spec(value, tile) for value in terms[:-2]]
        + [whole_spec(value) for value in terms[-2:]]
        + [tiled_spec(rows, tile), tiled_spec(grad_middle, tile), whole_spec(vectors)],
        out_specs=tiled_spec(rows, tile),
        compiler_params=limit(62),
        cost_estimate=cost(20 * rows.size, 14 * rows.size),
        name="input_back",
    )(*terms, rows, grad_middle, vectors)


def per_device(
    tokens,
    output_cotangent,
    lengths,
    block_place,
    random_blocks,
    qkv_weight,
    out_weight,
    up_weight,
    down_weight,
    vectors,
    hidden_bias,
):
    ways = lax.axis_size("tensor")
    spread_ways = lax.axis_size("dp")
    position = lax.axis_index("tensor")
    index = lax.axis_index("dp") * ways + position
    near = tokens.shape[0]
    rows = near * ways
    features = tokens.shape[1]
    width = qkv_weight.shape[2]
    heads = width // HEAD_DIM
    units = up_weight.shape[1]
    own = features // spread_ways
    piece = vectors.shape[1]
    unit_piece = hidden_bias.shape[1]

    small = jnp.zeros((8, features), F32)
    small = lax.dynamic_update_slice(small, vectors, (0, index * piece))
    small_hidden = jnp.zeros((1, units * ways), F32)
    small_hidden = lax.dynamic_update_slice(small_hidden, hidden_bias, (0, index * unit_piece))
    packed = jnp.concatenate([small.reshape(-1), small_hidden.reshape(-1)])
    packed = summed_everywhere(packed, ("tensor",))

    unit_near = unit_rows(tokens)
    unit_near, packed = together(unit_near, packed)
    unit_far = far(unit_near, "tensor")

    facts = attention_facts(lengths[0], position, block_place, random_blocks)

    bits = bits_of("dp")
    order_a = bits[::-1]
    order_b = bits[-1:] + bits[:1] + bits[-2:0:-1]
    owner_a = block_owners("dp", order_a)
    owner_b = block_owners("dp", order_b)
    split = 2 * width
    qkv_flat = qkv_weight.reshape(own, 3 * width)
    first_blocks = doubled(qkv_flat[:, :split], "dp", order_a)
    last_flat = jnp.concatenate([qkv_flat[:, split:], out_weight], axis=1)
    last_blocks = doubled(last_flat, "dp", order_b)
    packed = summed_everywhere(packed, ("dp",))
    feed_flat = jnp.concatenate([up_weight, down_weight], axis=1)
    piece_rows = near // 4
    first_going, next_going = output_cotangent[:piece_rows], output_cotangent[piece_rows:]
    next_going, last_going = next_going[:piece_rows], next_going[piece_rows:]
    first_going, unit_far = together(first_going, unit_far)
    cotangent_first = far(first_going, "tensor")
    feed_flat, first_blocks, last_blocks, packed, cotangent_first, next_going = together(
        feed_flat, first_blocks, last_blocks, packed, cotangent_first, next_going
    )
    cotangent_next = far(next_going, "tensor")
    feed_full = lax.all_gather(feed_flat, "dp", axis=0, tiled=True)
    unit_parts = gathered_parts(unit_near, unit_far, "tensor")

    vectors_full = packed[: 8 * features].reshape(8, features)
    hidden_full = packed[8 * features :]
    bias_query = lax.dynamic_slice_in_dim(vectors_full[6], position * width, width)
    bias_value = lax.dynamic_slice_in_dim(vectors_full[7], position * width, width)
    bias_qkv = jnp.concatenate([bias_query, jnp.zeros_like(bias_query), bias_value])[None]
    bias_hidden = lax.dynamic_slice_in_dim(hidden_full, position * units, units)[None]
    norm_one = vectors_full[:2]
    norm_two = jnp.stack([vectors_full[4], vectors_full[2], vectors_full[3]])


    last_blocks, cotangent_next = together(last_blocks, cotangent_next)
    out_group = placed_rows(last_blocks, owner_b, width)
    out_far = far(out_group, "tensor")
    last_going, out_group = together(last_going, out_group)
    cotangent_last = far(last_going, "tensor")
    *context, qkv, qkv_full, log_totals = project_attend(
        unit_parts,
        first_blocks,
        last_blocks,
        owner_a,
        owner_b,
        norm_one,
        bias_qkv,
        facts,
        heads,
    )
    context = context[0]
    *context, out_far, cotangent_last = together(*context, out_far, cotangent_last)
    cotangent_far = jnp.concatenate([cotangent_first, cotangent_next, cotangent_last], axis=0)
    grad_parts = gathered_parts(output_cotangent, cotangent_far, "tensor")

    out_parts = gathered_parts(out_group, out_far, "tensor")
    context_near = exchanged_parts(context, "tensor")
    middle, normed_two = middle_rows(context_near, out_parts, tokens, norm_two)

    half = ways // 2
    normed_far = far(normed_two, "tensor")
    normed_parts = gathered_parts(normed_two, normed_far, "tensor")
    near_back, near_out, stacks = feed(
        normed_parts[:half], grad_parts[:half], feed_full, bias_hidden, (), 0, ways
    )
    normed_far, *stacks = together(normed_far, *stacks)
    normed_parts = gathered_parts(normed_two, normed_far, "tensor")
    far_back, far_out, stacks = feed(
        normed_parts[half:], grad_parts[half:], feed_full, bias_hidden, stacks, half, ways
    )
    back_parts, feed_parts = near_back + far_back, near_out + far_out
    back_terms, far_sum = summed_halves(back_parts, "tensor")
    back_terms.append(far(far_sum, "tensor"))
    feed_sums, sum_hidden = feed_grads(stacks)
    feed_terms, feed_far = summed_halves(feed_parts, "tensor")
    early, late_rows = feed_far[: near // 2], feed_far[near // 2 :]
    feed_weight_grads = lax.psum_scatter(feed_sums, "dp", scatter_dimension=0, tiled=True)
    feed_weight_grads = feed_weight_grads.astype(F32)
    *back_terms, sum_hidden, early = together(*back_terms, sum_hidden, early)
    early = far(early, "tensor")

    grad_middle, sums_two, grad_heads, out_blocks = middle_back(
        back_terms, out_parts, context_near, middle, output_cotangent, norm_two, owner_b
    )
    grad_context = exchanged_parts(grad_heads, "tensor")

    *out_blocks, early = together(*out_blocks, early)
    out_terms, out_far = summed_halves(out_blocks, "tensor")
    *grad_context, out_far, late_rows = together(*grad_context, out_far, late_rows)
    out_terms.append(far(out_far, "tensor"))
    late_rows = far(late_rows, "tensor")
    first_keep, first_send, last_keep, last_send, *back_parts, late, sum_qkv = attend_back(
        qkv,
        grad_context,
        log_totals,
        unit_parts,
        qkv_full,
        owner_a,
        owner_b,
        split,
        facts,
        heads,
    )
    first_send, last_send, late, late_rows, *rest = together(
        first_send, last_send, late, late_rows, *out_terms, *back_parts
    )
    out_terms, back_parts = rest[: len(out_terms)], rest[len(out_terms) :]
    near_rows, far_rows = back_parts[:half], back_parts[half:]
    feed_terms.append(jnp.concatenate([early, late_rows], axis=0))
    output = total([term.astype(F32) for term in (*feed_terms, middle)]) + vectors_full[5]
    output = output.astype(BF16)
    out_sums = total([term.astype(F32) for term in out_terms]).astype(BF16)
    last_keep = jnp.concatenate([last_keep, out_sums[: spread_ways // 2]], axis=2)
    last_send = jnp.concatenate([last_send, out_sums[spread_ways // 2 :]], axis=2)
    head_sums = lax.dynamic_update_slice(
        jnp.zeros((3, features), F32), sum_qkv.reshape(3, width), (0, position * width)
    )
    hidden_sums = lax.dynamic_update_slice(
        jnp.zeros((1, units * ways), F32), sum_hidden, (0, position * units)
    )
    packed = jnp.concatenate(
        [late.reshape(-1), sums_two.reshape(-1), head_sums.reshape(-1), hidden_sums.reshape(-1)]
    )
    packed = summed_everywhere(packed, ("dp",))
    far_sum = added(far_rows[0], swapped(far_rows[1], "tensor", 1))
    far_sum, first_keep, last_keep, *near_rows = together(
        far_sum, first_keep, last_keep, *near_rows
    )
    far_first = far(far_sum[: near // 2], "tensor")
    far_last = far(far_sum[near // 2 :], "tensor")
    first_keep, first_send = halved(first_keep, first_send, "dp", order_a)
    last_keep, last_send = halved(last_keep, last_send, "dp", order_b)
    first_send, last_send, far_first = together(first_send, last_send, far_first)
    while first_send.shape[0] > 1:
        first_keep, first_send = halved(first_keep, first_send, "dp", order_a)
        last_keep, last_send = halved(last_keep, last_send, "dp", order_b)
    first_send, last_send, far_last, output = together(first_send, last_send, far_last, output)
    near_terms = [near_rows[0], swapped(near_rows[1], "tensor", 1), far_first, far_last]
    input_grad = input_back(near_terms, tokens, grad_middle, norm_one)
    first_keep, last_keep, input_grad, packed = together(
        first_keep, last_keep, input_grad, packed
    )
    first_raw = halved(first_keep, first_send, "dp", order_a)[0][0].astype(F32)
    last_raw = halved(last_keep, last_send, "dp", order_b)[0][0].astype(F32)
    out_weight_grad = last_raw[:, width:]
    last_raw = last_raw[:, :width]

    packed = summed_everywhere(packed, ("tensor",), direct=True)
    by_feature = packed[: 9 * features].reshape(9, features)
    hidden_sums = packed[9 * features :]
    vectors_grad = lax.dynamic_slice_in_dim(by_feature, index * piece, piece, axis=1)
    vectors_grad = jnp.concatenate([vectors_grad[:7], vectors_grad[8:]], axis=0)
    hidden_bias_grad = lax.dynamic_slice_in_dim(hidden_sums, index * unit_piece, unit_piece)

    sum_qkv = lax.dynamic_slice_in_dim(by_feature[6:], position * width, width, axis=1)
    mine = lax.dynamic_slice_in_dim(norm_one, lax.axis_index("dp") * own, own, axis=1)
    raw = jnp.concatenate([first_raw, last_raw], axis=1).reshape(own, 3, width)
    qkv_weight_grad = mine[0][:, None, None] * raw + mine[1][:, None, None] * sum_qkv
    return (
        output,
        input_grad,
        qkv_weight_grad,
        out_weight_grad,
        feed_weight_grads[:, :units],
        feed_weight_grads[:, units:],
        vectors_grad,
        hidden_bias_grad[None, :],
    )


def solution(mesh):
    placed = (
        P(("dp", "tensor"), None),
        P(("dp", "tensor"), None),
        P("dp"),
        P("dp", None),
        P("dp", "tensor", None, None),
        P("dp", None, "tensor"),
        P("dp", "tensor"),
        P("dp", "tensor"),
        P("dp", "tensor"),
        P(None, ("dp", "tensor")),
        P(None, ("dp", "tensor")),
    )
    return jax.shard_map(
        per_device,
        mesh=mesh,
        in_specs=placed,
        out_specs=(
            P(("dp", "tensor"), None),
            P(("dp", "tensor"), None),
            P("dp", None, "tensor"),
            P("dp", "tensor"),
            P("dp", "tensor"),
            P("dp", "tensor"),
            P(None, ("dp", "tensor")),
            P(None, ("dp", "tensor")),
        ),
        check_vma=False,
    )
```
